32 devices in a mesh: fsdp: 8 (over y, x, core), tp: 4 (over z).
Axes of the slice: x: 2, y: 2, z: 4, core: 2. Of those that a mesh axis runs over, the one named last changes fastest.
Arguments:
- hidden_in: bfloat16 [2, 8, 1024, 2048], P(None, 'fsdp', 'tp'), may hold values from -6 to 6
- segment_ids: int32 [2, 8, 1024], P(None, 'fsdp'), may hold values from 0 to 15, never falling along the last dimension, each value on 1 to 512 neighbouring positions
- cotangent: bfloat16 [2, 8, 1024, 2048], P(None, 'fsdp', 'tp'), may hold values from -6 to 6
- norm_gain: float32 [2048], replicated, may hold values from 0.5 to 1.5
- proj_gate: bfloat16 [2048, 4096], P('fsdp', 'tp'), may hold values from -0.125 to 0.125
- proj_value: bfloat16 [2048, 4096], P('fsdp', 'tp'), may hold values from -0.125 to 0.125
- proj_state: bfloat16 [2048, 256], P('fsdp'), may hold values from -0.125 to 0.125
- proj_step: bfloat16 [2048, 64], P('fsdp', 'tp'), may hold values from -0.125 to 0.125
- conv_value: float32 [4, 4096], P(None, 'tp'), may hold values from -3 to 3
- conv_value_bias: float32 [4096], P('tp'), may hold values from -3 to 3
- conv_state: float32 [4, 256], replicated, may hold values from -3 to 3
- conv_state_bias: float32 [256], replicated, may hold values from -3 to 3
- step_bias: float32 [64], P('tp'), may hold values from -7 to -3
- decay_log: float32 [64], P('tp'), may hold values from -1.5 to 1.5
- skip_gain: float32 [64], P('tp'), may hold values from 0.5 to 1.5
- gate_gain: float32 [4096], P('tp'), may hold values from 0.25 to 1.75
- proj_out: bfloat16 [4096, 2048], P('tp', 'fsdp'), may hold values from -0.09375 to 0.09375
Outputs:
- block_out: bfloat16 [2, 8, 1024, 2048], P(None, 'fsdp', 'tp')
- grad_hidden: bfloat16 [2, 8, 1024, 2048], P(None, 'fsdp', 'tp')
- grad_norm_gain: float32 [2048], replicated
- grad_proj_gate: float32 [2048, 4096], P('fsdp', 'tp')
- grad_proj_value: float32 [2048, 4096], P('fsdp', 'tp')
- grad_proj_state: float32 [2048, 256], P('fsdp')
- grad_proj_step: float32 [2048, 64], P('fsdp', 'tp')
- grad_conv_value: float32 [4, 4096], P(None, 'tp')
- grad_conv_value_bias: float32 [4096], P('tp')
- grad_conv_state: float32 [4, 256], replicated
- grad_conv_state_bias: float32 [256], replicated
- grad_step_bias: float32 [64], P('tp')
- grad_decay_log: float32 [64], P('tp')
- grad_skip_gain: float32 [64], P('tp')
- grad_gate_gain: float32 [4096], P('tp')
- grad_proj_out: float32 [4096, 2048], P('tp', 'fsdp')
The draws below stay inside these ranges and needn't reach their ends.
Inputs may be any that keep to these rules, and one draw needn't show every extreme that they name: `segment_ids`: ids of the documents packed in each sequence, from 0 and never falling; a document starts where the id changes; each sequence holds 16 documents, one of exactly 512 tokens.
All inputs are finite; a program needn't handle non-finite values.
Results may differ from the reference program's by a relative error of at most 0.019.
Values may be sent and summed in bfloat16 or wider, within the bound.
A program may use at most 96 MiB of HBM per device.

```python
import math
import jax
import jax.numpy as jnp
import numpy as np
from jax import lax

MODEL = 2048
HEADS = 64
HEAD_DIM = 64
STATE = 128
CONV = 4
GROUP = 256
LENGTH = 1024
MICRO = 2
INNER = 4096
SEQS = 8
DOCS = 16
LONGEST = 512


def block_scale(key, dims, shards, least, high):
    level = 1.0
    for axis_at, blocks in shards:
        draws = jax.random.uniform(jax.random.fold_in(jax.random.fold_in(key, 6), axis_at), (blocks,), jnp.float32, least / len(shards), high / len(shards))
        level = level * jnp.repeat(jnp.exp(draws), dims[axis_at] // blocks).reshape((-1,) + (1,) * (len(dims) - 1 - axis_at))
    return level


def profile(amount, total, most, skew):
    loads = [(1 << 20) // math.isqrt(rank ** skew) + 1 for rank in range(2, amount + 1)]
    rest, given = total - most - (amount - 1), [1] * (amount - 1)
    while rest > 0:
        candidates = [i for i in range(amount - 1) if given[i] < most]
        whole, remaining = sum([loads[i] for i in candidates]), rest
        for i in candidates:
            more = min(most - given[i], max(1, remaining * loads[i] // whole), rest)
            given[i] = given[i] + more
            rest = rest - more
    return np.array([most] + given)


def ragged_sizes(own_key, number_of, total, most, lean):
    if number_of == 2:
        one = jax.random.randint(own_key, (), max(1, total - most), min(most, total - 1) + 1)
        return jnp.stack([one, total - one])
    sizes = jnp.asarray(profile(number_of, total, most, lean), jnp.int32)
    twos = (number_of - 1) // 2
    giver, receiver = sizes[1:1 + 2 * twos:2], sizes[2:2 + 2 * twos:2]
    margin = jnp.minimum(giver - 1, most - receiver)
    passed = jax.random.randint(jax.random.fold_in(own_key, 1), (twos,), 0, 1 << 20) % (margin + 1)
    sizes = sizes.at[1:1 + 2 * twos:2].set(giver - passed).at[2:2 + 2 * twos:2].set(receiver + passed)
    return sizes[jax.random.permutation(jax.random.fold_in(own_key, 2), number_of)]


def noise(rng, shape, scale, reach, cuts=(), kind=jnp.bfloat16):
    array = scale * jax.random.normal(rng, shape, jnp.float32)
    if cuts:
        array = array * block_scale(rng, shape, cuts, -0.22, 0.18)
    return jnp.clip(array, -reach, reach).astype(kind)


def setup_inputs(seed: int = 0) -> dict:
    streams_of = jax.random.split(jax.random.key(seed), 18)
    hidden_in = noise(streams_of[0], (MICRO, SEQS, LENGTH, MODEL), 1.0, 6.0, ((1, 8), (2, 4)))
    segment_ids = jax.vmap(lambda own: jnp.searchsorted(jnp.cumsum(ragged_sizes(own, DOCS, LENGTH, LONGEST, 2)), jnp.arange(LENGTH), side="right"))(jax.random.split(streams_of[1], MICRO * SEQS)).reshape((MICRO, SEQS, LENGTH)).astype(jnp.int32)
    cotangent = noise(streams_of[2], (MICRO, SEQS, LENGTH, MODEL), 1.0, 6.0, ((1, 8), (2, 4)))
    norm_gain = jnp.clip(1.0 + 0.1 * jax.random.normal(streams_of[3], (MODEL,), jnp.float32), 0.5, 1.5)
    proj_gate = noise(streams_of[4], (MODEL, INNER), MODEL ** -0.5, 0.125, ((0, 8), (1, 4)))
    proj_value = noise(streams_of[5], (MODEL, INNER), MODEL ** -0.5, 0.125, ((0, 8), (1, 4)))
    proj_state = noise(streams_of[6], (MODEL, 2 * STATE), MODEL ** -0.5, 0.125, ((0, 8),))
    proj_step = noise(streams_of[7], (MODEL, HEADS), MODEL ** -0.5, 0.125, ((0, 8), (1, 4)))
    conv_value = noise(streams_of[8], (CONV, INNER), 0.5, 3.0, ((1, 4),), jnp.float32)
    conv_value_bias = noise(streams_of[9], (INNER,), 0.5, 3.0, ((0, 4),), jnp.float32)
    conv_state = noise(streams_of[10], (CONV, 2 * STATE), 0.5, 3.0, (), jnp.float32)
    conv_state_bias = noise(streams_of[11], (2 * STATE,), 0.5, 3.0, (), jnp.float32)
    step_bias = jnp.clip(-7.0 + 4.0 * jax.random.uniform(streams_of[12], (HEADS,), jnp.float32) ** block_scale(streams_of[12], (HEADS,), ((0, 4),), -0.2, 0.2), -7.0, -3.0)
    decay_log = jnp.clip(jax.random.uniform(streams_of[13], (HEADS,), jnp.float32, -1.5, 1.5) * block_scale(streams_of[13], (HEADS,), ((0, 4),), -0.4, 0.0), -1.5, 1.5)
    skip_gain = jnp.clip(0.5 + 1.0 * jax.random.uniform(streams_of[14], (HEADS,), jnp.float32) ** block_scale(streams_of[14], (HEADS,), ((0, 4),), -0.2, 0.2), 0.5, 1.5)
    gate_gain = jnp.clip(1.0 + 0.15 * jax.random.normal(streams_of[15], (INNER,), jnp.float32), 0.25, 1.75)
    proj_out = noise(streams_of[16], (INNER, MODEL), INNER ** -0.5, 0.09375, ((0, 4), (1, 8)))
    return dict(hidden_in=hidden_in, segment_ids=segment_ids, cotangent=cotangent, norm_gain=norm_gain, proj_gate=proj_gate, proj_value=proj_value, proj_state=proj_state, proj_step=proj_step, conv_value=conv_value, conv_value_bias=conv_value_bias, conv_state=conv_state, conv_state_bias=conv_state_bias, step_bias=step_bias, decay_log=decay_log, skip_gain=skip_gain, gate_gain=gate_gain, proj_out=proj_out)


EPSILON = 1e-05
PRECISE = lax.Precision.HIGHEST

@jax.custom_vjp
def low(v):
    return lax.optimization_barrier(v.astype(jnp.bfloat16)).astype(jnp.float32)

@jax.custom_vjp
def low_back(v):
    return v

def low_keep(v):
    return (low(v), None)

def low_pass(kept, grad):
    return (grad,)

def back_keep(v):
    return (v, None)

def back_low(kept, grad):
    return (low(grad),)
low.defvjp(low_keep, low_pass)
low_back.defvjp(back_keep, back_low)

def matmul_high(former, latter):
    return jnp.dot(former, latter, precision=PRECISE, preferred_element_type=jnp.float32)

def causal_conv(values, kernel, bias, seg_row):
    summed = bias[None, :] + kernel[0][None, :] * values
    for offset in range(1, CONV):
        moved = jnp.pad(values, ((offset, 0), (0, 0)))[:values.shape[0]]
        before = jnp.pad(seg_row, (offset, 0), constant_values=-1)[:seg_row.shape[0]]
        summed = summed + kernel[offset][None, :] * moved * (before == seg_row).astype(jnp.float32)[:, None]
    return summed

def ssd_group(hidden, piece, rate_neg):
    x_values, b_values, c_values, step_size, seg_row, previous = piece
    width = seg_row.shape[0]
    cumulated = jnp.cumsum(step_size * rate_neg[None, :], axis=0)
    final_cum = cumulated[-1]
    positions = jnp.arange(width)
    within = (positions[:, None] >= positions[None, :]) & (seg_row[:, None] == seg_row[None, :])
    within_f = within.astype(jnp.float32)[None]
    decays = jnp.exp(jnp.where(within[None], cumulated.T[:, :, None] - cumulated.T[:, None, :], 0.0)) * within_f
    inner_cb = low_back(matmul_high(c_values, b_values.T))
    mixing = low(inner_cb[None] * decays * step_size.T[:, None, :])
    intra = jnp.einsum('hts,shp->thp', mixing, x_values, precision=PRECISE)
    entering = jnp.exp(cumulated) * (seg_row == previous).astype(jnp.float32)[:, None]
    entry_low = low(entering.T[:, :, None] * c_values[None])
    carried = jnp.einsum('htn,hnp->thp', entry_low, low(hidden), precision=PRECISE)
    at_end = (seg_row == seg_row[-1]).astype(jnp.float32)[:, None]
    weights = jnp.exp(final_cum[None, :] - cumulated) * at_end * step_size
    weighted = low(weights[:, :, None] * x_values)
    own_state = low_back(jnp.einsum('sn,shp->hnp', b_values, weighted, precision=PRECISE))
    retain = jnp.exp(final_cum) * (seg_row[-1] == previous).astype(jnp.float32)
    return (retain[:, None, None] * hidden + own_state, intra + carried)

def forward(params, tokens, seg_row):
    norm_gain, proj_gate, proj_value, proj_state, proj_step, conv_value, conv_value_bias, conv_state, conv_state_bias, step_bias, decay_log, skip_gain, gate_gain, proj_out = params
    length = tokens.shape[0]
    normed = tokens * lax.rsqrt(lax.optimization_barrier(jnp.mean(tokens * tokens, axis=-1, keepdims=True)) + EPSILON) * norm_gain[None, :]
    inputs = low(normed)
    gate_raw = low_back(matmul_high(inputs, proj_gate))
    value_raw = low_back(matmul_high(inputs, proj_value))
    state_raw = low_back(matmul_high(inputs, proj_state))
    step_raw = low_back(matmul_high(inputs, proj_step))
    x_values = low(jax.nn.silu(causal_conv(value_raw, conv_value, conv_value_bias, seg_row)))
    bc_values = low(jax.nn.silu(causal_conv(state_raw, conv_state, conv_state_bias, seg_row)))
    b_values = bc_values[:, :STATE]
    c_values = bc_values[:, STATE:]
    step_size = jax.nn.softplus(step_raw + step_bias[None, :])
    rate_neg = -jnp.exp(decay_log)
    head_view = x_values.reshape(length, HEADS, HEAD_DIM)
    group_count = length // GROUP
    previous = jnp.concatenate([jnp.full((1,), -1, seg_row.dtype), seg_row[GROUP - 1:-1:GROUP]])
    pieces = (head_view.reshape(group_count, GROUP, HEADS, HEAD_DIM), b_values.reshape(group_count, GROUP, STATE), c_values.reshape(group_count, GROUP, STATE), step_size.reshape(group_count, GROUP, HEADS), seg_row.reshape(group_count, GROUP), previous)
    group_step = jax.checkpoint(lambda hidden, piece: ssd_group(hidden, piece, rate_neg))
    start_state = jnp.zeros((HEADS, STATE, HEAD_DIM), jnp.float32)
    _, scan_outs = lax.scan(group_step, start_state, pieces)
    scanned = low_back(scan_outs.reshape(length, HEADS, HEAD_DIM))
    mixed = scanned + skip_gain[None, :, None] * head_view
    gated = mixed.reshape(length, HEADS * HEAD_DIM) * jax.nn.silu(gate_raw)
    scaling = lax.rsqrt(lax.optimization_barrier(jnp.mean(gated * gated, axis=-1, keepdims=True)) + EPSILON)
    branch = low(gated * scaling * gate_gain[None, :])
    return tokens + matmul_high(branch, proj_out)

def reference(hidden_in, segment_ids, cotangent, norm_gain, proj_gate, proj_value, proj_state, proj_step, conv_value, conv_value_bias, conv_state, conv_state_bias, step_bias, decay_log, skip_gain, gate_gain, proj_out):
    params = (norm_gain, proj_gate.astype(jnp.float32), proj_value.astype(jnp.float32), proj_state.astype(jnp.float32), proj_step.astype(jnp.float32), conv_value, conv_value_bias, conv_state, conv_state_bias, step_bias, decay_log, skip_gain, gate_gain, proj_out.astype(jnp.float32))
    flat_tokens = hidden_in.reshape(-1, LENGTH, MODEL).astype(jnp.float32)
    flat_segs = segment_ids.reshape(-1, LENGTH)
    flat_cotan = cotangent.reshape(-1, LENGTH, MODEL).astype(jnp.float32)

    def one_sequence(grad_total, seq_item):
        tokens, seg_row, cotan_row = seq_item
        block_value, pullback = jax.vjp(lambda param_set, values: forward(param_set, values, seg_row), params, tokens)
        grad_params, grad_tokens = pullback(cotan_row)
        grad_total = jax.tree.map(lambda former, latter: former + latter, grad_total, grad_params)
        return (grad_total, (block_value, grad_tokens))
    zero_grads = jax.tree.map(jnp.zeros_like, params)
    grad_total, (block_values, grad_values) = lax.scan(one_sequence, zero_grads, (flat_tokens, flat_segs, flat_cotan))
    block_out = block_values.reshape(hidden_in.shape).astype(jnp.bfloat16)
    grad_hidden = grad_values.reshape(hidden_in.shape).astype(jnp.bfloat16)
    return (block_out, grad_hidden, grad_total[0], grad_total[1], grad_total[2], grad_total[3], grad_total[4], grad_total[5], grad_total[6], grad_total[7], grad_total[8], grad_total[9], grad_total[10], grad_total[11], grad_total[12], grad_total[13])
```

```python
from functools import partial

import jax
import jax.numpy as jnp
from jax import lax
from jax.experimental import pallas as pl
from jax.experimental.pallas import tpu as pltpu
from jax.sharding import PartitionSpec as P

HEAD_DIM = 64
STATE = 128
CONV = 4
GROUP = 256
HALF = GROUP // 2
BLOCK = 256
PER_BLOCK = BLOCK // HEAD_DIM
HALO = 8
INNER = 4096
EPSILON = 1e-05
PRECISE = lax.Precision.HIGHEST
F32 = jnp.float32
BF16 = jnp.bfloat16


def mm(former, latter, precision=None):
    return jnp.dot(former, latter, preferred_element_type=F32, precision=precision)


def mm_nt(former, latter):
    return lax.dot_general(
        former, latter, (((1,), (1,)), ((), ())), preferred_element_type=F32
    )


def mm_tn(former, latter):
    return lax.dot_general(
        former, latter, (((0,), (0,)), ((), ())), preferred_element_type=F32
    )


def iota(shape, axis):
    return lax.broadcasted_iota(jnp.int32, shape, axis)


def expand(columns):
    rows = columns.shape[0]
    lane = iota((rows, 128), 1)
    parts = []
    for pair in range(PER_BLOCK // 2):
        former = jnp.broadcast_to(columns[:, 2 * pair : 2 * pair + 1], (rows, 128))
        latter = jnp.broadcast_to(columns[:, 2 * pair + 1 : 2 * pair + 2], (rows, 128))
        parts.append(jnp.where(lane < HEAD_DIM, former, latter))
    return jnp.concatenate(parts, axis=1)


def lane_mask(head):
    lane = iota((1, BLOCK), 1)
    return ((lane // HEAD_DIM) == head).astype(F32).astype(BF16)


def spread(ref, values, blocks):
    for block in range(blocks):
        shift = (128 - PER_BLOCK * block) % 128
        ref[block] = pltpu.roll(values, shift, 1) if shift else values


def token_quantities(step_in, cums, cols, decay_rate):
    step = jnp.maximum(step_in, 0.0) + jnp.log1p(jnp.exp(-jnp.abs(step_in)))
    final = cums[GROUP - 1 : GROUP, :]
    entering = jnp.exp(cums) * cols[:, 6:7]
    fading = jnp.exp(final - cums) * cols[:, 7:8]
    retain = jnp.exp(final) * cols[0:1, 8:9]
    return step, entering, fading, retain


def shifted_values(buf, cols):
    moved = [buf[HALO : HALO + GROUP, :]]
    for offset in range(1, CONV):
        before = buf[HALO - offset : HALO - offset + GROUP, :]
        moved.append(jnp.where(cols[:, offset - 1 : offset] > 0.0, before, 0.0))
    return moved


def conv_of(moved, taps, bias):
    total = bias + taps[0:1, :] * moved[0]
    for offset in range(1, CONV):
        total = total + taps[offset : offset + 1, :] * moved[offset]
    return total


def forward_kernel(
    in_ref, gate_w, value_w, state_w, step_w, taps_ref, bias_ref, staps_ref, sbias_ref,
    step_bias_ref, rate_ref, skip_ref, cols_ref, seg_ref,
    gate_out, value_out, mixed_out, bc_out, sraw_out, stepin_out, cums_out, held_out,
    vbuf, sbuf, gram_s, b_t, c_s, step_s, ent_s, fade_s, cums_s, cums_t, keep_s, hidden,
):
    g, j = pl.program_id(0), pl.program_id(1)
    blocks = pl.num_programs(1)
    nblocks = hidden.shape[0]
    rows = in_ref[...]
    cols = cols_ref[...]

    @pl.when(j == 0)
    def _():
        sbuf[0:HALO, :] = sbuf[GROUP : GROUP + HALO, :]
        raw = mm(rows, state_w[...])
        sbuf[HALO : HALO + GROUP, :] = raw
        sraw_out[...] = raw
        conv = conv_of(shifted_values(sbuf, cols), staps_ref[...], sbias_ref[...])
        bc = (conv * jax.nn.sigmoid(conv)).astype(BF16)
        bc_out[...] = bc
        b_low, c_low = bc[:, :STATE], bc[:, STATE:]
        b_t[...] = jnp.transpose(b_low.astype(F32)).astype(BF16)
        c_s[...] = c_low
        step_in = mm(rows, step_w[...]) + step_bias_ref[...]
        stepin_out[...] = step_in
        step = jnp.maximum(step_in, 0.0) + jnp.log1p(jnp.exp(-jnp.abs(step_in)))
        at_row, at_col = iota((GROUP, GROUP), 0), iota((GROUP, GROUP), 1)
        lower = (at_row >= at_col).astype(F32)
        cums = mm(lower, step * rate_ref[...], PRECISE)
        cums_out[...] = cums
        step, entering, fading, retain = token_quantities(step_in, cums, cols, rate_ref[...])
        spread(step_s, step, nblocks)
        spread(ent_s, entering, nblocks)
        spread(fade_s, fading, nblocks)
        spread(cums_s, cums, nblocks)
        spread(keep_s, jnp.broadcast_to(retain, (8, 128)), nblocks)
        cums_t[...] = jnp.transpose(cums)
        within = (at_row >= at_col) & (cols[:, 9:10] == seg_ref[...])
        gram_s[...] = jnp.where(within, mm_nt(c_low, b_low), 0.0)

    at = pl.multiple_of(j * BLOCK, BLOCK)
    gate_out[...] = mm(rows, gate_w[:, pl.ds(at, BLOCK)]).astype(BF16)
    value = mm(rows, value_w[:, pl.ds(at, BLOCK)])
    value_out[...] = value
    mine = vbuf.at[j]
    mine[0:HALO, :] = mine[GROUP : GROUP + HALO, :]
    mine[HALO : HALO + GROUP, :] = value
    conv = conv_of(shifted_values(mine, cols), taps_ref[...], bias_ref[...])
    x_low = (conv * jax.nn.sigmoid(conv)).astype(BF16)
    x_float = x_low.astype(F32)
    scaled_float = expand(step_s[j]) * x_float
    scaled = scaled_float.astype(BF16)

    @pl.when(g == 0)
    def _():
        hidden[j] = jnp.zeros((STATE, BLOCK), F32)

    state = hidden[j]
    held_out[0] = state
    total = expand(ent_s[j]) * mm(c_s[...], state.astype(BF16))
    weighted = (expand(fade_s[j]) * scaled.astype(F32)).astype(BF16)
    hidden[j] = expand(keep_s[j])[0:1, :] * state + mm(b_t[...], weighted)
    cums_here = cums_s[j]
    top = jnp.zeros((HALF, BLOCK), F32)
    bottom = jnp.zeros((HALF, BLOCK), F32)
    for i in range(PER_BLOCK):
        to = cums_here[:, i : i + 1]
        frm = cums_t[pl.ds(j * PER_BLOCK + i, 1), :]
        only = scaled * lane_mask(i)
        decay = jnp.exp(jnp.minimum(to[:HALF] - frm[:, :HALF], 0.0))
        top = top + mm((gram_s[:HALF, :HALF] * decay).astype(BF16), only[:HALF])
        decay = jnp.exp(jnp.minimum(to[HALF:] - frm, 0.0))
        bottom = bottom + mm((gram_s[HALF:, :] * decay).astype(BF16), only)
    mixed_out[...] = total + jnp.concatenate([top, bottom], axis=0) + skip_ref[...] * x_float


def branch_kernel(cot_ref, out_w, gate_ref, mixed_ref, gain_ref, grad_out, stats_out):
    grad = mm_nt(cot_ref[...], out_w[...])
    grad_out[...] = grad.astype(BF16)
    gate = gate_ref[...].astype(F32)
    gated = mixed_ref[...] * (gate * jax.nn.sigmoid(gate))
    squares = jnp.sum(gated * gated, axis=1, keepdims=True)
    inner = jnp.sum(grad * gain_ref[...] * gated, axis=1, keepdims=True)
    lane = iota((GROUP, 128), 1)
    stats_out[...] = jnp.where(lane == 0, squares, jnp.where(lane == 1, inner, 0.0))


def backward_kernel(
    gate_ref, value_ref, before_ref, mixed_ref, grad_ref, bc_ref, stepin_ref, cums_ref, held_ref,
    stats_ref, gate_w, value_w, out_w, step_w, taps_ref, bias_ref, rate_ref, skip_ref, gain_ref,
    cols_ref, seg_ref,
    branch_out, lowgate_out, lowvalue_out, lowstep_out, gbc_out, made_out, gin_out, small_out, sums_out,
    vbuf, gcbuf, gram_s, dgram, b_s, c_t, step_s, ent_s, fade_s, cums_s, cums_t, keep_s, grad_state,
    made, gin, gb_s, gc_s, u_s, v_s, fin_s, small_s, sums_s,
):
    g, j = pl.program_id(0), pl.program_id(1)
    groups, blocks = pl.num_programs(0), pl.num_programs(1)
    nblocks = grad_state.shape[0]
    cols = cols_ref[...]
    at_row, at_col = iota((GROUP, GROUP), 0), iota((GROUP, GROUP), 1)

    @pl.when((g == 0) & (j == 0))
    def _():
        grad_state[...] = jnp.zeros(grad_state.shape, F32)
        small_s[...] = jnp.zeros(small_s.shape, F32)
        sums_s[...] = jnp.zeros(sums_s.shape, F32)
        gcbuf[...] = jnp.zeros(gcbuf.shape, F32)

    @pl.when(j == 0)
    def _():
        bc = bc_ref[...]
        b_low, c_low = bc[:, :STATE], bc[:, STATE:]
        b_s[...] = b_low
        c_t[...] = jnp.transpose(c_low.astype(F32)).astype(BF16)
        cums = cums_ref[...]
        step, entering, fading, retain = token_quantities(stepin_ref[...], cums, cols, rate_ref[...])
        spread(step_s, step, nblocks)
        spread(ent_s, entering, nblocks)
        spread(fade_s, fading, nblocks)
        spread(cums_s, cums, nblocks)
        spread(keep_s, jnp.broadcast_to(retain, (8, 128)), nblocks)
        cums_t[...] = jnp.transpose(cums)
        within = (at_row <= at_col) & (cols[:, 9:10] == seg_ref[...])
        gram_s[...] = jnp.where(within, mm_nt(b_low, c_low), 0.0)
        dgram[...] = jnp.zeros(dgram.shape, F32)
        made[...] = jnp.zeros(made.shape, F32)
        gin[...] = jnp.zeros(gin.shape, F32)
        gb_s[...] = jnp.zeros(gb_s.shape, F32)
        gc_s[...] = jnp.zeros(gc_s.shape, F32)
        u_s[...] = jnp.zeros(u_s.shape, F32)
        v_s[...] = jnp.zeros(v_s.shape, F32)
        fin_s[...] = jnp.zeros(fin_s.shape, F32)

    at = pl.multiple_of(j * BLOCK, BLOCK)
    gate, mixed, grad = gate_ref[...].astype(F32), mixed_ref[...], grad_ref[...].astype(F32)
    gain, skip, taps = gain_ref[...], skip_ref[...], taps_ref[...]
    scale = stats_ref[:, 0:1]
    inner = stats_ref[:, 1:2]
    sig = jax.nn.sigmoid(gate)
    act = gate * sig
    gated = mixed * act
    scaled_gated = gated * scale
    branch = (scaled_gated * gain).astype(BF16)
    branch_out[...] = branch
    made[...] += mm(branch, out_w[pl.ds(at, BLOCK), :])
    grad_gain = jnp.sum(grad * scaled_gated, axis=0, keepdims=True)
    grad_gated = scale * (grad * gain) - gated * inner
    grad_mixed = grad_gated * act
    low_gate = (grad_gated * mixed * (sig * (1.0 + gate * (1.0 - sig)))).astype(BF16)
    lowgate_out[...] = low_gate

    vbuf[0:HALO, :] = before_ref[...]
    vbuf[HALO : HALO + GROUP, :] = value_ref[...]
    moved = shifted_values(vbuf, cols)
    conv = conv_of(moved, taps, bias_ref[...])
    sig = jax.nn.sigmoid(conv)
    x_float = (conv * sig).astype(BF16).astype(F32)
    slope = sig * (1.0 + conv * (1.0 - sig))
    step_wide = expand(step_s[j])
    fade_wide = expand(fade_s[j])
    scaled = (step_wide * x_float).astype(BF16)
    scaled_float = scaled.astype(F32)
    grad_skip = jnp.sum(grad_mixed * x_float, axis=0, keepdims=True)
    grad_scan = grad_mixed.astype(BF16)
    grad_scan_float = grad_scan.astype(F32)
    scanned = mixed - skip * x_float

    own = grad_state[j]
    state = held_ref[0]
    own_low, state_low = own.astype(BF16), state.astype(BF16)
    grad_weighted = mm(b_s[...], own_low)
    weighted = (fade_wide * scaled_float).astype(BF16)
    entered = (expand(ent_s[j]) * grad_scan_float).astype(BF16)
    gb_s[...] += mm_nt(weighted, own_low)
    gc_s[...] += mm_nt(entered, state_low)
    keep_wide = expand(keep_s[j])[0:1, :]
    kept = keep_wide * jnp.sum(state * own, axis=0, keepdims=True)
    grad_state[j] = keep_wide * own + mm(c_t[...], entered)

    cums_here = cums_s[j]
    top = jnp.zeros((HALF, BLOCK), F32)
    bottom = jnp.zeros((HALF, BLOCK), F32)
    dtop = dgram[:HALF, :]
    dbottom = dgram[HALF:, HALF:]
    for i in range(PER_BLOCK):
        frm = cums_here[:, i : i + 1]
        to = cums_t[pl.ds(j * PER_BLOCK + i, 1), :]
        mask = lane_mask(i)
        only_grad = grad_scan * mask
        only = scaled * mask
        decay = jnp.exp(jnp.minimum(to - frm[:HALF], 0.0))
        top = top + mm((gram_s[:HALF, :] * decay).astype(BF16), only_grad)
        dtop = dtop + mm_nt(only[:HALF], grad_scan) * decay
        decay = jnp.exp(jnp.minimum(to[:, HALF:] - frm[HALF:], 0.0))
        bottom = bottom + mm((gram_s[HALF:, HALF:] * decay).astype(BF16), only_grad[HALF:])
        dbottom = dbottom + mm_nt(only[HALF:], grad_scan[HALF:]) * decay
    dgram[:HALF, :] = dtop
    dgram[HALF:, HALF:] = dbottom
    faded = fade_wide * grad_weighted
    through = jnp.concatenate([top, bottom], axis=0) + faded
    column = scaled_float * through
    final = kept + jnp.sum(scaled_float * faded, axis=0, keepdims=True)
    place = (iota((BLOCK, 128), 1) == j * PER_BLOCK + iota((BLOCK, 128), 0) // HEAD_DIM).astype(F32)
    u_s[...] += mm(grad_scan_float * scanned - column, place, PRECISE)
    v_s[...] += mm(column, place, PRECISE)
    fin_s[...] += mm(jnp.broadcast_to(final, (8, BLOCK)), place, PRECISE)

    grad_conv = (step_wide * through + skip * grad_mixed) * slope
    after = gcbuf.at[j]
    after[GROUP : GROUP + HALO, :] = after[0:HALO, :]
    after[0:GROUP, :] = grad_conv
    grad_value = taps[0:1, :] * grad_conv
    for offset in range(1, CONV):
        up = jnp.where(cols[:, 2 + offset : 3 + offset] > 0.0, after[offset : offset + GROUP, :], 0.0)
        grad_value = grad_value + taps[offset : offset + 1, :] * up
    low_value = grad_value.astype(BF16)
    lowvalue_out[...] = low_value
    gin[...] += mm_nt(low_gate, gate_w[:, pl.ds(at, BLOCK)]) + mm_nt(low_value, value_w[:, pl.ds(at, BLOCK)])
    lines = [grad_gain, grad_skip]
    lines += [jnp.sum(grad_conv * moved[offset], axis=0, keepdims=True) for offset in range(CONV)]
    lines += [jnp.sum(grad_conv, axis=0, keepdims=True)]
    for at_line, line in enumerate(lines):
        small_s[j, at_line : at_line + 1, :] += line
    small_out[...] = small_s[j]

    @pl.when(j == blocks - 1)
    def _():
        bc = bc_ref[...]
        dg = jnp.where(gram_s[...] == gram_s[...], dgram[...], 0.0)
        within = (at_row <= at_col) & (cols[:, 9:10] == seg_ref[...])
        dg = jnp.where(within, dg, 0.0)
        grad_b = gb_s[...] + mm(dg.astype(BF16), bc[:, STATE:])
        grad_c = gc_s[...] + mm(jnp.transpose(dg).astype(BF16), bc[:, :STATE])
        gbc_out[:, :STATE] = grad_b.astype(BF16)
        gbc_out[:, STATE:] = grad_c.astype(BF16)
        last = iota((GROUP, 128), 0) == GROUP - 1
        grad_cums = u_s[...] + jnp.where(last, fin_s[0:1, :], 0.0)
        upper = (at_row <= at_col).astype(F32)
        grad_a = mm(upper, grad_cums, PRECISE)
        step_in = stepin_ref[...]
        step = jnp.maximum(step_in, 0.0) + jnp.log1p(jnp.exp(-jnp.abs(step_in)))
        sig_in = jax.nn.sigmoid(step_in)
        ratio = jnp.where(step_in < -15.0, 1.0, sig_in / step)
        grad_step = v_s[...] * ratio + grad_a * rate_ref[...] * sig_in
        low_step = grad_step.astype(BF16)
        lowstep_out[...] = low_step
        sums_s[0:1, :] += jnp.sum(grad_step, axis=0, keepdims=True)
        sums_s[1:2, :] += jnp.sum(grad_a * step, axis=0, keepdims=True)
        sums_out[...] = sums_s[...]
        gin_out[...] = (gin[...] + mm_nt(low_step, step_w[...])).astype(BF16)
        made_out[...] = made[...].astype(BF16)


def shape(dims, kind=F32):
    return jax.ShapeDtypeStruct(dims, kind)


def params(limit=60 << 20):
    return pltpu.CompilerParams(
        dimension_semantics=("arbitrary", "arbitrary"), vmem_limit_bytes=limit
    )


def whole(array):
    return pl.BlockSpec(
        array.shape, lambda g, j: (0,) * array.ndim, pipeline_mode=pl.Buffered(1)
    )


def forward_call(inputs, weights, vectors, cols, seg_line):
    gate_w, value_w, state_w, step_w = weights
    taps, bias, staps, sbias, step_bias, rate, skip = vectors
    length, model = inputs.shape
    inner = gate_w.shape[1]
    groups, blocks = length // GROUP, inner // BLOCK
    wide = pl.BlockSpec((GROUP, BLOCK), lambda g, j: (g, j))
    line = lambda rows: pl.BlockSpec((rows, BLOCK), lambda g, j: (0, j))
    rows_of = lambda width: pl.BlockSpec((GROUP, width), lambda g, j: (g, 0))
    return pl.pallas_call(
        forward_kernel,
        grid=(groups, blocks),
        in_specs=[
            rows_of(model), whole(gate_w), whole(value_w), whole(state_w), whole(step_w),
            line(CONV), line(1), whole(staps), whole(sbias), whole(step_bias), whole(rate), line(1),
            rows_of(cols.shape[1]), pl.BlockSpec((1, GROUP), lambda g, j: (0, g)),
        ],
        out_specs=[
            wide, wide, wide, rows_of(2 * STATE), rows_of(2 * STATE), rows_of(128), rows_of(128),
            pl.BlockSpec((1, STATE, BLOCK), lambda g, j: (g, 0, j)),
        ],
        out_shape=[
            shape((length, inner), BF16), shape((length, inner)), shape((length, inner)),
            shape((length, 2 * STATE), BF16), shape((length, 2 * STATE)), shape((length, 128)),
            shape((length, 128)), shape((groups, STATE, inner)),
        ],
        scratch_shapes=[
            pltpu.VMEM((blocks, GROUP + HALO, BLOCK), F32),
            pltpu.VMEM((GROUP + HALO, 2 * STATE), F32),
            pltpu.VMEM((GROUP, GROUP), F32),
            pltpu.VMEM((STATE, GROUP), BF16),
            pltpu.VMEM((GROUP, STATE), BF16),
            pltpu.VMEM((blocks, GROUP, 128), F32),
            pltpu.VMEM((blocks, GROUP, 128), F32),
            pltpu.VMEM((blocks, GROUP, 128), F32),
            pltpu.VMEM((blocks, GROUP, 128), F32),
            pltpu.VMEM((128, GROUP), F32),
            pltpu.VMEM((blocks, 8, 128), F32),
            pltpu.VMEM((blocks, STATE, BLOCK), F32),
        ],
        compiler_params=params(),
        cost_estimate=pl.CostEstimate(
            flops=2 * length * model * (2 * inner + 512), bytes_accessed=40 << 20, transcendentals=0
        ),
        name="ssd_forward",
    )(
        inputs, gate_w, value_w, state_w, step_w, taps, bias, staps, sbias, step_bias, rate, skip,
        cols, seg_line,
    )


def branch_call(cotan, out_w, gate_raw, mixed, gain):
    length, model = cotan.shape
    inner = out_w.shape[0]
    rows_of = lambda width: pl.BlockSpec((GROUP, width), lambda g: (g, 0))
    return pl.pallas_call(
        branch_kernel,
        grid=(length // GROUP,),
        in_specs=[
            rows_of(model),
            pl.BlockSpec(out_w.shape, lambda g: (0, 0), pipeline_mode=pl.Buffered(1)),
            rows_of(inner), rows_of(inner),
            pl.BlockSpec(gain.shape, lambda g: (0, 0)),
        ],
        out_specs=[rows_of(inner), rows_of(128)],
        out_shape=[shape((length, inner), BF16), shape((length, 128))],
        compiler_params=pltpu.CompilerParams(vmem_limit_bytes=60 << 20),
        cost_estimate=pl.CostEstimate(
            flops=2 * length * model * inner, bytes_accessed=24 << 20, transcendentals=0
        ),
        name="branch_gradient",
    )(cotan, out_w, gate_raw, mixed, gain)


def backward_call(saved, grad_branch, stats, weights, vectors, gain, cols, seg_line):
    gate_raw, value_raw, mixed, bc, _, step_in, cums, held = saved
    gate_w, value_w, out_w, step_w = weights
    taps, bias, rate, skip = vectors
    length, inner = gate_raw.shape
    model = out_w.shape[1]
    groups, blocks = length // GROUP, inner // BLOCK
    last = groups - 1
    wide = pl.BlockSpec((GROUP, BLOCK), lambda g, j: (last - g, j))
    line = lambda rows: pl.BlockSpec((rows, BLOCK), lambda g, j: (0, j))
    rows_of = lambda width: pl.BlockSpec((GROUP, width), lambda g, j: (last - g, 0))
    steps = GROUP // HALO
    before = pl.BlockSpec(
        (HALO, BLOCK), lambda g, j: (jnp.maximum((last - g) * steps - 1, 0), j)
    )
    return pl.pallas_call(
        backward_kernel,
        grid=(groups, blocks),
        in_specs=[
            wide, wide, before, wide, wide, rows_of(2 * STATE), rows_of(128), rows_of(128),
            pl.BlockSpec((1, STATE, BLOCK), lambda g, j: (last - g, 0, j)),
            rows_of(128), whole(gate_w), whole(value_w), whole(out_w), whole(step_w),
            line(CONV), line(1), whole(rate), line(1), line(1),
            rows_of(cols.shape[1]), pl.BlockSpec((1, GROUP), lambda g, j: (0, last - g)),
        ],
        out_specs=[
            wide, wide, wide, rows_of(128), rows_of(2 * STATE), rows_of(model), rows_of(model),
            line(8), pl.BlockSpec((8, 128), lambda g, j: (0, 0)),
        ],
        out_shape=[
            shape((length, inner), BF16), shape((length, inner), BF16), shape((length, inner), BF16),
            shape((length, 128), BF16), shape((length, 2 * STATE), BF16),
            shape((length, model), BF16), shape((length, model), BF16),
            shape((8, inner)), shape((8, 128)),
        ],
        scratch_shapes=[
            pltpu.VMEM((GROUP + HALO, BLOCK), F32),
            pltpu.VMEM((blocks, GROUP + HALO, BLOCK), F32),
            pltpu.VMEM((GROUP, GROUP), F32),
            pltpu.VMEM((GROUP, GROUP), F32),
            pltpu.VMEM((GROUP, STATE), BF16),
            pltpu.VMEM((STATE, GROUP), BF16),
            pltpu.VMEM((blocks, GROUP, 128), F32),
            pltpu.VMEM((blocks, GROUP, 128), F32),
            pltpu.VMEM((blocks, GROUP, 128), F32),
            pltpu.VMEM((blocks, GROUP, 128), F32),
            pltpu.VMEM((128, GROUP), F32),
            pltpu.VMEM((blocks, 8, 128), F32),
            pltpu.VMEM((blocks, STATE, BLOCK), F32),
            pltpu.VMEM((GROUP, model), F32),
            pltpu.VMEM((GROUP, model), F32),
            pltpu.VMEM((GROUP, STATE), F32),
            pltpu.VMEM((GROUP, STATE), F32),
            pltpu.VMEM((GROUP, 128), F32),
            pltpu.VMEM((GROUP, 128), F32),
            pltpu.VMEM((8, 128), F32),
            pltpu.VMEM((blocks, 8, BLOCK), F32),
            pltpu.VMEM((8, 128), F32),
        ],
        compiler_params=params(),
        cost_estimate=pl.CostEstimate(
            flops=6 * length * model * inner, bytes_accessed=60 << 20, transcendentals=0
        ),
        name="ssd_backward",
    )(
        gate_raw, value_raw, value_raw, mixed, grad_branch, bc, step_in, cums, held, stats,
        gate_w, value_w, out_w, step_w, taps, bias, rate, skip, gain, cols, seg_line,
    )

MESH = pl.DeviceIdType.MESH


def part_of(ref, at, size, axis):
    if axis == 0:
        return ref.at[pl.ds(pl.multiple_of(at * size, size), size), :]
    if axis == 1:
        return ref.at[:, pl.ds(pl.multiple_of(at * size, size), size)]
    return ref.at[at]


def greet(devices):
    barrier = pltpu.get_barrier_semaphore()
    for device in devices:
        pl.semaphore_signal(barrier, inc=1, device_id=device, device_id_type=MESH)
    pl.semaphore_wait(barrier, len(devices))


def gather_kernel(count, pieces, *refs):
    amount = len(pieces)
    sources, targets = refs[:amount], refs[amount : 2 * amount]
    own_sem, send_sem, recv_sem, pass_sem, took_sem = refs[2 * amount :]
    me, line = lax.axis_index("fsdp"), lax.axis_index("tp")
    chips = count // 2
    partner = me + 1 - 2 * lax.rem(me, 2)
    others = [lax.rem(me + 2 * hop, count) for hop in range(1, chips)]
    greet([(device, line) for device in others + [partner]])

    def remote(source, target, sends, receives, device):
        return pltpu.make_async_remote_copy(
            src_ref=source, dst_ref=target, send_sem=sends, recv_sem=receives,
            device_id=(device, line), device_id_type=MESH,
        )

    def place(which, at):
        size, axis = pieces[which]
        return part_of(targets[which], at, size, axis)

    started = []
    for which in range(amount):
        for hop in range(1, chips):
            copy = remote(
                sources[which], place(which, me), send_sem.at[hop, which],
                recv_sem.at[hop, which], lax.rem(me + 2 * hop, count),
            )
            copy.start()
            started.append(copy)
    for which in range(amount):
        copy = remote(
            sources[which], place(which, me), pass_sem.at[0, which], took_sem.at[0, which], partner
        )
        copy.start()
        started.append(copy)
    own = []
    for which in range(amount):
        copy = pltpu.make_async_copy(sources[which], place(which, me), own_sem.at[which])
        copy.start()
        own.append(copy)
    for which in range(amount):
        for hop in range(1, chips):
            origin = lax.rem(me - 2 * hop + count, count)
            block = place(which, origin)
            remote(
                block, block, send_sem.at[hop, which], recv_sem.at[hop, which], partner
            ).wait_recv()
            copy = remote(
                block, block, pass_sem.at[hop, which], took_sem.at[hop, which], partner
            )
            copy.start()
            started.append(copy)
    for which in range(amount):
        for hop in range(chips):
            block = place(which, lax.rem(partner - 2 * hop + count, count))
            remote(
                block, block, pass_sem.at[hop, which], took_sem.at[hop, which], partner
            ).wait_recv()
    for copy in started:
        copy.wait_send()
    for copy in own:
        copy.wait()


def gather_call(count, blocks, axes):
    pieces, shapes = [], []
    for block, axis in zip(blocks, axes):
        if axis == 2:
            pieces.append((0, 2))
            shapes.append(shape((count,) + block.shape, BF16))
        else:
            pieces.append((block.shape[axis], axis))
            dims = list(block.shape)
            dims[axis] *= count
            shapes.append(shape(tuple(dims), BF16))
    amount = len(blocks)
    sems = lambda: pltpu.SemaphoreType.DMA((count // 2, amount))
    return pl.pallas_call(
        partial(gather_kernel, count, pieces),
        in_specs=[pl.BlockSpec(memory_space=pl.ANY)] * amount,
        out_specs=[pl.BlockSpec(memory_space=pl.ANY)] * amount,
        out_shape=shapes,
        scratch_shapes=[pltpu.SemaphoreType.DMA((amount,)), sems(), sems(), sems(), sems()],
        compiler_params=pltpu.CompilerParams(collective_id=0, has_side_effects=True),
        cost_estimate=pl.CostEstimate(flops=0, bytes_accessed=250 << 20, transcendentals=0),
        name="gather_weights",
    )(*blocks)


def scatter_kernel(count, pieces, *refs):
    amount = len(pieces)
    sources, targets = refs[:amount], refs[amount : 2 * amount]
    scratch = refs[2 * amount :]
    mine, took, came = (scratch[at * amount : (at + 1) * amount] for at in range(3))
    own_sem, pass_sem, took_sem, send_sem, recv_sem = scratch[3 * amount :]
    me, line = lax.axis_index("fsdp"), lax.axis_index("tp")
    chips = count // 2
    partner = me + 1 - 2 * lax.rem(me, 2)
    others = [lax.rem(me + 2 * hop, count) for hop in range(1, chips)]
    greet([(device, line) for device in others + [partner]])

    def remote(source, target, sends, receives, device):
        return pltpu.make_async_remote_copy(
            src_ref=source, dst_ref=target, send_sem=sends, recv_sem=receives,
            device_id=(device, line), device_id_type=MESH,
        )

    def piece(which, at):
        size, axis = pieces[which]
        return part_of(sources[which], at, size, axis)

    order = list(range(1, chips)) + [0]
    handed, own = {}, {}
    for hop in order:
        for which in range(amount):
            copy = remote(
                piece(which, lax.rem(partner + 2 * hop, count)), took[which].at[hop],
                pass_sem.at[hop, which], took_sem.at[hop, which], partner,
            )
            copy.start()
            handed[hop, which] = copy
            copy = pltpu.make_async_copy(
                piece(which, lax.rem(me + 2 * hop, count)), mine[which].at[hop],
                own_sem.at[hop, which],
            )
            copy.start()
            own[hop, which] = copy
    sent = []
    for hop in order:
        for which in range(amount):
            own[hop, which].wait()
            handed[hop, which].wait_recv()
            total = mine[which][hop].astype(F32) + took[which][hop].astype(F32)
            if hop == 0:
                targets[which][...] = total
                continue
            mine[which][hop] = total.astype(BF16)
            copy = remote(
                mine[which].at[hop], came[which].at[hop - 1], send_sem.at[hop, which],
                recv_sem.at[hop, which], lax.rem(me + 2 * hop, count),
            )
            copy.start()
            sent.append(copy)
    for which in range(amount):
        for hop in range(1, chips):
            block = came[which].at[hop - 1]
            remote(
                block, block, send_sem.at[hop, which], recv_sem.at[hop, which], partner
            ).wait_recv()
            targets[which][...] += block[...].astype(F32)
    for copy in list(handed.values()) + sent:
        copy.wait_send()


def scatter_call(count, arrays, axes):
    pieces, shapes = [], []
    for array, axis in zip(arrays, axes):
        if axis == 2:
            pieces.append((0, 2))
            shapes.append(array.shape[1:])
        else:
            dims = list(array.shape)
            dims[axis] //= count
            pieces.append((dims[axis], axis))
            shapes.append(tuple(dims))
    amount, chips = len(arrays), count // 2
    sems = lambda: pltpu.SemaphoreType.DMA((chips, amount))
    return pl.pallas_call(
        partial(scatter_kernel, count, pieces),
        in_specs=[pl.BlockSpec(memory_space=pl.ANY)] * amount,
        out_specs=[pl.BlockSpec(memory_space=pltpu.VMEM)] * amount,
        out_shape=[shape(dims) for dims in shapes],
        scratch_shapes=[pltpu.VMEM((chips,) + dims, BF16) for dims in shapes]
        + [pltpu.VMEM((chips,) + dims, BF16) for dims in shapes]
        + [pltpu.VMEM((chips - 1,) + dims, BF16) for dims in shapes]
        + [sems(), sems(), sems(), sems(), sems()],
        compiler_params=pltpu.CompilerParams(
            collective_id=1, has_side_effects=True, vmem_limit_bytes=48 << 20
        ),
        cost_estimate=pl.CostEstimate(flops=0, bytes_accessed=250 << 20, transcendentals=0),
        name="scatter_gradients",
    )(*arrays)


def weight_kernel(micro, *refs):
    outs = refs[-4:]
    rows, lows = refs[:micro], refs[micro : 5 * micro]
    for which in range(4):
        total = mm_tn(rows[0][...], lows[which][...])
        for at in range(1, micro):
            total = total + mm_tn(rows[at][...], lows[4 * at + which][...])
        outs[which][...] = total.astype(BF16)


def weight_call(inputs, lows):
    micro, (length, model) = len(inputs), inputs[0].shape
    full = lambda array: pl.BlockSpec(array.shape, lambda g: (0, 0), pipeline_mode=pl.Buffered(1))
    flat = [array for low in lows for array in low]
    widths = [array.shape[1] for array in lows[0]]
    return pl.pallas_call(
        partial(weight_kernel, micro),
        grid=(model // BLOCK,),
        in_specs=[pl.BlockSpec((length, BLOCK), lambda g: (0, g))] * micro
        + [full(array) for array in flat],
        out_specs=[pl.BlockSpec((BLOCK, width), lambda g: (g, 0)) for width in widths],
        out_shape=[shape((model, width), BF16) for width in widths],
        compiler_params=pltpu.CompilerParams(vmem_limit_bytes=50 << 20),
        cost_estimate=pl.CostEstimate(
            flops=2 * micro * length * model * sum(widths), bytes_accessed=40 << 20, transcendentals=0
        ),
        name="weight_gradients",
    )(*inputs, *flat)


def outer_kernel(micro, *refs):
    total = mm_tn(refs[0][...], refs[micro][...])
    for at in range(1, micro):
        total = total + mm_tn(refs[at][...], refs[micro + at][...])
    refs[-1][...] = total.astype(BF16)


def outer_call(branches, cotans):
    micro, (length, inner) = len(branches), branches[0].shape
    model = cotans[0].shape[1]
    full = lambda array: pl.BlockSpec(array.shape, lambda g: (0, 0), pipeline_mode=pl.Buffered(1))
    return pl.pallas_call(
        partial(outer_kernel, micro),
        grid=(inner // BLOCK,),
        in_specs=[pl.BlockSpec((length, BLOCK), lambda g: (0, g))] * micro
        + [full(array) for array in cotans],
        out_specs=pl.BlockSpec((BLOCK, model), lambda g: (g, 0)),
        out_shape=shape((inner, model), BF16),
        compiler_params=pltpu.CompilerParams(vmem_limit_bytes=50 << 20),
        cost_estimate=pl.CostEstimate(
            flops=2 * micro * length * model * inner, bytes_accessed=30 << 20, transcendentals=0
        ),
        name="out_gradients",
    )(*branches, *cotans)


def shift_down(values, offset):
    return jnp.pad(values, ((offset, 0), (0, 0)))[: values.shape[0]]


def shift_up(values, offset):
    return jnp.pad(values, ((0, offset), (0, 0)))[offset:]


def document_columns(seg_row):
    length = seg_row.shape[0]
    previous = jnp.concatenate([jnp.full((1,), -1, seg_row.dtype), seg_row[GROUP - 1 : -1 : GROUP]])
    last = seg_row[GROUP - 1 :: GROUP]
    columns = []
    for offset in range(1, CONV):
        columns.append(jnp.pad(seg_row, (offset, 0), constant_values=-1)[:length] == seg_row)
    for offset in range(1, CONV):
        columns.append(jnp.pad(seg_row, (0, offset), constant_values=-1)[offset:] == seg_row)
    columns.append(seg_row == jnp.repeat(previous, GROUP))
    columns.append(seg_row == jnp.repeat(last, GROUP))
    columns.append(jnp.repeat(last == previous, GROUP))
    columns.append(seg_row)
    columns = [column.astype(F32) for column in columns]
    return jnp.stack(columns + [columns[0]] * (16 - len(columns)), axis=1)


def state_gradient(grad_bc, state_raw, taps, bias, cols):
    moved = [state_raw]
    for offset in range(1, CONV):
        moved.append(shift_down(state_raw, offset) * cols[:, offset - 1 : offset])
    conv = bias
    for offset in range(CONV):
        conv = conv + taps[offset][None, :] * moved[offset]
    sig = jax.nn.sigmoid(conv)
    grad_conv = grad_bc * (sig * (1.0 + conv * (1.0 - sig)))
    grad_raw = taps[0][None, :] * grad_conv
    for offset in range(1, CONV):
        grad_raw = grad_raw + taps[offset][None, :] * (
            shift_up(grad_conv, offset) * cols[:, 2 + offset : 3 + offset]
        )
    grad_taps = jnp.stack([jnp.sum(grad_conv * each, axis=0) for each in moved])
    return grad_raw.astype(BF16), grad_taps, jnp.sum(grad_conv, axis=0)


def local(
    hidden_in, segment_ids, cotangent, norm_gain, proj_gate, proj_value, proj_state, proj_step,
    conv_value, conv_value_bias, conv_state, conv_state_bias, step_bias, decay_log, skip_gain,
    gate_gain, proj_out,
):
    micro = hidden_in.shape[0]
    heads = step_bias.shape[0]
    rows_here = hidden_in.shape[2]
    tp_size = lax.axis_size("tp")
    me = lax.axis_index("tp")
    decay_rate = -jnp.exp(decay_log)
    pad_heads = lambda values: jnp.pad(values, (0, 128 - heads))[None, :]
    rate = pad_heads(decay_rate)
    step_bias_line = pad_heads(step_bias)
    skip = jnp.repeat(skip_gain, HEAD_DIM)[None, :]
    gain = gate_gain[None, :]
    taps, bias = conv_value, conv_value_bias[None, :]
    staps, sbias = conv_state, conv_state_bias[None, :]

    rows_float = hidden_in[:, 0].astype(F32)
    inv_root = lax.rsqrt(jnp.mean(rows_float * rows_float, axis=-1, keepdims=True) + EPSILON)
    input_rows = (rows_float * inv_root * norm_gain).astype(BF16)

    def gather_tp(values, *after):
        values = lax.optimization_barrier((values,) + after)[0]
        return lax.all_gather(values, "tp", axis=0, tiled=True)

    def scatter_tp(values, *after):
        values = lax.optimization_barrier((values,) + after)[0]
        return lax.psum_scatter(values, "tp", scatter_dimension=0, tiled=True)

    inputs = [gather_tp(input_rows[0])]
    fsdp_size = lax.axis_size("fsdp")
    model = hidden_in.shape[3]
    aligned = proj_out.shape[1] % 128 == 0
    axes = (0, 0, 0, 0, 1 if aligned else 2)
    step_block = jnp.pad(proj_step, ((0, 0), (0, 128 - heads)))
    gate_w, value_w, state_w, step_w, out_w = gather_call(
        fsdp_size, (proj_gate, proj_value, proj_state, step_block, proj_out), axes
    )
    if not aligned:
        out_w = jnp.transpose(out_w, (1, 0, 2)).reshape(-1, model)
    cotans = [gather_tp(cotangent[0, 0], inputs[0], step_w)]
    lows, block_rows, gin_rows, smalls = [], [], [], []
    token = cotans[0]
    for at in range(micro):
        seg_row = segment_ids[at, 0]
        cols = document_columns(seg_row)
        seg_line = seg_row.astype(F32)[None, :]
        saved = forward_call(
            inputs[at], (gate_w, value_w, state_w, step_w),
            (taps, bias, staps, sbias, step_bias_line, rate, skip), cols, seg_line,
        )
        grad_branch, partial_stats = branch_call(cotans[at], out_w, saved[0], saved[2], gain)
        sums = lax.psum(partial_stats[:, :2].T, "tp")
        scale = lax.rsqrt(sums[0] / INNER + EPSILON)
        pair = jnp.stack([scale, scale**3 * (sums[1] / INNER)], axis=1)
        stats = jnp.pad(pair, ((0, 0), (0, 126)))
        if at + 1 < micro:
            inputs.append(gather_tp(input_rows[at + 1], token))
            token = inputs[-1]
        branch, low_gate, low_value, low_step, grad_bc, made, gin, small, step_sums = backward_call(
            saved, grad_branch, stats, (gate_w, value_w, out_w, step_w), (taps, bias, rate, skip),
            gain, cols, seg_line,
        )
        if at + 1 < micro:
            inputs[-1] = lax.optimization_barrier((inputs[-1], gin))[0]
            cotans.append(gather_tp(cotangent[at + 1, 0], token))
            token = cotans[-1]
            produced = scatter_tp(made, token)
            summed = scatter_tp(gin, produced)
        else:
            summed = scatter_tp(gin, token)
            produced = scatter_tp(made, summed)
        token = produced
        block_rows.append((rows_float[at] + produced.astype(F32)).astype(BF16))
        grad_bc = lax.psum(grad_bc, "tp").astype(F32)
        low_state, grad_staps, grad_sbias = state_gradient(grad_bc, saved[4], staps, sbias, cols)
        mine = lax.dynamic_slice_in_dim(low_state, me * rows_here, rows_here, axis=0)
        gin_rows.append(summed.astype(F32) + mm_nt(mine, state_w))
        lows.append((low_gate, low_value, low_state, low_step, branch))
        smalls.append((small, step_sums, grad_staps, grad_sbias))

    grad_out = outer_call([low[4] for low in lows], cotans)
    grad_gate, grad_value, grad_state, grad_step = weight_call(inputs, [low[:4] for low in lows])
    if not aligned:
        grad_out = jnp.transpose(grad_out.reshape(-1, fsdp_size, proj_out.shape[1]), (1, 0, 2))
    grad_gate, grad_value, grad_state, grad_step, grad_out = scatter_call(
        fsdp_size, (grad_gate, grad_value, grad_state, grad_step, grad_out), axes
    )
    grad_step = grad_step[:, :heads]

    grad_inputs = jnp.stack(gin_rows)
    grad_norm_gain = jnp.sum(grad_inputs * rows_float * inv_root, axis=(0, 1))
    grad_normed = grad_inputs * norm_gain
    grad_rows = inv_root * grad_normed - rows_float * inv_root**3 * jnp.mean(
        grad_normed * rows_float, axis=-1, keepdims=True
    )
    grad_hidden = (cotangent[:, 0].astype(F32) + grad_rows).astype(BF16)

    small, step_sums, grad_staps, grad_sbias = (sum(parts) for parts in zip(*smalls))
    small, step_sums, grad_staps, grad_sbias = lax.psum(
        (small, step_sums, grad_staps, grad_sbias), "fsdp"
    )
    gain_total = lax.psum(grad_norm_gain, ("fsdp", "tp"))
    return (
        jnp.stack(block_rows)[:, None],
        grad_hidden[:, None],
        gain_total,
        grad_gate,
        grad_value,
        grad_state,
        grad_step,
        small[2 : 2 + CONV],
        small[2 + CONV],
        grad_staps,
        grad_sbias,
        step_sums[0, :heads],
        step_sums[1, :heads] * decay_rate,
        jnp.sum(small[1].reshape(heads, HEAD_DIM), axis=1),
        small[0],
        grad_out,
    )


def solution(mesh):
    in_specs = (
        P(None, "fsdp", "tp", None), P(None, "fsdp", None), P(None, "fsdp", "tp", None), P(),
        P("fsdp", "tp"), P("fsdp", "tp"), P("fsdp", None), P("fsdp", "tp"), P(None, "tp"), P("tp"),
        P(), P(), P("tp"), P("tp"), P("tp"), P("tp"), P("tp", "fsdp"),
    )
    out_specs = (
        P(None, "fsdp", "tp", None), P(None, "fsdp", "tp", None), P(), P("fsdp", "tp"),
        P("fsdp", "tp"), P("fsdp", None), P("fsdp", "tp"), P(None, "tp"), P("tp"), P(), P(),
        P("tp"), P("tp"), P("tp"), P("tp"), P("tp", "fsdp"),
    )
    return jax.shard_map(local, mesh=mesh, in_specs=in_specs, out_specs=out_specs, check_vma=False)
```

```python
from functools import partial

import jax
import jax.numpy as jnp
from jax import lax
from jax.experimental import pallas as pl
from jax.experimental.pallas import tpu as pltpu
from jax.sharding import PartitionSpec as P

HEAD_DIM = 64
STATE = 128
CONV = 4
GROUP = 256
HALF = GROUP // 2
BLOCK = 256
PER_BLOCK = BLOCK // HEAD_DIM
HALO = 8
INNER = 4096
EPSILON = 1e-05
PRECISE = lax.Precision.HIGHEST
FORWARD_INS, FORWARD_OUTS = 16, 9
BACKWARD_INS, BACKWARD_OUTS = 20, 8
F32 = jnp.float32
BF16 = jnp.bfloat16


def mm(former, latter, precision=None):
    return jnp.dot(former, latter, preferred_element_type=F32, precision=precision)


def mm_nt(former, latter):
    return lax.dot_general(
        former, latter, (((1,), (1,)), ((), ())), preferred_element_type=F32
    )


def mm_tn(former, latter):
    return lax.dot_general(
        former, latter, (((0,), (0,)), ((), ())), preferred_element_type=F32
    )


def iota(shape, axis):
    return lax.broadcasted_iota(jnp.int32, shape, axis)


def expand(columns):
    rows = columns.shape[0]
    lane = iota((rows, 128), 1)
    parts = []
    for pair in range(PER_BLOCK // 2):
        former = jnp.broadcast_to(columns[:, 2 * pair : 2 * pair + 1], (rows, 128))
        latter = jnp.broadcast_to(columns[:, 2 * pair + 1 : 2 * pair + 2], (rows, 128))
        parts.append(jnp.where(lane < HEAD_DIM, former, latter))
    return jnp.concatenate(parts, axis=1)


def lane_mask(head):
    lane = iota((1, BLOCK), 1)
    return ((lane // HEAD_DIM) == head).astype(F32).astype(BF16)


def spread(ref, values, blocks):
    for block in range(blocks):
        shift = (128 - PER_BLOCK * block) % 128
        ref[block] = pltpu.roll(values, shift, 1) if shift else values


def token_quantities(step_in, cums, cols, decay_rate):
    step = jnp.maximum(step_in, 0.0) + jnp.log1p(jnp.exp(-jnp.abs(step_in)))
    final = cums[GROUP - 1 : GROUP, :]
    entering = jnp.exp(cums) * cols[:, 6:7]
    fading = jnp.exp(final - cums) * cols[:, 7:8]
    retain = jnp.exp(final) * cols[0:1, 8:9]
    return step, entering, fading, retain


def shifted_values(buf, cols):
    moved = [buf[HALO : HALO + GROUP, :]]
    for offset in range(1, CONV):
        before = buf[HALO - offset : HALO - offset + GROUP, :]
        moved.append(jnp.where(cols[:, offset - 1 : offset] > 0.0, before, 0.0))
    return moved


def conv_of(moved, taps, bias):
    total = bias + taps[0:1, :] * moved[0]
    for offset in range(1, CONV):
        total = total + taps[offset : offset + 1, :] * moved[offset]
    return total


MESH = pl.DeviceIdType.MESH


def part_of(ref, at, size, axis):
    if axis == 0:
        return ref.at[pl.ds(pl.multiple_of(at * size, size), size), :]
    if axis == 1:
        return ref.at[:, pl.ds(pl.multiple_of(at * size, size), size)]
    return ref.at[at]


def greet(devices):
    barrier = pltpu.get_barrier_semaphore()
    for device in devices:
        pl.semaphore_signal(barrier, inc=1, device_id=device, device_id_type=MESH)
    pl.semaphore_wait(barrier, len(devices))


def remote_copy(source, target, sends, receives, device):
    return pltpu.make_async_remote_copy(
        src_ref=source, dst_ref=target, send_sem=sends, recv_sem=receives,
        device_id=device, device_id_type=MESH,
    )


class LineScatter:
    def __init__(self, size, source, own, slots, last, own_sem, send_sem, recv_sem, last_sem):
        self.size, self.source, self.own, self.slots, self.last = size, source, own, slots, last
        self.own_sem, self.send_sem, self.recv_sem, self.last_sem = own_sem, send_sem, recv_sem, last_sem
        self.me, self.column = lax.axis_index("tp"), lax.axis_index("fsdp")
        self.rows = last.shape[0]

    @staticmethod
    def scratch(size, rows, width):
        hops = size - 1
        return [
            pltpu.VMEM((2, hops, rows, width), BF16), pltpu.VMEM((2, hops, rows, width), BF16),
            pltpu.VMEM((rows, width), BF16), pltpu.SemaphoreType.DMA((2, hops)),
            pltpu.SemaphoreType.DMA((2, hops)), pltpu.SemaphoreType.DMA((2, hops)),
            pltpu.SemaphoreType.DMA((1,)),
        ]

    def place(self, flow):
        return self.me if flow == 0 else self.size - 1 - self.me

    def local(self, flow, hop):
        block = self.size - 1 - hop + self.place(flow)
        if flow:
            block = self.size - 1 - block
        at = pl.multiple_of(block * self.rows, self.rows)
        return pltpu.make_async_copy(
            self.source.at[pl.ds(at, self.rows), :], self.own.at[flow, hop], self.own_sem.at[flow, hop]
        )

    def final(self):
        at = pl.multiple_of(self.me * self.rows, self.rows)
        return pltpu.make_async_copy(
            self.source.at[pl.ds(at, self.rows), :], self.last, self.last_sem.at[0]
        )

    def sending(self, flow, hop):
        neighbour = self.me + 1 if flow == 0 else self.me - 1
        neighbour = jnp.clip(neighbour, 0, self.size - 1)
        return remote_copy(
            self.own.at[flow, hop], self.slots.at[flow, hop], self.send_sem.at[flow, hop],
            self.recv_sem.at[flow, hop], (self.column, neighbour),
        )

    def greet(self):
        barrier = pltpu.get_barrier_semaphore()
        for flow in range(2):
            neighbour = self.me + 1 if flow == 0 else self.me - 1

            @pl.when((neighbour >= 0) & (neighbour < self.size))
            def _():
                pl.semaphore_signal(
                    barrier, inc=1, device_id=(self.column, neighbour), device_id_type=MESH
                )

        inside = (self.me > 0) & (self.me < self.size - 1)
        pl.semaphore_wait(barrier, 1 + inside.astype(jnp.int32))

    def begin(self):
        self.final().start()
        for hop in range(self.size - 1):
            for flow in range(2):

                @pl.when(self.place(flow) <= hop)
                def _():
                    self.local(flow, hop).start()

    def hop(self, hop):
        for flow in range(2):
            place = self.place(flow)

            @pl.when(place <= hop)
            def _():
                self.local(flow, hop).wait()
                if hop > 0:

                    @pl.when(place >= 1)
                    def _():
                        self.sending(flow, hop - 1).wait_recv()
                        total = self.own[flow, hop].astype(F32) + self.slots[flow, hop - 1].astype(F32)
                        self.own[flow, hop] = total.astype(BF16)

                self.sending(flow, hop).start()

    def end(self, out):
        hops = self.size - 1
        self.final().wait()
        out[...] = self.last[...].astype(F32)
        for flow in range(2):

            @pl.when(self.place(flow) >= 1)
            def _():
                self.sending(flow, hops - 1).wait_recv()
                out[...] += self.slots[flow, hops - 1].astype(F32)

        for hop in range(hops):
            for flow in range(2):

                @pl.when(self.place(flow) <= hop)
                def _():
                    self.sending(flow, hop).wait_send()


class LineGather:
    def __init__(self, size, source, target, own_sem, send_sem, recv_sem):
        self.size, self.source, self.target = size, source, target
        self.own_sem, self.send_sem, self.recv_sem = own_sem, send_sem, recv_sem
        self.me, self.column = lax.axis_index("tp"), lax.axis_index("fsdp")
        self.rows = source.shape[0]

    @staticmethod
    def scratch(size):
        return [
            pltpu.SemaphoreType.DMA((1,)), pltpu.SemaphoreType.DMA((2, size - 1)),
            pltpu.SemaphoreType.DMA((2, size - 1)),
        ]

    def place(self, flow):
        return self.me if flow == 0 else self.size - 1 - self.me

    def block(self, at):
        at = pl.multiple_of(jnp.clip(at, 0, self.size - 1) * self.rows, self.rows)
        return self.target.at[pl.ds(at, self.rows), :]

    def sending(self, flow, hop):
        neighbour = self.me + 1 if flow == 0 else self.me - 1
        neighbour = jnp.clip(neighbour, 0, self.size - 1)
        block = self.block(self.me - hop if flow == 0 else self.me + hop)
        return remote_copy(
            self.source if hop == 0 else block, block, self.send_sem.at[flow, hop],
            self.recv_sem.at[flow, hop], (self.column, neighbour),
        )

    def local(self):
        return pltpu.make_async_copy(self.source, self.block(self.me), self.own_sem.at[0])

    def begin(self):
        self.local().start()
        self.hop(0)

    def hop(self, hop):
        for flow in range(2):
            place = self.place(flow)
            if hop > 0:

                @pl.when(place >= hop)
                def _():
                    self.sending(flow, hop - 1).wait_recv()

            if hop < self.size - 1:

                @pl.when((place >= hop) & (place < self.size - 1))
                def _():
                    self.sending(flow, hop).start()

    def end(self):
        self.hop(self.size - 1)
        self.local().wait()
        for hop in range(self.size - 1):
            for flow in range(2):
                place = self.place(flow)

                @pl.when((place >= hop) & (place < self.size - 1))
                def _():
                    self.sending(flow, hop).wait_send()


def run_line(step, steps, scatter, gather, out):
    size = (scatter or gather).size
    actions = [[] for _ in range(size + 1)]
    if scatter:
        first = 1 if gather else 0
        actions[0] += [scatter.greet, scatter.begin]
        for hop in range(size - 1):
            actions[first + hop].append(partial(scatter.hop, hop))
        actions[first + size - 1].append(partial(scatter.end, out))
    if gather:
        if not scatter:
            actions[0].append(partial(LineScatter.greet, gather))
        actions[0].append(gather.begin)
        for hop in range(1, size - 1):
            actions[hop].insert(0, partial(gather.hop, hop))
        actions[size - 1].insert(0, gather.end)
    for at, todo in zip(steps, actions):
        if todo:

            @pl.when(step == at)
            def _():
                for action in todo:
                    action()


class Hosted:
    def __init__(self, size, scatter=None, gather=None):
        self.size, self.scatter, self.gather = size, scatter, gather

    def operands(self):
        return [each for each in (self.scatter, self.gather) if each is not None]

    def in_specs(self):
        return [pl.BlockSpec(memory_space=pl.ANY)] * len(self.operands())

    def outs(self):
        shapes, specs = [], []
        if self.scatter is not None:
            rows, width = self.scatter.shape[0] // self.size, self.scatter.shape[1]
            shapes.append(shape((rows, width)))
            specs.append(pl.BlockSpec((rows, width), lambda g, j: (0, 0)))
        if self.gather is not None:
            rows, width = self.gather.shape
            shapes.append(shape((rows * self.size, width), BF16))
            specs.append(pl.BlockSpec(memory_space=pl.ANY))
        return specs, shapes

    def scratch(self):
        needed = []
        if self.scatter is not None:
            rows, width = self.scatter.shape[0] // self.size, self.scatter.shape[1]
            needed += LineScatter.scratch(self.size, rows, width)
        if self.gather is not None:
            needed += LineGather.scratch(self.size)
        return needed

    def wrap(self, body, ins, outs, pace):
        has_scatter, has_gather = self.scatter is not None, self.gather is not None
        hosts = has_scatter + has_gather
        size, spare = self.size, len(self.scratch())
        if not hosts:
            return body

        def kernel(*refs):
            sources, targets = refs[ins : ins + hosts], refs[ins + hosts + outs : ins + outs + 2 * hosts]
            tail = refs[len(refs) - spare :]
            body(
                *refs[:ins], *refs[ins + hosts : ins + hosts + outs],
                *refs[ins + outs + 2 * hosts : len(refs) - spare],
            )
            scatter = LineScatter(size, sources[0], *tail[:7]) if has_scatter else None
            gather = LineGather(size, sources[-1], targets[-1], *tail[-3:]) if has_gather else None
            step = pl.program_id(0) * pl.num_programs(1) + pl.program_id(1)
            run_line(step, pace, scatter, gather, targets[0])

        return kernel


def forward_kernel(
    in_ref, gate_w, value_w, state_w, step_w, taps_ref, bias_ref, staps_ref, sbias_ref,
    step_bias_ref, rate_ref, skip_ref, cols_ref, seg_ref, out_w, gain_ref,
    gate_out, value_out, mixed_out, bc_out, sraw_out, stepin_out, cums_out, held_out, made_out,
    vbuf, sbuf, gram_s, b_t, c_s, step_s, ent_s, fade_s, cums_s, cums_t, keep_s, hidden, made,
):
    g, j = pl.program_id(0), pl.program_id(1)
    blocks = pl.num_programs(1)
    nblocks = hidden.shape[0]
    rows = in_ref[...]
    cols = cols_ref[...]

    @pl.when(j == 0)
    def _():
        sbuf[0:HALO, :] = sbuf[GROUP : GROUP + HALO, :]
        raw = mm(rows, state_w[...])
        sbuf[HALO : HALO + GROUP, :] = raw
        sraw_out[...] = raw
        conv = conv_of(shifted_values(sbuf, cols), staps_ref[...], sbias_ref[...])
        bc = (conv * jax.nn.sigmoid(conv)).astype(BF16)
        bc_out[...] = bc
        b_low, c_low = bc[:, :STATE], bc[:, STATE:]
        b_t[...] = jnp.transpose(b_low.astype(F32)).astype(BF16)
        c_s[...] = c_low
        step_in = mm(rows, step_w[...]) + step_bias_ref[...]
        stepin_out[...] = step_in
        step = jnp.maximum(step_in, 0.0) + jnp.log1p(jnp.exp(-jnp.abs(step_in)))
        at_row, at_col = iota((GROUP, GROUP), 0), iota((GROUP, GROUP), 1)
        lower = (at_row >= at_col).astype(F32)
        cums = mm(lower, step * rate_ref[...], PRECISE)
        cums_out[...] = cums
        step, entering, fading, retain = token_quantities(step_in, cums, cols, rate_ref[...])
        spread(step_s, step, nblocks)
        spread(ent_s, entering, nblocks)
        spread(fade_s, fading, nblocks)
        spread(cums_s, cums, nblocks)
        spread(keep_s, jnp.broadcast_to(retain, (8, 128)), nblocks)
        cums_t[...] = jnp.transpose(cums)
        within = (at_row >= at_col) & (cols[:, 9:10] == seg_ref[...])
        gram_s[...] = jnp.where(within, mm_nt(c_low, b_low), 0.0)

    at = pl.multiple_of(j * BLOCK, BLOCK)
    gate = mm(rows, gate_w[:, pl.ds(at, BLOCK)])
    gate_out[...] = gate.astype(BF16)
    value = mm(rows, value_w[:, pl.ds(at, BLOCK)])
    value_out[...] = value
    mine = vbuf.at[j]
    mine[0:HALO, :] = mine[GROUP : GROUP + HALO, :]
    mine[HALO : HALO + GROUP, :] = value
    conv = conv_of(shifted_values(mine, cols), taps_ref[...], bias_ref[...])
    x_low = (conv * jax.nn.sigmoid(conv)).astype(BF16)
    x_float = x_low.astype(F32)
    scaled_float = expand(step_s[j]) * x_float
    scaled = scaled_float.astype(BF16)

    @pl.when(g == 0)
    def _():
        hidden[j] = jnp.zeros((STATE, BLOCK), F32)

    state = hidden[j]
    state_low = state.astype(BF16)
    held_out[0] = state_low
    total = expand(ent_s[j]) * mm(c_s[...], state_low)
    weighted = (expand(fade_s[j]) * scaled.astype(F32)).astype(BF16)
    hidden[j] = expand(keep_s[j])[0:1, :] * state + mm(b_t[...], weighted)
    cums_here = cums_s[j]
    top = jnp.zeros((HALF, BLOCK), F32)
    bottom = jnp.zeros((HALF, BLOCK), F32)
    for i in range(PER_BLOCK):
        to = cums_here[:, i : i + 1]
        frm = cums_t[pl.ds(j * PER_BLOCK + i, 1), :]
        only = scaled * lane_mask(i)
        decay = jnp.exp(jnp.minimum(to[:HALF] - frm[:, :HALF], 0.0))
        top = top + mm((gram_s[:HALF, :HALF] * decay).astype(BF16), only[:HALF])
        decay = jnp.exp(jnp.minimum(to[HALF:] - frm, 0.0))
        bottom = bottom + mm((gram_s[HALF:, :] * decay).astype(BF16), only)
    mixed = total + jnp.concatenate([top, bottom], axis=0) + skip_ref[...] * x_float
    mixed_out[...] = mixed
    scaled_gate = (mixed * (gate * jax.nn.sigmoid(gate)) * gain_ref[...]).astype(BF16)

    @pl.when(j == 0)
    def _():
        made[...] = mm(scaled_gate, out_w[pl.ds(at, BLOCK), :])

    @pl.when(j > 0)
    def _():
        made[...] += mm(scaled_gate, out_w[pl.ds(at, BLOCK), :])

    @pl.when(j == blocks - 1)
    def _():
        made_out[...] = made[...].astype(BF16)


def branch_kernel(
    tp_size, total_inner, cot_ref, out_w, gate_ref, mixed_ref, gain_ref,
    grad_out, stats_out, sums_s, slots, turn_s, send_sem, recv_sem,
):
    step, groups = pl.program_id(0), pl.num_programs(0)
    me, column = lax.axis_index("tp"), lax.axis_index("fsdp")
    grad = mm_nt(cot_ref[...], out_w[...])
    grad_out[...] = grad.astype(BF16)
    gate = gate_ref[...].astype(F32)
    gated = mixed_ref[...] * (gate * jax.nn.sigmoid(gate))
    squares = jnp.sum(gated * gated, axis=1, keepdims=True)
    inner = jnp.sum(grad * gain_ref[...] * gated, axis=1, keepdims=True)
    lane = iota((GROUP, 128), 1)
    both = jnp.where(lane == 0, squares, jnp.where(lane == 1, inner, 0.0))
    sums_s[step] = jnp.transpose(both)[:8]

    @pl.when(step == groups - 1)
    def _():
        greet([(column, lax.rem(me + hop, tp_size)) for hop in range(1, tp_size)])
        slots[me] = sums_s[...]
        copies = [
            remote_copy(
                sums_s, slots.at[me], send_sem.at[hop - 1], recv_sem.at[hop - 1],
                (column, lax.rem(me + hop, tp_size)),
            )
            for hop in range(1, tp_size)
        ]
        for copy in copies:
            copy.start()
        for copy in copies:
            copy.wait()
        total = slots[0]
        for at in range(1, tp_size):
            total = total + slots[at]
        turn_s[...] = jnp.zeros(turn_s.shape, F32)
        scale = lax.rsqrt(total[:, 0:1, :] / total_inner + EPSILON)
        turn_s[:, 0:1, :] = scale
        turn_s[:, 1:2, :] = scale * scale * scale * (total[:, 1:2, :] / total_inner)
        for group in range(turn_s.shape[0]):
            stats_out[group * GROUP : (group + 1) * GROUP, :] = jnp.transpose(turn_s[group])


def backward_kernel(
    gate_ref, value_ref, before_ref, mixed_ref, grad_ref, bc_ref, stepin_ref, cums_ref, held_ref,
    stats_ref, gate_w, value_w, step_w, taps_ref, bias_ref, rate_ref, skip_ref, gain_ref,
    cols_ref, seg_ref,
    branch_out, lowgate_out, lowvalue_out, lowstep_out, gbc_out, gin_out, small_out, sums_out,
    vbuf, gcbuf, gram_s, dgram, b_s, c_t, step_s, ent_s, fade_s, cums_s, cums_t, keep_s, grad_state,
    gin, gb_s, gc_s, u_s, v_s, fin_s, small_s, sums_s,
):
    g, j = pl.program_id(0), pl.program_id(1)
    groups, blocks = pl.num_programs(0), pl.num_programs(1)
    nblocks = grad_state.shape[0]
    cols = cols_ref[...]
    at_row, at_col = iota((GROUP, GROUP), 0), iota((GROUP, GROUP), 1)

    @pl.when((g == 0) & (j == 0))
    def _():
        grad_state[...] = jnp.zeros(grad_state.shape, F32)
        small_s[...] = jnp.zeros(small_s.shape, F32)
        sums_s[...] = jnp.zeros(sums_s.shape, F32)
        gcbuf[...] = jnp.zeros(gcbuf.shape, F32)

    @pl.when(j == 0)
    def _():
        bc = bc_ref[...]
        b_low, c_low = bc[:, :STATE], bc[:, STATE:]
        b_s[...] = b_low
        c_t[...] = jnp.transpose(c_low.astype(F32)).astype(BF16)
        cums = cums_ref[...]
        step, entering, fading, retain = token_quantities(stepin_ref[...], cums, cols, rate_ref[...])
        spread(step_s, step, nblocks)
        spread(ent_s, entering, nblocks)
        spread(fade_s, fading, nblocks)
        spread(cums_s, cums, nblocks)
        spread(keep_s, jnp.broadcast_to(retain, (8, 128)), nblocks)
        cums_t[...] = jnp.transpose(cums)
        within = (at_row <= at_col) & (cols[:, 9:10] == seg_ref[...])
        gram_s[...] = jnp.where(within, mm_nt(b_low, c_low), 0.0)
        dgram[...] = jnp.zeros(dgram.shape, F32)
        gin[...] = jnp.zeros(gin.shape, F32)
        gb_s[...] = jnp.zeros(gb_s.shape, F32)
        gc_s[...] = jnp.zeros(gc_s.shape, F32)
        u_s[...] = jnp.zeros(u_s.shape, F32)
        v_s[...] = jnp.zeros(v_s.shape, F32)
        fin_s[...] = jnp.zeros(fin_s.shape, F32)

    at = pl.multiple_of(j * BLOCK, BLOCK)
    gate, mixed, grad = gate_ref[...].astype(F32), mixed_ref[...], grad_ref[...].astype(F32)
    gain, skip, taps = gain_ref[...], skip_ref[...], taps_ref[...]
    scale = stats_ref[:, 0:1]
    inner = stats_ref[:, 1:2]
    sig = jax.nn.sigmoid(gate)
    act = gate * sig
    gated = mixed * act
    scaled_gated = gated * scale
    branch_out[...] = (scaled_gated * gain).astype(BF16)
    grad_gain = jnp.sum(grad * scaled_gated, axis=0, keepdims=True)
    grad_gated = scale * (grad * gain) - gated * inner
    grad_mixed = grad_gated * act
    low_gate = (grad_gated * mixed * (sig * (1.0 + gate * (1.0 - sig)))).astype(BF16)
    lowgate_out[...] = low_gate

    vbuf[0:HALO, :] = before_ref[...]
    vbuf[HALO : HALO + GROUP, :] = value_ref[...]
    moved = shifted_values(vbuf, cols)
    conv = conv_of(moved, taps, bias_ref[...])
    sig = jax.nn.sigmoid(conv)
    x_float = (conv * sig).astype(BF16).astype(F32)
    slope = sig * (1.0 + conv * (1.0 - sig))
    step_wide = expand(step_s[j])
    fade_wide = expand(fade_s[j])
    scaled = (step_wide * x_float).astype(BF16)
    scaled_float = scaled.astype(F32)
    grad_skip = jnp.sum(grad_mixed * x_float, axis=0, keepdims=True)
    grad_scan = grad_mixed.astype(BF16)
    grad_scan_float = grad_scan.astype(F32)
    scanned = mixed - skip * x_float

    own = grad_state[j]
    state_low = held_ref[0]
    own_low = own.astype(BF16)
    grad_weighted = mm(b_s[...], own_low)
    weighted = (fade_wide * scaled_float).astype(BF16)
    entered = (expand(ent_s[j]) * grad_scan_float).astype(BF16)
    gb_s[...] += mm_nt(weighted, own_low)
    gc_s[...] += mm_nt(entered, state_low)
    keep_wide = expand(keep_s[j])[0:1, :]
    kept = keep_wide * jnp.sum(state_low.astype(F32) * own, axis=0, keepdims=True)
    grad_state[j] = keep_wide * own + mm(c_t[...], entered)

    cums_here = cums_s[j]
    top = jnp.zeros((HALF, BLOCK), F32)
    bottom = jnp.zeros((HALF, BLOCK), F32)
    dtop = dgram[:HALF, :]
    dbottom = dgram[HALF:, HALF:]
    for i in range(PER_BLOCK):
        frm = cums_here[:, i : i + 1]
        to = cums_t[pl.ds(j * PER_BLOCK + i, 1), :]
        mask = lane_mask(i)
        only_grad = grad_scan * mask
        only = scaled * mask
        decay = jnp.exp(jnp.minimum(to - frm[:HALF], 0.0))
        top = top + mm((gram_s[:HALF, :] * decay).astype(BF16), only_grad)
        dtop = dtop + mm_nt(only[:HALF], grad_scan) * decay
        decay = jnp.exp(jnp.minimum(to[:, HALF:] - frm[HALF:], 0.0))
        bottom = bottom + mm((gram_s[HALF:, HALF:] * decay).astype(BF16), only_grad[HALF:])
        dbottom = dbottom + mm_nt(only[HALF:], grad_scan[HALF:]) * decay
    dgram[:HALF, :] = dtop
    dgram[HALF:, HALF:] = dbottom
    faded = fade_wide * grad_weighted
    through = jnp.concatenate([top, bottom], axis=0) + faded
    column = scaled_float * through
    final = kept + jnp.sum(scaled_float * faded, axis=0, keepdims=True)
    place = (iota((BLOCK, 128), 1) == j * PER_BLOCK + iota((BLOCK, 128), 0) // HEAD_DIM).astype(F32)
    u_s[...] += mm(grad_scan_float * scanned - column, place, PRECISE)
    v_s[...] += mm(column, place, PRECISE)
    fin_s[...] += mm(jnp.broadcast_to(final, (8, BLOCK)), place, PRECISE)

    grad_conv = (step_wide * through + skip * grad_mixed) * slope
    after = gcbuf.at[j]
    after[GROUP : GROUP + HALO, :] = after[0:HALO, :]
    after[0:GROUP, :] = grad_conv
    grad_value = taps[0:1, :] * grad_conv
    for offset in range(1, CONV):
        up = jnp.where(cols[:, 2 + offset : 3 + offset] > 0.0, after[offset : offset + GROUP, :], 0.0)
        grad_value = grad_value + taps[offset : offset + 1, :] * up
    low_value = grad_value.astype(BF16)
    lowvalue_out[...] = low_value
    gin[...] += mm_nt(low_gate, gate_w[:, pl.ds(at, BLOCK)]) + mm_nt(low_value, value_w[:, pl.ds(at, BLOCK)])
    lines = [grad_gain, grad_skip]
    lines += [jnp.sum(grad_conv * moved[offset], axis=0, keepdims=True) for offset in range(CONV)]
    lines += [jnp.sum(grad_conv, axis=0, keepdims=True)]
    for at_line, line in enumerate(lines):
        small_s[j, at_line : at_line + 1, :] += line

    @pl.when(g == groups - 1)
    def _():
        small_out[:, pl.ds(at, BLOCK)] = small_s[j]

    @pl.when(j == blocks - 1)
    def _():
        bc = bc_ref[...]
        within = (at_row <= at_col) & (cols[:, 9:10] == seg_ref[...])
        dg = jnp.where(within, dgram[...], 0.0)
        grad_b = gb_s[...] + mm(dg.astype(BF16), bc[:, STATE:])
        grad_c = gc_s[...] + mm(jnp.transpose(dg).astype(BF16), bc[:, :STATE])
        gbc_out[:, :STATE] = grad_b.astype(BF16)
        gbc_out[:, STATE:] = grad_c.astype(BF16)
        last = iota((GROUP, 128), 0) == GROUP - 1
        grad_cums = u_s[...] + jnp.where(last, fin_s[0:1, :], 0.0)
        upper = (at_row <= at_col).astype(F32)
        grad_a = mm(upper, grad_cums, PRECISE)
        step_in = stepin_ref[...]
        step = jnp.maximum(step_in, 0.0) + jnp.log1p(jnp.exp(-jnp.abs(step_in)))
        sig_in = jax.nn.sigmoid(step_in)
        ratio = jnp.where(step_in < -15.0, 1.0, sig_in / step)
        grad_step = v_s[...] * ratio + grad_a * rate_ref[...] * sig_in
        low_step = grad_step.astype(BF16)
        lowstep_out[...] = low_step
        sums_s[0:1, :] += jnp.sum(grad_step, axis=0, keepdims=True)
        sums_s[1:2, :] += jnp.sum(grad_a * step, axis=0, keepdims=True)
        sums_out[...] = sums_s[...]
        gin_out[...] = (gin[...] + mm_nt(low_step, step_w[...])).astype(BF16)


def shape(dims, kind=F32):
    return jax.ShapeDtypeStruct(dims, kind)


def params(collective=None):
    extra = {} if collective is None else dict(collective_id=collective, has_side_effects=True)
    return pltpu.CompilerParams(
        dimension_semantics=("arbitrary", "arbitrary"), vmem_limit_bytes=60 << 20, **extra
    )


def whole(array):
    return pl.BlockSpec(
        array.shape, lambda g, j: (0,) * array.ndim, pipeline_mode=pl.Buffered(1)
    )


def forward_call(inputs, weights, vectors, gain, cols, seg_line, hosted, pace):
    gate_w, value_w, state_w, step_w, out_w = weights
    taps, bias, staps, sbias, step_bias, rate, skip = vectors
    length, model = inputs.shape
    inner = gate_w.shape[1]
    groups, blocks = length // GROUP, inner // BLOCK
    wide = pl.BlockSpec((GROUP, BLOCK), lambda g, j: (g, j))
    line = lambda rows: pl.BlockSpec((rows, BLOCK), lambda g, j: (0, j))
    rows_of = lambda width: pl.BlockSpec((GROUP, width), lambda g, j: (g, 0))
    specs, shapes = hosted.outs()
    return pl.pallas_call(
        hosted.wrap(forward_kernel, FORWARD_INS, FORWARD_OUTS, pace),
        grid=(groups, blocks),
        in_specs=[
            rows_of(model), whole(gate_w), whole(value_w), whole(state_w), whole(step_w),
            line(CONV), line(1), whole(staps), whole(sbias), whole(step_bias), whole(rate), line(1),
            rows_of(cols.shape[1]), pl.BlockSpec((1, GROUP), lambda g, j: (0, g)),
            whole(out_w), line(1),
        ] + hosted.in_specs(),
        out_specs=[
            wide, wide, wide, rows_of(2 * STATE), rows_of(2 * STATE), rows_of(128), rows_of(128),
            pl.BlockSpec((1, STATE, BLOCK), lambda g, j: (g, 0, j)), rows_of(model),
        ] + specs,
        out_shape=[
            shape((length, inner), BF16), shape((length, inner)), shape((length, inner)),
            shape((length, 2 * STATE), BF16), shape((length, 2 * STATE)), shape((length, 128)),
            shape((length, 128)), shape((groups, STATE, inner), BF16), shape((length, model), BF16),
        ] + shapes,
        scratch_shapes=[
            pltpu.VMEM((blocks, GROUP + HALO, BLOCK), F32),
            pltpu.VMEM((GROUP + HALO, 2 * STATE), F32),
            pltpu.VMEM((GROUP, GROUP), F32),
            pltpu.VMEM((STATE, GROUP), BF16),
            pltpu.VMEM((GROUP, STATE), BF16),
            pltpu.VMEM((blocks, GROUP, 128), F32),
            pltpu.VMEM((blocks, GROUP, 128), F32),
            pltpu.VMEM((blocks, GROUP, 128), F32),
            pltpu.VMEM((blocks, GROUP, 128), F32),
            pltpu.VMEM((128, GROUP), F32),
            pltpu.VMEM((blocks, 8, 128), F32),
            pltpu.VMEM((blocks, STATE, BLOCK), F32),
            pltpu.VMEM((GROUP, model), F32),
        ] + hosted.scratch(),
        compiler_params=params(2 if hosted.operands() else None),
        cost_estimate=pl.CostEstimate(
            flops=2 * length * model * (3 * inner + 512), bytes_accessed=40 << 20, transcendentals=0
        ),
        name="ssd_forward",
    )(
        inputs, gate_w, value_w, state_w, step_w, taps, bias, staps, sbias, step_bias, rate, skip,
        cols, seg_line, out_w, gain, *hosted.operands(),
    )


def branch_call(cotan, out_w, gate_raw, mixed, gain, tp_size):
    length, model = cotan.shape
    inner = out_w.shape[0]
    groups = length // GROUP
    rows_of = lambda width: pl.BlockSpec((GROUP, width), lambda i: (i, 0))
    full = lambda dims, **extra: pl.BlockSpec(dims, lambda i: (0, 0), **extra)
    return pl.pallas_call(
        partial(branch_kernel, tp_size, inner * tp_size),
        grid=(groups,),
        in_specs=[
            rows_of(model), full(out_w.shape, pipeline_mode=pl.Buffered(1)),
            rows_of(inner), rows_of(inner), full(gain.shape),
        ],
        out_specs=[rows_of(inner), full((length, 128))],
        out_shape=[shape((length, inner), BF16), shape((length, 128))],
        scratch_shapes=[
            pltpu.VMEM((groups, 8, GROUP), F32),
            pltpu.VMEM((tp_size, groups, 8, GROUP), F32),
            pltpu.VMEM((groups, 128, GROUP), F32),
            pltpu.SemaphoreType.DMA((tp_size - 1,)),
            pltpu.SemaphoreType.DMA((tp_size - 1,)),
        ],
        compiler_params=pltpu.CompilerParams(
            collective_id=3, has_side_effects=True, vmem_limit_bytes=50 << 20
        ),
        cost_estimate=pl.CostEstimate(
            flops=2 * length * model * inner, bytes_accessed=20 << 20, transcendentals=0
        ),
        name="branch_gradient",
    )(cotan, out_w, gate_raw, mixed, gain)


def backward_call(saved, grad_branch, stats, weights, vectors, gain, cols, seg_line, hosted, pace, collective):
    gate_raw, value_raw, mixed, bc, _, step_in, cums, held, _ = saved
    gate_w, value_w, step_w = weights
    taps, bias, rate, skip = vectors
    length, inner = gate_raw.shape
    model = gate_w.shape[0]
    specs, shapes = hosted.outs()
    groups, blocks = length // GROUP, inner // BLOCK
    last = groups - 1
    wide = pl.BlockSpec((GROUP, BLOCK), lambda g, j: (last - g, j))
    line = lambda rows: pl.BlockSpec((rows, BLOCK), lambda g, j: (0, j))
    rows_of = lambda width: pl.BlockSpec((GROUP, width), lambda g, j: (last - g, 0))
    steps = GROUP // HALO
    before = pl.BlockSpec(
        (HALO, BLOCK), lambda g, j: (jnp.maximum((last - g) * steps - 1, 0), j)
    )
    return pl.pallas_call(
        hosted.wrap(backward_kernel, BACKWARD_INS, BACKWARD_OUTS, pace),
        grid=(groups, blocks),
        in_specs=[
            wide, wide, before, wide, wide, rows_of(2 * STATE), rows_of(128), rows_of(128),
            pl.BlockSpec((1, STATE, BLOCK), lambda g, j: (last - g, 0, j)),
            rows_of(128), whole(gate_w), whole(value_w), whole(step_w),
            line(CONV), line(1), whole(rate), line(1), line(1),
            rows_of(cols.shape[1]), pl.BlockSpec((1, GROUP), lambda g, j: (0, last - g)),
        ] + hosted.in_specs(),
        out_specs=[
            wide, wide, wide, rows_of(128), rows_of(2 * STATE), rows_of(model),
            pl.BlockSpec((8, inner), lambda g, j: (0, 0)), pl.BlockSpec((8, 128), lambda g, j: (0, 0)),
        ] + specs,
        out_shape=[
            shape((length, inner), BF16), shape((length, inner), BF16), shape((length, inner), BF16),
            shape((length, 128), BF16), shape((length, 2 * STATE), BF16),
            shape((length, model), BF16), shape((8, inner)), shape((8, 128)),
        ] + shapes,
        scratch_shapes=[
            pltpu.VMEM((GROUP + HALO, BLOCK), F32),
            pltpu.VMEM((blocks, GROUP + HALO, BLOCK), F32),
            pltpu.VMEM((GROUP, GROUP), F32),
            pltpu.VMEM((GROUP, GROUP), F32),
            pltpu.VMEM((GROUP, STATE), BF16),
            pltpu.VMEM((STATE, GROUP), BF16),
            pltpu.VMEM((blocks, GROUP, 128), F32),
            pltpu.VMEM((blocks, GROUP, 128), F32),
            pltpu.VMEM((blocks, GROUP, 128), F32),
            pltpu.VMEM((blocks, GROUP, 128), F32),
            pltpu.VMEM((128, GROUP), F32),
            pltpu.VMEM((blocks, 8, 128), F32),
            pltpu.VMEM((blocks, STATE, BLOCK), F32),
            pltpu.VMEM((GROUP, model), F32),
            pltpu.VMEM((GROUP, STATE), F32),
            pltpu.VMEM((GROUP, STATE), F32),
            pltpu.VMEM((GROUP, 128), F32),
            pltpu.VMEM((GROUP, 128), F32),
            pltpu.VMEM((8, 128), F32),
            pltpu.VMEM((blocks, 8, BLOCK), F32),
            pltpu.VMEM((8, 128), F32),
        ] + hosted.scratch(),
        compiler_params=params(collective),
        cost_estimate=pl.CostEstimate(
            flops=6 * length * model * inner, bytes_accessed=60 << 20, transcendentals=0
        ),
        name="ssd_backward",
    )(
        gate_raw, value_raw, value_raw, mixed, grad_branch, bc, step_in, cums, held, stats,
        gate_w, value_w, step_w, taps, bias, rate, skip, gain, cols, seg_line, *hosted.operands(),
    )

def gather_kernel(count, pieces, *refs):
    amount = len(pieces)
    sources, targets = refs[:amount], refs[amount : 2 * amount]
    own_sem, send_sem, recv_sem, pass_sem, took_sem = refs[2 * amount :]
    me, line = lax.axis_index("fsdp"), lax.axis_index("tp")
    chips = count // 2
    partner = me + 1 - 2 * lax.rem(me, 2)
    others = [lax.rem(me + 2 * hop, count) for hop in range(1, chips)]
    greet([(device, line) for device in others + [partner]])

    def remote(source, target, sends, receives, device):
        return pltpu.make_async_remote_copy(
            src_ref=source, dst_ref=target, send_sem=sends, recv_sem=receives,
            device_id=(device, line), device_id_type=MESH,
        )

    def place(which, at):
        size, axis = pieces[which]
        return part_of(targets[which], at, size, axis)

    started = []
    for which in range(amount):
        for hop in range(1, chips):
            copy = remote(
                sources[which], place(which, me), send_sem.at[hop, which],
                recv_sem.at[hop, which], lax.rem(me + 2 * hop, count),
            )
            copy.start()
            started.append(copy)
    for which in range(amount):
        copy = remote(
            sources[which], place(which, me), pass_sem.at[0, which], took_sem.at[0, which], partner
        )
        copy.start()
        started.append(copy)
    own = []
    for which in range(amount):
        copy = pltpu.make_async_copy(sources[which], place(which, me), own_sem.at[which])
        copy.start()
        own.append(copy)
    for which in range(amount):
        for hop in range(1, chips):
            origin = lax.rem(me - 2 * hop + count, count)
            block = place(which, origin)
            remote(
                block, block, send_sem.at[hop, which], recv_sem.at[hop, which], partner
            ).wait_recv()
            copy = remote(
                block, block, pass_sem.at[hop, which], took_sem.at[hop, which], partner
            )
            copy.start()
            started.append(copy)
    for which in range(amount):
        for hop in range(chips):
            block = place(which, lax.rem(partner - 2 * hop + count, count))
            remote(
                block, block, pass_sem.at[hop, which], took_sem.at[hop, which], partner
            ).wait_recv()
    for copy in started:
        copy.wait_send()
    for copy in own:
        copy.wait()


def gather_call(count, blocks, axes):
    pieces, shapes = [], []
    for block, axis in zip(blocks, axes):
        if axis == 2:
            pieces.append((0, 2))
            shapes.append(shape((count,) + block.shape, BF16))
        else:
            pieces.append((block.shape[axis], axis))
            dims = list(block.shape)
            dims[axis] *= count
            shapes.append(shape(tuple(dims), BF16))
    amount = len(blocks)
    sems = lambda: pltpu.SemaphoreType.DMA((count // 2, amount))
    return pl.pallas_call(
        partial(gather_kernel, count, pieces),
        in_specs=[pl.BlockSpec(memory_space=pl.ANY)] * amount,
        out_specs=[pl.BlockSpec(memory_space=pl.ANY)] * amount,
        out_shape=shapes,
        scratch_shapes=[pltpu.SemaphoreType.DMA((amount,)), sems(), sems(), sems(), sems()],
        compiler_params=pltpu.CompilerParams(collective_id=0, has_side_effects=True),
        cost_estimate=pl.CostEstimate(flops=0, bytes_accessed=250 << 20, transcendentals=0),
        name="gather_weights",
    )(*blocks)


def scatter_kernel(count, pieces, *refs):
    amount = len(pieces)
    sources, targets = refs[:amount], refs[amount : 2 * amount]
    scratch = refs[2 * amount :]
    mine, took, came = (scratch[at * amount : (at + 1) * amount] for at in range(3))
    own_sem, pass_sem, took_sem, send_sem, recv_sem = scratch[3 * amount :]
    me, line = lax.axis_index("fsdp"), lax.axis_index("tp")
    chips = count // 2
    partner = me + 1 - 2 * lax.rem(me, 2)
    others = [lax.rem(me + 2 * hop, count) for hop in range(1, chips)]
    greet([(device, line) for device in others + [partner]])

    def remote(source, target, sends, receives, device):
        return pltpu.make_async_remote_copy(
            src_ref=source, dst_ref=target, send_sem=sends, recv_sem=receives,
            device_id=(device, line), device_id_type=MESH,
        )

    def piece(which, at):
        size, axis = pieces[which]
        return part_of(sources[which], at, size, axis)

    order = list(range(1, chips)) + [0]
    handed, own = {}, {}
    for hop in order:
        for which in range(amount):
            copy = remote(
                piece(which, lax.rem(partner + 2 * hop, count)), took[which].at[hop],
                pass_sem.at[hop, which], took_sem.at[hop, which], partner,
            )
            copy.start()
            handed[hop, which] = copy
            copy = pltpu.make_async_copy(
                piece(which, lax.rem(me + 2 * hop, count)), mine[which].at[hop],
                own_sem.at[hop, which],
            )
            copy.start()
            own[hop, which] = copy
    sent = []
    for hop in order:
        for which in range(amount):
            own[hop, which].wait()
            handed[hop, which].wait_recv()
            total = mine[which][hop].astype(F32) + took[which][hop].astype(F32)
            if hop == 0:
                targets[which][...] = total
                continue
            mine[which][hop] = total.astype(BF16)
            copy = remote(
                mine[which].at[hop], came[which].at[hop - 1], send_sem.at[hop, which],
                recv_sem.at[hop, which], lax.rem(me + 2 * hop, count),
            )
            copy.start()
            sent.append(copy)
    for which in range(amount):
        for hop in range(1, chips):
            block = came[which].at[hop - 1]
            remote(
                block, block, send_sem.at[hop, which], recv_sem.at[hop, which], partner
            ).wait_recv()
            targets[which][...] += block[...].astype(F32)
    for copy in list(handed.values()) + sent:
        copy.wait_send()


def scatter_call(count, arrays, axes):
    pieces, shapes = [], []
    for array, axis in zip(arrays, axes):
        if axis == 2:
            pieces.append((0, 2))
            shapes.append(array.shape[1:])
        else:
            dims = list(array.shape)
            dims[axis] //= count
            pieces.append((dims[axis], axis))
            shapes.append(tuple(dims))
    amount, chips = len(arrays), count // 2
    sems = lambda: pltpu.SemaphoreType.DMA((chips, amount))
    return pl.pallas_call(
        partial(scatter_kernel, count, pieces),
        in_specs=[pl.BlockSpec(memory_space=pl.ANY)] * amount,
        out_specs=[pl.BlockSpec(memory_space=pltpu.VMEM)] * amount,
        out_shape=[shape(dims) for dims in shapes],
        scratch_shapes=[pltpu.VMEM((chips,) + dims, BF16) for dims in shapes]
        + [pltpu.VMEM((chips,) + dims, BF16) for dims in shapes]
        + [pltpu.VMEM((chips - 1,) + dims, BF16) for dims in shapes]
        + [sems(), sems(), sems(), sems(), sems()],
        compiler_params=pltpu.CompilerParams(
            collective_id=1, has_side_effects=True, vmem_limit_bytes=48 << 20
        ),
        cost_estimate=pl.CostEstimate(flops=0, bytes_accessed=250 << 20, transcendentals=0),
        name="scatter_gradients",
    )(*arrays)


def weight_kernel(micro, *refs):
    outs = refs[-4:]
    rows, lows = refs[:micro], refs[micro : 5 * micro]
    for which in range(4):
        total = mm_tn(rows[0][...], lows[which][...])
        for at in range(1, micro):
            total = total + mm_tn(rows[at][...], lows[4 * at + which][...])
        outs[which][...] = total.astype(BF16)


def weight_call(inputs, lows):
    micro, (length, model) = len(inputs), inputs[0].shape
    full = lambda array: pl.BlockSpec(array.shape, lambda g: (0, 0), pipeline_mode=pl.Buffered(1))
    flat = [array for low in lows for array in low]
    widths = [array.shape[1] for array in lows[0]]
    return pl.pallas_call(
        partial(weight_kernel, micro),
        grid=(model // BLOCK,),
        in_specs=[pl.BlockSpec((length, BLOCK), lambda g: (0, g))] * micro
        + [full(array) for array in flat],
        out_specs=[pl.BlockSpec((BLOCK, width), lambda g: (g, 0)) for width in widths],
        out_shape=[shape((model, width), BF16) for width in widths],
        compiler_params=pltpu.CompilerParams(vmem_limit_bytes=50 << 20),
        cost_estimate=pl.CostEstimate(
            flops=2 * micro * length * model * sum(widths), bytes_accessed=40 << 20, transcendentals=0
        ),
        name="weight_gradients",
    )(*inputs, *flat)


def outer_kernel(micro, *refs):
    total = mm_tn(refs[0][...], refs[micro][...])
    for at in range(1, micro):
        total = total + mm_tn(refs[at][...], refs[micro + at][...])
    refs[-1][...] = total.astype(BF16)


def outer_call(branches, cotans):
    micro, (length, inner) = len(branches), branches[0].shape
    model = cotans[0].shape[1]
    full = lambda array: pl.BlockSpec(array.shape, lambda g: (0, 0), pipeline_mode=pl.Buffered(1))
    return pl.pallas_call(
        partial(outer_kernel, micro),
        grid=(inner // BLOCK,),
        in_specs=[pl.BlockSpec((length, BLOCK), lambda g: (0, g))] * micro
        + [full(array) for array in cotans],
        out_specs=pl.BlockSpec((BLOCK, model), lambda g: (g, 0)),
        out_shape=shape((inner, model), BF16),
        compiler_params=pltpu.CompilerParams(vmem_limit_bytes=50 << 20),
        cost_estimate=pl.CostEstimate(
            flops=2 * micro * length * model * inner, bytes_accessed=30 << 20, transcendentals=0
        ),
        name="out_gradients",
    )(*branches, *cotans)


def shift_down(values, offset):
    return jnp.pad(values, ((offset, 0), (0, 0)))[: values.shape[0]]


def shift_up(values, offset):
    return jnp.pad(values, ((0, offset), (0, 0)))[offset:]


def document_columns(seg_row):
    length = seg_row.shape[0]
    previous = jnp.concatenate([jnp.full((1,), -1, seg_row.dtype), seg_row[GROUP - 1 : -1 : GROUP]])
    last = seg_row[GROUP - 1 :: GROUP]
    columns = []
    for offset in range(1, CONV):
        columns.append(jnp.pad(seg_row, (offset, 0), constant_values=-1)[:length] == seg_row)
    for offset in range(1, CONV):
        columns.append(jnp.pad(seg_row, (0, offset), constant_values=-1)[offset:] == seg_row)
    columns.append(seg_row == jnp.repeat(previous, GROUP))
    columns.append(seg_row == jnp.repeat(last, GROUP))
    columns.append(jnp.repeat(last == previous, GROUP))
    columns.append(seg_row)
    columns = [column.astype(F32) for column in columns]
    return jnp.stack(columns + [columns[0]] * (16 - len(columns)), axis=1)


def state_gradient(grad_bc, state_raw, taps, bias, cols):
    moved = [state_raw]
    for offset in range(1, CONV):
        moved.append(shift_down(state_raw, offset) * cols[:, offset - 1 : offset])
    conv = bias
    for offset in range(CONV):
        conv = conv + taps[offset][None, :] * moved[offset]
    sig = jax.nn.sigmoid(conv)
    grad_conv = grad_bc * (sig * (1.0 + conv * (1.0 - sig)))
    grad_raw = taps[0][None, :] * grad_conv
    for offset in range(1, CONV):
        grad_raw = grad_raw + taps[offset][None, :] * (
            shift_up(grad_conv, offset) * cols[:, 2 + offset : 3 + offset]
        )
    grad_taps = jnp.stack([jnp.sum(grad_conv * each, axis=0) for each in moved])
    return grad_raw.astype(BF16), grad_taps, jnp.sum(grad_conv, axis=0)


def local(
    hidden_in, segment_ids, cotangent, norm_gain, proj_gate, proj_value, proj_state, proj_step,
    conv_value, conv_value_bias, conv_state, conv_state_bias, step_bias, decay_log, skip_gain,
    gate_gain, proj_out,
):
    micro = hidden_in.shape[0]
    heads = step_bias.shape[0]
    rows_here = hidden_in.shape[2]
    tp_size = lax.axis_size("tp")
    me = lax.axis_index("tp")
    decay_rate = -jnp.exp(decay_log)
    pad_heads = lambda values: jnp.pad(values, (0, 128 - heads))[None, :]
    rate = pad_heads(decay_rate)
    step_bias_line = pad_heads(step_bias)
    skip = jnp.repeat(skip_gain, HEAD_DIM)[None, :]
    gain = gate_gain[None, :]
    taps, bias = conv_value, conv_value_bias[None, :]
    staps, sbias = conv_state, conv_state_bias[None, :]

    rows_float = hidden_in[:, 0].astype(F32)
    inv_root = lax.rsqrt(jnp.mean(rows_float * rows_float, axis=-1, keepdims=True) + EPSILON)
    input_rows = (rows_float * inv_root * norm_gain).astype(BF16)

    def gather_tp(values, *after):
        values = lax.optimization_barrier((values,) + after)[0]
        return lax.all_gather(values, "tp", axis=0, tiled=True)

    def scatter_tp(values, *after):
        values = lax.optimization_barrier((values,) + after)[0]
        return lax.psum_scatter(values, "tp", scatter_dimension=0, tiled=True)

    inputs = [gather_tp(input_rows[0])]
    fsdp_size = lax.axis_size("fsdp")
    model = hidden_in.shape[3]
    aligned = proj_out.shape[1] % 128 == 0
    axes = (0, 0, 0, 0, 1 if aligned else 2)
    step_block = jnp.pad(proj_step, ((0, 0), (0, 128 - heads)))
    gate_w, value_w, state_w, step_w, out_w = gather_call(
        fsdp_size, (proj_gate, proj_value, proj_state, step_block, proj_out), axes
    )
    if not aligned:
        out_w = jnp.transpose(out_w, (1, 0, 2)).reshape(-1, model)
    inputs.append(gather_tp(input_rows[1], inputs[0], step_w))
    forward_weights = (gate_w, value_w, state_w, step_w, out_w)
    vectors = (taps, bias, staps, sbias, step_bias_line, rate, skip)
    columns = [document_columns(segment_ids[at, 0]) for at in range(micro)]
    seg_lines = [segment_ids[at, 0].astype(F32)[None, :] for at in range(micro)]
    quick, slow = [0, 7, 15, 15, 15], [0, 5, 10, 15, 15]

    def forward(at, hosted):
        return forward_call(
            inputs[at], forward_weights, vectors, gain, columns[at], seg_lines[at], hosted, quick
        )

    def backward(at, hosted, collective):
        grad_branch, stats = branch_call(cotans[at], out_w, saved[at][0], saved[at][2], gain, tp_size)
        scales.append(stats)
        return backward_call(
            saved[at], grad_branch, stats, (gate_w, value_w, step_w), (taps, bias, rate, skip),
            gain, columns[at], seg_lines[at], hosted, slow, collective,
        )

    scales, produced, summed = [], [], []
    saved = [forward(0, Hosted(tp_size))]
    *kept, made_sum, cotan = forward(1, Hosted(tp_size, saved[0][8], cotangent[0, 0]))
    saved.append(kept)
    produced.append(made_sum)
    cotans = [cotan]
    *former, made_sum, cotan = backward(0, Hosted(tp_size, saved[1][8], cotangent[1, 0]), 4)
    produced.append(made_sum)
    cotans.append(cotan)
    grad_bcs = [lax.psum(former[4], "tp")]
    *latter, gin_sum = backward(1, Hosted(tp_size, former[5]), 5)
    summed.append(gin_sum)
    grad_bcs.append(lax.psum(lax.optimization_barrier((latter[4], grad_bcs[0]))[0], "tp"))
    summed.append(scatter_tp(latter[5], grad_bcs[1]).astype(F32))
    lows = [[each[1], each[2], each[3], each[0]] for each in (former, latter)]
    smalls = [(each[6], each[7]) for each in (former, latter)]
    raws = [each[4] for each in saved]

    gin_rows = []
    for at in range(micro):
        low_state, grad_staps, grad_sbias = state_gradient(
            grad_bcs[at].astype(F32), raws[at], staps, sbias, columns[at]
        )
        mine = lax.dynamic_slice_in_dim(low_state, me * rows_here, rows_here, axis=0)
        gin_rows.append(summed[at] + mm_nt(mine, state_w))
        low_gate, low_value, low_step, branch = lows[at]
        lows[at] = (low_gate, low_value, low_state, low_step, branch)
        smalls[at] = smalls[at] + (grad_staps, grad_sbias)
    block_rows = []
    for at in range(micro):
        scale = lax.dynamic_slice_in_dim(scales[at], me * rows_here, rows_here, axis=0)[:, 0:1]
        block_rows.append((rows_float[at] + produced[at] * scale).astype(BF16))

    grad_out = outer_call([low[4] for low in lows], cotans)
    grad_gate, grad_value, grad_state, grad_step = weight_call(inputs, [low[:4] for low in lows])
    if not aligned:
        grad_out = jnp.transpose(grad_out.reshape(-1, fsdp_size, proj_out.shape[1]), (1, 0, 2))
    grad_gate, grad_value, grad_state, grad_step, grad_out = scatter_call(
        fsdp_size, (grad_gate, grad_value, grad_state, grad_step, grad_out), axes
    )
    grad_step = grad_step[:, :heads]

    grad_inputs = jnp.stack(gin_rows)
    grad_norm_gain = jnp.sum(grad_inputs * rows_float * inv_root, axis=(0, 1))
    grad_normed = grad_inputs * norm_gain
    grad_rows = inv_root * grad_normed - rows_float * inv_root**3 * jnp.mean(
        grad_normed * rows_float, axis=-1, keepdims=True
    )
    grad_hidden = (cotangent[:, 0].astype(F32) + grad_rows).astype(BF16)

    small, step_sums, grad_staps, grad_sbias = (sum(parts) for parts in zip(*smalls))
    small, step_sums, grad_staps, grad_sbias = lax.psum(
        (small, step_sums, grad_staps, grad_sbias), "fsdp"
    )
    gain_total = lax.psum(grad_norm_gain, ("fsdp", "tp"))
    return (
        jnp.stack(block_rows)[:, None],
        grad_hidden[:, None],
        gain_total,
        grad_gate,
        grad_value,
        grad_state,
        grad_step,
        small[2 : 2 + CONV],
        small[2 + CONV],
        grad_staps,
        grad_sbias,
        step_sums[0, :heads],
        step_sums[1, :heads] * decay_rate,
        jnp.sum(small[1].reshape(heads, HEAD_DIM), axis=1),
        small[0],
        grad_out,
    )


def solution(mesh):
    in_specs = (
        P(None, "fsdp", "tp", None), P(None, "fsdp", None), P(None, "fsdp", "tp", None), P(),
        P("fsdp", "tp"), P("fsdp", "tp"), P("fsdp", None), P("fsdp", "tp"), P(None, "tp"), P("tp"),
        P(), P(), P("tp"), P("tp"), P("tp"), P("tp"), P("tp", "fsdp"),
    )
    out_specs = (
        P(None, "fsdp", "tp", None), P(None, "fsdp", "tp", None), P(), P("fsdp", "tp"),
        P("fsdp", "tp"), P("fsdp", None), P("fsdp", "tp"), P(None, "tp"), P("tp"), P(), P(),
        P("tp"), P("tp"), P("tp"), P("tp"), P("tp", "fsdp"),
    )
    return jax.shard_map(local, mesh=mesh, in_specs=in_specs, out_specs=out_specs, check_vma=False)
```

```python
from functools import partial

import jax
import jax.numpy as jnp
from jax import lax
from jax.experimental import pallas as pl
from jax.experimental.pallas import tpu as pltpu
from jax.sharding import PartitionSpec as P

HEAD_DIM = 64
STATE = 128
CONV = 4
GROUP = 256
HALF = GROUP // 2
BLOCK = 256
PER_BLOCK = BLOCK // HEAD_DIM
HALO = 8
INNER = 4096
EPSILON = 1e-05
PRECISE = lax.Precision.HIGHEST
FORWARD_INS, FORWARD_OUTS = 16, 9
BACKWARD_INS, BACKWARD_OUTS = 20, 8
F32 = jnp.float32
BF16 = jnp.bfloat16


def mm(former, latter, precision=None):
    return jnp.dot(former, latter, preferred_element_type=F32, precision=precision)


def mm_nt(former, latter):
    return lax.dot_general(
        former, latter, (((1,), (1,)), ((), ())), preferred_element_type=F32
    )


def mm_tn(former, latter):
    return lax.dot_general(
        former, latter, (((0,), (0,)), ((), ())), preferred_element_type=F32
    )


def iota(shape, axis):
    return lax.broadcasted_iota(jnp.int32, shape, axis)


def expand(columns):
    rows = columns.shape[0]
    lane = iota((rows, 128), 1)
    parts = []
    for pair in range(PER_BLOCK // 2):
        former = jnp.broadcast_to(columns[:, 2 * pair : 2 * pair + 1], (rows, 128))
        latter = jnp.broadcast_to(columns[:, 2 * pair + 1 : 2 * pair + 2], (rows, 128))
        parts.append(jnp.where(lane < HEAD_DIM, former, latter))
    return jnp.concatenate(parts, axis=1)


def lane_mask(head):
    lane = iota((1, BLOCK), 1)
    return ((lane // HEAD_DIM) == head).astype(F32).astype(BF16)


def spread(ref, values, blocks):
    for block in range(blocks):
        shift = (128 - PER_BLOCK * block) % 128
        ref[block] = pltpu.roll(values, shift, 1) if shift else values


def token_quantities(step_in, cums, cols, decay_rate):
    step = jnp.maximum(step_in, 0.0) + jnp.log1p(jnp.exp(-jnp.abs(step_in)))
    final = cums[GROUP - 1 : GROUP, :]
    entering = jnp.exp(cums) * cols[:, 6:7]
    fading = jnp.exp(final - cums) * cols[:, 7:8]
    retain = jnp.exp(final) * cols[0:1, 8:9]
    return step, entering, fading, retain


def shifted_values(buf, cols):
    moved = [buf[HALO : HALO + GROUP, :]]
    for offset in range(1, CONV):
        before = buf[HALO - offset : HALO - offset + GROUP, :]
        moved.append(jnp.where(cols[:, offset - 1 : offset] > 0.0, before, 0.0))
    return moved


def conv_of(moved, taps, bias):
    total = bias + taps[0:1, :] * moved[0]
    for offset in range(1, CONV):
        total = total + taps[offset : offset + 1, :] * moved[offset]
    return total


MESH = pl.DeviceIdType.MESH


def part_of(ref, at, size, axis):
    if axis == 0:
        return ref.at[pl.ds(pl.multiple_of(at * size, size), size), :]
    if axis == 1:
        return ref.at[:, pl.ds(pl.multiple_of(at * size, size), size)]
    return ref.at[at]


def greet(devices):
    barrier = pltpu.get_barrier_semaphore()
    for device in devices:
        pl.semaphore_signal(barrier, inc=1, device_id=device, device_id_type=MESH)
    pl.semaphore_wait(barrier, len(devices))


def remote_copy(source, target, sends, receives, device):
    return pltpu.make_async_remote_copy(
        src_ref=source, dst_ref=target, send_sem=sends, recv_sem=receives,
        device_id=device, device_id_type=MESH,
    )


class LineScatter:
    def __init__(self, size, source, own, slots, last, own_sem, send_sem, recv_sem, last_sem):
        self.size, self.source, self.own, self.slots, self.last = size, source, own, slots, last
        self.own_sem, self.send_sem, self.recv_sem, self.last_sem = own_sem, send_sem, recv_sem, last_sem
        self.me, self.column = lax.axis_index("tp"), lax.axis_index("fsdp")
        self.rows = last.shape[0]

    @staticmethod
    def scratch(size, rows, width):
        hops = size - 1
        return [
            pltpu.VMEM((2, hops, rows, width), BF16), pltpu.VMEM((2, hops, rows, width), BF16),
            pltpu.VMEM((rows, width), BF16), pltpu.SemaphoreType.DMA((2, hops)),
            pltpu.SemaphoreType.DMA((2, hops)), pltpu.SemaphoreType.DMA((2, hops)),
            pltpu.SemaphoreType.DMA((1,)),
        ]

    def place(self, flow):
        return self.me if flow == 0 else self.size - 1 - self.me

    def local(self, flow, hop):
        block = self.size - 1 - hop + self.place(flow)
        if flow:
            block = self.size - 1 - block
        at = pl.multiple_of(block * self.rows, self.rows)
        return pltpu.make_async_copy(
            self.source.at[pl.ds(at, self.rows), :], self.own.at[flow, hop], self.own_sem.at[flow, hop]
        )

    def final(self):
        at = pl.multiple_of(self.me * self.rows, self.rows)
        return pltpu.make_async_copy(
            self.source.at[pl.ds(at, self.rows), :], self.last, self.last_sem.at[0]
        )

    def sending(self, flow, hop):
        neighbour = self.me + 1 if flow == 0 else self.me - 1
        neighbour = jnp.clip(neighbour, 0, self.size - 1)
        return remote_copy(
            self.own.at[flow, hop], self.slots.at[flow, hop], self.send_sem.at[flow, hop],
            self.recv_sem.at[flow, hop], (self.column, neighbour),
        )

    def begin(self):
        self.final().start()
        for hop in range(self.size - 1):
            for flow in range(2):

                @pl.when(self.place(flow) <= hop)
                def _():
                    self.local(flow, hop).start()

    def hop(self, hop):
        for flow in range(2):
            place = self.place(flow)

            @pl.when(place <= hop)
            def _():
                self.local(flow, hop).wait()
                if hop > 0:

                    @pl.when(place >= 1)
                    def _():
                        self.sending(flow, hop - 1).wait_recv()
                        total = self.own[flow, hop].astype(F32) + self.slots[flow, hop - 1].astype(F32)
                        self.own[flow, hop] = total.astype(BF16)

                self.sending(flow, hop).start()

    def end(self, out):
        hops = self.size - 1
        self.final().wait()
        out[...] = self.last[...].astype(F32)
        for flow in range(2):

            @pl.when(self.place(flow) >= 1)
            def _():
                self.sending(flow, hops - 1).wait_recv()
                out[...] += self.slots[flow, hops - 1].astype(F32)

        for hop in range(hops):
            for flow in range(2):

                @pl.when(self.place(flow) <= hop)
                def _():
                    self.sending(flow, hop).wait_send()


class LineGather:
    def __init__(self, size, source, target, own_sem, send_sem, recv_sem):
        self.size, self.source, self.target = size, source, target
        self.own_sem, self.send_sem, self.recv_sem = own_sem, send_sem, recv_sem
        self.me, self.column = lax.axis_index("tp"), lax.axis_index("fsdp")
        self.rows = source.shape[0]

    @staticmethod
    def scratch(size):
        return [
            pltpu.SemaphoreType.DMA((1,)), pltpu.SemaphoreType.DMA((2, size - 1)),
            pltpu.SemaphoreType.DMA((2, size - 1)),
        ]

    def place(self, flow):
        return self.me if flow == 0 else self.size - 1 - self.me

    def block(self, at):
        at = pl.multiple_of(jnp.clip(at, 0, self.size - 1) * self.rows, self.rows)
        return self.target.at[pl.ds(at, self.rows), :]

    def sending(self, flow, hop):
        neighbour = self.me + 1 if flow == 0 else self.me - 1
        neighbour = jnp.clip(neighbour, 0, self.size - 1)
        block = self.block(self.me - hop if flow == 0 else self.me + hop)
        return remote_copy(
            self.source if hop == 0 else block, block, self.send_sem.at[flow, hop],
            self.recv_sem.at[flow, hop], (self.column, neighbour),
        )

    def local(self):
        return pltpu.make_async_copy(self.source, self.block(self.me), self.own_sem.at[0])

    def begin(self):
        self.local().start()
        self.hop(0)

    def hop(self, hop):
        for flow in range(2):
            place = self.place(flow)
            if hop > 0:

                @pl.when(place >= hop)
                def _():
                    self.sending(flow, hop - 1).wait_recv()

            if hop < self.size - 1:

                @pl.when((place >= hop) & (place < self.size - 1))
                def _():
                    self.sending(flow, hop).start()

    def end(self):
        self.hop(self.size - 1)
        self.local().wait()
        for hop in range(self.size - 1):
            for flow in range(2):
                place = self.place(flow)

                @pl.when((place >= hop) & (place < self.size - 1))
                def _():
                    self.sending(flow, hop).wait_send()


def run_line(step, steps, scatter, gather, out):
    size = (scatter or gather).size
    actions = [[] for _ in range(size + 1)]
    if scatter:
        first = 1 if gather else 0
        actions[0].append(scatter.begin)
        for hop in range(size - 1):
            actions[first + hop].append(partial(scatter.hop, hop))
        actions[first + size - 1].append(partial(scatter.end, out))
    if gather:
        actions[0].append(gather.begin)
        for hop in range(1, size - 1):
            actions[hop].insert(0, partial(gather.hop, hop))
        actions[size - 1].insert(0, gather.end)
    actions = [todo for todo in actions if todo]
    for at, todo in zip(steps, actions):
        if todo:

            @pl.when(step == at)
            def _():
                for action in todo:
                    action()


class Hosted:
    def __init__(self, size, scatter=None, gather=None):
        self.size, self.scatter, self.gather = size, scatter, gather

    def operands(self):
        return [each for each in (self.scatter, self.gather) if each is not None]

    def in_specs(self):
        return [pl.BlockSpec(memory_space=pl.ANY)] * len(self.operands())

    def outs(self):
        shapes, specs = [], []
        if self.scatter is not None:
            rows, width = self.scatter.shape[0] // self.size, self.scatter.shape[1]
            shapes.append(shape((rows, width)))
            specs.append(pl.BlockSpec((rows, width), lambda g, j: (0, 0)))
        if self.gather is not None:
            rows, width = self.gather.shape
            shapes.append(shape((rows * self.size, width), BF16))
            specs.append(pl.BlockSpec(memory_space=pl.ANY))
        return specs, shapes

    def scratch(self):
        needed = []
        if self.scatter is not None:
            rows, width = self.scatter.shape[0] // self.size, self.scatter.shape[1]
            needed += LineScatter.scratch(self.size, rows, width)
        if self.gather is not None:
            needed += LineGather.scratch(self.size)
        return needed

    def wrap(self, body, ins, outs, pace):
        has_scatter, has_gather = self.scatter is not None, self.gather is not None
        hosts = has_scatter + has_gather
        size, spare = self.size, len(self.scratch())
        if not hosts:
            return body

        def kernel(*refs):
            sources, targets = refs[ins : ins + hosts], refs[ins + hosts + outs : ins + outs + 2 * hosts]
            tail = refs[len(refs) - spare :]
            step = pl.program_id(0) * pl.num_programs(1) + pl.program_id(1)
            me, column = lax.axis_index("tp"), lax.axis_index("fsdp")

            @pl.when(step == 0)
            def _():
                greet([(column, lax.rem(me + hop, size)) for hop in range(1, size)])

            body(
                *refs[:ins], *refs[ins + hosts : ins + hosts + outs],
                *refs[ins + outs + 2 * hosts : len(refs) - spare],
            )
            scatter = LineScatter(size, sources[0], *tail[:7]) if has_scatter else None
            gather = LineGather(size, sources[-1], targets[-1], *tail[-3:]) if has_gather else None
            run_line(step, pace, scatter, gather, targets[0])

        return kernel


def forward_kernel(
    in_ref, gate_w, value_w, state_w, step_w, taps_ref, bias_ref, staps_ref, sbias_ref,
    step_bias_ref, rate_ref, skip_ref, cols_ref, seg_ref, out_w, gain_ref,
    gate_out, value_out, mixed_out, bc_out, sraw_out, stepin_out, cums_out, held_out, made_out,
    vbuf, sbuf, gram_s, b_t, c_s, step_s, ent_s, fade_s, cums_s, cums_t, keep_s, hidden, made,
):
    g, j = pl.program_id(0), pl.program_id(1)
    blocks = pl.num_programs(1)
    nblocks = hidden.shape[0]
    rows = in_ref[...]
    cols = cols_ref[...]

    @pl.when(j == 0)
    def _():
        sbuf[0:HALO, :] = sbuf[GROUP : GROUP + HALO, :]
        raw = mm(rows, state_w[...])
        sbuf[HALO : HALO + GROUP, :] = raw
        sraw_out[...] = raw
        conv = conv_of(shifted_values(sbuf, cols), staps_ref[...], sbias_ref[...])
        bc = (conv * jax.nn.sigmoid(conv)).astype(BF16)
        bc_out[...] = bc
        b_low, c_low = bc[:, :STATE], bc[:, STATE:]
        b_t[...] = jnp.transpose(b_low.astype(F32)).astype(BF16)
        c_s[...] = c_low
        step_in = mm(rows, step_w[...]) + step_bias_ref[...]
        stepin_out[...] = step_in
        step = jnp.maximum(step_in, 0.0) + jnp.log1p(jnp.exp(-jnp.abs(step_in)))
        at_row, at_col = iota((GROUP, GROUP), 0), iota((GROUP, GROUP), 1)
        lower = (at_row >= at_col).astype(F32)
        cums = mm(lower, step * rate_ref[...], PRECISE)
        cums_out[...] = cums
        step, entering, fading, retain = token_quantities(step_in, cums, cols, rate_ref[...])
        spread(step_s, step, nblocks)
        spread(ent_s, entering, nblocks)
        spread(fade_s, fading, nblocks)
        spread(cums_s, cums, nblocks)
        spread(keep_s, jnp.broadcast_to(retain, (8, 128)), nblocks)
        cums_t[...] = jnp.transpose(cums)
        within = (at_row >= at_col) & (cols[:, 9:10] == seg_ref[...])
        gram_s[...] = jnp.where(within, mm_nt(c_low, b_low), 0.0)

    at = pl.multiple_of(j * BLOCK, BLOCK)
    gate = mm(rows, gate_w[:, pl.ds(at, BLOCK)])
    gate_out[...] = gate.astype(BF16)
    value = mm(rows, value_w[:, pl.ds(at, BLOCK)])
    value_out[...] = value
    mine = vbuf.at[j]
    mine[0:HALO, :] = mine[GROUP : GROUP + HALO, :]
    mine[HALO : HALO + GROUP, :] = value
    conv = conv_of(shifted_values(mine, cols), taps_ref[...], bias_ref[...])
    x_low = (conv * jax.nn.sigmoid(conv)).astype(BF16)
    x_float = x_low.astype(F32)
    scaled_float = expand(step_s[j]) * x_float
    scaled = scaled_float.astype(BF16)

    @pl.when(g == 0)
    def _():
        hidden[j] = jnp.zeros((STATE, BLOCK), F32)

    state = hidden[j]
    state_low = state.astype(BF16)
    held_out[0] = state_low
    total = expand(ent_s[j]) * mm(c_s[...], state_low)
    weighted = (expand(fade_s[j]) * scaled.astype(F32)).astype(BF16)
    hidden[j] = expand(keep_s[j])[0:1, :] * state + mm(b_t[...], weighted)
    cums_here = cums_s[j]
    top = jnp.zeros((HALF, BLOCK), F32)
    bottom = jnp.zeros((HALF, BLOCK), F32)
    for i in range(PER_BLOCK):
        to = cums_here[:, i : i + 1]
        frm = cums_t[pl.ds(j * PER_BLOCK + i, 1), :]
        only = scaled * lane_mask(i)
        decay = jnp.exp(jnp.minimum(to[:HALF] - frm[:, :HALF], 0.0))
        top = top + mm((gram_s[:HALF, :HALF] * decay).astype(BF16), only[:HALF])
        decay = jnp.exp(jnp.minimum(to[HALF:] - frm, 0.0))
        bottom = bottom + mm((gram_s[HALF:, :] * decay).astype(BF16), only)
    mixed = total + jnp.concatenate([top, bottom], axis=0) + skip_ref[...] * x_float
    mixed_out[...] = mixed
    scaled_gate = (mixed * (gate * jax.nn.sigmoid(gate)) * gain_ref[...]).astype(BF16)

    @pl.when(j == 0)
    def _():
        made[...] = mm(scaled_gate, out_w[pl.ds(at, BLOCK), :])

    @pl.when(j > 0)
    def _():
        made[...] += mm(scaled_gate, out_w[pl.ds(at, BLOCK), :])

    @pl.when(j == blocks - 1)
    def _():
        made_out[...] = made[...].astype(BF16)


def branch_kernel(
    tp_size, total_inner, cot_ref, out_w, gate_ref, mixed_ref, gain_ref,
    grad_out, stats_out, sums_s, slots, turn_s, send_sem, recv_sem,
):
    step, groups = pl.program_id(0), pl.num_programs(0)
    me, column = lax.axis_index("tp"), lax.axis_index("fsdp")
    grad = mm_nt(cot_ref[...], out_w[...])
    grad_out[...] = grad.astype(BF16)
    gate = gate_ref[...].astype(F32)
    gated = mixed_ref[...] * (gate * jax.nn.sigmoid(gate))
    squares = jnp.sum(gated * gated, axis=1, keepdims=True)
    inner = jnp.sum(grad * gain_ref[...] * gated, axis=1, keepdims=True)
    lane = iota((GROUP, 128), 1)
    both = jnp.where(lane == 0, squares, jnp.where(lane == 1, inner, 0.0))
    sums_s[step] = jnp.transpose(both)[:8]

    @pl.when(step == groups - 1)
    def _():
        greet([(column, lax.rem(me + hop, tp_size)) for hop in range(1, tp_size)])
        slots[me] = sums_s[...]
        copies = [
            remote_copy(
                sums_s, slots.at[me], send_sem.at[hop - 1], recv_sem.at[hop - 1],
                (column, lax.rem(me + hop, tp_size)),
            )
            for hop in range(1, tp_size)
        ]
        for copy in copies:
            copy.start()
        for copy in copies:
            copy.wait()
        total = slots[0]
        for at in range(1, tp_size):
            total = total + slots[at]
        turn_s[...] = jnp.zeros(turn_s.shape, F32)
        scale = lax.rsqrt(total[:, 0:1, :] / total_inner + EPSILON)
        turn_s[:, 0:1, :] = scale
        turn_s[:, 1:2, :] = scale * scale * scale * (total[:, 1:2, :] / total_inner)
        for group in range(turn_s.shape[0]):
            stats_out[group * GROUP : (group + 1) * GROUP, :] = jnp.transpose(turn_s[group])


def backward_kernel(
    gate_ref, value_ref, before_ref, mixed_ref, grad_ref, bc_ref, stepin_ref, cums_ref, held_ref,
    stats_ref, gate_w, value_w, step_w, taps_ref, bias_ref, rate_ref, skip_ref, gain_ref,
    cols_ref, seg_ref,
    branch_out, lowgate_out, lowvalue_out, lowstep_out, gbc_out, gin_out, small_out, sums_out,
    vbuf, gcbuf, gram_s, dgram, b_s, c_t, step_s, ent_s, fade_s, cums_s, cums_t, keep_s, grad_state,
    gin, gb_s, gc_s, u_s, v_s, fin_s, small_s, sums_s,
):
    g, j = pl.program_id(0), pl.program_id(1)
    groups, blocks = pl.num_programs(0), pl.num_programs(1)
    nblocks = grad_state.shape[0]
    cols = cols_ref[...]
    at_row, at_col = iota((GROUP, GROUP), 0), iota((GROUP, GROUP), 1)

    @pl.when((g == 0) & (j == 0))
    def _():
        grad_state[...] = jnp.zeros(grad_state.shape, F32)
        small_s[...] = jnp.zeros(small_s.shape, F32)
        sums_s[...] = jnp.zeros(sums_s.shape, F32)
        gcbuf[...] = jnp.zeros(gcbuf.shape, F32)

    @pl.when(j == 0)
    def _():
        bc = bc_ref[...]
        b_low, c_low = bc[:, :STATE], bc[:, STATE:]
        b_s[...] = b_low
        c_t[...] = jnp.transpose(c_low.astype(F32)).astype(BF16)
        cums = cums_ref[...]
        step, entering, fading, retain = token_quantities(stepin_ref[...], cums, cols, rate_ref[...])
        spread(step_s, step, nblocks)
        spread(ent_s, entering, nblocks)
        spread(fade_s, fading, nblocks)
        spread(cums_s, cums, nblocks)
        spread(keep_s, jnp.broadcast_to(retain, (8, 128)), nblocks)
        cums_t[...] = jnp.transpose(cums)
        within = (at_row <= at_col) & (cols[:, 9:10] == seg_ref[...])
        gram_s[...] = jnp.where(within, mm_nt(b_low, c_low), 0.0)
        dgram[...] = jnp.zeros(dgram.shape, F32)
        gin[...] = jnp.zeros(gin.shape, F32)
        gb_s[...] = jnp.zeros(gb_s.shape, F32)
        gc_s[...] = jnp.zeros(gc_s.shape, F32)
        u_s[...] = jnp.zeros(u_s.shape, F32)
        v_s[...] = jnp.zeros(v_s.shape, F32)
        fin_s[...] = jnp.zeros(fin_s.shape, F32)

    at = pl.multiple_of(j * BLOCK, BLOCK)
    gate, mixed, grad = gate_ref[...].astype(F32), mixed_ref[...], grad_ref[...].astype(F32)
    gain, skip, taps = gain_ref[...], skip_ref[...], taps_ref[...]
    scale = stats_ref[:, 0:1]
    inner = stats_ref[:, 1:2]
    sig = jax.nn.sigmoid(gate)
    act = gate * sig
    gated = mixed * act
    scaled_gated = gated * scale
    branch_out[...] = (scaled_gated * gain).astype(BF16)
    grad_gain = jnp.sum(grad * scaled_gated, axis=0, keepdims=True)
    grad_gated = scale * (grad * gain) - gated * inner
    grad_mixed = grad_gated * act
    low_gate = (grad_gated * mixed * (sig * (1.0 + gate * (1.0 - sig)))).astype(BF16)
    lowgate_out[...] = low_gate

    vbuf[0:HALO, :] = before_ref[...]
    vbuf[HALO : HALO + GROUP, :] = value_ref[...]
    moved = shifted_values(vbuf, cols)
    conv = conv_of(moved, taps, bias_ref[...])
    sig = jax.nn.sigmoid(conv)
    x_float = (conv * sig).astype(BF16).astype(F32)
    slope = sig * (1.0 + conv * (1.0 - sig))
    step_wide = expand(step_s[j])
    fade_wide = expand(fade_s[j])
    scaled = (step_wide * x_float).astype(BF16)
    scaled_float = scaled.astype(F32)
    grad_skip = jnp.sum(grad_mixed * x_float, axis=0, keepdims=True)
    grad_scan = grad_mixed.astype(BF16)
    grad_scan_float = grad_scan.astype(F32)
    scanned = mixed - skip * x_float

    own = grad_state[j]
    state_low = held_ref[0]
    own_low = own.astype(BF16)
    grad_weighted = mm(b_s[...], own_low)
    weighted = (fade_wide * scaled_float).astype(BF16)
    entered = (expand(ent_s[j]) * grad_scan_float).astype(BF16)
    gb_s[...] += mm_nt(weighted, own_low)
    gc_s[...] += mm_nt(entered, state_low)
    keep_wide = expand(keep_s[j])[0:1, :]
    kept = keep_wide * jnp.sum(state_low.astype(F32) * own, axis=0, keepdims=True)
    grad_state[j] = keep_wide * own + mm(c_t[...], entered)

    cums_here = cums_s[j]
    top = jnp.zeros((HALF, BLOCK), F32)
    bottom = jnp.zeros((HALF, BLOCK), F32)
    dtop = dgram[:HALF, :]
    dbottom = dgram[HALF:, HALF:]
    for i in range(PER_BLOCK):
        frm = cums_here[:, i : i + 1]
        to = cums_t[pl.ds(j * PER_BLOCK + i, 1), :]
        mask = lane_mask(i)
        only_grad = grad_scan * mask
        only = scaled * mask
        decay = jnp.exp(jnp.minimum(to - frm[:HALF], 0.0))
        top = top + mm((gram_s[:HALF, :] * decay).astype(BF16), only_grad)
        dtop = dtop + mm_nt(only[:HALF], grad_scan) * decay
        decay = jnp.exp(jnp.minimum(to[:, HALF:] - frm[HALF:], 0.0))
        bottom = bottom + mm((gram_s[HALF:, HALF:] * decay).astype(BF16), only_grad[HALF:])
        dbottom = dbottom + mm_nt(only[HALF:], grad_scan[HALF:]) * decay
    dgram[:HALF, :] = dtop
    dgram[HALF:, HALF:] = dbottom
    faded = fade_wide * grad_weighted
    through = jnp.concatenate([top, bottom], axis=0) + faded
    column = scaled_float * through
    final = kept + jnp.sum(scaled_float * faded, axis=0, keepdims=True)
    place = (iota((BLOCK, 128), 1) == j * PER_BLOCK + iota((BLOCK, 128), 0) // HEAD_DIM).astype(F32)
    u_s[...] += mm(grad_scan_float * scanned - column, place, PRECISE)
    v_s[...] += mm(column, place, PRECISE)
    fin_s[...] += mm(jnp.broadcast_to(final, (8, BLOCK)), place, PRECISE)

    grad_conv = (step_wide * through + skip * grad_mixed) * slope
    after = gcbuf.at[j]
    after[GROUP : GROUP + HALO, :] = after[0:HALO, :]
    after[0:GROUP, :] = grad_conv
    grad_value = taps[0:1, :] * grad_conv
    for offset in range(1, CONV):
        up = jnp.where(cols[:, 2 + offset : 3 + offset] > 0.0, after[offset : offset + GROUP, :], 0.0)
        grad_value = grad_value + taps[offset : offset + 1, :] * up
    low_value = grad_value.astype(BF16)
    lowvalue_out[...] = low_value
    gin[...] += mm_nt(low_gate, gate_w[:, pl.ds(at, BLOCK)]) + mm_nt(low_value, value_w[:, pl.ds(at, BLOCK)])
    lines = [grad_gain, grad_skip]
    lines += [jnp.sum(grad_conv * moved[offset], axis=0, keepdims=True) for offset in range(CONV)]
    lines += [jnp.sum(grad_conv, axis=0, keepdims=True)]
    for at_line, line in enumerate(lines):
        small_s[j, at_line : at_line + 1, :] += line

    @pl.when(g == groups - 1)
    def _():
        small_out[:, pl.ds(at, BLOCK)] = small_s[j]

    @pl.when(j == blocks - 1)
    def _():
        bc = bc_ref[...]
        within = (at_row <= at_col) & (cols[:, 9:10] == seg_ref[...])
        dg = jnp.where(within, dgram[...], 0.0)
        grad_b = gb_s[...] + mm(dg.astype(BF16), bc[:, STATE:])
        grad_c = gc_s[...] + mm(jnp.transpose(dg).astype(BF16), bc[:, :STATE])
        gbc_out[:, :STATE] = grad_b.astype(BF16)
        gbc_out[:, STATE:] = grad_c.astype(BF16)
        last = iota((GROUP, 128), 0) == GROUP - 1
        grad_cums = u_s[...] + jnp.where(last, fin_s[0:1, :], 0.0)
        upper = (at_row <= at_col).astype(F32)
        grad_a = mm(upper, grad_cums, PRECISE)
        step_in = stepin_ref[...]
        step = jnp.maximum(step_in, 0.0) + jnp.log1p(jnp.exp(-jnp.abs(step_in)))
        sig_in = jax.nn.sigmoid(step_in)
        ratio = jnp.where(step_in < -15.0, 1.0, sig_in / step)
        grad_step = v_s[...] * ratio + grad_a * rate_ref[...] * sig_in
        low_step = grad_step.astype(BF16)
        lowstep_out[...] = low_step
        sums_s[0:1, :] += jnp.sum(grad_step, axis=0, keepdims=True)
        sums_s[1:2, :] += jnp.sum(grad_a * step, axis=0, keepdims=True)
        sums_out[...] = sums_s[...]
        gin_out[...] = (gin[...] + mm_nt(low_step, step_w[...])).astype(BF16)


def shape(dims, kind=F32):
    return jax.ShapeDtypeStruct(dims, kind)


def params(collective=None):
    extra = {} if collective is None else dict(collective_id=collective, has_side_effects=True)
    return pltpu.CompilerParams(
        dimension_semantics=("arbitrary", "arbitrary"), vmem_limit_bytes=60 << 20, **extra
    )


def whole(array):
    return pl.BlockSpec(
        array.shape, lambda g, j: (0,) * array.ndim, pipeline_mode=pl.Buffered(1)
    )


def forward_call(inputs, weights, vectors, gain, cols, seg_line, hosted, pace):
    gate_w, value_w, state_w, step_w, out_w = weights
    taps, bias, staps, sbias, step_bias, rate, skip = vectors
    length, model = inputs.shape
    inner = gate_w.shape[1]
    groups, blocks = length // GROUP, inner // BLOCK
    wide = pl.BlockSpec((GROUP, BLOCK), lambda g, j: (g, j))
    line = lambda rows: pl.BlockSpec((rows, BLOCK), lambda g, j: (0, j))
    rows_of = lambda width: pl.BlockSpec((GROUP, width), lambda g, j: (g, 0))
    specs, shapes = hosted.outs()
    return pl.pallas_call(
        hosted.wrap(forward_kernel, FORWARD_INS, FORWARD_OUTS, pace),
        grid=(groups, blocks),
        in_specs=[
            rows_of(model), whole(gate_w), whole(value_w), whole(state_w), whole(step_w),
            line(CONV), line(1), whole(staps), whole(sbias), whole(step_bias), whole(rate), line(1),
            rows_of(cols.shape[1]), pl.BlockSpec((1, GROUP), lambda g, j: (0, g)),
            whole(out_w), line(1),
        ] + hosted.in_specs(),
        out_specs=[
            wide, wide, wide, rows_of(2 * STATE), rows_of(2 * STATE), rows_of(128), rows_of(128),
            pl.BlockSpec((1, STATE, BLOCK), lambda g, j: (g, 0, j)), rows_of(model),
        ] + specs,
        out_shape=[
            shape((length, inner), BF16), shape((length, inner)), shape((length, inner)),
            shape((length, 2 * STATE), BF16), shape((length, 2 * STATE)), shape((length, 128)),
            shape((length, 128)), shape((groups, STATE, inner), BF16), shape((length, model), BF16),
        ] + shapes,
        scratch_shapes=[
            pltpu.VMEM((blocks, GROUP + HALO, BLOCK), F32),
            pltpu.VMEM((GROUP + HALO, 2 * STATE), F32),
            pltpu.VMEM((GROUP, GROUP), F32),
            pltpu.VMEM((STATE, GROUP), BF16),
            pltpu.VMEM((GROUP, STATE), BF16),
            pltpu.VMEM((blocks, GROUP, 128), F32),
            pltpu.VMEM((blocks, GROUP, 128), F32),
            pltpu.VMEM((blocks, GROUP, 128), F32),
            pltpu.VMEM((blocks, GROUP, 128), F32),
            pltpu.VMEM((128, GROUP), F32),
            pltpu.VMEM((blocks, 8, 128), F32),
            pltpu.VMEM((blocks, STATE, BLOCK), F32),
            pltpu.VMEM((GROUP, model), F32),
        ] + hosted.scratch(),
        compiler_params=params(2 if hosted.operands() else None),
        cost_estimate=pl.CostEstimate(
            flops=2 * length * model * (3 * inner + 512), bytes_accessed=40 << 20, transcendentals=0
        ),
        name="ssd_forward",
    )(
        inputs, gate_w, value_w, state_w, step_w, taps, bias, staps, sbias, step_bias, rate, skip,
        cols, seg_line, out_w, gain, *hosted.operands(),
    )


def branch_call(cotan, out_w, gate_raw, mixed, gain, tp_size):
    length, model = cotan.shape
    inner = out_w.shape[0]
    groups = length // GROUP
    rows_of = lambda width: pl.BlockSpec((GROUP, width), lambda i: (i, 0))
    full = lambda dims, **extra: pl.BlockSpec(dims, lambda i: (0, 0), **extra)
    return pl.pallas_call(
        partial(branch_kernel, tp_size, inner * tp_size),
        grid=(groups,),
        in_specs=[
            rows_of(model), full(out_w.shape, pipeline_mode=pl.Buffered(1)),
            rows_of(inner), rows_of(inner), full(gain.shape),
        ],
        out_specs=[rows_of(inner), full((length, 128))],
        out_shape=[shape((length, inner), BF16), shape((length, 128))],
        scratch_shapes=[
            pltpu.VMEM((groups, 8, GROUP), F32),
            pltpu.VMEM((tp_size, groups, 8, GROUP), F32),
            pltpu.VMEM((groups, 128, GROUP), F32),
            pltpu.SemaphoreType.DMA((tp_size - 1,)),
            pltpu.SemaphoreType.DMA((tp_size - 1,)),
        ],
        compiler_params=pltpu.CompilerParams(
            collective_id=3, has_side_effects=True, vmem_limit_bytes=50 << 20
        ),
        cost_estimate=pl.CostEstimate(
            flops=2 * length * model * inner, bytes_accessed=20 << 20, transcendentals=0
        ),
        name="branch_gradient",
    )(cotan, out_w, gate_raw, mixed, gain)


def backward_call(saved, grad_branch, stats, weights, vectors, gain, cols, seg_line, hosted, pace, collective):
    gate_raw, value_raw, mixed, bc, _, step_in, cums, held, _ = saved
    gate_w, value_w, step_w = weights
    taps, bias, rate, skip = vectors
    length, inner = gate_raw.shape
    model = gate_w.shape[0]
    specs, shapes = hosted.outs()
    groups, blocks = length // GROUP, inner // BLOCK
    last = groups - 1
    wide = pl.BlockSpec((GROUP, BLOCK), lambda g, j: (last - g, j))
    line = lambda rows: pl.BlockSpec((rows, BLOCK), lambda g, j: (0, j))
    rows_of = lambda width: pl.BlockSpec((GROUP, width), lambda g, j: (last - g, 0))
    steps = GROUP // HALO
    before = pl.BlockSpec(
        (HALO, BLOCK), lambda g, j: (jnp.maximum((last - g) * steps - 1, 0), j)
    )
    return pl.pallas_call(
        hosted.wrap(backward_kernel, BACKWARD_INS, BACKWARD_OUTS, pace),
        grid=(groups, blocks),
        in_specs=[
            wide, wide, before, wide, wide, rows_of(2 * STATE), rows_of(128), rows_of(128),
            pl.BlockSpec((1, STATE, BLOCK), lambda g, j: (last - g, 0, j)),
            rows_of(128), whole(gate_w), whole(value_w), whole(step_w),
            line(CONV), line(1), whole(rate), line(1), line(1),
            rows_of(cols.shape[1]), pl.BlockSpec((1, GROUP), lambda g, j: (0, last - g)),
        ] + hosted.in_specs(),
        out_specs=[
            wide, wide, wide, rows_of(128), rows_of(2 * STATE),
            rows_of(model), pl.BlockSpec((8, inner), lambda g, j: (0, 0)), pl.BlockSpec((8, 128), lambda g, j: (0, 0)),
        ] + specs,
        out_shape=[
            shape((length, inner), BF16), shape((length, inner), BF16), shape((length, inner), BF16),
            shape((length, 128), BF16), shape((length, 2 * STATE), BF16),
            shape((length, model), BF16), shape((8, inner)), shape((8, 128)),
        ] + shapes,
        scratch_shapes=[
            pltpu.VMEM((GROUP + HALO, BLOCK), F32),
            pltpu.VMEM((blocks, GROUP + HALO, BLOCK), F32),
            pltpu.VMEM((GROUP, GROUP), F32),
            pltpu.VMEM((GROUP, GROUP), F32),
            pltpu.VMEM((GROUP, STATE), BF16),
            pltpu.VMEM((STATE, GROUP), BF16),
            pltpu.VMEM((blocks, GROUP, 128), F32),
            pltpu.VMEM((blocks, GROUP, 128), F32),
            pltpu.VMEM((blocks, GROUP, 128), F32),
            pltpu.VMEM((blocks, GROUP, 128), F32),
            pltpu.VMEM((128, GROUP), F32),
            pltpu.VMEM((blocks, 8, 128), F32),
            pltpu.VMEM((blocks, STATE, BLOCK), F32),
            pltpu.VMEM((GROUP, model), F32),
            pltpu.VMEM((GROUP, STATE), F32),
            pltpu.VMEM((GROUP, STATE), F32),
            pltpu.VMEM((GROUP, 128), F32),
            pltpu.VMEM((GROUP, 128), F32),
            pltpu.VMEM((8, 128), F32),
            pltpu.VMEM((blocks, 8, BLOCK), F32),
            pltpu.VMEM((8, 128), F32),
        ] + hosted.scratch(),
        compiler_params=params(collective),
        cost_estimate=pl.CostEstimate(
            flops=6 * length * model * inner, bytes_accessed=60 << 20, transcendentals=0
        ),
        name="ssd_backward",
    )(
        gate_raw, value_raw, value_raw, mixed, grad_branch, bc, step_in, cums, held, stats,
        gate_w, value_w, step_w, taps, bias, rate, skip, gain, cols, seg_line, *hosted.operands(),
    )

def gather_kernel(count, pieces, *refs):
    amount = len(pieces)
    sources, targets = refs[:amount], refs[amount : 2 * amount]
    own_sem, send_sem, recv_sem, pass_sem, took_sem = refs[2 * amount :]
    me, line = lax.axis_index("fsdp"), lax.axis_index("tp")
    chips = count // 2
    partner = me + 1 - 2 * lax.rem(me, 2)
    others = [lax.rem(me + 2 * hop, count) for hop in range(1, chips)]
    greet([(device, line) for device in others + [partner]])

    def remote(source, target, sends, receives, device):
        return pltpu.make_async_remote_copy(
            src_ref=source, dst_ref=target, send_sem=sends, recv_sem=receives,
            device_id=(device, line), device_id_type=MESH,
        )

    def place(which, at):
        size, axis = pieces[which]
        return part_of(targets[which], at, size, axis)

    started = []
    for which in range(amount):
        for hop in range(1, chips):
            copy = remote(
                sources[which], place(which, me), send_sem.at[hop, which],
                recv_sem.at[hop, which], lax.rem(me + 2 * hop, count),
            )
            copy.start()
            started.append(copy)
    for which in range(amount):
        copy = remote(
            sources[which], place(which, me), pass_sem.at[0, which], took_sem.at[0, which], partner
        )
        copy.start()
        started.append(copy)
    own = []
    for which in range(amount):
        copy = pltpu.make_async_copy(sources[which], place(which, me), own_sem.at[which])
        copy.start()
        own.append(copy)
    for which in range(amount):
        for hop in range(1, chips):
            origin = lax.rem(me - 2 * hop + count, count)
            block = place(which, origin)
            remote(
                block, block, send_sem.at[hop, which], recv_sem.at[hop, which], partner
            ).wait_recv()
            copy = remote(
                block, block, pass_sem.at[hop, which], took_sem.at[hop, which], partner
            )
            copy.start()
            started.append(copy)
    for which in range(amount):
        for hop in range(chips):
            block = place(which, lax.rem(partner - 2 * hop + count, count))
            remote(
                block, block, pass_sem.at[hop, which], took_sem.at[hop, which], partner
            ).wait_recv()
    for copy in started:
        copy.wait_send()
    for copy in own:
        copy.wait()


def gather_call(count, blocks, axes):
    pieces, shapes = [], []
    for block, axis in zip(blocks, axes):
        if axis == 2:
            pieces.append((0, 2))
            shapes.append(shape((count,) + block.shape, BF16))
        else:
            pieces.append((block.shape[axis], axis))
            dims = list(block.shape)
            dims[axis] *= count
            shapes.append(shape(tuple(dims), BF16))
    amount = len(blocks)
    sems = lambda: pltpu.SemaphoreType.DMA((count // 2, amount))
    return pl.pallas_call(
        partial(gather_kernel, count, pieces),
        in_specs=[pl.BlockSpec(memory_space=pl.ANY)] * amount,
        out_specs=[pl.BlockSpec(memory_space=pl.ANY)] * amount,
        out_shape=shapes,
        scratch_shapes=[pltpu.SemaphoreType.DMA((amount,)), sems(), sems(), sems(), sems()],
        compiler_params=pltpu.CompilerParams(collective_id=0, has_side_effects=True),
        cost_estimate=pl.CostEstimate(flops=0, bytes_accessed=250 << 20, transcendentals=0),
        name="gather_weights",
    )(*blocks)


def scatter_kernel(count, pieces, *refs):
    amount = len(pieces)
    sources, targets = refs[:amount], refs[amount : 2 * amount]
    scratch = refs[2 * amount :]
    mine, took, came = (scratch[at * amount : (at + 1) * amount] for at in range(3))
    own_sem, pass_sem, took_sem, send_sem, recv_sem = scratch[3 * amount :]
    me, line = lax.axis_index("fsdp"), lax.axis_index("tp")
    chips = count // 2
    partner = me + 1 - 2 * lax.rem(me, 2)
    others = [lax.rem(me + 2 * hop, count) for hop in range(1, chips)]
    greet([(device, line) for device in others + [partner]])

    def remote(source, target, sends, receives, device):
        return pltpu.make_async_remote_copy(
            src_ref=source, dst_ref=target, send_sem=sends, recv_sem=receives,
            device_id=(device, line), device_id_type=MESH,
        )

    def piece(which, at):
        size, axis = pieces[which]
        return part_of(sources[which], at, size, axis)

    order = list(range(1, chips)) + [0]
    handed, own = {}, {}
    for hop in order:
        for which in range(amount):
            copy = remote(
                piece(which, lax.rem(partner + 2 * hop, count)), took[which].at[hop],
                pass_sem.at[hop, which], took_sem.at[hop, which], partner,
            )
            copy.start()
            handed[hop, which] = copy
            copy = pltpu.make_async_copy(
                piece(which, lax.rem(me + 2 * hop, count)), mine[which].at[hop],
                own_sem.at[hop, which],
            )
            copy.start()
            own[hop, which] = copy
    sent = []
    for hop in order:
        for which in range(amount):
            own[hop, which].wait()
            handed[hop, which].wait_recv()
            total = mine[which][hop].astype(F32) + took[which][hop].astype(F32)
            if hop == 0:
                targets[which][...] = total
                continue
            mine[which][hop] = total.astype(BF16)
            copy = remote(
                mine[which].at[hop], came[which].at[hop - 1], send_sem.at[hop, which],
                recv_sem.at[hop, which], lax.rem(me + 2 * hop, count),
            )
            copy.start()
            sent.append(copy)
    for which in range(amount):
        for hop in range(1, chips):
            block = came[which].at[hop - 1]
            remote(
                block, block, send_sem.at[hop, which], recv_sem.at[hop, which], partner
            ).wait_recv()
            targets[which][...] += block[...].astype(F32)
    for copy in list(handed.values()) + sent:
        copy.wait_send()


def scatter_call(count, arrays, axes):
    pieces, shapes = [], []
    for array, axis in zip(arrays, axes):
        if axis == 2:
            pieces.append((0, 2))
            shapes.append(array.shape[1:])
        else:
            dims = list(array.shape)
            dims[axis] //= count
            pieces.append((dims[axis], axis))
            shapes.append(tuple(dims))
    amount, chips = len(arrays), count // 2
    sems = lambda: pltpu.SemaphoreType.DMA((chips, amount))
    return pl.pallas_call(
        partial(scatter_kernel, count, pieces),
        in_specs=[pl.BlockSpec(memory_space=pl.ANY)] * amount,
        out_specs=[pl.BlockSpec(memory_space=pltpu.VMEM)] * amount,
        out_shape=[shape(dims) for dims in shapes],
        scratch_shapes=[pltpu.VMEM((chips,) + dims, BF16) for dims in shapes]
        + [pltpu.VMEM((chips,) + dims, BF16) for dims in shapes]
        + [pltpu.VMEM((chips - 1,) + dims, BF16) for dims in shapes]
        + [sems(), sems(), sems(), sems(), sems()],
        compiler_params=pltpu.CompilerParams(
            collective_id=1, has_side_effects=True, vmem_limit_bytes=48 << 20
        ),
        cost_estimate=pl.CostEstimate(flops=0, bytes_accessed=250 << 20, transcendentals=0),
        name="scatter_gradients",
    )(*arrays)


def weight_kernel(micro, *refs):
    outs = refs[-4:]
    rows, lows = refs[:micro], refs[micro : 5 * micro]
    for which in range(4):
        total = mm_tn(rows[0][...], lows[which][...])
        for at in range(1, micro):
            total = total + mm_tn(rows[at][...], lows[4 * at + which][...])
        outs[which][...] = total.astype(BF16)


def weight_call(inputs, lows):
    micro, (length, model) = len(inputs), inputs[0].shape
    full = lambda array: pl.BlockSpec(array.shape, lambda g: (0, 0), pipeline_mode=pl.Buffered(1))
    flat = [array for low in lows for array in low]
    widths = [array.shape[1] for array in lows[0]]
    return pl.pallas_call(
        partial(weight_kernel, micro),
        grid=(model // BLOCK,),
        in_specs=[pl.BlockSpec((length, BLOCK), lambda g: (0, g))] * micro
        + [full(array) for array in flat],
        out_specs=[pl.BlockSpec((BLOCK, width), lambda g: (g, 0)) for width in widths],
        out_shape=[shape((model, width), BF16) for width in widths],
        compiler_params=pltpu.CompilerParams(vmem_limit_bytes=50 << 20),
        cost_estimate=pl.CostEstimate(
            flops=2 * micro * length * model * sum(widths), bytes_accessed=40 << 20, transcendentals=0
        ),
        name="weight_gradients",
    )(*inputs, *flat)


def outer_kernel(micro, *refs):
    total = mm_tn(refs[0][...], refs[micro][...])
    for at in range(1, micro):
        total = total + mm_tn(refs[at][...], refs[micro + at][...])
    refs[-1][...] = total.astype(BF16)


def outer_call(branches, cotans):
    micro, (length, inner) = len(branches), branches[0].shape
    model = cotans[0].shape[1]
    full = lambda array: pl.BlockSpec(array.shape, lambda g: (0, 0), pipeline_mode=pl.Buffered(1))
    return pl.pallas_call(
        partial(outer_kernel, micro),
        grid=(inner // BLOCK,),
        in_specs=[pl.BlockSpec((length, BLOCK), lambda g: (0, g))] * micro
        + [full(array) for array in cotans],
        out_specs=pl.BlockSpec((BLOCK, model), lambda g: (g, 0)),
        out_shape=shape((inner, model), BF16),
        compiler_params=pltpu.CompilerParams(vmem_limit_bytes=50 << 20),
        cost_estimate=pl.CostEstimate(
            flops=2 * micro * length * model * inner, bytes_accessed=30 << 20, transcendentals=0
        ),
        name="out_gradients",
    )(*branches, *cotans)


def tail_kernel(chips, tp_size, micro, widths, *refs):
    columns, lows, parts, raws = refs[:4], refs[4:12], refs[12:14], refs[14:16]
    cols_ref, staps_ref, sbias_ref, pack = refs[16:20]
    outs, state_out, pack_out, ssum_out, low_out = refs[20:24], refs[24], refs[25], refs[26], refs[27]
    (
        cols_s, give, took, mine, came, passed, total_s, kept_s,
        sgive, stook, smine, scame, stotal, skept_s,
        pack_took, pack_sum, pack_slots, ssum, ssum_took, ssum_sum, ssum_slots,
        raw_s, own_s, slots_s, whole_s, sum_s, low_s, vbuf, gcbuf,
        cols_sem, give_sem, took_sem, send_sem, recv_sem, sgive_sem, stook_sem, ssend_sem, srecv_sem,
        pass_sem, pack_sem, ssum_sem, raw_sem, own_sem, part_send, part_recv, whole_send, whole_recv,
    ) = refs[28:]
    step, steps = pl.program_id(0), pl.num_programs(0)
    me, line = lax.axis_index("fsdp"), lax.axis_index("tp")
    count = 2 * chips
    core, chip = lax.rem(me, 2), me // 2
    partner = me + 1 - 2 * core
    split = total_s.shape[1] // 256 * 128

    def flipped(hop, which_core):
        x, y = lax.rem(chip, 2), chip // 2
        hop_x, hop_y = hop % 2, hop // 2
        x, y = x + hop_x - 2 * x * hop_x, y + hop_y - 2 * y * hop_y
        return (2 * y + x) * 2 + which_core

    def tile_of(at):
        pair = lax.rem(at, count) // 2
        hop = jnp.where(pair == 0, 3, pair - 1)
        return hop, flipped(hop, jnp.where(lax.rem(at, 2) == 0, 1 - core, core))

    def fetch(at, which):
        _, shard = tile_of(at)
        slot = lax.rem(at, 2)
        return pltpu.make_async_copy(
            columns[which].at[:, pl.ds(pl.multiple_of(shard * BLOCK, BLOCK), BLOCK)],
            cols_s.at[slot, which], cols_sem.at[slot, which],
        )

    def far(hop):
        return (flipped(hop, core), line)

    def giving(hop):
        return remote_copy(
            give.at[hop], took.at[hop], give_sem.at[hop], took_sem.at[hop], (partner, line)
        )

    def sending(hop):
        return remote_copy(
            mine.at[hop - 1], came.at[hop - 1], send_sem.at[hop - 1], recv_sem.at[hop - 1], far(hop)
        )

    def passing(hop):
        columns = pl.ds(0, split) if hop == 1 else pl.ds(split, total_s.shape[1] - split)
        return remote_copy(
            mine.at[2, :, columns], passed.at[:, columns], pass_sem.at[0, hop - 1],
            pass_sem.at[1, hop - 1], far(hop),
        )

    def sgiving(hop):
        return remote_copy(
            sgive.at[hop], stook.at[hop], sgive_sem.at[hop], stook_sem.at[hop], (partner, line)
        )

    def ssending(hop):
        return remote_copy(
            smine.at[hop - 1], scame.at[hop - 1], ssend_sem.at[hop - 1], srecv_sem.at[hop - 1], far(hop)
        )

    pack_pass = remote_copy(pack, pack_took, pack_sem.at[0, 0], pack_sem.at[1, 0], (partner, line))
    ssum_pass = remote_copy(ssum, ssum_took, ssum_sem.at[0, 0], ssum_sem.at[1, 0], (partner, line))

    def pack_send(hop):
        return remote_copy(
            pack_sum, pack_slots.at[chip], pack_sem.at[0, hop], pack_sem.at[1, hop], far(hop)
        )

    def ssum_send(hop):
        return remote_copy(
            ssum_sum, ssum_slots.at[chip], ssum_sem.at[0, hop], ssum_sem.at[1, hop], far(hop)
        )

    def rows_at(ref, at):
        return ref.at[pl.ds(pl.multiple_of(at * GROUP, GROUP), GROUP), :]

    def handing(hop):
        owner = lax.rem(line + hop, tp_size)
        return remote_copy(
            rows_at(parts[late], owner), slots_s.at[line], part_send.at[hop - 1],
            part_recv.at[hop - 1], (me, owner),
        )

    late = micro - 1

    def own_part():
        return pltpu.make_async_copy(rows_at(parts[late], line), own_s, own_sem.at[late])

    def ready(at):
        length = raws[at].shape[0]
        return pltpu.make_async_copy(
            parts[at], whole_s.at[pl.ds(at * length, length), :], own_sem.at[at]
        )

    def raw_copy(at):
        length = raws[at].shape[0]
        return pltpu.make_async_copy(
            raws[at], raw_s.at[pl.ds(at * length, length), :], raw_sem.at[at]
        )

    groups = raws[0].shape[0] // GROUP

    def spreading(hop):
        block = rows_at(whole_s, late * groups + line)
        return remote_copy(
            sum_s, block, whole_send.at[hop - 1], whole_recv.at[hop - 1],
            (me, lax.rem(line + hop, tp_size)),
        )

    @pl.when(step == 0)
    def _():
        for which in range(4):
            fetch(step, which).start()
        own_part().start()
        for at in range(micro):
            raw_copy(at).start()
            if at != late:
                ready(at).start()
        greet(
            [far(hop) for hop in range(1, chips)] + [(partner, line)]
            + [(me, lax.rem(line + hop, tp_size)) for hop in range(1, tp_size)]
        )
        for hop in range(1, tp_size):
            handing(hop).start()
        pack_pass.start()

    @pl.when(step + 1 < count)
    def _():
        for which in range(4):
            fetch(step + 1, which).start()

    @pl.when((step + 1 >= count) & (step + 1 < steps))
    def _():
        for which in range(2):
            fetch(step + 1, which).start()

    for which in range(2):
        fetch(step, which).wait()

    @pl.when(step < count)
    def _():
        for which in range(2, 4):
            fetch(step, which).wait()

    slot = lax.rem(step, 2)
    hop, _ = tile_of(step)
    even = lax.rem(step, 2) == 0

    def tile(which):
        sides = (0, 1) if which < 3 else (2, 3)
        return mm_tn(cols_s[slot, sides[0]], lows[2 * which][...]) + mm_tn(
            cols_s[slot, sides[1]], lows[2 * which + 1][...]
        )

    @pl.when((step < count) & even)
    def _():
        at = 0
        for which, width in enumerate(widths):
            give[hop, :, at : at + width] = tile(which).astype(BF16)
            at += width
        giving(hop).start()

    @pl.when((step < count) & jnp.logical_not(even))
    def _():
        at = 0
        for which, width in enumerate(widths):
            total_s[:, at : at + width] = tile(which)
            at += width
        giving(hop).wait_recv()
        total_s[...] += took[hop].astype(F32)

        @pl.when(hop == 3)
        def _():
            mine[2] = total_s[...].astype(BF16)
            passing(1).start()
            passing(2).start()

        @pl.when(hop == 0)
        def _():
            kept_s[...] = total_s[...]

        @pl.when(hop == 1)
        def _():
            passing(2).wait_recv()
            total_s[:, split:] += passed[:, split:].astype(F32)
            mine[0] = total_s[...].astype(BF16)
            sending(1).start()

        @pl.when(hop == 2)
        def _():
            passing(1).wait_recv()
            total_s[:, :split] += passed[:, :split].astype(F32)
            mine[1] = total_s[...].astype(BF16)
            sending(2).start()

    @pl.when(step == 1)
    def _():
        pack_pass.wait()
        pack_sum[...] = pack[...] + pack_took[...]
        pack_slots[chip] = pack_sum[...]
        for other in range(1, chips):
            pack_send(other).start()

    @pl.when(step == 5)
    def _():
        own_part().wait()
        slots_s[line] = own_s[...]
        for hop in range(1, tp_size):
            handing(hop).wait()
        total = slots_s[0].astype(F32)
        for other in range(1, tp_size):
            total = total + slots_s[other].astype(F32)
        sum_s[...] = total.astype(BF16)
        mine_rows = rows_at(whole_s, late * groups + line)
        mine_rows[...] = sum_s[...]
        for hop in range(1, tp_size):
            spreading(hop).start()

    @pl.when(step == count - 1)
    def _():
        for at in range(micro):
            raw_copy(at).wait()
            if at != late:
                ready(at).wait()
        for hop in range(1, tp_size):
            spreading(hop).wait()
        ssum[...] = jnp.zeros(ssum.shape, F32)
        taps, bias = staps_ref[...], sbias_ref[...]

        def state_group(turn, carry):
            group = micro * groups - 1 - turn
            at = pl.multiple_of(group * GROUP, GROUP)
            cols = cols_ref[pl.ds(at, GROUP), :]
            vbuf[HALO : HALO + GROUP, :] = raw_s[pl.ds(at, GROUP), :]
            ahead = pl.multiple_of(jnp.maximum(group * (GROUP // HALO) - 1, 0) * HALO, HALO)
            vbuf[0:HALO, :] = raw_s[pl.ds(ahead, HALO), :]
            moved = shifted_values(vbuf, cols)
            conv = conv_of(moved, taps, bias)
            sig = jax.nn.sigmoid(conv)
            grad = whole_s[pl.ds(at, GROUP), :].astype(F32) * (sig * (1.0 + conv * (1.0 - sig)))
            gcbuf[GROUP : GROUP + HALO, :] = gcbuf[0:HALO, :]
            gcbuf[0:GROUP, :] = grad
            back = taps[0:1, :] * grad
            for offset in range(1, CONV):
                up = jnp.where(
                    cols[:, 2 + offset : 3 + offset] > 0.0, gcbuf[offset : offset + GROUP, :], 0.0
                )
                back = back + taps[offset : offset + 1, :] * up
            low_s[pl.ds(at, GROUP), :] = back.astype(BF16)
            for offset in range(CONV):
                ssum[offset : offset + 1, :] += jnp.sum(grad * moved[offset], axis=0, keepdims=True)
            ssum[CONV : CONV + 1, :] += jnp.sum(grad, axis=0, keepdims=True)
            return carry

        lax.fori_loop(0, micro * groups, state_group, 0)
        ssum_pass.start()
        for at in range(micro):
            low_out[at] = low_s[pl.ds(pl.multiple_of((at * groups + line) * GROUP, GROUP), GROUP), :]

    def state_tile():
        length = groups * GROUP
        return mm_tn(cols_s[slot, 0], low_s[0:length, :]) + mm_tn(
            cols_s[slot, 1], low_s[length : 2 * length, :]
        )

    @pl.when((step >= count) & even)
    def _():
        sgive[hop] = state_tile().astype(BF16)
        sgiving(hop).start()

    @pl.when((step >= count) & jnp.logical_not(even))
    def _():
        stotal[...] = state_tile()
        sgiving(hop).wait_recv()
        stotal[...] += stook[hop].astype(F32)

        @pl.when(hop == 0)
        def _():
            skept_s[...] = stotal[...]

        @pl.when(hop > 0)
        def _():
            smine[hop - 1] = stotal[...].astype(BF16)
            ssending(hop).start()

    @pl.when(step == count + 1)
    def _():
        ssum_pass.wait()
        ssum_sum[...] = ssum[...] + ssum_took[...]
        ssum_slots[chip] = ssum_sum[...]
        for other in range(1, chips):
            ssum_send(other).start()

    @pl.when(step == steps - 1)
    def _():
        for sends, slots, out in ((pack_send, pack_slots, pack_out), (ssum_send, ssum_slots, ssum_out)):
            for other in range(1, chips):
                sends(other).wait()
            total = slots[0]
            for other in range(1, chips):
                total = total + slots[other]
            out[...] = total
        for other in (1, 2):
            sending(other).wait_recv()
            kept_s[...] += came[other - 1].astype(F32)
        for other in range(1, chips):
            ssending(other).wait_recv()
            skept_s[...] += scame[other - 1].astype(F32)
        state_out[...] = skept_s[...]
        at = 0
        for which, width in enumerate(widths):
            part = kept_s[:, at : at + width]
            outs[which][...] = part if which < 3 else jnp.transpose(part)
            at += width
        for other in (1, 2):
            passing(other).wait_send()
            sending(other).wait_send()
        for other in range(1, chips):
            ssending(other).wait_send()
        for other in range(chips):
            giving(other).wait_send()
            sgiving(other).wait_send()


def tail_call(count, tp_size, inputs, cotans, lows, parts, raws, cols, staps, sbias, pack):
    micro, length = len(inputs), inputs[0].shape[0]
    chips = count // 2
    order = [low[which] for which in range(4) for low in lows]
    widths = [low.shape[1] for low in order[::2]]
    total, narrow = sum(widths), 2 * STATE
    hbm = pl.BlockSpec(memory_space=pl.ANY)
    full = lambda array: pl.BlockSpec(array.shape, lambda i: (0,) * array.ndim, pipeline_mode=pl.Buffered(1))
    out_dims = [(BLOCK, width) for width in widths[:3]] + [(widths[3], BLOCK), (BLOCK, narrow)]
    out_shapes = [shape(dims) for dims in out_dims] + [
        shape(pack.shape), shape((8, narrow)), shape((micro, GROUP, narrow), BF16)
    ]
    dma = lambda *dims: pltpu.SemaphoreType.DMA(dims)
    return pl.pallas_call(
        partial(tail_kernel, chips, tp_size, micro, widths),
        grid=(2 * count,),
        in_specs=[hbm] * 4 + [full(low) for low in order] + [hbm] * 4
        + [full(cols), full(staps), full(sbias), full(pack)],
        out_specs=[full(each) for each in out_shapes],
        out_shape=out_shapes,
        scratch_shapes=[
            pltpu.VMEM((2, 4, length, BLOCK), BF16),
            pltpu.VMEM((chips, BLOCK, total), BF16),
            pltpu.VMEM((chips, BLOCK, total), BF16),
            pltpu.VMEM((3, BLOCK, total), BF16),
            pltpu.VMEM((2, BLOCK, total), BF16),
            pltpu.VMEM((BLOCK, total), BF16),
            pltpu.VMEM((BLOCK, total), F32),
            pltpu.VMEM((BLOCK, total), F32),
            pltpu.VMEM((chips, BLOCK, narrow), BF16),
            pltpu.VMEM((chips, BLOCK, narrow), BF16),
            pltpu.VMEM((chips - 1, BLOCK, narrow), BF16),
            pltpu.VMEM((chips - 1, BLOCK, narrow), BF16),
            pltpu.VMEM((BLOCK, narrow), F32),
            pltpu.VMEM((BLOCK, narrow), F32),
            pltpu.VMEM(pack.shape, F32),
            pltpu.VMEM(pack.shape, F32),
            pltpu.VMEM((chips,) + pack.shape, F32),
            pltpu.VMEM((8, narrow), F32),
            pltpu.VMEM((8, narrow), F32),
            pltpu.VMEM((8, narrow), F32),
            pltpu.VMEM((chips, 8, narrow), F32),
            pltpu.VMEM((micro * length, narrow), F32),
            pltpu.VMEM((GROUP, narrow), BF16),
            pltpu.VMEM((tp_size, GROUP, narrow), BF16),
            pltpu.VMEM((micro * length, narrow), BF16),
            pltpu.VMEM((GROUP, narrow), BF16),
            pltpu.VMEM((micro * length, narrow), BF16),
            pltpu.VMEM((GROUP + HALO, narrow), F32),
            pltpu.VMEM((GROUP + HALO, narrow), F32),
            dma(2, 4), dma(chips), dma(chips), dma(2), dma(2),
            dma(chips), dma(chips), dma(chips - 1), dma(chips - 1),
            dma(2, 2), dma(2, chips), dma(2, chips), dma(micro), dma(micro),
            dma(tp_size - 1), dma(tp_size - 1), dma(tp_size - 1), dma(tp_size - 1),
        ],
        compiler_params=pltpu.CompilerParams(
            collective_id=6, has_side_effects=True, vmem_limit_bytes=62 << 20
        ),
        cost_estimate=pl.CostEstimate(
            flops=4 * length * BLOCK * count * total, bytes_accessed=250 << 20, transcendentals=0
        ),
        name="weight_gradients",
    )(*inputs, *cotans, *order, *parts, *raws, cols, staps, sbias, pack)


def rows_kernel(
    sum0, sum1, low_ref, state_w, rows_ref, cot_ref, gain_ref, made0, made1, scale_ref,
    hidden_out, block_out, gain_out,
):
    step = pl.program_id(0)
    half = pl.num_programs(0) // 2
    gain = gain_ref[...]

    def work(summed, made):
        grad = summed[...].astype(F32) + mm_nt(low_ref[0], state_w[...])
        rows = rows_ref[0].astype(F32)
        inv_root = lax.rsqrt(jnp.mean(rows * rows, axis=1, keepdims=True) + EPSILON)
        part = jnp.sum(grad * (rows * inv_root), axis=0, keepdims=True)
        normed = grad * gain
        inner = jnp.mean(normed * rows, axis=1, keepdims=True)
        back = inv_root * normed - rows * (inv_root * inv_root * inv_root * inner)
        hidden_out[0] = (cot_ref[0].astype(F32) + back).astype(BF16)
        block_out[0] = (rows + made[...] * scale_ref[0][:, 0:1]).astype(BF16)
        width = gain_out.shape[1]
        for at in range(gain_out.shape[0]):
            piece = part[:, at * width : (at + 1) * width]

            @pl.when(step == 0)
            def _():
                gain_out[at : at + 1, :] = piece

            @pl.when(step > 0)
            def _():
                gain_out[at : at + 1, :] += piece

    @pl.when(step < half)
    def _():
        work(sum0, made0)

    @pl.when(step >= half)
    def _():
        work(sum1, made1)


def rows_call(sums, lows, state_w, rows, cotan, gain, made, scales):
    micro, length, model = rows.shape
    tiles = 2
    tile = length // tiles
    both = lambda width: pl.BlockSpec((1, tile, width), lambda i: (i // tiles, i % tiles, 0))
    former = pl.BlockSpec((tile, model), lambda i: (jnp.minimum(i, tiles - 1), 0))
    latter = pl.BlockSpec((tile, model), lambda i: (jnp.maximum(i - tiles, 0), 0))
    full = lambda dims: pl.BlockSpec(dims, lambda i: (0, 0))
    return pl.pallas_call(
        rows_kernel,
        grid=(micro * tiles,),
        in_specs=[
            former, latter, both(2 * STATE), full(state_w.shape), both(model), both(model),
            full(gain.shape), former, latter, both(128),
        ],
        out_specs=[both(model), both(model), full((8, model // 8))],
        out_shape=[shape(rows.shape, BF16), shape(rows.shape, BF16), shape((8, model // 8))],
        compiler_params=pltpu.CompilerParams(vmem_limit_bytes=50 << 20),
        cost_estimate=pl.CostEstimate(flops=1 << 30, bytes_accessed=18 << 20, transcendentals=0),
        name="finish_rows",
    )(*sums, lows, state_w, rows, cotan, gain, *made, scales)


def gain_kernel(
    tp_size, count, part, gain_out, line_slots, line_sum, slots, send_sem, recv_sem, far_send, far_recv,
):
    me, column = lax.axis_index("tp"), lax.axis_index("fsdp")
    greet(
        [(column, lax.rem(me + hop, tp_size)) for hop in range(1, tp_size)]
        + [(lax.rem(column + hop, count), me) for hop in range(1, count)]
    )
    line_slots[me] = part[...]
    copies = [
        remote_copy(
            part, line_slots.at[me], send_sem.at[hop - 1], recv_sem.at[hop - 1],
            (column, lax.rem(me + hop, tp_size)),
        )
        for hop in range(1, tp_size)
    ]
    for copy in copies:
        copy.start()
    for copy in copies:
        copy.wait()
    total = line_slots[0]
    for at in range(1, tp_size):
        total = total + line_slots[at]
    line_sum[...] = total
    slots[column] = total
    copies = [
        remote_copy(
            line_sum, slots.at[column], far_send.at[hop - 1], far_recv.at[hop - 1],
            (lax.rem(column + hop, count), me),
        )
        for hop in range(1, count)
    ]
    for copy in copies:
        copy.start()
    for copy in copies:
        copy.wait()
    total = slots[0]
    for at in range(1, count):
        total = total + slots[at]
    gain_out[...] = total


def gain_call(tp_size, count, part):
    vmem = pl.BlockSpec(memory_space=pltpu.VMEM)
    return pl.pallas_call(
        partial(gain_kernel, tp_size, count),
        in_specs=[vmem],
        out_specs=vmem,
        out_shape=shape(part.shape),
        scratch_shapes=[
            pltpu.VMEM((tp_size,) + part.shape, F32), pltpu.VMEM(part.shape, F32),
            pltpu.VMEM((count,) + part.shape, F32),
            pltpu.SemaphoreType.DMA((tp_size - 1,)), pltpu.SemaphoreType.DMA((tp_size - 1,)),
            pltpu.SemaphoreType.DMA((count - 1,)), pltpu.SemaphoreType.DMA((count - 1,)),
        ],
        compiler_params=pltpu.CompilerParams(
            collective_id=7, has_side_effects=True, vmem_limit_bytes=32 << 20
        ),
        cost_estimate=pl.CostEstimate(flops=0, bytes_accessed=1 << 20, transcendentals=0),
        name="gain_sum",
    )(part)


def unpack_kernel(heads, pack_ref, ssum_ref, rate_ref, gain, skip, conv, bias, sconv, sbias, step, decay):
    gain[...] = pack_ref[0:1, :]
    lanes = pack_ref.shape[1]
    place = (iota((lanes, 128), 0) // HEAD_DIM == iota((lanes, 128), 1)).astype(F32)
    sums = mm(pack_ref[0:8, :], place, PRECISE)
    skip[...] = sums[1:2, :heads]
    conv[...] = pack_ref[2 : 2 + CONV, :]
    bias[...] = pack_ref[2 + CONV : 3 + CONV, :]
    sconv[...] = ssum_ref[0:CONV, :]
    sbias[...] = ssum_ref[CONV : CONV + 1, :]
    step[...] = pack_ref[8:9, :heads]
    decay[...] = pack_ref[9:10, :heads] * rate_ref[:, :heads]


def unpack_call(pack, ssum, rate, heads):
    inner = pack.shape[1]
    vmem = pl.BlockSpec(memory_space=pltpu.VMEM)
    dims = [(1, inner), (1, heads), (CONV, inner), (1, inner), (CONV, 2 * STATE), (1, 2 * STATE),
            (1, heads), (1, heads)]
    return pl.pallas_call(
        partial(unpack_kernel, heads), in_specs=[vmem] * 3, out_specs=[vmem] * 8,
        out_shape=[shape(each) for each in dims], name="small_gradients",
        cost_estimate=pl.CostEstimate(flops=0, bytes_accessed=1 << 18, transcendentals=0),
    )(pack, ssum, rate)


def shift_down(values, offset):
    return jnp.pad(values, ((offset, 0), (0, 0)))[: values.shape[0]]


def shift_up(values, offset):
    return jnp.pad(values, ((0, offset), (0, 0)))[offset:]


def document_columns(seg_row):
    length = seg_row.shape[0]
    previous = jnp.concatenate([jnp.full((1,), -1, seg_row.dtype), seg_row[GROUP - 1 : -1 : GROUP]])
    last = seg_row[GROUP - 1 :: GROUP]
    columns = []
    for offset in range(1, CONV):
        columns.append(jnp.pad(seg_row, (offset, 0), constant_values=-1)[:length] == seg_row)
    for offset in range(1, CONV):
        columns.append(jnp.pad(seg_row, (0, offset), constant_values=-1)[offset:] == seg_row)
    columns.append(seg_row == jnp.repeat(previous, GROUP))
    columns.append(seg_row == jnp.repeat(last, GROUP))
    columns.append(jnp.repeat(last == previous, GROUP))
    columns.append(seg_row)
    columns = [column.astype(F32) for column in columns]
    return jnp.stack(columns + [columns[0]] * (16 - len(columns)), axis=1)


def state_gradient(grad_bc, state_raw, taps, bias, cols):
    moved = [state_raw]
    for offset in range(1, CONV):
        moved.append(shift_down(state_raw, offset) * cols[:, offset - 1 : offset])
    conv = bias
    for offset in range(CONV):
        conv = conv + taps[offset][None, :] * moved[offset]
    sig = jax.nn.sigmoid(conv)
    grad_conv = grad_bc * (sig * (1.0 + conv * (1.0 - sig)))
    grad_raw = taps[0][None, :] * grad_conv
    for offset in range(1, CONV):
        grad_raw = grad_raw + taps[offset][None, :] * (
            shift_up(grad_conv, offset) * cols[:, 2 + offset : 3 + offset]
        )
    grad_taps = jnp.stack([jnp.sum(grad_conv * each, axis=0) for each in moved])
    return grad_raw.astype(BF16), grad_taps, jnp.sum(grad_conv, axis=0)


def local(
    hidden_in, segment_ids, cotangent, norm_gain, proj_gate, proj_value, proj_state, proj_step,
    conv_value, conv_value_bias, conv_state, conv_state_bias, step_bias, decay_log, skip_gain,
    gate_gain, proj_out,
):
    micro = hidden_in.shape[0]
    heads = step_bias.shape[0]
    rows_here = hidden_in.shape[2]
    tp_size = lax.axis_size("tp")
    me = lax.axis_index("tp")
    decay_rate = -jnp.exp(decay_log)
    pad_heads = lambda values: jnp.pad(values, (0, 128 - heads))[None, :]
    rate = pad_heads(decay_rate)
    step_bias_line = pad_heads(step_bias)
    skip = jnp.repeat(skip_gain, HEAD_DIM)[None, :]
    gain = gate_gain[None, :]
    taps, bias = conv_value, conv_value_bias[None, :]
    staps, sbias = conv_state, conv_state_bias[None, :]

    rows_float = hidden_in[:, 0].astype(F32)
    inv_root = lax.rsqrt(jnp.mean(rows_float * rows_float, axis=-1, keepdims=True) + EPSILON)
    input_rows = (rows_float * inv_root * norm_gain).astype(BF16)

    def gather_tp(values, *after):
        values = lax.optimization_barrier((values,) + after)[0]
        return lax.all_gather(values, "tp", axis=0, tiled=True)

    def scatter_tp(values, *after):
        values = lax.optimization_barrier((values,) + after)[0]
        return lax.psum_scatter(values, "tp", scatter_dimension=0, tiled=True)

    inputs = [gather_tp(input_rows[0])]
    fsdp_size = lax.axis_size("fsdp")
    model = hidden_in.shape[3]
    aligned = proj_out.shape[1] % 128 == 0
    axes = (0, 0, 0, 0, 1 if aligned else 2)
    step_block = jnp.pad(proj_step, ((0, 0), (0, 128 - heads)))
    gate_w, value_w, state_w, step_w, out_w = gather_call(
        fsdp_size, (proj_gate, proj_value, proj_state, step_block, proj_out), axes
    )
    if not aligned:
        out_w = jnp.transpose(out_w, (1, 0, 2)).reshape(-1, model)
    inputs.append(gather_tp(input_rows[1], inputs[0], step_w))
    forward_weights = (gate_w, value_w, state_w, step_w, out_w)
    vectors = (taps, bias, staps, sbias, step_bias_line, rate, skip)
    columns = [document_columns(segment_ids[at, 0]) for at in range(micro)]
    seg_lines = [segment_ids[at, 0].astype(F32)[None, :] for at in range(micro)]
    quick, slow = [0, 7, 15, 15, 15], [0, 5, 10, 15, 15]

    def forward(at, hosted):
        return forward_call(
            inputs[at], forward_weights, vectors, gain, columns[at], seg_lines[at], hosted, quick
        )

    def backward(at, hosted, collective):
        grad_branch, stats = branch_call(cotans[at], out_w, saved[at][0], saved[at][2], gain, tp_size)
        scales.append(stats)
        return backward_call(
            saved[at], grad_branch, stats, (gate_w, value_w, step_w), (taps, bias, rate, skip),
            gain, columns[at], seg_lines[at], hosted, slow, collective,
        )

    scales, produced, summed = [], [], []
    saved = [forward(0, Hosted(tp_size))]
    *kept, made_sum, cotan = forward(1, Hosted(tp_size, saved[0][8], cotangent[0, 0]))
    saved.append(kept)
    produced.append(made_sum)
    cotans = [cotan]
    *former, made_sum, cotan = backward(0, Hosted(tp_size, saved[1][8], cotangent[1, 0]), 4)
    produced.append(made_sum)
    cotans.append(cotan)
    early = lax.psum(former[4], "tp")
    *latter, gin_sum = backward(1, Hosted(tp_size, former[5]), 5)
    summed = [gin_sum, scatter_tp(latter[5])]
    lows = [[each[1], each[2], each[3], each[0]] for each in (former, latter)]
    parts, raws = (early, latter[4]), [each[4] for each in saved]
    inner_here = proj_gate.shape[1]
    pack = jnp.concatenate(
        [former[6] + latter[6], jnp.pad(former[7] + latter[7], ((0, 0), (0, inner_here - 128)))], axis=0
    )
    if aligned and fsdp_size == 8 and model // fsdp_size == BLOCK:
        grad_gate, grad_value, grad_step, grad_out, grad_state, pack, state_sum, mine = tail_call(
            fsdp_size, tp_size, inputs, cotans, lows, parts, raws, jnp.concatenate(columns, axis=0),
            staps, sbias, pack,
        )
    else:
        mine, state_sum = [], 0.0
        for at in range(micro):
            grad_bc = (parts[at] if at == 0 else lax.psum(parts[at], "tp")).astype(F32)
            low_state, grad_staps, grad_sbias = state_gradient(
                grad_bc, raws[at], staps, sbias, columns[at]
            )
            mine.append(lax.dynamic_slice_in_dim(low_state, me * rows_here, rows_here, axis=0))
            lows[at].insert(2, low_state)
            state_sum = state_sum + jnp.concatenate(
                [grad_staps, grad_sbias[None, :], jnp.zeros((3, 2 * STATE), F32)], axis=0
            )
        mine = jnp.stack(mine)
        grad_out = outer_call([low[4] for low in lows], cotans)
        grad_gate, grad_value, grad_state, grad_step = weight_call(inputs, [low[:4] for low in lows])
        if not aligned:
            grad_out = jnp.transpose(grad_out.reshape(-1, fsdp_size, proj_out.shape[1]), (1, 0, 2))
        grad_gate, grad_value, grad_state, grad_step, grad_out = scatter_call(
            fsdp_size, (grad_gate, grad_value, grad_state, grad_step, grad_out), axes
        )
        pack, state_sum = lax.psum((pack, state_sum), "fsdp")
    grad_step = grad_step[:, :heads]
    my_scales = jnp.stack(
        [lax.dynamic_slice_in_dim(each, me * rows_here, rows_here, axis=0) for each in scales]
    )
    grad_hidden, block_rows, gain_part = rows_call(
        summed, mine, state_w, hidden_in[:, 0], cotangent[:, 0], norm_gain[None, :],
        produced, my_scales,
    )
    gain_total = gain_call(tp_size, fsdp_size, gain_part)
    grad_gain, grad_skip, grad_conv, grad_bias, grad_sconv, grad_sbias, grad_in, grad_decay = (
        unpack_call(pack, state_sum, rate, heads)
    )
    return (
        block_rows[:, None],
        grad_hidden[:, None],
        gain_total.reshape(-1),
        grad_gate,
        grad_value,
        grad_state,
        grad_step,
        grad_conv,
        grad_bias.reshape(-1),
        grad_sconv,
        grad_sbias.reshape(-1),
        grad_in.reshape(-1),
        grad_decay.reshape(-1),
        grad_skip.reshape(-1),
        grad_gain.reshape(-1),
        grad_out,
    )


def solution(mesh):
    in_specs = (
        P(None, "fsdp", "tp", None), P(None, "fsdp", None), P(None, "fsdp", "tp", None), P(),
        P("fsdp", "tp"), P("fsdp", "tp"), P("fsdp", None), P("fsdp", "tp"), P(None, "tp"), P("tp"),
        P(), P(), P("tp"), P("tp"), P("tp"), P("tp"), P("tp", "fsdp"),
    )
    out_specs = (
        P(None, "fsdp", "tp", None), P(None, "fsdp", "tp", None), P(), P("fsdp", "tp"),
        P("fsdp", "tp"), P("fsdp", None), P("fsdp", "tp"), P(None, "tp"), P("tp"), P(), P(),
        P("tp"), P("tp"), P("tp"), P("tp"), P("tp", "fsdp"),
    )
    return jax.shard_map(local, mesh=mesh, in_specs=in_specs, out_specs=out_specs, check_vma=False)
```

```python
from functools import partial

import jax
import jax.numpy as jnp
from jax import lax
from jax.experimental import pallas as pl
from jax.experimental.pallas import tpu as pltpu
from jax.sharding import PartitionSpec as P

HEAD_DIM = 64
STATE = 128
CONV = 4
GROUP = 256
HALF = GROUP // 2
BLOCK = 256
PER_BLOCK = BLOCK // HEAD_DIM
HALO = 8
INNER = 4096
EPSILON = 1e-05
PRECISE = lax.Precision.HIGHEST
PARTS = 2
FORWARD_INS, FORWARD_OUTS = 16, 9
BACKWARD_INS, BACKWARD_OUTS = 23, 9
F32 = jnp.float32
BF16 = jnp.bfloat16


def mm(former, latter, precision=None):
    return jnp.dot(former, latter, preferred_element_type=F32, precision=precision)


def mm_nt(former, latter):
    return lax.dot_general(
        former, latter, (((1,), (1,)), ((), ())), preferred_element_type=F32
    )


def mm_tn(former, latter):
    return lax.dot_general(
        former, latter, (((0,), (0,)), ((), ())), preferred_element_type=F32
    )


def iota(shape, axis):
    return lax.broadcasted_iota(jnp.int32, shape, axis)


def expand(columns):
    rows = columns.shape[0]
    lane = iota((rows, 128), 1)
    parts = []
    for pair in range(PER_BLOCK // 2):
        former = jnp.broadcast_to(columns[:, 2 * pair : 2 * pair + 1], (rows, 128))
        latter = jnp.broadcast_to(columns[:, 2 * pair + 1 : 2 * pair + 2], (rows, 128))
        parts.append(jnp.where(lane < HEAD_DIM, former, latter))
    return jnp.concatenate(parts, axis=1)


def lane_mask(head):
    lane = iota((1, BLOCK), 1)
    return ((lane // HEAD_DIM) == head).astype(F32).astype(BF16)


def spread(ref, values, blocks):
    for block in range(blocks):
        shift = (128 - PER_BLOCK * block) % 128
        ref[block] = pltpu.roll(values, shift, 1) if shift else values


def token_quantities(step_in, cums, cols, decay_rate):
    step = jnp.maximum(step_in, 0.0) + jnp.log1p(jnp.exp(-jnp.abs(step_in)))
    final = cums[GROUP - 1 : GROUP, :]
    entering = jnp.exp(cums) * cols[:, 6:7]
    fading = jnp.exp(final - cums) * cols[:, 7:8]
    retain = jnp.exp(final) * cols[0:1, 8:9]
    return step, entering, fading, retain


def shifted_values(buf, cols):
    moved = [buf[HALO : HALO + GROUP, :]]
    for offset in range(1, CONV):
        before = buf[HALO - offset : HALO - offset + GROUP, :]
        moved.append(jnp.where(cols[:, offset - 1 : offset] > 0.0, before, 0.0))
    return moved


def conv_of(moved, taps, bias):
    total = bias + taps[0:1, :] * moved[0]
    for offset in range(1, CONV):
        total = total + taps[offset : offset + 1, :] * moved[offset]
    return total


MESH = pl.DeviceIdType.MESH


def part_of(ref, at, size, axis):
    if axis == 0:
        return ref.at[pl.ds(pl.multiple_of(at * size, size), size), :]
    if axis == 1:
        return ref.at[:, pl.ds(pl.multiple_of(at * size, size), size)]
    return ref.at[at]


def greet(devices):
    barrier = pltpu.get_barrier_semaphore()
    for device in devices:
        pl.semaphore_signal(barrier, inc=1, device_id=device, device_id_type=MESH)
    pl.semaphore_wait(barrier, len(devices))


def remote_copy(source, target, sends, receives, device):
    return pltpu.make_async_remote_copy(
        src_ref=source, dst_ref=target, send_sem=sends, recv_sem=receives,
        device_id=device, device_id_type=MESH,
    )


class LineScatter:
    def __init__(self, size, source, own, slots, last, own_sem, send_sem, recv_sem, last_sem):
        self.size, self.source, self.own, self.slots, self.last = size, source, own, slots, last
        self.own_sem, self.send_sem, self.recv_sem, self.last_sem = own_sem, send_sem, recv_sem, last_sem
        self.me, self.column = lax.axis_index("tp"), lax.axis_index("fsdp")
        self.rows = last.shape[0]

    @staticmethod
    def scratch(size, rows, width):
        hops = size - 1
        return [
            pltpu.VMEM((2, hops, rows, width), BF16), pltpu.VMEM((2, hops, rows, width), BF16),
            pltpu.VMEM((rows, width), BF16), pltpu.SemaphoreType.DMA((2, hops)),
            pltpu.SemaphoreType.DMA((2, hops, PARTS)), pltpu.SemaphoreType.DMA((2, hops, PARTS)),
            pltpu.SemaphoreType.DMA((1,)),
        ]

    def place(self, flow):
        return self.me if flow == 0 else self.size - 1 - self.me

    def part(self, part):
        rows = self.rows // PARTS
        return pl.ds(part * rows, rows)

    def local(self, flow, hop):
        block = self.size - 1 - hop + self.place(flow)
        if flow:
            block = self.size - 1 - block
        at = pl.multiple_of(block * self.rows, self.rows)
        return pltpu.make_async_copy(
            self.source.at[pl.ds(at, self.rows), :], self.own.at[flow, hop], self.own_sem.at[flow, hop]
        )

    def final(self):
        at = pl.multiple_of(self.me * self.rows, self.rows)
        return pltpu.make_async_copy(
            self.source.at[pl.ds(at, self.rows), :], self.last, self.last_sem.at[0]
        )

    def sending(self, flow, hop, part):
        neighbour = self.me + 1 if flow == 0 else self.me - 1
        neighbour = jnp.clip(neighbour, 0, self.size - 1)
        return remote_copy(
            self.own.at[flow, hop, self.part(part), :], self.slots.at[flow, hop, self.part(part), :],
            self.send_sem.at[flow, hop, part], self.recv_sem.at[flow, hop, part],
            (self.column, neighbour),
        )

    def begin(self):
        self.final().start()
        for hop in range(self.size - 1):
            for flow in range(2):

                @pl.when(self.place(flow) <= hop)
                def _():
                    self.local(flow, hop).start()

    def hop(self, hop, part):
        rows = self.part(part)
        for flow in range(2):
            place = self.place(flow)

            @pl.when(place <= hop)
            def _():
                if part == 0:
                    self.local(flow, hop).wait()
                if hop > 0:

                    @pl.when(place >= 1)
                    def _():
                        self.sending(flow, hop - 1, part).wait_recv()
                        total = self.own[flow, hop, rows, :].astype(F32)
                        total = total + self.slots[flow, hop - 1, rows, :].astype(F32)
                        self.own[flow, hop, rows, :] = total.astype(BF16)

                self.sending(flow, hop, part).start()

    def end(self, out, part):
        hops = self.size - 1
        rows = self.part(part)
        if part == 0:
            self.final().wait()
        out[rows, :] = self.last[rows, :].astype(F32)
        for flow in range(2):

            @pl.when(self.place(flow) >= 1)
            def _():
                self.sending(flow, hops - 1, part).wait_recv()
                out[rows, :] += self.slots[flow, hops - 1, rows, :].astype(F32)

        for hop in range(hops):
            for flow in range(2):

                @pl.when(self.place(flow) <= hop)
                def _():
                    self.sending(flow, hop, part).wait_send()


class LineGather:
    def __init__(self, size, source, target, own_sem, send_sem, recv_sem):
        self.size, self.source, self.target = size, source, target
        self.own_sem, self.send_sem, self.recv_sem = own_sem, send_sem, recv_sem
        self.me, self.column = lax.axis_index("tp"), lax.axis_index("fsdp")
        self.rows = source.shape[0]

    @staticmethod
    def scratch(size):
        return [
            pltpu.SemaphoreType.DMA((1,)), pltpu.SemaphoreType.DMA((2, size - 1, PARTS)),
            pltpu.SemaphoreType.DMA((2, size - 1, PARTS)),
        ]

    def place(self, flow):
        return self.me if flow == 0 else self.size - 1 - self.me

    def block(self, at):
        at = pl.multiple_of(jnp.clip(at, 0, self.size - 1) * self.rows, self.rows)
        return self.target.at[pl.ds(at, self.rows), :]

    def sending(self, flow, hop, part):
        neighbour = self.me + 1 if flow == 0 else self.me - 1
        neighbour = jnp.clip(neighbour, 0, self.size - 1)
        rows = pl.ds(part * (self.rows // PARTS), self.rows // PARTS)
        block = self.block(self.me - hop if flow == 0 else self.me + hop).at[rows, :]
        return remote_copy(
            self.source.at[rows, :] if hop == 0 else block, block, self.send_sem.at[flow, hop, part],
            self.recv_sem.at[flow, hop, part], (self.column, neighbour),
        )

    def local(self):
        return pltpu.make_async_copy(self.source, self.block(self.me), self.own_sem.at[0])

    def hop(self, hop, part):
        if hop == 0 and part == 0:
            self.local().start()
        for flow in range(2):
            place = self.place(flow)
            if hop > 0:

                @pl.when(place >= hop)
                def _():
                    self.sending(flow, hop - 1, part).wait_recv()

            if hop < self.size - 1:

                @pl.when((place >= hop) & (place < self.size - 1))
                def _():
                    self.sending(flow, hop, part).start()

    def end(self, part):
        self.hop(self.size - 1, part)
        if part == 0:
            self.local().wait()
        for hop in range(self.size - 1):
            for flow in range(2):
                place = self.place(flow)

                @pl.when((place >= hop) & (place < self.size - 1))
                def _():
                    self.sending(flow, hop, part).wait_send()


def run_line(step, steps, scatter, gather, out):
    size = (scatter or gather).size
    first = 1 if scatter and gather else 0
    actions = [[] for _ in range(PARTS * (size + first))]
    for part in range(PARTS):
        if gather:
            for hop in range(size - 1):
                actions[PARTS * hop + part].append(partial(gather.hop, hop, part))
            actions[PARTS * (size - 1) + part].append(partial(gather.end, part))
        if scatter:
            for hop in range(size - 1):
                actions[PARTS * (first + hop) + part].append(partial(scatter.hop, hop, part))
            actions[PARTS * (first + size - 1) + part].append(partial(scatter.end, out, part))
    if scatter:
        actions[0].insert(0, scatter.begin)
    for at in sorted(set(steps)):
        todo = [action for when, each in zip(steps, actions) if when == at for action in each]

        @pl.when(step == at)
        def _():
            for action in todo:
                action()


class Hosted:
    def __init__(self, size, scatter=None, gather=None):
        self.size, self.scatter, self.gather = size, scatter, gather

    def operands(self):
        return [each for each in (self.scatter, self.gather) if each is not None]

    def in_specs(self):
        return [pl.BlockSpec(memory_space=pl.ANY)] * len(self.operands())

    def outs(self):
        shapes, specs = [], []
        if self.scatter is not None:
            rows, width = self.scatter.shape[0] // self.size, self.scatter.shape[1]
            shapes.append(shape((rows, width)))
            specs.append(pl.BlockSpec((rows, width), lambda g, j: (0, 0)))
        if self.gather is not None:
            rows, width = self.gather.shape
            shapes.append(shape((rows * self.size, width), BF16))
            specs.append(pl.BlockSpec(memory_space=pl.ANY))
        return specs, shapes

    def scratch(self):
        needed = []
        if self.scatter is not None:
            rows, width = self.scatter.shape[0] // self.size, self.scatter.shape[1]
            needed += LineScatter.scratch(self.size, rows, width)
        if self.gather is not None:
            needed += LineGather.scratch(self.size)
        return needed

    def wrap(self, body, ins, outs, pace):
        has_scatter, has_gather = self.scatter is not None, self.gather is not None
        hosts = has_scatter + has_gather
        size, spare = self.size, len(self.scratch())
        if not hosts:
            return body

        def kernel(*refs):
            sources, targets = refs[ins : ins + hosts], refs[ins + hosts + outs : ins + outs + 2 * hosts]
            tail = refs[len(refs) - spare :]
            step = pl.program_id(0) * pl.num_programs(1) + pl.program_id(1)
            me, column = lax.axis_index("tp"), lax.axis_index("fsdp")

            @pl.when(step == 0)
            def _():
                greet([(column, lax.rem(me + hop, size)) for hop in range(1, size)])

            body(
                *refs[:ins], *refs[ins + hosts : ins + hosts + outs],
                *refs[ins + outs + 2 * hosts : len(refs) - spare],
            )
            scatter = LineScatter(size, sources[0], *tail[:7]) if has_scatter else None
            gather = LineGather(size, sources[-1], targets[-1], *tail[-3:]) if has_gather else None
            run_line(step, pace, scatter, gather, targets[0])

        return kernel


def forward_kernel(
    in_ref, gate_w, value_w, state_w, step_w, taps_ref, bias_ref, staps_ref, sbias_ref,
    step_bias_ref, rate_ref, skip_ref, cols_ref, seg_ref, out_w, gain_ref,
    gate_out, value_out, mixed_out, bc_out, sraw_out, stepin_out, cums_out, held_out, made_out,
    vbuf, sbuf, gram_s, b_t, c_s, step_s, ent_s, fade_s, cums_s, cums_t, keep_s, hidden, made,
):
    g, j = pl.program_id(0), pl.program_id(1)
    blocks = pl.num_programs(1)
    nblocks = hidden.shape[0]
    rows = in_ref[...]
    cols = cols_ref[...]

    @pl.when(j == 0)
    def _():
        sbuf[0:HALO, :] = sbuf[GROUP : GROUP + HALO, :]
        raw = mm(rows, state_w[...])
        sbuf[HALO : HALO + GROUP, :] = raw
        sraw_out[...] = raw
        conv = conv_of(shifted_values(sbuf, cols), staps_ref[...], sbias_ref[...])
        bc = (conv * jax.nn.sigmoid(conv)).astype(BF16)
        bc_out[...] = bc
        b_low, c_low = bc[:, :STATE], bc[:, STATE:]
        b_t[...] = jnp.transpose(b_low.astype(F32)).astype(BF16)
        c_s[...] = c_low
        step_in = mm(rows, step_w[...]) + step_bias_ref[...]
        stepin_out[...] = step_in
        step = jnp.maximum(step_in, 0.0) + jnp.log1p(jnp.exp(-jnp.abs(step_in)))
        at_row, at_col = iota((GROUP, GROUP), 0), iota((GROUP, GROUP), 1)
        lower = (at_row >= at_col).astype(F32)
        cums = mm(lower, step * rate_ref[...], PRECISE)
        cums_out[...] = cums
        step, entering, fading, retain = token_quantities(step_in, cums, cols, rate_ref[...])
        spread(step_s, step, nblocks)
        spread(ent_s, entering, nblocks)
        spread(fade_s, fading, nblocks)
        spread(cums_s, cums, nblocks)
        spread(keep_s, jnp.broadcast_to(retain, (8, 128)), nblocks)
        cums_t[...] = jnp.transpose(cums)
        within = (at_row >= at_col) & (cols[:, 9:10] == seg_ref[...])
        gram_s[...] = jnp.where(within, mm_nt(c_low, b_low), 0.0)

    at = pl.multiple_of(j * BLOCK, BLOCK)
    gate = mm(rows, gate_w[:, pl.ds(at, BLOCK)])
    gate_out[...] = gate.astype(BF16)
    value = mm(rows, value_w[:, pl.ds(at, BLOCK)])
    value_out[...] = value
    mine = vbuf.at[j]
    mine[0:HALO, :] = mine[GROUP : GROUP + HALO, :]
    mine[HALO : HALO + GROUP, :] = value
    conv = conv_of(shifted_values(mine, cols), taps_ref[...], bias_ref[...])
    x_low = (conv * jax.nn.sigmoid(conv)).astype(BF16)
    x_float = x_low.astype(F32)
    scaled_float = expand(step_s[j]) * x_float
    scaled = scaled_float.astype(BF16)

    @pl.when(g == 0)
    def _():
        hidden[j] = jnp.zeros((STATE, BLOCK), F32)

    state = hidden[j]
    state_low = state.astype(BF16)
    held_out[0] = state_low
    total = expand(ent_s[j]) * mm(c_s[...], state_low)
    weighted = (expand(fade_s[j]) * scaled.astype(F32)).astype(BF16)
    hidden[j] = expand(keep_s[j])[0:1, :] * state + mm(b_t[...], weighted)
    cums_here = cums_s[j]
    top = jnp.zeros((HALF, BLOCK), F32)
    bottom = jnp.zeros((HALF, BLOCK), F32)
    for i in range(PER_BLOCK):
        to = cums_here[:, i : i + 1]
        frm = cums_t[pl.ds(j * PER_BLOCK + i, 1), :]
        only = scaled * lane_mask(i)
        decay = jnp.exp(jnp.minimum(to[:HALF] - frm[:, :HALF], 0.0))
        top = top + mm((gram_s[:HALF, :HALF] * decay).astype(BF16), only[:HALF])
        decay = jnp.exp(jnp.minimum(to[HALF:] - frm, 0.0))
        bottom = bottom + mm((gram_s[HALF:, :] * decay).astype(BF16), only)
    mixed = total + jnp.concatenate([top, bottom], axis=0) + skip_ref[...] * x_float
    mixed_out[...] = mixed
    scaled_gate = (mixed * (gate * jax.nn.sigmoid(gate)) * gain_ref[...]).astype(BF16)

    @pl.when(j == 0)
    def _():
        made[...] = mm(scaled_gate, out_w[pl.ds(at, BLOCK), :])

    @pl.when(j > 0)
    def _():
        made[...] += mm(scaled_gate, out_w[pl.ds(at, BLOCK), :])

    @pl.when(j == blocks - 1)
    def _():
        made_out[...] = made[...].astype(BF16)


def backward_kernel(
    tp_size, cot_ref, out_w, gate_rows, mixed_rows, gain_row,
    gate_ref, value_ref, before_ref, mixed_ref, bc_ref, stepin_ref, cums_ref, held_ref,
    gate_w, value_w, step_w, taps_ref, bias_ref, rate_ref, skip_ref, gain_ref, cols_ref, seg_ref,
    branch_out, lowgate_out, lowvalue_out, lowstep_out, gbc_out, gin_out, small_out, sums_out, stats_out,
    vbuf, gcbuf, gram_s, dgram, b_s, c_t, step_s, ent_s, fade_s, cums_s, cums_t, keep_s, grad_state,
    gin, gb_s, gc_s, u_s, v_s, fin_s, small_s, sums_s,
    branch_s, rowsum_s, slots_s, turn_s, swap_send, swap_recv,
):
    g, j = pl.program_id(0) - 1, pl.program_id(1)
    groups, blocks = pl.num_programs(0) - 1, pl.num_programs(1)

    @pl.when(g < 0)
    def _():
        row_sums(
            tp_size, cot_ref, out_w, gate_rows, mixed_rows, gain_row,
            branch_s, rowsum_s, slots_s, turn_s, swap_send, swap_recv, stats_out,
        )

    @pl.when(g >= 0)
    def _():
        backward_step(
            g, j, groups, blocks, gate_ref, value_ref, before_ref, mixed_ref,
            bc_ref, stepin_ref, cums_ref, held_ref,
            gate_w, value_w, step_w, taps_ref, bias_ref, rate_ref, skip_ref, gain_ref, cols_ref, seg_ref,
            branch_out, lowgate_out, lowvalue_out, lowstep_out, gbc_out, gin_out, small_out, sums_out,
            vbuf, gcbuf, gram_s, dgram, b_s, c_t, step_s, ent_s, fade_s, cums_s, cums_t, keep_s,
            grad_state, gin, gb_s, gc_s, u_s, v_s, fin_s, small_s, sums_s, branch_s, stats_out,
        )


def row_sums(
    tp_size, cot_ref, out_w, gate_rows, mixed_rows, gain_row,
    branch_s, rowsum_s, slots_s, turn_s, swap_send, swap_recv, stats_out,
):
    step, groups = pl.program_id(1), pl.num_programs(1)
    me, column = lax.axis_index("tp"), lax.axis_index("fsdp")
    total_inner = gain_row.shape[1] * tp_size
    grad = mm_nt(cot_ref[...], out_w[...])
    branch_s[step] = grad.astype(BF16)
    gate = gate_rows[...].astype(F32)
    gated = mixed_rows[...] * (gate * jax.nn.sigmoid(gate))
    squares = jnp.sum(gated * gated, axis=1, keepdims=True)
    inner = jnp.sum(grad * gain_row[...] * gated, axis=1, keepdims=True)
    lane = iota((GROUP, 128), 1)
    both = jnp.where(lane == 0, squares, jnp.where(lane == 1, inner, 0.0))
    rowsum_s[step] = jnp.transpose(both)[:8]

    @pl.when(step == groups - 1)
    def _():
        slots_s[me] = rowsum_s[...]
        copies = [
            remote_copy(
                rowsum_s, slots_s.at[me], swap_send.at[hop - 1], swap_recv.at[hop - 1],
                (column, lax.rem(me + hop, tp_size)),
            )
            for hop in range(1, tp_size)
        ]
        for copy in copies:
            copy.start()
        for copy in copies:
            copy.wait()
        total = slots_s[0]
        for at in range(1, tp_size):
            total = total + slots_s[at]
        turn_s[...] = jnp.zeros(turn_s.shape, F32)
        scale = lax.rsqrt(total[:, 0:1, :] / total_inner + EPSILON)
        turn_s[:, 0:1, :] = scale
        turn_s[:, 1:2, :] = scale * scale * scale * (total[:, 1:2, :] / total_inner)
        for group in range(turn_s.shape[0]):
            stats_out[group * GROUP : (group + 1) * GROUP, :] = jnp.transpose(turn_s[group])


def backward_step(
    g, j, groups, blocks, gate_ref, value_ref, before_ref, mixed_ref,
    bc_ref, stepin_ref, cums_ref, held_ref,
    gate_w, value_w, step_w, taps_ref, bias_ref, rate_ref, skip_ref, gain_ref, cols_ref, seg_ref,
    branch_out, lowgate_out, lowvalue_out, lowstep_out, gbc_out, gin_out, small_out, sums_out,
    vbuf, gcbuf, gram_s, dgram, b_s, c_t, step_s, ent_s, fade_s, cums_s, cums_t, keep_s,
    grad_state, gin, gb_s, gc_s, u_s, v_s, fin_s, small_s, sums_s, branch_s, stats_ref,
):
    group = groups - 1 - g
    nblocks = grad_state.shape[0]
    cols = cols_ref[...]
    at_row, at_col = iota((GROUP, GROUP), 0), iota((GROUP, GROUP), 1)

    @pl.when((g == 0) & (j == 0))
    def _():
        grad_state[...] = jnp.zeros(grad_state.shape, F32)
        small_s[...] = jnp.zeros(small_s.shape, F32)
        sums_s[...] = jnp.zeros(sums_s.shape, F32)
        gcbuf[...] = jnp.zeros(gcbuf.shape, F32)

    @pl.when(j == 0)
    def _():
        bc = bc_ref[...]
        b_low, c_low = bc[:, :STATE], bc[:, STATE:]
        b_s[...] = b_low
        c_t[...] = jnp.transpose(c_low.astype(F32)).astype(BF16)
        cums = cums_ref[...]
        step, entering, fading, retain = token_quantities(stepin_ref[...], cums, cols, rate_ref[...])
        spread(step_s, step, nblocks)
        spread(ent_s, entering, nblocks)
        spread(fade_s, fading, nblocks)
        spread(cums_s, cums, nblocks)
        spread(keep_s, jnp.broadcast_to(retain, (8, 128)), nblocks)
        cums_t[...] = jnp.transpose(cums)
        within = (at_row <= at_col) & (cols[:, 9:10] == seg_ref[...])
        gram_s[...] = jnp.where(within, mm_nt(b_low, c_low), 0.0)
        dgram[...] = jnp.zeros(dgram.shape, F32)
        gin[...] = jnp.zeros(gin.shape, F32)
        gb_s[...] = jnp.zeros(gb_s.shape, F32)
        gc_s[...] = jnp.zeros(gc_s.shape, F32)
        u_s[...] = jnp.zeros(u_s.shape, F32)
        v_s[...] = jnp.zeros(v_s.shape, F32)
        fin_s[...] = jnp.zeros(fin_s.shape, F32)

    at = pl.multiple_of(j * BLOCK, BLOCK)
    gate, mixed = gate_ref[...].astype(F32), mixed_ref[...]
    grad = branch_s[group, :, pl.ds(at, BLOCK)].astype(F32)
    gain, skip, taps = gain_ref[...], skip_ref[...], taps_ref[...]
    stats = stats_ref[pl.ds(pl.multiple_of(group * GROUP, GROUP), GROUP), :]
    scale, inner = stats[:, 0:1], stats[:, 1:2]
    sig = jax.nn.sigmoid(gate)
    act = gate * sig
    gated = mixed * act
    scaled_gated = gated * scale
    branch_out[...] = (scaled_gated * gain).astype(BF16)
    grad_gain = jnp.sum(grad * scaled_gated, axis=0, keepdims=True)
    grad_gated = scale * (grad * gain) - gated * inner
    grad_mixed = grad_gated * act
    low_gate = (grad_gated * mixed * (sig * (1.0 + gate * (1.0 - sig)))).astype(BF16)
    lowgate_out[...] = low_gate

    vbuf[0:HALO, :] = before_ref[...]
    vbuf[HALO : HALO + GROUP, :] = value_ref[...]
    moved = shifted_values(vbuf, cols)
    conv = conv_of(moved, taps, bias_ref[...])
    sig = jax.nn.sigmoid(conv)
    x_float = (conv * sig).astype(BF16).astype(F32)
    slope = sig * (1.0 + conv * (1.0 - sig))
    step_wide = expand(step_s[j])
    fade_wide = expand(fade_s[j])
    scaled = (step_wide * x_float).astype(BF16)
    scaled_float = scaled.astype(F32)
    grad_skip = jnp.sum(grad_mixed * x_float, axis=0, keepdims=True)
    grad_scan = grad_mixed.astype(BF16)
    grad_scan_float = grad_scan.astype(F32)
    scanned = mixed - skip * x_float

    own = grad_state[j]
    state_low = held_ref[0]
    own_low = own.astype(BF16)
    grad_weighted = mm(b_s[...], own_low)
    weighted = (fade_wide * scaled_float).astype(BF16)
    entered = (expand(ent_s[j]) * grad_scan_float).astype(BF16)
    gb_s[...] += mm_nt(weighted, own_low)
    gc_s[...] += mm_nt(entered, state_low)
    keep_wide = expand(keep_s[j])[0:1, :]
    kept = keep_wide * jnp.sum(state_low.astype(F32) * own, axis=0, keepdims=True)
    grad_state[j] = keep_wide * own + mm(c_t[...], entered)

    cums_here = cums_s[j]
    top = jnp.zeros((HALF, BLOCK), F32)
    bottom = jnp.zeros((HALF, BLOCK), F32)
    dtop = dgram[:HALF, :]
    dbottom = dgram[HALF:, HALF:]
    for i in range(PER_BLOCK):
        frm = cums_here[:, i : i + 1]
        to = cums_t[pl.ds(j * PER_BLOCK + i, 1), :]
        mask = lane_mask(i)
        only_grad = grad_scan * mask
        only = scaled * mask
        decay = jnp.exp(jnp.minimum(to - frm[:HALF], 0.0))
        top = top + mm((gram_s[:HALF, :] * decay).astype(BF16), only_grad)
        dtop = dtop + mm_nt(only[:HALF], grad_scan) * decay
        decay = jnp.exp(jnp.minimum(to[:, HALF:] - frm[HALF:], 0.0))
        bottom = bottom + mm((gram_s[HALF:, HALF:] * decay).astype(BF16), only_grad[HALF:])
        dbottom = dbottom + mm_nt(only[HALF:], grad_scan[HALF:]) * decay
    dgram[:HALF, :] = dtop
    dgram[HALF:, HALF:] = dbottom
    faded = fade_wide * grad_weighted
    through = jnp.concatenate([top, bottom], axis=0) + faded
    column = scaled_float * through
    final = kept + jnp.sum(scaled_float * faded, axis=0, keepdims=True)
    place = (iota((BLOCK, 128), 1) == j * PER_BLOCK + iota((BLOCK, 128), 0) // HEAD_DIM).astype(F32)
    u_s[...] += mm(grad_scan_float * scanned - column, place, PRECISE)
    v_s[...] += mm(column, place, PRECISE)
    fin_s[...] += mm(jnp.broadcast_to(final, (8, BLOCK)), place, PRECISE)

    grad_conv = (step_wide * through + skip * grad_mixed) * slope
    after = gcbuf.at[j]
    after[GROUP : GROUP + HALO, :] = after[0:HALO, :]
    after[0:GROUP, :] = grad_conv
    grad_value = taps[0:1, :] * grad_conv
    for offset in range(1, CONV):
        up = jnp.where(cols[:, 2 + offset : 3 + offset] > 0.0, after[offset : offset + GROUP, :], 0.0)
        grad_value = grad_value + taps[offset : offset + 1, :] * up
    low_value = grad_value.astype(BF16)
    lowvalue_out[...] = low_value
    gin[...] += mm_nt(low_gate, gate_w[:, pl.ds(at, BLOCK)]) + mm_nt(low_value, value_w[:, pl.ds(at, BLOCK)])
    lines = [grad_gain, grad_skip]
    lines += [jnp.sum(grad_conv * moved[offset], axis=0, keepdims=True) for offset in range(CONV)]
    lines += [jnp.sum(grad_conv, axis=0, keepdims=True)]
    for at_line, line in enumerate(lines):
        small_s[j, at_line : at_line + 1, :] += line

    @pl.when(g == groups - 1)
    def _():
        small_out[:, pl.ds(at, BLOCK)] = small_s[j]

    @pl.when(j == blocks - 1)
    def _():
        bc = bc_ref[...]
        within = (at_row <= at_col) & (cols[:, 9:10] == seg_ref[...])
        dg = jnp.where(within, dgram[...], 0.0)
        grad_b = gb_s[...] + mm(dg.astype(BF16), bc[:, STATE:])
        grad_c = gc_s[...] + mm(jnp.transpose(dg).astype(BF16), bc[:, :STATE])
        gbc_out[:, :STATE] = grad_b.astype(BF16)
        gbc_out[:, STATE:] = grad_c.astype(BF16)
        last = iota((GROUP, 128), 0) == GROUP - 1
        grad_cums = u_s[...] + jnp.where(last, fin_s[0:1, :], 0.0)
        upper = (at_row <= at_col).astype(F32)
        grad_a = mm(upper, grad_cums, PRECISE)
        step_in = stepin_ref[...]
        step = jnp.maximum(step_in, 0.0) + jnp.log1p(jnp.exp(-jnp.abs(step_in)))
        sig_in = jax.nn.sigmoid(step_in)
        ratio = jnp.where(step_in < -15.0, 1.0, sig_in / step)
        grad_step = v_s[...] * ratio + grad_a * rate_ref[...] * sig_in
        low_step = grad_step.astype(BF16)
        lowstep_out[...] = low_step
        sums_s[0:1, :] += jnp.sum(grad_step, axis=0, keepdims=True)
        sums_s[1:2, :] += jnp.sum(grad_a * step, axis=0, keepdims=True)
        sums_out[...] = sums_s[...]
        gin_out[...] = (gin[...] + mm_nt(low_step, step_w[...])).astype(BF16)


def shape(dims, kind=F32):
    return jax.ShapeDtypeStruct(dims, kind)


def params(collective=None):
    extra = {} if collective is None else dict(collective_id=collective, has_side_effects=True)
    return pltpu.CompilerParams(
        dimension_semantics=("arbitrary", "arbitrary"), vmem_limit_bytes=60 << 20, **extra
    )


def whole(array):
    return pl.BlockSpec(
        array.shape, lambda g, j: (0,) * array.ndim, pipeline_mode=pl.Buffered(1)
    )


def forward_call(inputs, weights, vectors, gain, cols, seg_line, hosted, pace):
    gate_w, value_w, state_w, step_w, out_w = weights
    taps, bias, staps, sbias, step_bias, rate, skip = vectors
    length, model = inputs.shape
    inner = gate_w.shape[1]
    groups, blocks = length // GROUP, inner // BLOCK
    wide = pl.BlockSpec((GROUP, BLOCK), lambda g, j: (g, j))
    line = lambda rows: pl.BlockSpec((rows, BLOCK), lambda g, j: (0, j))
    rows_of = lambda width: pl.BlockSpec((GROUP, width), lambda g, j: (g, 0))
    specs, shapes = hosted.outs()
    return pl.pallas_call(
        hosted.wrap(forward_kernel, FORWARD_INS, FORWARD_OUTS, pace),
        grid=(groups, blocks),
        in_specs=[
            rows_of(model), whole(gate_w), whole(value_w), whole(state_w), whole(step_w),
            line(CONV), line(1), whole(staps), whole(sbias), whole(step_bias), whole(rate), line(1),
            rows_of(cols.shape[1]), pl.BlockSpec((1, GROUP), lambda g, j: (0, g)),
            whole(out_w), line(1),
        ] + hosted.in_specs(),
        out_specs=[
            wide, wide, wide, rows_of(2 * STATE), rows_of(2 * STATE), rows_of(128), rows_of(128),
            pl.BlockSpec((1, STATE, BLOCK), lambda g, j: (g, 0, j)), rows_of(model),
        ] + specs,
        out_shape=[
            shape((length, inner), BF16), shape((length, inner)), shape((length, inner)),
            shape((length, 2 * STATE), BF16), shape((length, 2 * STATE)), shape((length, 128)),
            shape((length, 128)), shape((groups, STATE, inner), BF16), shape((length, model), BF16),
        ] + shapes,
        scratch_shapes=[
            pltpu.VMEM((blocks, GROUP + HALO, BLOCK), F32),
            pltpu.VMEM((GROUP + HALO, 2 * STATE), F32),
            pltpu.VMEM((GROUP, GROUP), F32),
            pltpu.VMEM((STATE, GROUP), BF16),
            pltpu.VMEM((GROUP, STATE), BF16),
            pltpu.VMEM((blocks, GROUP, 128), F32),
            pltpu.VMEM((blocks, GROUP, 128), F32),
            pltpu.VMEM((blocks, GROUP, 128), F32),
            pltpu.VMEM((blocks, GROUP, 128), F32),
            pltpu.VMEM((128, GROUP), F32),
            pltpu.VMEM((blocks, 8, 128), F32),
            pltpu.VMEM((blocks, STATE, BLOCK), F32),
            pltpu.VMEM((GROUP, model), F32),
        ] + hosted.scratch(),
        compiler_params=params(2 if hosted.operands() else None),
        cost_estimate=pl.CostEstimate(
            flops=2 * length * model * (3 * inner + 512), bytes_accessed=40 << 20, transcendentals=0
        ),
        name="ssd_forward",
    )(
        inputs, gate_w, value_w, state_w, step_w, taps, bias, staps, sbias, step_bias, rate, skip,
        cols, seg_line, out_w, gain, *hosted.operands(),
    )


def backward_call(saved, cotan, weights, vectors, gain, cols, seg_line, hosted, pace, collective):
    gate_raw, value_raw, mixed, bc, _, step_in, cums, held, _ = saved
    gate_w, value_w, step_w, out_w = weights
    taps, bias, rate, skip = vectors
    length, inner = gate_raw.shape
    model, tp_size = gate_w.shape[0], hosted.size
    specs, shapes = hosted.outs()
    groups, blocks = length // GROUP, inner // BLOCK
    assert groups == blocks
    last = groups - 1
    row = lambda g: last - jnp.maximum(g - 1, 0)
    column = lambda g, j: jnp.where(g == 0, 0, j)
    wide = pl.BlockSpec((GROUP, BLOCK), lambda g, j: (row(g), column(g, j)))
    line = lambda rows: pl.BlockSpec((rows, BLOCK), lambda g, j: (0, column(g, j)))
    rows_of = lambda width: pl.BlockSpec((GROUP, width), lambda g, j: (row(g), 0))
    first = lambda width: pl.BlockSpec((GROUP, width), lambda g, j: (jnp.where(g == 0, j, last), 0))
    steps = GROUP // HALO
    before = pl.BlockSpec(
        (HALO, BLOCK), lambda g, j: (jnp.maximum(row(g) * steps - 1, 0), column(g, j))
    )
    return pl.pallas_call(
        hosted.wrap(partial(backward_kernel, tp_size), BACKWARD_INS, BACKWARD_OUTS, pace),
        grid=(groups + 1, blocks),
        in_specs=[
            first(model), whole(out_w), first(inner), first(inner), whole(gain),
            wide, wide, before, wide, rows_of(2 * STATE), rows_of(128), rows_of(128),
            pl.BlockSpec((1, STATE, BLOCK), lambda g, j: (row(g), 0, column(g, j))),
            whole(gate_w), whole(value_w), whole(step_w),
            line(CONV), line(1), whole(rate), line(1), line(1),
            rows_of(cols.shape[1]), pl.BlockSpec((1, GROUP), lambda g, j: (0, row(g))),
        ] + hosted.in_specs(),
        out_specs=[
            wide, wide, wide, rows_of(128), rows_of(2 * STATE),
            rows_of(model), pl.BlockSpec((8, inner), lambda g, j: (0, 0)), pl.BlockSpec((8, 128), lambda g, j: (0, 0)),
            pl.BlockSpec((length, 128), lambda g, j: (0, 0)),
        ] + specs,
        out_shape=[
            shape((length, inner), BF16), shape((length, inner), BF16), shape((length, inner), BF16),
            shape((length, 128), BF16), shape((length, 2 * STATE), BF16),
            shape((length, model), BF16), shape((8, inner)), shape((8, 128)), shape((length, 128)),
        ] + shapes,
        scratch_shapes=[
            pltpu.VMEM((GROUP + HALO, BLOCK), F32),
            pltpu.VMEM((blocks, GROUP + HALO, BLOCK), F32),
            pltpu.VMEM((GROUP, GROUP), F32),
            pltpu.VMEM((GROUP, GROUP), F32),
            pltpu.VMEM((GROUP, STATE), BF16),
            pltpu.VMEM((STATE, GROUP), BF16),
            pltpu.VMEM((blocks, GROUP, 128), F32),
            pltpu.VMEM((blocks, GROUP, 128), F32),
            pltpu.VMEM((blocks, GROUP, 128), F32),
            pltpu.VMEM((blocks, GROUP, 128), F32),
            pltpu.VMEM((128, GROUP), F32),
            pltpu.VMEM((blocks, 8, 128), F32),
            pltpu.VMEM((blocks, STATE, BLOCK), F32),
            pltpu.VMEM((GROUP, model), F32),
            pltpu.VMEM((GROUP, STATE), F32),
            pltpu.VMEM((GROUP, STATE), F32),
            pltpu.VMEM((GROUP, 128), F32),
            pltpu.VMEM((GROUP, 128), F32),
            pltpu.VMEM((8, 128), F32),
            pltpu.VMEM((blocks, 8, BLOCK), F32),
            pltpu.VMEM((8, 128), F32),
            pltpu.VMEM((groups, GROUP, inner), BF16),
            pltpu.VMEM((groups, 8, GROUP), F32),
            pltpu.VMEM((tp_size, groups, 8, GROUP), F32),
            pltpu.VMEM((groups, 128, GROUP), F32),
            pltpu.SemaphoreType.DMA((tp_size - 1,)),
            pltpu.SemaphoreType.DMA((tp_size - 1,)),
        ] + hosted.scratch(),
        compiler_params=params(collective),
        cost_estimate=pl.CostEstimate(
            flops=6 * length * model * inner, bytes_accessed=60 << 20, transcendentals=0
        ),
        name="ssd_backward",
    )(
        cotan, out_w, gate_raw, mixed, gain,
        gate_raw, value_raw, value_raw, mixed, bc, step_in, cums, held,
        gate_w, value_w, step_w, taps, bias, rate, skip, gain, cols, seg_line, *hosted.operands(),
    )

def gather_kernel(count, pieces, *refs):
    amount = len(pieces)
    sources, targets = refs[:amount], refs[amount : 2 * amount]
    own_sem, send_sem, recv_sem, pass_sem, took_sem = refs[2 * amount :]
    me, line = lax.axis_index("fsdp"), lax.axis_index("tp")
    chips = count // 2
    partner = me + 1 - 2 * lax.rem(me, 2)
    others = [lax.rem(me + 2 * hop, count) for hop in range(1, chips)]
    greet([(device, line) for device in others + [partner]])

    def remote(source, target, sends, receives, device):
        return pltpu.make_async_remote_copy(
            src_ref=source, dst_ref=target, send_sem=sends, recv_sem=receives,
            device_id=(device, line), device_id_type=MESH,
        )

    def place(which, at):
        size, axis = pieces[which]
        return part_of(targets[which], at, size, axis)

    started = []
    for which in range(amount):
        for hop in range(1, chips):
            copy = remote(
                sources[which], place(which, me), send_sem.at[hop, which],
                recv_sem.at[hop, which], lax.rem(me + 2 * hop, count),
            )
            copy.start()
            started.append(copy)
    for which in range(amount):
        copy = remote(
            sources[which], place(which, me), pass_sem.at[0, which], took_sem.at[0, which], partner
        )
        copy.start()
        started.append(copy)
    own = []
    for which in range(amount):
        copy = pltpu.make_async_copy(sources[which], place(which, me), own_sem.at[which])
        copy.start()
        own.append(copy)
    for which in range(amount):
        for hop in range(1, chips):
            origin = lax.rem(me - 2 * hop + count, count)
            block = place(which, origin)
            remote(
                block, block, send_sem.at[hop, which], recv_sem.at[hop, which], partner
            ).wait_recv()
            copy = remote(
                block, block, pass_sem.at[hop, which], took_sem.at[hop, which], partner
            )
            copy.start()
            started.append(copy)
    for which in range(amount):
        for hop in range(chips):
            block = place(which, lax.rem(partner - 2 * hop + count, count))
            remote(
                block, block, pass_sem.at[hop, which], took_sem.at[hop, which], partner
            ).wait_recv()
    for copy in started:
        copy.wait_send()
    for copy in own:
        copy.wait()


def gather_call(count, blocks, axes):
    pieces, shapes = [], []
    for block, axis in zip(blocks, axes):
        if axis == 2:
            pieces.append((0, 2))
            shapes.append(shape((count,) + block.shape, BF16))
        else:
            pieces.append((block.shape[axis], axis))
            dims = list(block.shape)
            dims[axis] *= count
            shapes.append(shape(tuple(dims), BF16))
    amount = len(blocks)
    sems = lambda: pltpu.SemaphoreType.DMA((count // 2, amount))
    return pl.pallas_call(
        partial(gather_kernel, count, pieces),
        in_specs=[pl.BlockSpec(memory_space=pl.ANY)] * amount,
        out_specs=[pl.BlockSpec(memory_space=pl.ANY)] * amount,
        out_shape=shapes,
        scratch_shapes=[pltpu.SemaphoreType.DMA((amount,)), sems(), sems(), sems(), sems()],
        compiler_params=pltpu.CompilerParams(collective_id=0, has_side_effects=True),
        cost_estimate=pl.CostEstimate(flops=0, bytes_accessed=250 << 20, transcendentals=0),
        name="gather_weights",
    )(*blocks)


def scatter_kernel(count, pieces, *refs):
    amount = len(pieces)
    sources, targets = refs[:amount], refs[amount : 2 * amount]
    scratch = refs[2 * amount :]
    mine, took, came = (scratch[at * amount : (at + 1) * amount] for at in range(3))
    own_sem, pass_sem, took_sem, send_sem, recv_sem = scratch[3 * amount :]
    me, line = lax.axis_index("fsdp"), lax.axis_index("tp")
    chips = count // 2
    partner = me + 1 - 2 * lax.rem(me, 2)
    others = [lax.rem(me + 2 * hop, count) for hop in range(1, chips)]
    greet([(device, line) for device in others + [partner]])

    def remote(source, target, sends, receives, device):
        return pltpu.make_async_remote_copy(
            src_ref=source, dst_ref=target, send_sem=sends, recv_sem=receives,
            device_id=(device, line), device_id_type=MESH,
        )

    def piece(which, at):
        size, axis = pieces[which]
        return part_of(sources[which], at, size, axis)

    order = list(range(1, chips)) + [0]
    handed, own = {}, {}
    for hop in order:
        for which in range(amount):
            copy = remote(
                piece(which, lax.rem(partner + 2 * hop, count)), took[which].at[hop],
                pass_sem.at[hop, which], took_sem.at[hop, which], partner,
            )
            copy.start()
            handed[hop, which] = copy
            copy = pltpu.make_async_copy(
                piece(which, lax.rem(me + 2 * hop, count)), mine[which].at[hop],
                own_sem.at[hop, which],
            )
            copy.start()
            own[hop, which] = copy
    sent = []
    for hop in order:
        for which in range(amount):
            own[hop, which].wait()
            handed[hop, which].wait_recv()
            total = mine[which][hop].astype(F32) + took[which][hop].astype(F32)
            if hop == 0:
                targets[which][...] = total
                continue
            mine[which][hop] = total.astype(BF16)
            copy = remote(
                mine[which].at[hop], came[which].at[hop - 1], send_sem.at[hop, which],
                recv_sem.at[hop, which], lax.rem(me + 2 * hop, count),
            )
            copy.start()
            sent.append(copy)
    for which in range(amount):
        for hop in range(1, chips):
            block = came[which].at[hop - 1]
            remote(
                block, block, send_sem.at[hop, which], recv_sem.at[hop, which], partner
            ).wait_recv()
            targets[which][...] += block[...].astype(F32)
    for copy in list(handed.values()) + sent:
        copy.wait_send()


def scatter_call(count, arrays, axes):
    pieces, shapes = [], []
    for array, axis in zip(arrays, axes):
        if axis == 2:
            pieces.append((0, 2))
            shapes.append(array.shape[1:])
        else:
            dims = list(array.shape)
            dims[axis] //= count
            pieces.append((dims[axis], axis))
            shapes.append(tuple(dims))
    amount, chips = len(arrays), count // 2
    sems = lambda: pltpu.SemaphoreType.DMA((chips, amount))
    return pl.pallas_call(
        partial(scatter_kernel, count, pieces),
        in_specs=[pl.BlockSpec(memory_space=pl.ANY)] * amount,
        out_specs=[pl.BlockSpec(memory_space=pltpu.VMEM)] * amount,
        out_shape=[shape(dims) for dims in shapes],
        scratch_shapes=[pltpu.VMEM((chips,) + dims, BF16) for dims in shapes]
        + [pltpu.VMEM((chips,) + dims, BF16) for dims in shapes]
        + [pltpu.VMEM((chips - 1,) + dims, BF16) for dims in shapes]
        + [sems(), sems(), sems(), sems(), sems()],
        compiler_params=pltpu.CompilerParams(
            collective_id=1, has_side_effects=True, vmem_limit_bytes=48 << 20
        ),
        cost_estimate=pl.CostEstimate(flops=0, bytes_accessed=250 << 20, transcendentals=0),
        name="scatter_gradients",
    )(*arrays)


def weight_kernel(micro, *refs):
    outs = refs[-4:]
    rows, lows = refs[:micro], refs[micro : 5 * micro]
    for which in range(4):
        total = mm_tn(rows[0][...], lows[which][...])
        for at in range(1, micro):
            total = total + mm_tn(rows[at][...], lows[4 * at + which][...])
        outs[which][...] = total.astype(BF16)


def weight_call(inputs, lows):
    micro, (length, model) = len(inputs), inputs[0].shape
    full = lambda array: pl.BlockSpec(array.shape, lambda g: (0, 0), pipeline_mode=pl.Buffered(1))
    flat = [array for low in lows for array in low]
    widths = [array.shape[1] for array in lows[0]]
    return pl.pallas_call(
        partial(weight_kernel, micro),
        grid=(model // BLOCK,),
        in_specs=[pl.BlockSpec((length, BLOCK), lambda g: (0, g))] * micro
        + [full(array) for array in flat],
        out_specs=[pl.BlockSpec((BLOCK, width), lambda g: (g, 0)) for width in widths],
        out_shape=[shape((model, width), BF16) for width in widths],
        compiler_params=pltpu.CompilerParams(vmem_limit_bytes=50 << 20),
        cost_estimate=pl.CostEstimate(
            flops=2 * micro * length * model * sum(widths), bytes_accessed=40 << 20, transcendentals=0
        ),
        name="weight_gradients",
    )(*inputs, *flat)


def outer_kernel(micro, *refs):
    total = mm_tn(refs[0][...], refs[micro][...])
    for at in range(1, micro):
        total = total + mm_tn(refs[at][...], refs[micro + at][...])
    refs[-1][...] = total.astype(BF16)


def outer_call(branches, cotans):
    micro, (length, inner) = len(branches), branches[0].shape
    model = cotans[0].shape[1]
    full = lambda array: pl.BlockSpec(array.shape, lambda g: (0, 0), pipeline_mode=pl.Buffered(1))
    return pl.pallas_call(
        partial(outer_kernel, micro),
        grid=(inner // BLOCK,),
        in_specs=[pl.BlockSpec((length, BLOCK), lambda g: (0, g))] * micro
        + [full(array) for array in cotans],
        out_specs=pl.BlockSpec((BLOCK, model), lambda g: (g, 0)),
        out_shape=shape((inner, model), BF16),
        compiler_params=pltpu.CompilerParams(vmem_limit_bytes=50 << 20),
        cost_estimate=pl.CostEstimate(
            flops=2 * micro * length * model * inner, bytes_accessed=30 << 20, transcendentals=0
        ),
        name="out_gradients",
    )(*branches, *cotans)


def tail_kernel(chips, tp_size, micro, widths, *refs):
    columns, lows, parts, raws = refs[:4], refs[4:12], refs[12:14], refs[14:16]
    cols_ref, staps_ref, sbias_ref, pack = refs[16:20]
    outs, state_out, pack_out, ssum_out, low_out = refs[20:24], refs[24], refs[25], refs[26], refs[27]
    (
        cols_s, give, took, mine, came, passed, total_s, kept_s,
        sgive, stook, smine, scame, stotal, skept_s,
        pack_took, pack_sum, pack_slots, ssum, ssum_took, ssum_sum, ssum_slots,
        raw_s, own_s, slots_s, whole_s, sum_s, low_s, vbuf, gcbuf,
        cols_sem, give_sem, took_sem, send_sem, recv_sem, sgive_sem, stook_sem, ssend_sem, srecv_sem,
        pass_sem, pack_sem, ssum_sem, raw_sem, own_sem, part_send, part_recv, whole_send, whole_recv,
    ) = refs[28:]
    step, steps = pl.program_id(0), pl.num_programs(0)
    me, line = lax.axis_index("fsdp"), lax.axis_index("tp")
    count = 2 * chips
    core, chip = lax.rem(me, 2), me // 2
    partner = me + 1 - 2 * core
    split = total_s.shape[1] // 256 * 128

    def flipped(hop, which_core):
        x, y = lax.rem(chip, 2), chip // 2
        hop_x, hop_y = hop % 2, hop // 2
        x, y = x + hop_x - 2 * x * hop_x, y + hop_y - 2 * y * hop_y
        return (2 * y + x) * 2 + which_core

    def tile_of(at):
        pair = lax.rem(at, count) // 2
        hop = jnp.where(pair == 0, 3, pair - 1)
        return hop, flipped(hop, jnp.where(lax.rem(at, 2) == 0, 1 - core, core))

    def fetch(at, which):
        _, shard = tile_of(at)
        slot = lax.rem(at, 2)
        return pltpu.make_async_copy(
            columns[which].at[:, pl.ds(pl.multiple_of(shard * BLOCK, BLOCK), BLOCK)],
            cols_s.at[slot, which], cols_sem.at[slot, which],
        )

    def far(hop):
        return (flipped(hop, core), line)

    def giving(hop):
        return remote_copy(
            give.at[hop], took.at[hop], give_sem.at[hop], took_sem.at[hop], (partner, line)
        )

    def sending(hop):
        return remote_copy(
            mine.at[hop - 1], came.at[hop - 1], send_sem.at[hop - 1], recv_sem.at[hop - 1], far(hop)
        )

    def passing(hop):
        columns = pl.ds(0, split) if hop == 1 else pl.ds(split, total_s.shape[1] - split)
        return remote_copy(
            mine.at[2, :, columns], passed.at[:, columns], pass_sem.at[0, hop - 1],
            pass_sem.at[1, hop - 1], far(hop),
        )

    def sgiving(hop):
        return remote_copy(
            sgive.at[hop], stook.at[hop], sgive_sem.at[hop], stook_sem.at[hop], (partner, line)
        )

    def ssending(hop):
        return remote_copy(
            smine.at[hop - 1], scame.at[hop - 1], ssend_sem.at[hop - 1], srecv_sem.at[hop - 1], far(hop)
        )

    pack_pass = remote_copy(pack, pack_took, pack_sem.at[0, 0], pack_sem.at[1, 0], (partner, line))
    ssum_pass = remote_copy(ssum, ssum_took, ssum_sem.at[0, 0], ssum_sem.at[1, 0], (partner, line))

    def pack_send(hop):
        return remote_copy(
            pack_sum, pack_slots.at[chip], pack_sem.at[0, hop], pack_sem.at[1, hop], far(hop)
        )

    def ssum_send(hop):
        return remote_copy(
            ssum_sum, ssum_slots.at[chip], ssum_sem.at[0, hop], ssum_sem.at[1, hop], far(hop)
        )

    def rows_at(ref, at):
        return ref.at[pl.ds(pl.multiple_of(at * GROUP, GROUP), GROUP), :]

    def handing(hop):
        owner = lax.rem(line + hop, tp_size)
        return remote_copy(
            rows_at(parts[late], owner), slots_s.at[line], part_send.at[hop - 1],
            part_recv.at[hop - 1], (me, owner),
        )

    late = micro - 1

    def own_part():
        return pltpu.make_async_copy(rows_at(parts[late], line), own_s, own_sem.at[late])

    def ready(at):
        length = raws[at].shape[0]
        return pltpu.make_async_copy(
            parts[at], whole_s.at[pl.ds(at * length, length), :], own_sem.at[at]
        )

    def raw_copy(at):
        length = raws[at].shape[0]
        return pltpu.make_async_copy(
            raws[at], raw_s.at[pl.ds(at * length, length), :], raw_sem.at[at]
        )

    groups = raws[0].shape[0] // GROUP

    def spreading(hop):
        block = rows_at(whole_s, late * groups + line)
        return remote_copy(
            sum_s, block, whole_send.at[hop - 1], whole_recv.at[hop - 1],
            (me, lax.rem(line + hop, tp_size)),
        )

    @pl.when(step == 0)
    def _():
        for which in range(4):
            fetch(step, which).start()
        own_part().start()
        for at in range(micro):
            raw_copy(at).start()
            if at != late:
                ready(at).start()
        greet(
            [far(hop) for hop in range(1, chips)] + [(partner, line)]
            + [(me, lax.rem(line + hop, tp_size)) for hop in range(1, tp_size)]
        )
        for hop in range(1, tp_size):
            handing(hop).start()
        pack_pass.start()

    @pl.when(step + 1 < count)
    def _():
        for which in range(4):
            fetch(step + 1, which).start()

    @pl.when((step + 1 >= count) & (step + 1 < steps))
    def _():
        for which in range(2):
            fetch(step + 1, which).start()

    for which in range(2):
        fetch(step, which).wait()

    @pl.when(step < count)
    def _():
        for which in range(2, 4):
            fetch(step, which).wait()

    slot = lax.rem(step, 2)
    hop, _ = tile_of(step)
    even = lax.rem(step, 2) == 0

    def tile(which):
        sides = (0, 1) if which < 3 else (2, 3)
        return mm_tn(cols_s[slot, sides[0]], lows[2 * which][...]) + mm_tn(
            cols_s[slot, sides[1]], lows[2 * which + 1][...]
        )

    @pl.when((step < count) & even)
    def _():
        at = 0
        for which, width in enumerate(widths):
            give[hop, :, at : at + width] = tile(which).astype(BF16)
            at += width
        giving(hop).start()

    @pl.when((step < count) & jnp.logical_not(even))
    def _():
        at = 0
        for which, width in enumerate(widths):
            total_s[:, at : at + width] = tile(which)
            at += width
        giving(hop).wait_recv()
        total_s[...] += took[hop].astype(F32)

        @pl.when(hop == 3)
        def _():
            mine[2] = total_s[...].astype(BF16)
            passing(1).start()
            passing(2).start()

        @pl.when(hop == 0)
        def _():
            kept_s[...] = total_s[...]

        @pl.when(hop == 1)
        def _():
            passing(2).wait_recv()
            total_s[:, split:] += passed[:, split:].astype(F32)
            mine[0] = total_s[...].astype(BF16)
            sending(1).start()

        @pl.when(hop == 2)
        def _():
            passing(1).wait_recv()
            total_s[:, :split] += passed[:, :split].astype(F32)
            mine[1] = total_s[...].astype(BF16)
            sending(2).start()

    @pl.when(step == 1)
    def _():
        pack_pass.wait()
        pack_sum[...] = pack[...] + pack_took[...]
        pack_slots[chip] = pack_sum[...]
        for other in range(1, chips):
            pack_send(other).start()

    @pl.when(step == 5)
    def _():
        own_part().wait()
        slots_s[line] = own_s[...]
        for hop in range(1, tp_size):
            handing(hop).wait()
        total = slots_s[0].astype(F32)
        for other in range(1, tp_size):
            total = total + slots_s[other].astype(F32)
        sum_s[...] = total.astype(BF16)
        mine_rows = rows_at(whole_s, late * groups + line)
        mine_rows[...] = sum_s[...]
        for hop in range(1, tp_size):
            spreading(hop).start()

    @pl.when(step == count - 1)
    def _():
        for at in range(micro):
            raw_copy(at).wait()
            if at != late:
                ready(at).wait()
        for hop in range(1, tp_size):
            spreading(hop).wait()
        ssum[...] = jnp.zeros(ssum.shape, F32)
        taps, bias = staps_ref[...], sbias_ref[...]

        def state_group(turn, carry):
            group = micro * groups - 1 - turn
            at = pl.multiple_of(group * GROUP, GROUP)
            cols = cols_ref[pl.ds(at, GROUP), :]
            vbuf[HALO : HALO + GROUP, :] = raw_s[pl.ds(at, GROUP), :]
            ahead = pl.multiple_of(jnp.maximum(group * (GROUP // HALO) - 1, 0) * HALO, HALO)
            vbuf[0:HALO, :] = raw_s[pl.ds(ahead, HALO), :]
            moved = shifted_values(vbuf, cols)
            conv = conv_of(moved, taps, bias)
            sig = jax.nn.sigmoid(conv)
            grad = whole_s[pl.ds(at, GROUP), :].astype(F32) * (sig * (1.0 + conv * (1.0 - sig)))
            gcbuf[GROUP : GROUP + HALO, :] = gcbuf[0:HALO, :]
            gcbuf[0:GROUP, :] = grad
            back = taps[0:1, :] * grad
            for offset in range(1, CONV):
                up = jnp.where(
                    cols[:, 2 + offset : 3 + offset] > 0.0, gcbuf[offset : offset + GROUP, :], 0.0
                )
                back = back + taps[offset : offset + 1, :] * up
            low_s[pl.ds(at, GROUP), :] = back.astype(BF16)
            for offset in range(CONV):
                ssum[offset : offset + 1, :] += jnp.sum(grad * moved[offset], axis=0, keepdims=True)
            ssum[CONV : CONV + 1, :] += jnp.sum(grad, axis=0, keepdims=True)
            return carry

        lax.fori_loop(0, micro * groups, state_group, 0)
        ssum_pass.start()
        for at in range(micro):
            low_out[at] = low_s[pl.ds(pl.multiple_of((at * groups + line) * GROUP, GROUP), GROUP), :]

    def state_tile():
        length = groups * GROUP
        return mm_tn(cols_s[slot, 0], low_s[0:length, :]) + mm_tn(
            cols_s[slot, 1], low_s[length : 2 * length, :]
        )

    @pl.when((step >= count) & even)
    def _():
        sgive[hop] = state_tile().astype(BF16)
        sgiving(hop).start()

    @pl.when((step >= count) & jnp.logical_not(even))
    def _():
        stotal[...] = state_tile()
        sgiving(hop).wait_recv()
        stotal[...] += stook[hop].astype(F32)

        @pl.when(hop == 0)
        def _():
            skept_s[...] = stotal[...]

        @pl.when(hop > 0)
        def _():
            smine[hop - 1] = stotal[...].astype(BF16)
            ssending(hop).start()

    @pl.when(step == count + 1)
    def _():
        ssum_pass.wait()
        ssum_sum[...] = ssum[...] + ssum_took[...]
        ssum_slots[chip] = ssum_sum[...]
        for other in range(1, chips):
            ssum_send(other).start()

    @pl.when(step == steps - 1)
    def _():
        for sends, slots, out in ((pack_send, pack_slots, pack_out), (ssum_send, ssum_slots, ssum_out)):
            for other in range(1, chips):
                sends(other).wait()
            total = slots[0]
            for other in range(1, chips):
                total = total + slots[other]
            out[...] = total
        for other in (1, 2):
            sending(other).wait_recv()
            kept_s[...] += came[other - 1].astype(F32)
        for other in range(1, chips):
            ssending(other).wait_recv()
            skept_s[...] += scame[other - 1].astype(F32)
        state_out[...] = skept_s[...]
        at = 0
        for which, width in enumerate(widths):
            part = kept_s[:, at : at + width]
            outs[which][...] = part if which < 3 else jnp.transpose(part)
            at += width
        for other in (1, 2):
            passing(other).wait_send()
            sending(other).wait_send()
        for other in range(1, chips):
            ssending(other).wait_send()
        for other in range(chips):
            giving(other).wait_send()
            sgiving(other).wait_send()


def tail_call(count, tp_size, inputs, cotans, lows, parts, raws, cols, staps, sbias, pack):
    micro, length = len(inputs), inputs[0].shape[0]
    chips = count // 2
    order = [low[which] for which in range(4) for low in lows]
    widths = [low.shape[1] for low in order[::2]]
    total, narrow = sum(widths), 2 * STATE
    hbm = pl.BlockSpec(memory_space=pl.ANY)
    full = lambda array: pl.BlockSpec(array.shape, lambda i: (0,) * array.ndim, pipeline_mode=pl.Buffered(1))
    out_dims = [(BLOCK, width) for width in widths[:3]] + [(widths[3], BLOCK), (BLOCK, narrow)]
    out_shapes = [shape(dims) for dims in out_dims] + [
        shape(pack.shape), shape((8, narrow)), shape((micro, GROUP, narrow), BF16)
    ]
    dma = lambda *dims: pltpu.SemaphoreType.DMA(dims)
    return pl.pallas_call(
        partial(tail_kernel, chips, tp_size, micro, widths),
        grid=(2 * count,),
        in_specs=[hbm] * 4 + [full(low) for low in order] + [hbm] * 4
        + [full(cols), full(staps), full(sbias), full(pack)],
        out_specs=[full(each) for each in out_shapes],
        out_shape=out_shapes,
        scratch_shapes=[
            pltpu.VMEM((2, 4, length, BLOCK), BF16),
            pltpu.VMEM((chips, BLOCK, total), BF16),
            pltpu.VMEM((chips, BLOCK, total), BF16),
            pltpu.VMEM((3, BLOCK, total), BF16),
            pltpu.VMEM((2, BLOCK, total), BF16),
            pltpu.VMEM((BLOCK, total), BF16),
            pltpu.VMEM((BLOCK, total), F32),
            pltpu.VMEM((BLOCK, total), F32),
            pltpu.VMEM((chips, BLOCK, narrow), BF16),
            pltpu.VMEM((chips, BLOCK, narrow), BF16),
            pltpu.VMEM((chips - 1, BLOCK, narrow), BF16),
            pltpu.VMEM((chips - 1, BLOCK, narrow), BF16),
            pltpu.VMEM((BLOCK, narrow), F32),
            pltpu.VMEM((BLOCK, narrow), F32),
            pltpu.VMEM(pack.shape, F32),
            pltpu.VMEM(pack.shape, F32),
            pltpu.VMEM((chips,) + pack.shape, F32),
            pltpu.VMEM((8, narrow), F32),
            pltpu.VMEM((8, narrow), F32),
            pltpu.VMEM((8, narrow), F32),
            pltpu.VMEM((chips, 8, narrow), F32),
            pltpu.VMEM((micro * length, narrow), F32),
            pltpu.VMEM((GROUP, narrow), BF16),
            pltpu.VMEM((tp_size, GROUP, narrow), BF16),
            pltpu.VMEM((micro * length, narrow), BF16),
            pltpu.VMEM((GROUP, narrow), BF16),
            pltpu.VMEM((micro * length, narrow), BF16),
            pltpu.VMEM((GROUP + HALO, narrow), F32),
            pltpu.VMEM((GROUP + HALO, narrow), F32),
            dma(2, 4), dma(chips), dma(chips), dma(2), dma(2),
            dma(chips), dma(chips), dma(chips - 1), dma(chips - 1),
            dma(2, 2), dma(2, chips), dma(2, chips), dma(micro), dma(micro),
            dma(tp_size - 1), dma(tp_size - 1), dma(tp_size - 1), dma(tp_size - 1),
        ],
        compiler_params=pltpu.CompilerParams(
            collective_id=6, has_side_effects=True, vmem_limit_bytes=62 << 20
        ),
        cost_estimate=pl.CostEstimate(
            flops=4 * length * BLOCK * count * total, bytes_accessed=250 << 20, transcendentals=0
        ),
        name="weight_gradients",
    )(*inputs, *cotans, *order, *parts, *raws, cols, staps, sbias, pack)


def rows_kernel(
    sum0, sum1, low_ref, state_w, rows_ref, cot_ref, gain_ref, made0, made1, scale_ref,
    hidden_out, block_out, gain_out,
):
    step = pl.program_id(0)
    half = pl.num_programs(0) // 2
    gain = gain_ref[...]

    def work(summed, made):
        grad = summed[...].astype(F32) + mm_nt(low_ref[0], state_w[...])
        rows = rows_ref[0].astype(F32)
        inv_root = lax.rsqrt(jnp.mean(rows * rows, axis=1, keepdims=True) + EPSILON)
        part = jnp.sum(grad * (rows * inv_root), axis=0, keepdims=True)
        normed = grad * gain
        inner = jnp.mean(normed * rows, axis=1, keepdims=True)
        back = inv_root * normed - rows * (inv_root * inv_root * inv_root * inner)
        hidden_out[0] = (cot_ref[0].astype(F32) + back).astype(BF16)
        block_out[0] = (rows + made[...] * scale_ref[0][:, 0:1]).astype(BF16)
        width = gain_out.shape[1]
        for at in range(gain_out.shape[0]):
            piece = part[:, at * width : (at + 1) * width]

            @pl.when(step == 0)
            def _():
                gain_out[at : at + 1, :] = piece

            @pl.when(step > 0)
            def _():
                gain_out[at : at + 1, :] += piece

    @pl.when(step < half)
    def _():
        work(sum0, made0)

    @pl.when(step >= half)
    def _():
        work(sum1, made1)


def rows_call(sums, lows, state_w, rows, cotan, gain, made, scales):
    micro, length, model = rows.shape
    tiles = 2
    tile = length // tiles
    both = lambda width: pl.BlockSpec((1, tile, width), lambda i: (i // tiles, i % tiles, 0))
    former = pl.BlockSpec((tile, model), lambda i: (jnp.minimum(i, tiles - 1), 0))
    latter = pl.BlockSpec((tile, model), lambda i: (jnp.maximum(i - tiles, 0), 0))
    full = lambda dims: pl.BlockSpec(dims, lambda i: (0, 0))
    return pl.pallas_call(
        rows_kernel,
        grid=(micro * tiles,),
        in_specs=[
            former, latter, both(2 * STATE), full(state_w.shape), both(model), both(model),
            full(gain.shape), former, latter, both(128),
        ],
        out_specs=[both(model), both(model), full((8, model // 8))],
        out_shape=[shape(rows.shape, BF16), shape(rows.shape, BF16), shape((8, model // 8))],
        compiler_params=pltpu.CompilerParams(vmem_limit_bytes=50 << 20),
        cost_estimate=pl.CostEstimate(flops=1 << 30, bytes_accessed=18 << 20, transcendentals=0),
        name="finish_rows",
    )(*sums, lows, state_w, rows, cotan, gain, *made, scales)


def gain_kernel(
    tp_size, count, part, gain_out, line_slots, line_sum, slots, send_sem, recv_sem, far_send, far_recv,
):
    me, column = lax.axis_index("tp"), lax.axis_index("fsdp")
    greet(
        [(column, lax.rem(me + hop, tp_size)) for hop in range(1, tp_size)]
        + [(lax.rem(column + hop, count), me) for hop in range(1, count)]
    )
    line_slots[me] = part[...]
    copies = [
        remote_copy(
            part, line_slots.at[me], send_sem.at[hop - 1], recv_sem.at[hop - 1],
            (column, lax.rem(me + hop, tp_size)),
        )
        for hop in range(1, tp_size)
    ]
    for copy in copies:
        copy.start()
    for copy in copies:
        copy.wait()
    total = line_slots[0]
    for at in range(1, tp_size):
        total = total + line_slots[at]
    line_sum[...] = total
    slots[column] = total
    copies = [
        remote_copy(
            line_sum, slots.at[column], far_send.at[hop - 1], far_recv.at[hop - 1],
            (lax.rem(column + hop, count), me),
        )
        for hop in range(1, count)
    ]
    for copy in copies:
        copy.start()
    for copy in copies:
        copy.wait()
    total = slots[0]
    for at in range(1, count):
        total = total + slots[at]
    gain_out[...] = total


def gain_call(tp_size, count, part):
    vmem = pl.BlockSpec(memory_space=pltpu.VMEM)
    return pl.pallas_call(
        partial(gain_kernel, tp_size, count),
        in_specs=[vmem],
        out_specs=vmem,
        out_shape=shape(part.shape),
        scratch_shapes=[
            pltpu.VMEM((tp_size,) + part.shape, F32), pltpu.VMEM(part.shape, F32),
            pltpu.VMEM((count,) + part.shape, F32),
            pltpu.SemaphoreType.DMA((tp_size - 1,)), pltpu.SemaphoreType.DMA((tp_size - 1,)),
            pltpu.SemaphoreType.DMA((count - 1,)), pltpu.SemaphoreType.DMA((count - 1,)),
        ],
        compiler_params=pltpu.CompilerParams(
            collective_id=7, has_side_effects=True, vmem_limit_bytes=32 << 20
        ),
        cost_estimate=pl.CostEstimate(flops=0, bytes_accessed=1 << 20, transcendentals=0),
        name="gain_sum",
    )(part)


def unpack_kernel(heads, pack_ref, ssum_ref, rate_ref, gain, skip, conv, bias, sconv, sbias, step, decay):
    gain[...] = pack_ref[0:1, :]
    lanes = pack_ref.shape[1]
    place = (iota((lanes, 128), 0) // HEAD_DIM == iota((lanes, 128), 1)).astype(F32)
    sums = mm(pack_ref[0:8, :], place, PRECISE)
    skip[...] = sums[1:2, :heads]
    conv[...] = pack_ref[2 : 2 + CONV, :]
    bias[...] = pack_ref[2 + CONV : 3 + CONV, :]
    sconv[...] = ssum_ref[0:CONV, :]
    sbias[...] = ssum_ref[CONV : CONV + 1, :]
    step[...] = pack_ref[8:9, :heads]
    decay[...] = pack_ref[9:10, :heads] * rate_ref[:, :heads]


def unpack_call(pack, ssum, rate, heads):
    inner = pack.shape[1]
    vmem = pl.BlockSpec(memory_space=pltpu.VMEM)
    dims = [(1, inner), (1, heads), (CONV, inner), (1, inner), (CONV, 2 * STATE), (1, 2 * STATE),
            (1, heads), (1, heads)]
    return pl.pallas_call(
        partial(unpack_kernel, heads), in_specs=[vmem] * 3, out_specs=[vmem] * 8,
        out_shape=[shape(each) for each in dims], name="small_gradients",
        cost_estimate=pl.CostEstimate(flops=0, bytes_accessed=1 << 18, transcendentals=0),
    )(pack, ssum, rate)


def shift_down(values, offset):
    return jnp.pad(values, ((offset, 0), (0, 0)))[: values.shape[0]]


def shift_up(values, offset):
    return jnp.pad(values, ((0, offset), (0, 0)))[offset:]


def document_columns(seg_row):
    length = seg_row.shape[0]
    previous = jnp.concatenate([jnp.full((1,), -1, seg_row.dtype), seg_row[GROUP - 1 : -1 : GROUP]])
    last = seg_row[GROUP - 1 :: GROUP]
    columns = []
    for offset in range(1, CONV):
        columns.append(jnp.pad(seg_row, (offset, 0), constant_values=-1)[:length] == seg_row)
    for offset in range(1, CONV):
        columns.append(jnp.pad(seg_row, (0, offset), constant_values=-1)[offset:] == seg_row)
    columns.append(seg_row == jnp.repeat(previous, GROUP))
    columns.append(seg_row == jnp.repeat(last, GROUP))
    columns.append(jnp.repeat(last == previous, GROUP))
    columns.append(seg_row)
    columns = [column.astype(F32) for column in columns]
    return jnp.stack(columns + [columns[0]] * (16 - len(columns)), axis=1)


def state_gradient(grad_bc, state_raw, taps, bias, cols):
    moved = [state_raw]
    for offset in range(1, CONV):
        moved.append(shift_down(state_raw, offset) * cols[:, offset - 1 : offset])
    conv = bias
    for offset in range(CONV):
        conv = conv + taps[offset][None, :] * moved[offset]
    sig = jax.nn.sigmoid(conv)
    grad_conv = grad_bc * (sig * (1.0 + conv * (1.0 - sig)))
    grad_raw = taps[0][None, :] * grad_conv
    for offset in range(1, CONV):
        grad_raw = grad_raw + taps[offset][None, :] * (
            shift_up(grad_conv, offset) * cols[:, 2 + offset : 3 + offset]
        )
    grad_taps = jnp.stack([jnp.sum(grad_conv * each, axis=0) for each in moved])
    return grad_raw.astype(BF16), grad_taps, jnp.sum(grad_conv, axis=0)


def local(
    hidden_in, segment_ids, cotangent, norm_gain, proj_gate, proj_value, proj_state, proj_step,
    conv_value, conv_value_bias, conv_state, conv_state_bias, step_bias, decay_log, skip_gain,
    gate_gain, proj_out,
):
    micro = hidden_in.shape[0]
    heads = step_bias.shape[0]
    rows_here = hidden_in.shape[2]
    tp_size = lax.axis_size("tp")
    me = lax.axis_index("tp")
    decay_rate = -jnp.exp(decay_log)
    pad_heads = lambda values: jnp.pad(values, (0, 128 - heads))[None, :]
    rate = pad_heads(decay_rate)
    step_bias_line = pad_heads(step_bias)
    skip = jnp.repeat(skip_gain, HEAD_DIM)[None, :]
    gain = gate_gain[None, :]
    taps, bias = conv_value, conv_value_bias[None, :]
    staps, sbias = conv_state, conv_state_bias[None, :]

    input_rows = []
    for at in range(micro):
        rows_float = hidden_in[at, 0].astype(F32)
        inv_root = lax.rsqrt(jnp.mean(rows_float * rows_float, axis=-1, keepdims=True) + EPSILON)
        input_rows.append((rows_float * inv_root * norm_gain).astype(BF16))

    def gather_tp(values, *after):
        values = lax.optimization_barrier((values,) + after)[0]
        return lax.all_gather(values, "tp", axis=0, tiled=True)

    def scatter_tp(values, *after):
        values = lax.optimization_barrier((values,) + after)[0]
        return lax.psum_scatter(values, "tp", scatter_dimension=0, tiled=True)

    inputs = [gather_tp(input_rows[0])]
    fsdp_size = lax.axis_size("fsdp")
    model = hidden_in.shape[3]
    aligned = proj_out.shape[1] % 128 == 0
    axes = (0, 0, 0, 0, 1 if aligned else 2)
    step_block = jnp.pad(proj_step, ((0, 0), (0, 128 - heads)))
    gate_w, value_w, state_w, step_w, out_w = gather_call(
        fsdp_size, (proj_gate, proj_value, proj_state, step_block, proj_out), axes
    )
    if not aligned:
        out_w = jnp.transpose(out_w, (1, 0, 2)).reshape(-1, model)
    inputs.append(gather_tp(input_rows[1], inputs[0], step_w))
    forward_weights = (gate_w, value_w, state_w, step_w, out_w)
    vectors = (taps, bias, staps, sbias, step_bias_line, rate, skip)
    columns = [document_columns(segment_ids[at, 0]) for at in range(micro)]
    seg_lines = [segment_ids[at, 0].astype(F32)[None, :] for at in range(micro)]
    quick = [0, 3, 7, 11, 14, 15, 15, 15, 15, 15]
    paces = {4: [0, 3, 4, 6, 9, 12, 15, 17, 19, 19], 5: [4, 6, 9, 12, 14, 17, 19, 19]}

    def forward(at, hosted):
        return forward_call(
            inputs[at], forward_weights, vectors, gain, columns[at], seg_lines[at], hosted, quick
        )

    def backward(at, hosted, collective):
        done = backward_call(
            saved[at], cotans[at], (gate_w, value_w, step_w, out_w), (taps, bias, rate, skip),
            gain, columns[at], seg_lines[at], hosted, paces[collective], collective,
        )
        scales.append(done[8])
        return done

    scales, produced, summed = [], [], []
    saved = [forward(0, Hosted(tp_size))]
    *kept, made_sum, cotan = forward(1, Hosted(tp_size, saved[0][8], cotangent[0, 0]))
    saved.append(kept)
    produced.append(made_sum)
    cotans = [cotan]
    *former, made_sum, cotan = backward(0, Hosted(tp_size, saved[1][8], cotangent[1, 0]), 4)
    produced.append(made_sum)
    cotans.append(cotan)
    early = lax.psum(former[4], "tp")
    *latter, gin_sum = backward(1, Hosted(tp_size, former[5]), 5)
    summed = [gin_sum, scatter_tp(latter[5])]
    lows = [[each[1], each[2], each[3], each[0]] for each in (former, latter)]
    parts, raws = (early, latter[4]), [each[4] for each in saved]
    inner_here = proj_gate.shape[1]
    pack = jnp.concatenate(
        [former[6] + latter[6], jnp.pad(former[7] + latter[7], ((0, 0), (0, inner_here - 128)))], axis=0
    )
    if aligned and fsdp_size == 8 and model // fsdp_size == BLOCK:
        grad_gate, grad_value, grad_step, grad_out, grad_state, pack, state_sum, mine = tail_call(
            fsdp_size, tp_size, inputs, cotans, lows, parts, raws, jnp.concatenate(columns, axis=0),
            staps, sbias, pack,
        )
    else:
        mine, state_sum = [], 0.0
        for at in range(micro):
            grad_bc = (parts[at] if at == 0 else lax.psum(parts[at], "tp")).astype(F32)
            low_state, grad_staps, grad_sbias = state_gradient(
                grad_bc, raws[at], staps, sbias, columns[at]
            )
            mine.append(lax.dynamic_slice_in_dim(low_state, me * rows_here, rows_here, axis=0))
            lows[at].insert(2, low_state)
            state_sum = state_sum + jnp.concatenate(
                [grad_staps, grad_sbias[None, :], jnp.zeros((3, 2 * STATE), F32)], axis=0
            )
        mine = jnp.stack(mine)
        grad_out = outer_call([low[4] for low in lows], cotans)
        grad_gate, grad_value, grad_state, grad_step = weight_call(inputs, [low[:4] for low in lows])
        if not aligned:
            grad_out = jnp.transpose(grad_out.reshape(-1, fsdp_size, proj_out.shape[1]), (1, 0, 2))
        grad_gate, grad_value, grad_state, grad_step, grad_out = scatter_call(
            fsdp_size, (grad_gate, grad_value, grad_state, grad_step, grad_out), axes
        )
        pack, state_sum = lax.psum((pack, state_sum), "fsdp")
    grad_step = grad_step[:, :heads]
    my_scales = jnp.stack(
        [lax.dynamic_slice_in_dim(each, me * rows_here, rows_here, axis=0) for each in scales]
    )
    grad_hidden, block_rows, gain_part = rows_call(
        summed, mine, state_w, hidden_in[:, 0], cotangent[:, 0], norm_gain[None, :],
        produced, my_scales,
    )
    gain_total = gain_call(tp_size, fsdp_size, gain_part)
    grad_gain, grad_skip, grad_conv, grad_bias, grad_sconv, grad_sbias, grad_in, grad_decay = (
        unpack_call(pack, state_sum, rate, heads)
    )
    return (
        block_rows[:, None],
        grad_hidden[:, None],
        gain_total.reshape(-1),
        grad_gate,
        grad_value,
        grad_state,
        grad_step,
        grad_conv,
        grad_bias.reshape(-1),
        grad_sconv,
        grad_sbias.reshape(-1),
        grad_in.reshape(-1),
        grad_decay.reshape(-1),
        grad_skip.reshape(-1),
        grad_gain.reshape(-1),
        grad_out,
    )


def solution(mesh):
    in_specs = (
        P(None, "fsdp", "tp", None), P(None, "fsdp", None), P(None, "fsdp", "tp", None), P(),
        P("fsdp", "tp"), P("fsdp", "tp"), P("fsdp", None), P("fsdp", "tp"), P(None, "tp"), P("tp"),
        P(), P(), P("tp"), P("tp"), P("tp"), P("tp"), P("tp", "fsdp"),
    )
    out_specs = (
        P(None, "fsdp", "tp", None), P(None, "fsdp", "tp", None), P(), P("fsdp", "tp"),
        P("fsdp", "tp"), P("fsdp", None), P("fsdp", "tp"), P(None, "tp"), P("tp"), P(), P(),
        P("tp"), P("tp"), P("tp"), P("tp"), P("tp", "fsdp"),
    )
    return jax.shard_map(local, mesh=mesh, in_specs=in_specs, out_specs=out_specs, check_vma=False)
```

```python
from functools import partial

import jax
import jax.numpy as jnp
from jax import lax
from jax.experimental import pallas as pl
from jax.experimental.pallas import tpu as pltpu
from jax.sharding import PartitionSpec as P

HEAD_DIM = 64
STATE = 128
CONV = 4
GROUP = 256
HALF = GROUP // 2
BLOCK = 256
PER_BLOCK = BLOCK // HEAD_DIM
HALO = 8
INNER = 4096
EPSILON = 1e-05
PRECISE = lax.Precision.HIGHEST
PARTS = 2
FORWARD_INS, FORWARD_OUTS = 16, 9
BACKWARD_INS, BACKWARD_OUTS = 23, 9
F32 = jnp.float32
BF16 = jnp.bfloat16


def mm(former, latter, precision=None):
    return jnp.dot(former, latter, preferred_element_type=F32, precision=precision)


def head_sums(values, place):
    high = values.astype(BF16)
    rest = values - high.astype(F32)
    middle = rest.astype(BF16)
    low = (rest - middle.astype(F32)).astype(BF16)
    return mm(high, place) + (mm(middle, place) + mm(low, place))


def mm_nt(former, latter):
    return lax.dot_general(
        former, latter, (((1,), (1,)), ((), ())), preferred_element_type=F32
    )


def mm_tn(former, latter):
    return lax.dot_general(
        former, latter, (((0,), (0,)), ((), ())), preferred_element_type=F32
    )


def iota(shape, axis):
    return lax.broadcasted_iota(jnp.int32, shape, axis)


def expand(columns):
    rows = columns.shape[0]
    lane = iota((rows, 128), 1)
    parts = []
    for pair in range(PER_BLOCK // 2):
        former = jnp.broadcast_to(columns[:, 2 * pair : 2 * pair + 1], (rows, 128))
        latter = jnp.broadcast_to(columns[:, 2 * pair + 1 : 2 * pair + 2], (rows, 128))
        parts.append(jnp.where(lane < HEAD_DIM, former, latter))
    return jnp.concatenate(parts, axis=1)


def lane_mask(head):
    lane = iota((1, BLOCK), 1)
    return ((lane // HEAD_DIM) == head).astype(F32).astype(BF16)


def spread(ref, values, blocks):
    for block in range(blocks):
        shift = (128 - PER_BLOCK * block) % 128
        ref[block] = pltpu.roll(values, shift, 1) if shift else values


def token_quantities(step_in, cums, cols, decay_rate):
    step = jnp.maximum(step_in, 0.0) + jnp.log1p(jnp.exp(-jnp.abs(step_in)))
    final = cums[GROUP - 1 : GROUP, :]
    entering = jnp.exp(cums) * cols[:, 6:7]
    fading = jnp.exp(final - cums) * cols[:, 7:8]
    retain = jnp.exp(final) * cols[0:1, 8:9]
    return step, entering, fading, retain


def shifted_values(buf, cols):
    moved = [buf[HALO : HALO + GROUP, :]]
    for offset in range(1, CONV):
        before = buf[HALO - offset : HALO - offset + GROUP, :]
        moved.append(jnp.where(cols[:, offset - 1 : offset] > 0.0, before, 0.0))
    return moved


def conv_of(moved, taps, bias):
    total = bias + taps[0:1, :] * moved[0]
    for offset in range(1, CONV):
        total = total + taps[offset : offset + 1, :] * moved[offset]
    return total


MESH = pl.DeviceIdType.MESH


def part_of(ref, at, size, axis):
    if axis == 0:
        return ref.at[pl.ds(pl.multiple_of(at * size, size), size), :]
    if axis == 1:
        return ref.at[:, pl.ds(pl.multiple_of(at * size, size), size)]
    return ref.at[at]


def greet(devices):
    barrier = pltpu.get_barrier_semaphore()
    for device in devices:
        pl.semaphore_signal(barrier, inc=1, device_id=device, device_id_type=MESH)
    pl.semaphore_wait(barrier, len(devices))


def remote_copy(source, target, sends, receives, device):
    return pltpu.make_async_remote_copy(
        src_ref=source, dst_ref=target, send_sem=sends, recv_sem=receives,
        device_id=device, device_id_type=MESH,
    )


class LineScatter:
    def __init__(self, size, source, own, slots, last, own_sem, send_sem, recv_sem, last_sem):
        self.size, self.source, self.own, self.slots, self.last = size, source, own, slots, last
        self.own_sem, self.send_sem, self.recv_sem, self.last_sem = own_sem, send_sem, recv_sem, last_sem
        self.me, self.column = lax.axis_index("tp"), lax.axis_index("fsdp")
        self.rows = last.shape[0]

    @staticmethod
    def scratch(size, rows, width):
        hops = size - 1
        return [
            pltpu.VMEM((2, hops, rows, width), BF16), pltpu.VMEM((2, hops, rows, width), BF16),
            pltpu.VMEM((rows, width), BF16), pltpu.SemaphoreType.DMA((2, hops)),
            pltpu.SemaphoreType.DMA((2, hops, PARTS)), pltpu.SemaphoreType.DMA((2, hops, PARTS)),
            pltpu.SemaphoreType.DMA((1,)),
        ]

    def place(self, flow):
        return self.me if flow == 0 else self.size - 1 - self.me

    def part(self, part):
        rows = self.rows // PARTS
        return pl.ds(part * rows, rows)

    def local(self, flow, hop):
        block = self.size - 1 - hop + self.place(flow)
        if flow:
            block = self.size - 1 - block
        at = pl.multiple_of(block * self.rows, self.rows)
        return pltpu.make_async_copy(
            self.source.at[pl.ds(at, self.rows), :], self.own.at[flow, hop], self.own_sem.at[flow, hop]
        )

    def final(self):
        at = pl.multiple_of(self.me * self.rows, self.rows)
        return pltpu.make_async_copy(
            self.source.at[pl.ds(at, self.rows), :], self.last, self.last_sem.at[0]
        )

    def sending(self, flow, hop, part):
        neighbour = self.me + 1 if flow == 0 else self.me - 1
        neighbour = jnp.clip(neighbour, 0, self.size - 1)
        return remote_copy(
            self.own.at[flow, hop, self.part(part), :], self.slots.at[flow, hop, self.part(part), :],
            self.send_sem.at[flow, hop, part], self.recv_sem.at[flow, hop, part],
            (self.column, neighbour),
        )

    def begin(self):
        self.final().start()
        for hop in range(self.size - 1):
            for flow in range(2):

                @pl.when(self.place(flow) <= hop)
                def _():
                    self.local(flow, hop).start()

    def hop(self, hop, part):
        rows = self.part(part)
        for flow in range(2):
            place = self.place(flow)

            @pl.when(place <= hop)
            def _():
                if part == 0:
                    self.local(flow, hop).wait()
                if hop > 0:

                    @pl.when(place >= 1)
                    def _():
                        self.sending(flow, hop - 1, part).wait_recv()
                        total = self.own[flow, hop, rows, :].astype(F32)
                        total = total + self.slots[flow, hop - 1, rows, :].astype(F32)
                        self.own[flow, hop, rows, :] = total.astype(BF16)

                self.sending(flow, hop, part).start()

    def end(self, out, part):
        hops = self.size - 1
        rows = self.part(part)
        if part == 0:
            self.final().wait()
        out[rows, :] = self.last[rows, :].astype(F32)
        for flow in range(2):

            @pl.when(self.place(flow) >= 1)
            def _():
                self.sending(flow, hops - 1, part).wait_recv()
                out[rows, :] += self.slots[flow, hops - 1, rows, :].astype(F32)

        for hop in range(hops):
            for flow in range(2):

                @pl.when(self.place(flow) <= hop)
                def _():
                    self.sending(flow, hop, part).wait_send()


class LineGather:
    def __init__(self, size, source, target, own_sem, send_sem, recv_sem):
        self.size, self.source, self.target = size, source, target
        self.own_sem, self.send_sem, self.recv_sem = own_sem, send_sem, recv_sem
        self.me, self.column = lax.axis_index("tp"), lax.axis_index("fsdp")
        self.rows = source.shape[0]

    @staticmethod
    def scratch(size):
        return [
            pltpu.SemaphoreType.DMA((1,)), pltpu.SemaphoreType.DMA((2, size - 1, PARTS)),
            pltpu.SemaphoreType.DMA((2, size - 1, PARTS)),
        ]

    def place(self, flow):
        return self.me if flow == 0 else self.size - 1 - self.me

    def block(self, at):
        at = pl.multiple_of(jnp.clip(at, 0, self.size - 1) * self.rows, self.rows)
        return self.target.at[pl.ds(at, self.rows), :]

    def sending(self, flow, hop, part):
        neighbour = self.me + 1 if flow == 0 else self.me - 1
        neighbour = jnp.clip(neighbour, 0, self.size - 1)
        rows = pl.ds(part * (self.rows // PARTS), self.rows // PARTS)
        block = self.block(self.me - hop if flow == 0 else self.me + hop).at[rows, :]
        return remote_copy(
            self.source.at[rows, :] if hop == 0 else block, block, self.send_sem.at[flow, hop, part],
            self.recv_sem.at[flow, hop, part], (self.column, neighbour),
        )

    def local(self):
        return pltpu.make_async_copy(self.source, self.block(self.me), self.own_sem.at[0])

    def hop(self, hop, part):
        if hop == 0 and part == 0:
            self.local().start()
        for flow in range(2):
            place = self.place(flow)
            if hop > 0:

                @pl.when(place >= hop)
                def _():
                    self.sending(flow, hop - 1, part).wait_recv()

            if hop < self.size - 1:

                @pl.when((place >= hop) & (place < self.size - 1))
                def _():
                    self.sending(flow, hop, part).start()

    def end(self, part):
        self.hop(self.size - 1, part)
        if part == 0:
            self.local().wait()
        for hop in range(self.size - 1):
            for flow in range(2):
                place = self.place(flow)

                @pl.when((place >= hop) & (place < self.size - 1))
                def _():
                    self.sending(flow, hop, part).wait_send()


def run_line(step, steps, scatter, gather, out, early):
    size = (scatter or gather).size
    first = 1 if scatter and gather else 0
    actions = [[] for _ in range(PARTS * (size + first))]
    for part in range(PARTS):
        if gather:
            for hop in range(size - 1):
                actions[PARTS * hop + part].append(partial(gather.hop, hop, part))
            actions[PARTS * (size - 1) + part].append(partial(gather.end, part))
        if scatter:
            for hop in range(size - 1):
                actions[PARTS * (first + hop) + part].append(partial(scatter.hop, hop, part))
            actions[PARTS * (first + size - 1) + part].append(partial(scatter.end, out, part))
    if scatter:
        actions[0].insert(0, scatter.begin)
    for at in sorted(set(steps)):
        if (at == 0) != early:
            continue
        todo = [action for when, each in zip(steps, actions) if when == at for action in each]

        @pl.when(step == at)
        def _():
            for action in todo:
                action()


class Hosted:
    def __init__(self, size, scatter=None, gather=None):
        self.size, self.scatter, self.gather = size, scatter, gather

    def operands(self):
        return [each for each in (self.scatter, self.gather) if each is not None]

    def in_specs(self):
        return [pl.BlockSpec(memory_space=pl.ANY)] * len(self.operands())

    def outs(self):
        shapes, specs = [], []
        if self.scatter is not None:
            rows, width = self.scatter.shape[0] // self.size, self.scatter.shape[1]
            shapes.append(shape((rows, width)))
            specs.append(pl.BlockSpec((rows, width), lambda g, j: (0, 0)))
        if self.gather is not None:
            rows, width = self.gather.shape
            shapes.append(shape((rows * self.size, width), BF16))
            specs.append(pl.BlockSpec(memory_space=pl.ANY))
        return specs, shapes

    def scratch(self):
        needed = []
        if self.scatter is not None:
            rows, width = self.scatter.shape[0] // self.size, self.scatter.shape[1]
            needed += LineScatter.scratch(self.size, rows, width)
        if self.gather is not None:
            needed += LineGather.scratch(self.size)
        return needed

    def wrap(self, body, ins, outs, pace, resident):
        has_scatter, has_gather = self.scatter is not None, self.gather is not None
        hosts = has_scatter + has_gather
        size, spare, kept = self.size, len(self.scratch()), len(resident) + 1

        def kernel(*refs):
            refs, stored = refs[: len(refs) - kept], refs[len(refs) - kept :]
            tail = refs[len(refs) - spare :]
            sources, targets = refs[ins : ins + hosts], refs[ins + hosts + outs : ins + outs + 2 * hosts]
            step = pl.program_id(0) * pl.num_programs(1) + pl.program_id(1)
            me, column = lax.axis_index("tp"), lax.axis_index("fsdp")
            operands = list(refs[:ins])
            loads = []
            for at, (which, _, need) in enumerate(resident):
                copy = pltpu.make_async_copy(operands[which], stored[at], stored[-1].at[at])
                operands[which] = stored[at]
                loads.append((copy, need))

            @pl.when(step == 0)
            def _():
                for copy, _ in loads:
                    copy.start()
                if hosts:
                    greet([(column, lax.rem(me + hop, size)) for hop in range(1, size)])

            if hosts:
                scatter = LineScatter(size, sources[0], *tail[:7]) if has_scatter else None
                gather = LineGather(size, sources[-1], targets[-1], *tail[-3:]) if has_gather else None
                run_line(step, pace, scatter, gather, targets[0], True)
            for when in sorted(set(need for _, need in loads)):

                @pl.when(step == when)
                def _():
                    for copy, need in loads:
                        if need == when:
                            copy.wait()

            body(
                *operands, *refs[ins + hosts : ins + hosts + outs],
                *refs[ins + outs + 2 * hosts : len(refs) - spare],
            )
            if hosts:
                run_line(step, pace, scatter, gather, targets[0], False)

        return kernel


def resident_scratch(resident):
    return [pltpu.VMEM(array.shape, array.dtype) for _, array, _ in resident] + [
        pltpu.SemaphoreType.DMA((len(resident),))
    ]


def forward_kernel(
    in_ref, gate_w, value_w, state_w, step_w, taps_ref, bias_ref, staps_ref, sbias_ref,
    step_bias_ref, rate_ref, skip_ref, cols_ref, seg_ref, out_w, gain_ref,
    gate_out, value_out, mixed_out, bc_out, sraw_out, stepin_out, cums_out, held_out, made_out,
    vbuf, sbuf, gram_s, b_t, c_s, step_s, ent_s, fade_s, cums_s, cums_t, keep_s, hidden, made,
):
    g, j = pl.program_id(0), pl.program_id(1)
    blocks = pl.num_programs(1)
    nblocks = hidden.shape[0]
    rows = in_ref[...]
    cols = cols_ref[...]

    @pl.when(j == 0)
    def _():
        sbuf[0:HALO, :] = sbuf[GROUP : GROUP + HALO, :]
        raw = mm(rows, state_w[...])
        sbuf[HALO : HALO + GROUP, :] = raw
        sraw_out[...] = raw
        conv = conv_of(shifted_values(sbuf, cols), staps_ref[...], sbias_ref[...])
        bc = (conv * jax.nn.sigmoid(conv)).astype(BF16)
        bc_out[...] = bc
        b_low, c_low = bc[:, :STATE], bc[:, STATE:]
        b_t[...] = jnp.transpose(b_low.astype(F32)).astype(BF16)
        c_s[...] = c_low
        step_in = mm(rows, step_w[...]) + step_bias_ref[...]
        stepin_out[...] = step_in
        step = jnp.maximum(step_in, 0.0) + jnp.log1p(jnp.exp(-jnp.abs(step_in)))
        at_row, at_col = iota((GROUP, GROUP), 0), iota((GROUP, GROUP), 1)
        lower = (at_row >= at_col).astype(F32)
        cums = mm(lower, step * rate_ref[...], PRECISE)
        cums_out[...] = cums
        step, entering, fading, retain = token_quantities(step_in, cums, cols, rate_ref[...])
        spread(step_s, step, nblocks)
        spread(ent_s, entering, nblocks)
        spread(fade_s, fading, nblocks)
        spread(cums_s, cums, nblocks)
        spread(keep_s, jnp.broadcast_to(retain, (8, 128)), nblocks)
        cums_t[...] = jnp.transpose(cums)
        within = (at_row >= at_col) & (cols[:, 9:10] == seg_ref[...])
        gram_s[...] = jnp.where(within, mm_nt(c_low, b_low), 0.0)

    at = pl.multiple_of(j * BLOCK, BLOCK)
    gate = mm(rows, gate_w[:, pl.ds(at, BLOCK)])
    gate_out[...] = gate.astype(BF16)
    value = mm(rows, value_w[:, pl.ds(at, BLOCK)])
    value_out[...] = value
    mine = vbuf.at[j]
    mine[0:HALO, :] = mine[GROUP : GROUP + HALO, :]
    mine[HALO : HALO + GROUP, :] = value
    conv = conv_of(shifted_values(mine, cols), taps_ref[...], bias_ref[...])
    x_low = (conv * jax.nn.sigmoid(conv)).astype(BF16)
    x_float = x_low.astype(F32)
    scaled_float = expand(step_s[j]) * x_float
    scaled = scaled_float.astype(BF16)

    @pl.when(g == 0)
    def _():
        hidden[j] = jnp.zeros((STATE, BLOCK), F32)

    state = hidden[j]
    state_low = state.astype(BF16)
    held_out[0] = state_low
    total = expand(ent_s[j]) * mm(c_s[...], state_low)
    weighted = (expand(fade_s[j]) * scaled.astype(F32)).astype(BF16)
    hidden[j] = expand(keep_s[j])[0:1, :] * state + mm(b_t[...], weighted)
    cums_here = cums_s[j]
    top = jnp.zeros((HALF, BLOCK), F32)
    bottom = jnp.zeros((HALF, BLOCK), F32)
    for i in range(PER_BLOCK):
        to = cums_here[:, i : i + 1]
        frm = cums_t[pl.ds(j * PER_BLOCK + i, 1), :]
        only = scaled * lane_mask(i)
        decay = jnp.exp(jnp.minimum(to[:HALF] - frm[:, :HALF], 0.0))
        top = top + mm((gram_s[:HALF, :HALF] * decay).astype(BF16), only[:HALF])
        decay = jnp.exp(jnp.minimum(to[HALF:] - frm, 0.0))
        bottom = bottom + mm((gram_s[HALF:, :] * decay).astype(BF16), only)
    mixed = total + jnp.concatenate([top, bottom], axis=0) + skip_ref[...] * x_float
    mixed_out[...] = mixed
    scaled_gate = (mixed * (gate * jax.nn.sigmoid(gate)) * gain_ref[...]).astype(BF16)

    @pl.when(j == 0)
    def _():
        made[...] = mm(scaled_gate, out_w[pl.ds(at, BLOCK), :])

    @pl.when(j > 0)
    def _():
        made[...] += mm(scaled_gate, out_w[pl.ds(at, BLOCK), :])

    @pl.when(j == blocks - 1)
    def _():
        made_out[...] = made[...].astype(BF16)


def backward_kernel(
    tp_size, cot_ref, out_w, gate_rows, mixed_rows, gain_row,
    gate_ref, value_ref, before_ref, mixed_ref, bc_ref, stepin_ref, cums_ref, held_ref,
    gate_w, value_w, step_w, taps_ref, bias_ref, rate_ref, skip_ref, gain_ref, cols_ref, seg_ref,
    branch_out, lowgate_out, lowvalue_out, lowstep_out, gbc_out, gin_out, small_out, sums_out, stats_out,
    vbuf, gcbuf, gram_s, dgram, b_s, c_t, step_s, ent_s, fade_s, cums_s, cums_t, keep_s, grad_state,
    gin, gb_s, gc_s, u_s, v_s, fin_s, small_s, sums_s,
    branch_s, rowsum_s, slots_s, turn_s, swap_send, swap_recv,
):
    g, j = pl.program_id(0) - 1, pl.program_id(1)
    groups, blocks = pl.num_programs(0) - 1, pl.num_programs(1)

    @pl.when(g < 0)
    def _():
        row_sums(
            tp_size, cot_ref, out_w, gate_rows, mixed_rows, gain_row,
            branch_s, rowsum_s, slots_s, swap_send, swap_recv,
        )

    scales = partial(
        row_scales, tp_size, gain_row.shape[1] * tp_size, rowsum_s, slots_s, turn_s, swap_send,
        swap_recv, stats_out,
    )

    @pl.when(g >= 0)
    def _():
        backward_step(
            g, j, groups, blocks, gate_ref, value_ref, before_ref, mixed_ref,
            bc_ref, stepin_ref, cums_ref, held_ref,
            gate_w, value_w, step_w, taps_ref, bias_ref, rate_ref, skip_ref, gain_ref, cols_ref, seg_ref,
            branch_out, lowgate_out, lowvalue_out, lowstep_out, gbc_out, gin_out, small_out, sums_out,
            vbuf, gcbuf, gram_s, dgram, b_s, c_t, step_s, ent_s, fade_s, cums_s, cums_t, keep_s,
            grad_state, gin, gb_s, gc_s, u_s, v_s, fin_s, small_s, sums_s, branch_s, stats_out, scales,
        )


def row_sums(
    tp_size, cot_ref, out_w, gate_rows, mixed_rows, gain_row,
    branch_s, rowsum_s, slots_s, swap_send, swap_recv,
):
    step, groups = pl.program_id(1), pl.num_programs(1)
    me, column = lax.axis_index("tp"), lax.axis_index("fsdp")
    grad = mm_nt(cot_ref[...], out_w[...])
    branch_s[step] = grad.astype(BF16)
    gate = gate_rows[...].astype(F32)
    gated = mixed_rows[...] * (gate * jax.nn.sigmoid(gate))
    squares = jnp.sum(gated * gated, axis=1, keepdims=True)
    inner = jnp.sum(grad * gain_row[...] * gated, axis=1, keepdims=True)
    lane = iota((GROUP, 128), 1)
    both = jnp.where(lane == 0, squares, jnp.where(lane == 1, inner, 0.0))
    rowsum_s[step] = jnp.transpose(both)[:8]

    @pl.when(step == groups - 1)
    def _():
        slots_s[me] = rowsum_s[...]
        for copy in row_swaps(tp_size, rowsum_s, slots_s, swap_send, swap_recv):
            copy.start()


def row_swaps(tp_size, rowsum_s, slots_s, swap_send, swap_recv):
    me, column = lax.axis_index("tp"), lax.axis_index("fsdp")
    return [
        remote_copy(
            rowsum_s, slots_s.at[me], swap_send.at[hop - 1], swap_recv.at[hop - 1],
            (column, lax.rem(me + hop, tp_size)),
        )
        for hop in range(1, tp_size)
    ]


def row_scales(tp_size, total_inner, rowsum_s, slots_s, turn_s, swap_send, swap_recv, stats_out):
    for copy in row_swaps(tp_size, rowsum_s, slots_s, swap_send, swap_recv):
        copy.wait()
    total = slots_s[0]
    for at in range(1, tp_size):
        total = total + slots_s[at]
    turn_s[...] = jnp.zeros(turn_s.shape, F32)
    scale = lax.rsqrt(total[:, 0:1, :] / total_inner + EPSILON)
    turn_s[:, 0:1, :] = scale
    turn_s[:, 1:2, :] = scale * scale * scale * (total[:, 1:2, :] / total_inner)
    for group in range(turn_s.shape[0]):
        stats_out[group * GROUP : (group + 1) * GROUP, :] = jnp.transpose(turn_s[group])


def backward_step(
    g, j, groups, blocks, gate_ref, value_ref, before_ref, mixed_ref,
    bc_ref, stepin_ref, cums_ref, held_ref,
    gate_w, value_w, step_w, taps_ref, bias_ref, rate_ref, skip_ref, gain_ref, cols_ref, seg_ref,
    branch_out, lowgate_out, lowvalue_out, lowstep_out, gbc_out, gin_out, small_out, sums_out,
    vbuf, gcbuf, gram_s, dgram, b_s, c_t, step_s, ent_s, fade_s, cums_s, cums_t, keep_s,
    grad_state, gin, gb_s, gc_s, u_s, v_s, fin_s, small_s, sums_s, branch_s, stats_ref, scales,
):
    group = groups - 1 - g
    nblocks = grad_state.shape[0]
    cols = cols_ref[...]
    at_row, at_col = iota((GROUP, GROUP), 0), iota((GROUP, GROUP), 1)

    @pl.when((g == 0) & (j == 0))
    def _():
        grad_state[...] = jnp.zeros(grad_state.shape, F32)
        small_s[...] = jnp.zeros(small_s.shape, F32)
        sums_s[...] = jnp.zeros(sums_s.shape, F32)
        gcbuf[...] = jnp.zeros(gcbuf.shape, F32)

    @pl.when(j == 0)
    def _():
        bc = bc_ref[...]
        b_low, c_low = bc[:, :STATE], bc[:, STATE:]
        b_s[...] = b_low
        c_t[...] = jnp.transpose(c_low.astype(F32)).astype(BF16)
        cums = cums_ref[...]
        step, entering, fading, retain = token_quantities(stepin_ref[...], cums, cols, rate_ref[...])
        spread(step_s, step, nblocks)
        spread(ent_s, entering, nblocks)
        spread(fade_s, fading, nblocks)
        spread(cums_s, cums, nblocks)
        spread(keep_s, jnp.broadcast_to(retain, (8, 128)), nblocks)
        cums_t[...] = jnp.transpose(cums)
        within = (at_row <= at_col) & (cols[:, 9:10] == seg_ref[...])
        gram_s[...] = jnp.where(within, mm_nt(b_low, c_low), 0.0)
        dgram[...] = jnp.zeros(dgram.shape, F32)
        gin[...] = jnp.zeros(gin.shape, F32)
        gb_s[...] = jnp.zeros(gb_s.shape, F32)
        gc_s[...] = jnp.zeros(gc_s.shape, F32)
        u_s[...] = jnp.zeros(u_s.shape, F32)
        v_s[...] = jnp.zeros(v_s.shape, F32)
        fin_s[...] = jnp.zeros(fin_s.shape, F32)

    @pl.when((g == 0) & (j == 0))
    def _():
        scales()

    at = pl.multiple_of(j * BLOCK, BLOCK)
    gate, mixed = gate_ref[...].astype(F32), mixed_ref[...]
    grad = branch_s[group, :, pl.ds(at, BLOCK)].astype(F32)
    gain, skip, taps = gain_ref[...], skip_ref[...], taps_ref[...]
    stats = stats_ref[pl.ds(pl.multiple_of(group * GROUP, GROUP), GROUP), :]
    scale, inner = stats[:, 0:1], stats[:, 1:2]
    sig = jax.nn.sigmoid(gate)
    act = gate * sig
    gated = mixed * act
    scaled_gated = gated * scale
    branch_out[...] = (scaled_gated * gain).astype(BF16)
    grad_gain = jnp.sum(grad * scaled_gated, axis=0, keepdims=True)
    grad_gated = scale * (grad * gain) - gated * inner
    grad_mixed = grad_gated * act
    low_gate = (grad_gated * mixed * (sig * (1.0 + gate * (1.0 - sig)))).astype(BF16)
    lowgate_out[...] = low_gate

    vbuf[0:HALO, :] = before_ref[...]
    vbuf[HALO : HALO + GROUP, :] = value_ref[...]
    moved = shifted_values(vbuf, cols)
    conv = conv_of(moved, taps, bias_ref[...])
    sig = jax.nn.sigmoid(conv)
    x_float = (conv * sig).astype(BF16).astype(F32)
    slope = sig * (1.0 + conv * (1.0 - sig))
    step_wide = expand(step_s[j])
    fade_wide = expand(fade_s[j])
    scaled = (step_wide * x_float).astype(BF16)
    scaled_float = scaled.astype(F32)
    grad_skip = jnp.sum(grad_mixed * x_float, axis=0, keepdims=True)
    grad_scan = grad_mixed.astype(BF16)
    grad_scan_float = grad_scan.astype(F32)
    scanned = mixed - skip * x_float

    own = grad_state[j]
    state_low = held_ref[0]
    own_low = own.astype(BF16)
    grad_weighted = mm(b_s[...], own_low)
    weighted = (fade_wide * scaled_float).astype(BF16)
    entered = (expand(ent_s[j]) * grad_scan_float).astype(BF16)
    gb_s[...] += mm_nt(weighted, own_low)
    gc_s[...] += mm_nt(entered, state_low)
    keep_wide = expand(keep_s[j])[0:1, :]
    kept = keep_wide * jnp.sum(state_low.astype(F32) * own, axis=0, keepdims=True)
    grad_state[j] = keep_wide * own + mm(c_t[...], entered)

    cums_here = cums_s[j]
    top = jnp.zeros((HALF, BLOCK), F32)
    bottom = jnp.zeros((HALF, BLOCK), F32)
    dtop = dgram[:HALF, :]
    dbottom = dgram[HALF:, HALF:]
    for i in range(PER_BLOCK):
        frm = cums_here[:, i : i + 1]
        to = cums_t[pl.ds(j * PER_BLOCK + i, 1), :]
        mask = lane_mask(i)
        only_grad = grad_scan * mask
        only = scaled * mask
        decay = jnp.exp(jnp.minimum(to - frm[:HALF], 0.0))
        top = top + mm((gram_s[:HALF, :] * decay).astype(BF16), only_grad)
        dtop = dtop + mm_nt(only[:HALF], grad_scan) * decay
        decay = jnp.exp(jnp.minimum(to[:, HALF:] - frm[HALF:], 0.0))
        bottom = bottom + mm((gram_s[HALF:, HALF:] * decay).astype(BF16), only_grad[HALF:])
        dbottom = dbottom + mm_nt(only[HALF:], grad_scan[HALF:]) * decay
    dgram[:HALF, :] = dtop
    dgram[HALF:, HALF:] = dbottom
    faded = fade_wide * grad_weighted
    through = jnp.concatenate([top, bottom], axis=0) + faded
    column = scaled_float * through
    final = kept + jnp.sum(scaled_float * faded, axis=0, keepdims=True)
    place = iota((BLOCK, 128), 1) == j * PER_BLOCK + iota((BLOCK, 128), 0) // HEAD_DIM
    place = place.astype(F32).astype(BF16)
    u_s[...] += head_sums(grad_scan_float * scanned - column, place)
    v_s[...] += head_sums(column, place)
    fin_s[...] += head_sums(jnp.broadcast_to(final, (8, BLOCK)), place)

    grad_conv = (step_wide * through + skip * grad_mixed) * slope
    after = gcbuf.at[j]
    after[GROUP : GROUP + HALO, :] = after[0:HALO, :]
    after[0:GROUP, :] = grad_conv
    grad_value = taps[0:1, :] * grad_conv
    for offset in range(1, CONV):
        up = jnp.where(cols[:, 2 + offset : 3 + offset] > 0.0, after[offset : offset + GROUP, :], 0.0)
        grad_value = grad_value + taps[offset : offset + 1, :] * up
    low_value = grad_value.astype(BF16)
    lowvalue_out[...] = low_value
    gin[...] += mm_nt(low_gate, gate_w[:, pl.ds(at, BLOCK)]) + mm_nt(low_value, value_w[:, pl.ds(at, BLOCK)])
    lines = [grad_gain, grad_skip]
    lines += [jnp.sum(grad_conv * moved[offset], axis=0, keepdims=True) for offset in range(CONV)]
    lines += [jnp.sum(grad_conv, axis=0, keepdims=True)]
    for at_line, line in enumerate(lines):
        small_s[j, at_line : at_line + 1, :] += line

    @pl.when(g == groups - 1)
    def _():
        small_out[:, pl.ds(at, BLOCK)] = small_s[j]

    @pl.when(j == blocks - 1)
    def _():
        bc = bc_ref[...]
        within = (at_row <= at_col) & (cols[:, 9:10] == seg_ref[...])
        dg = jnp.where(within, dgram[...], 0.0)
        grad_b = gb_s[...] + mm(dg.astype(BF16), bc[:, STATE:])
        grad_c = gc_s[...] + mm(jnp.transpose(dg).astype(BF16), bc[:, :STATE])
        gbc_out[:, :STATE] = grad_b.astype(BF16)
        gbc_out[:, STATE:] = grad_c.astype(BF16)
        last = iota((GROUP, 128), 0) == GROUP - 1
        grad_cums = u_s[...] + jnp.where(last, fin_s[0:1, :], 0.0)
        upper = (at_row <= at_col).astype(F32)
        grad_a = mm(upper, grad_cums, PRECISE)
        step_in = stepin_ref[...]
        step = jnp.maximum(step_in, 0.0) + jnp.log1p(jnp.exp(-jnp.abs(step_in)))
        sig_in = jax.nn.sigmoid(step_in)
        ratio = jnp.where(step_in < -15.0, 1.0, sig_in / step)
        grad_step = v_s[...] * ratio + grad_a * rate_ref[...] * sig_in
        low_step = grad_step.astype(BF16)
        lowstep_out[...] = low_step
        sums_s[0:1, :] += jnp.sum(grad_step, axis=0, keepdims=True)
        sums_s[1:2, :] += jnp.sum(grad_a * step, axis=0, keepdims=True)
        sums_out[...] = sums_s[...]
        gin_out[...] = (gin[...] + mm_nt(low_step, step_w[...])).astype(BF16)


def shape(dims, kind=F32):
    return jax.ShapeDtypeStruct(dims, kind)


def params(collective=None):
    extra = {} if collective is None else dict(collective_id=collective, has_side_effects=True)
    return pltpu.CompilerParams(
        dimension_semantics=("arbitrary", "arbitrary"), vmem_limit_bytes=60 << 20, **extra
    )


def whole(array):
    return pl.BlockSpec(
        array.shape, lambda g, j: (0,) * array.ndim, pipeline_mode=pl.Buffered(1)
    )


def forward_call(inputs, weights, vectors, gain, cols, seg_line, hosted, pace):
    gate_w, value_w, state_w, step_w, out_w = weights
    taps, bias, staps, sbias, step_bias, rate, skip = vectors
    length, model = inputs.shape
    inner = gate_w.shape[1]
    groups, blocks = length // GROUP, inner // BLOCK
    wide = pl.BlockSpec((GROUP, BLOCK), lambda g, j: (g, j))
    line = lambda rows: pl.BlockSpec((rows, BLOCK), lambda g, j: (0, j))
    rows_of = lambda width: pl.BlockSpec((GROUP, width), lambda g, j: (g, 0))
    specs, shapes = hosted.outs()
    hbm = pl.BlockSpec(memory_space=pl.ANY)
    resident = [(1, gate_w, 0), (2, value_w, 0), (3, state_w, 0), (4, step_w, 0), (14, out_w, 0)]
    return pl.pallas_call(
        hosted.wrap(forward_kernel, FORWARD_INS, FORWARD_OUTS, pace, resident),
        grid=(groups, blocks),
        in_specs=[
            rows_of(model), hbm, hbm, hbm, hbm,
            line(CONV), line(1), whole(staps), whole(sbias), whole(step_bias), whole(rate), line(1),
            rows_of(cols.shape[1]), pl.BlockSpec((1, GROUP), lambda g, j: (0, g)),
            hbm, line(1),
        ] + hosted.in_specs(),
        out_specs=[
            wide, wide, wide, rows_of(2 * STATE), rows_of(2 * STATE), rows_of(128), rows_of(128),
            pl.BlockSpec((1, STATE, BLOCK), lambda g, j: (g, 0, j)), rows_of(model),
        ] + specs,
        out_shape=[
            shape((length, inner), BF16), shape((length, inner)), shape((length, inner)),
            shape((length, 2 * STATE), BF16), shape((length, 2 * STATE)), shape((length, 128)),
            shape((length, 128)), shape((groups, STATE, inner), BF16), shape((length, model), BF16),
        ] + shapes,
        scratch_shapes=[
            pltpu.VMEM((blocks, GROUP + HALO, BLOCK), F32),
            pltpu.VMEM((GROUP + HALO, 2 * STATE), F32),
            pltpu.VMEM((GROUP, GROUP), F32),
            pltpu.VMEM((STATE, GROUP), BF16),
            pltpu.VMEM((GROUP, STATE), BF16),
            pltpu.VMEM((blocks, GROUP, 128), F32),
            pltpu.VMEM((blocks, GROUP, 128), F32),
            pltpu.VMEM((blocks, GROUP, 128), F32),
            pltpu.VMEM((blocks, GROUP, 128), F32),
            pltpu.VMEM((128, GROUP), F32),
            pltpu.VMEM((blocks, 8, 128), F32),
            pltpu.VMEM((blocks, STATE, BLOCK), F32),
            pltpu.VMEM((GROUP, model), F32),
        ] + hosted.scratch() + resident_scratch(resident),
        compiler_params=params(2 if hosted.operands() else None),
        cost_estimate=pl.CostEstimate(
            flops=2 * length * model * (3 * inner + 512), bytes_accessed=40 << 20, transcendentals=0
        ),
        name="ssd_forward",
    )(
        inputs, gate_w, value_w, state_w, step_w, taps, bias, staps, sbias, step_bias, rate, skip,
        cols, seg_line, out_w, gain, *hosted.operands(),
    )


def backward_call(saved, cotan, weights, vectors, gain, cols, seg_line, hosted, pace, collective):
    gate_raw, value_raw, mixed, bc, _, step_in, cums, held, _ = saved
    gate_w, value_w, step_w, out_w = weights
    taps, bias, rate, skip = vectors
    length, inner = gate_raw.shape
    model, tp_size = gate_w.shape[0], hosted.size
    specs, shapes = hosted.outs()
    groups, blocks = length // GROUP, inner // BLOCK
    assert groups == blocks
    last = groups - 1
    hbm = pl.BlockSpec(memory_space=pl.ANY)
    resident = [(1, out_w, 0), (13, gate_w, blocks), (14, value_w, blocks), (15, step_w, blocks)]
    row = lambda g: last - jnp.maximum(g - 1, 0)
    column = lambda g, j: jnp.where(g == 0, 0, j)
    wide = pl.BlockSpec((GROUP, BLOCK), lambda g, j: (row(g), column(g, j)))
    line = lambda rows: pl.BlockSpec((rows, BLOCK), lambda g, j: (0, column(g, j)))
    rows_of = lambda width: pl.BlockSpec((GROUP, width), lambda g, j: (row(g), 0))
    first = lambda width: pl.BlockSpec((GROUP, width), lambda g, j: (jnp.where(g == 0, j, last), 0))
    steps = GROUP // HALO
    before = pl.BlockSpec(
        (HALO, BLOCK), lambda g, j: (jnp.maximum(row(g) * steps - 1, 0), column(g, j))
    )
    return pl.pallas_call(
        hosted.wrap(partial(backward_kernel, tp_size), BACKWARD_INS, BACKWARD_OUTS, pace, resident),
        grid=(groups + 1, blocks),
        in_specs=[
            first(model), hbm, first(inner), first(inner), whole(gain),
            wide, wide, before, wide, rows_of(2 * STATE), rows_of(128), rows_of(128),
            pl.BlockSpec((1, STATE, BLOCK), lambda g, j: (row(g), 0, column(g, j))),
            hbm, hbm, hbm,
            line(CONV), line(1), whole(rate), line(1), line(1),
            rows_of(cols.shape[1]), pl.BlockSpec((1, GROUP), lambda g, j: (0, row(g))),
        ] + hosted.in_specs(),
        out_specs=[
            wide, wide, wide, rows_of(128), rows_of(2 * STATE),
            rows_of(model), pl.BlockSpec((8, inner), lambda g, j: (0, 0)), pl.BlockSpec((8, 128), lambda g, j: (0, 0)),
            pl.BlockSpec((length, 128), lambda g, j: (0, 0)),
        ] + specs,
        out_shape=[
            shape((length, inner), BF16), shape((length, inner), BF16), shape((length, inner), BF16),
            shape((length, 128), BF16), shape((length, 2 * STATE), BF16),
            shape((length, model), BF16), shape((8, inner)), shape((8, 128)), shape((length, 128)),
        ] + shapes,
        scratch_shapes=[
            pltpu.VMEM((GROUP + HALO, BLOCK), F32),
            pltpu.VMEM((blocks, GROUP + HALO, BLOCK), F32),
            pltpu.VMEM((GROUP, GROUP), F32),
            pltpu.VMEM((GROUP, GROUP), F32),
            pltpu.VMEM((GROUP, STATE), BF16),
            pltpu.VMEM((STATE, GROUP), BF16),
            pltpu.VMEM((blocks, GROUP, 128), F32),
            pltpu.VMEM((blocks, GROUP, 128), F32),
            pltpu.VMEM((blocks, GROUP, 128), F32),
            pltpu.VMEM((blocks, GROUP, 128), F32),
            pltpu.VMEM((128, GROUP), F32),
            pltpu.VMEM((blocks, 8, 128), F32),
            pltpu.VMEM((blocks, STATE, BLOCK), F32),
            pltpu.VMEM((GROUP, model), F32),
            pltpu.VMEM((GROUP, STATE), F32),
            pltpu.VMEM((GROUP, STATE), F32),
            pltpu.VMEM((GROUP, 128), F32),
            pltpu.VMEM((GROUP, 128), F32),
            pltpu.VMEM((8, 128), F32),
            pltpu.VMEM((blocks, 8, BLOCK), F32),
            pltpu.VMEM((8, 128), F32),
            pltpu.VMEM((groups, GROUP, inner), BF16),
            pltpu.VMEM((groups, 8, GROUP), F32),
            pltpu.VMEM((tp_size, groups, 8, GROUP), F32),
            pltpu.VMEM((groups, 128, GROUP), F32),
            pltpu.SemaphoreType.DMA((tp_size - 1,)),
            pltpu.SemaphoreType.DMA((tp_size - 1,)),
        ] + hosted.scratch() + resident_scratch(resident),
        compiler_params=params(collective),
        cost_estimate=pl.CostEstimate(
            flops=6 * length * model * inner, bytes_accessed=60 << 20, transcendentals=0
        ),
        name="ssd_backward",
    )(
        cotan, out_w, gate_raw, mixed, gain,
        gate_raw, value_raw, value_raw, mixed, bc, step_in, cums, held,
        gate_w, value_w, step_w, taps, bias, rate, skip, gain, cols, seg_line, *hosted.operands(),
    )

def gather_kernel(count, pieces, *refs):
    amount = len(pieces)
    sources, targets = refs[:amount], refs[amount : 2 * amount]
    own_sem, send_sem, recv_sem, pass_sem, took_sem = refs[2 * amount :]
    me, line = lax.axis_index("fsdp"), lax.axis_index("tp")
    chips = count // 2
    partner = me + 1 - 2 * lax.rem(me, 2)
    others = [lax.rem(me + 2 * hop, count) for hop in range(1, chips)]
    greet([(device, line) for device in others + [partner]])

    def remote(source, target, sends, receives, device):
        return pltpu.make_async_remote_copy(
            src_ref=source, dst_ref=target, send_sem=sends, recv_sem=receives,
            device_id=(device, line), device_id_type=MESH,
        )

    def place(which, at):
        size, axis = pieces[which]
        return part_of(targets[which], at, size, axis)

    started = []
    for which in range(amount):
        for hop in range(1, chips):
            copy = remote(
                sources[which], place(which, me), send_sem.at[hop, which],
                recv_sem.at[hop, which], lax.rem(me + 2 * hop, count),
            )
            copy.start()
            started.append(copy)
    for which in range(amount):
        copy = remote(
            sources[which], place(which, me), pass_sem.at[0, which], took_sem.at[0, which], partner
        )
        copy.start()
        started.append(copy)
    own = []
    for which in range(amount):
        copy = pltpu.make_async_copy(sources[which], place(which, me), own_sem.at[which])
        copy.start()
        own.append(copy)
    for which in range(amount):
        for hop in range(1, chips):
            origin = lax.rem(me - 2 * hop + count, count)
            block = place(which, origin)
            remote(
                block, block, send_sem.at[hop, which], recv_sem.at[hop, which], partner
            ).wait_recv()
            copy = remote(
                block, block, pass_sem.at[hop, which], took_sem.at[hop, which], partner
            )
            copy.start()
            started.append(copy)
    for which in range(amount):
        for hop in range(chips):
            block = place(which, lax.rem(partner - 2 * hop + count, count))
            remote(
                block, block, pass_sem.at[hop, which], took_sem.at[hop, which], partner
            ).wait_recv()
    for copy in started:
        copy.wait_send()
    for copy in own:
        copy.wait()


def gather_call(count, blocks, axes):
    pieces, shapes = [], []
    for block, axis in zip(blocks, axes):
        if axis == 2:
            pieces.append((0, 2))
            shapes.append(shape((count,) + block.shape, BF16))
        else:
            pieces.append((block.shape[axis], axis))
            dims = list(block.shape)
            dims[axis] *= count
            shapes.append(shape(tuple(dims), BF16))
    amount = len(blocks)
    sems = lambda: pltpu.SemaphoreType.DMA((count // 2, amount))
    return pl.pallas_call(
        partial(gather_kernel, count, pieces),
        in_specs=[pl.BlockSpec(memory_space=pl.ANY)] * amount,
        out_specs=[pl.BlockSpec(memory_space=pl.ANY)] * amount,
        out_shape=shapes,
        scratch_shapes=[pltpu.SemaphoreType.DMA((amount,)), sems(), sems(), sems(), sems()],
        compiler_params=pltpu.CompilerParams(collective_id=0, has_side_effects=True),
        cost_estimate=pl.CostEstimate(flops=0, bytes_accessed=250 << 20, transcendentals=0),
        name="gather_weights",
    )(*blocks)


def scatter_kernel(count, pieces, *refs):
    amount = len(pieces)
    sources, targets = refs[:amount], refs[amount : 2 * amount]
    scratch = refs[2 * amount :]
    mine, took, came = (scratch[at * amount : (at + 1) * amount] for at in range(3))
    own_sem, pass_sem, took_sem, send_sem, recv_sem = scratch[3 * amount :]
    me, line = lax.axis_index("fsdp"), lax.axis_index("tp")
    chips = count // 2
    partner = me + 1 - 2 * lax.rem(me, 2)
    others = [lax.rem(me + 2 * hop, count) for hop in range(1, chips)]
    greet([(device, line) for device in others + [partner]])

    def remote(source, target, sends, receives, device):
        return pltpu.make_async_remote_copy(
            src_ref=source, dst_ref=target, send_sem=sends, recv_sem=receives,
            device_id=(device, line), device_id_type=MESH,
        )

    def piece(which, at):
        size, axis = pieces[which]
        return part_of(sources[which], at, size, axis)

    order = list(range(1, chips)) + [0]
    handed, own = {}, {}
    for hop in order:
        for which in range(amount):
            copy = remote(
                piece(which, lax.rem(partner + 2 * hop, count)), took[which].at[hop],
                pass_sem.at[hop, which], took_sem.at[hop, which], partner,
            )
            copy.start()
            handed[hop, which] = copy
            copy = pltpu.make_async_copy(
                piece(which, lax.rem(me + 2 * hop, count)), mine[which].at[hop],
                own_sem.at[hop, which],
            )
            copy.start()
            own[hop, which] = copy
    sent = []
    for hop in order:
        for which in range(amount):
            own[hop, which].wait()
            handed[hop, which].wait_recv()
            total = mine[which][hop].astype(F32) + took[which][hop].astype(F32)
            if hop == 0:
                targets[which][...] = total
                continue
            mine[which][hop] = total.astype(BF16)
            copy = remote(
                mine[which].at[hop], came[which].at[hop - 1], send_sem.at[hop, which],
                recv_sem.at[hop, which], lax.rem(me + 2 * hop, count),
            )
            copy.start()
            sent.append(copy)
    for which in range(amount):
        for hop in range(1, chips):
            block = came[which].at[hop - 1]
            remote(
                block, block, send_sem.at[hop, which], recv_sem.at[hop, which], partner
            ).wait_recv()
            targets[which][...] += block[...].astype(F32)
    for copy in list(handed.values()) + sent:
        copy.wait_send()


def scatter_call(count, arrays, axes):
    pieces, shapes = [], []
    for array, axis in zip(arrays, axes):
        if axis == 2:
            pieces.append((0, 2))
            shapes.append(array.shape[1:])
        else:
            dims = list(array.shape)
            dims[axis] //= count
            pieces.append((dims[axis], axis))
            shapes.append(tuple(dims))
    amount, chips = len(arrays), count // 2
    sems = lambda: pltpu.SemaphoreType.DMA((chips, amount))
    return pl.pallas_call(
        partial(scatter_kernel, count, pieces),
        in_specs=[pl.BlockSpec(memory_space=pl.ANY)] * amount,
        out_specs=[pl.BlockSpec(memory_space=pltpu.VMEM)] * amount,
        out_shape=[shape(dims) for dims in shapes],
        scratch_shapes=[pltpu.VMEM((chips,) + dims, BF16) for dims in shapes]
        + [pltpu.VMEM((chips,) + dims, BF16) for dims in shapes]
        + [pltpu.VMEM((chips - 1,) + dims, BF16) for dims in shapes]
        + [sems(), sems(), sems(), sems(), sems()],
        compiler_params=pltpu.CompilerParams(
            collective_id=1, has_side_effects=True, vmem_limit_bytes=48 << 20
        ),
        cost_estimate=pl.CostEstimate(flops=0, bytes_accessed=250 << 20, transcendentals=0),
        name="scatter_gradients",
    )(*arrays)


def weight_kernel(micro, *refs):
    outs = refs[-4:]
    rows, lows = refs[:micro], refs[micro : 5 * micro]
    for which in range(4):
        total = mm_tn(rows[0][...], lows[which][...])
        for at in range(1, micro):
            total = total + mm_tn(rows[at][...], lows[4 * at + which][...])
        outs[which][...] = total.astype(BF16)


def weight_call(inputs, lows):
    micro, (length, model) = len(inputs), inputs[0].shape
    full = lambda array: pl.BlockSpec(array.shape, lambda g: (0, 0), pipeline_mode=pl.Buffered(1))
    flat = [array for low in lows for array in low]
    widths = [array.shape[1] for array in lows[0]]
    return pl.pallas_call(
        partial(weight_kernel, micro),
        grid=(model // BLOCK,),
        in_specs=[pl.BlockSpec((length, BLOCK), lambda g: (0, g))] * micro
        + [full(array) for array in flat],
        out_specs=[pl.BlockSpec((BLOCK, width), lambda g: (g, 0)) for width in widths],
        out_shape=[shape((model, width), BF16) for width in widths],
        compiler_params=pltpu.CompilerParams(vmem_limit_bytes=50 << 20),
        cost_estimate=pl.CostEstimate(
            flops=2 * micro * length * model * sum(widths), bytes_accessed=40 << 20, transcendentals=0
        ),
        name="weight_gradients",
    )(*inputs, *flat)


def outer_kernel(micro, *refs):
    total = mm_tn(refs[0][...], refs[micro][...])
    for at in range(1, micro):
        total = total + mm_tn(refs[at][...], refs[micro + at][...])
    refs[-1][...] = total.astype(BF16)


def outer_call(branches, cotans):
    micro, (length, inner) = len(branches), branches[0].shape
    model = cotans[0].shape[1]
    full = lambda array: pl.BlockSpec(array.shape, lambda g: (0, 0), pipeline_mode=pl.Buffered(1))
    return pl.pallas_call(
        partial(outer_kernel, micro),
        grid=(inner // BLOCK,),
        in_specs=[pl.BlockSpec((length, BLOCK), lambda g: (0, g))] * micro
        + [full(array) for array in cotans],
        out_specs=pl.BlockSpec((BLOCK, model), lambda g: (g, 0)),
        out_shape=shape((inner, model), BF16),
        compiler_params=pltpu.CompilerParams(vmem_limit_bytes=50 << 20),
        cost_estimate=pl.CostEstimate(
            flops=2 * micro * length * model * inner, bytes_accessed=30 << 20, transcendentals=0
        ),
        name="out_gradients",
    )(*branches, *cotans)


def tail_kernel(chips, tp_size, micro, widths, *refs):
    columns, lows, parts, raws = refs[:4], refs[4:12], refs[12:14], refs[14:16]
    cols_ref, staps_ref, sbias_ref, pack = refs[16:20]
    outs, state_out, pack_out, ssum_out, low_out = refs[20:24], refs[24], refs[25], refs[26], refs[27]
    (
        cols_s, give, took, mine, came, passed, total_s, kept_s,
        sgive, stook, smine, scame, stotal, skept_s,
        pack_took, pack_sum, pack_slots, ssum, ssum_took, ssum_sum, ssum_slots,
        raw_s, own_s, slots_s, whole_s, sum_s, low_s, vbuf, gcbuf,
        cols_sem, give_sem, took_sem, send_sem, recv_sem, sgive_sem, stook_sem, ssend_sem, srecv_sem,
        pass_sem, pack_sem, ssum_sem, raw_sem, own_sem, part_send, part_recv, whole_send, whole_recv,
    ) = refs[28:]
    step, steps = pl.program_id(0), pl.num_programs(0)
    me, line = lax.axis_index("fsdp"), lax.axis_index("tp")
    count = 2 * chips
    core, chip = lax.rem(me, 2), me // 2
    partner = me + 1 - 2 * core
    split = total_s.shape[1] // 256 * 128

    def flipped(hop, which_core):
        x, y = lax.rem(chip, 2), chip // 2
        hop_x, hop_y = hop % 2, hop // 2
        x, y = x + hop_x - 2 * x * hop_x, y + hop_y - 2 * y * hop_y
        return (2 * y + x) * 2 + which_core

    def tile_of(at):
        pair = lax.rem(at, count) // 2
        hop = jnp.where(pair == 0, 3, pair - 1)
        return hop, flipped(hop, jnp.where(lax.rem(at, 2) == 0, 1 - core, core))

    def fetch(at, which):
        _, shard = tile_of(at)
        slot = lax.rem(at, 2)
        return pltpu.make_async_copy(
            columns[which].at[:, pl.ds(pl.multiple_of(shard * BLOCK, BLOCK), BLOCK)],
            cols_s.at[slot, which], cols_sem.at[slot, which],
        )

    def far(hop):
        return (flipped(hop, core), line)

    def giving(hop):
        return remote_copy(
            give.at[hop], took.at[hop], give_sem.at[hop], took_sem.at[hop], (partner, line)
        )

    def sending(hop):
        return remote_copy(
            mine.at[hop - 1], came.at[hop - 1], send_sem.at[hop - 1], recv_sem.at[hop - 1], far(hop)
        )

    def passing(hop):
        columns = pl.ds(0, split) if hop == 1 else pl.ds(split, total_s.shape[1] - split)
        return remote_copy(
            mine.at[2, :, columns], passed.at[:, columns], pass_sem.at[0, hop - 1],
            pass_sem.at[1, hop - 1], far(hop),
        )

    def sgiving(hop):
        return remote_copy(
            sgive.at[hop], stook.at[hop], sgive_sem.at[hop], stook_sem.at[hop], (partner, line)
        )

    def ssending(hop):
        return remote_copy(
            smine.at[hop - 1], scame.at[hop - 1], ssend_sem.at[hop - 1], srecv_sem.at[hop - 1], far(hop)
        )

    pack_pass = remote_copy(pack, pack_took, pack_sem.at[0, 0], pack_sem.at[1, 0], (partner, line))
    ssum_pass = remote_copy(ssum, ssum_took, ssum_sem.at[0, 0], ssum_sem.at[1, 0], (partner, line))

    def pack_send(hop):
        return remote_copy(
            pack_sum, pack_slots.at[chip], pack_sem.at[0, hop], pack_sem.at[1, hop], far(hop)
        )

    def ssum_send(hop):
        return remote_copy(
            ssum_sum, ssum_slots.at[chip], ssum_sem.at[0, hop], ssum_sem.at[1, hop], far(hop)
        )

    def rows_at(ref, at):
        return ref.at[pl.ds(pl.multiple_of(at * GROUP, GROUP), GROUP), :]

    def handing(hop):
        owner = lax.rem(line + hop, tp_size)
        return remote_copy(
            rows_at(parts[late], owner), slots_s.at[line], part_send.at[hop - 1],
            part_recv.at[hop - 1], (me, owner),
        )

    late = micro - 1

    def own_part():
        return pltpu.make_async_copy(rows_at(parts[late], line), own_s, own_sem.at[late])

    def ready(at):
        length = raws[at].shape[0]
        return pltpu.make_async_copy(
            parts[at], whole_s.at[pl.ds(at * length, length), :], own_sem.at[at]
        )

    def raw_copy(at):
        length = raws[at].shape[0]
        return pltpu.make_async_copy(
            raws[at], raw_s.at[pl.ds(at * length, length), :], raw_sem.at[at]
        )

    groups = raws[0].shape[0] // GROUP

    def spreading(hop):
        block = rows_at(whole_s, late * groups + line)
        return remote_copy(
            sum_s, block, whole_send.at[hop - 1], whole_recv.at[hop - 1],
            (me, lax.rem(line + hop, tp_size)),
        )

    @pl.when(step == 0)
    def _():
        for which in range(4):
            fetch(step, which).start()
        own_part().start()
        for at in range(micro):
            raw_copy(at).start()
            if at != late:
                ready(at).start()
        greet(
            [far(hop) for hop in range(1, chips)] + [(partner, line)]
            + [(me, lax.rem(line + hop, tp_size)) for hop in range(1, tp_size)]
        )
        for hop in range(1, tp_size):
            handing(hop).start()
        pack_pass.start()

    @pl.when(step + 1 < count)
    def _():
        for which in range(4):
            fetch(step + 1, which).start()

    @pl.when((step + 1 >= count) & (step + 1 < steps))
    def _():
        for which in range(2):
            fetch(step + 1, which).start()

    for which in range(2):
        fetch(step, which).wait()

    @pl.when(step < count)
    def _():
        for which in range(2, 4):
            fetch(step, which).wait()

    slot = lax.rem(step, 2)
    hop, _ = tile_of(step)
    even = lax.rem(step, 2) == 0

    def tile(which):
        sides = (0, 1) if which < 3 else (2, 3)
        return mm_tn(cols_s[slot, sides[0]], lows[2 * which][...]) + mm_tn(
            cols_s[slot, sides[1]], lows[2 * which + 1][...]
        )

    @pl.when((step < count) & even)
    def _():
        at = 0
        for which, width in enumerate(widths):
            give[hop, :, at : at + width] = tile(which).astype(BF16)
            at += width
        giving(hop).start()

    @pl.when((step < count) & jnp.logical_not(even))
    def _():
        at = 0
        for which, width in enumerate(widths):
            total_s[:, at : at + width] = tile(which)
            at += width
        giving(hop).wait_recv()
        total_s[...] += took[hop].astype(F32)

        @pl.when(hop == 3)
        def _():
            mine[2] = total_s[...].astype(BF16)
            passing(1).start()
            passing(2).start()

        @pl.when(hop == 0)
        def _():
            kept_s[...] = total_s[...]

        @pl.when(hop == 1)
        def _():
            passing(2).wait_recv()
            total_s[:, split:] += passed[:, split:].astype(F32)
            mine[0] = total_s[...].astype(BF16)
            sending(1).start()

        @pl.when(hop == 2)
        def _():
            passing(1).wait_recv()
            total_s[:, :split] += passed[:, :split].astype(F32)
            mine[1] = total_s[...].astype(BF16)
            sending(2).start()

    @pl.when(step == 1)
    def _():
        pack_pass.wait()
        pack_sum[...] = pack[...] + pack_took[...]
        pack_slots[chip] = pack_sum[...]
        for other in range(1, chips):
            pack_send(other).start()

    @pl.when(step == 5)
    def _():
        own_part().wait()
        slots_s[line] = own_s[...]
        for hop in range(1, tp_size):
            handing(hop).wait()
        total = slots_s[0].astype(F32)
        for other in range(1, tp_size):
            total = total + slots_s[other].astype(F32)
        sum_s[...] = total.astype(BF16)
        mine_rows = rows_at(whole_s, late * groups + line)
        mine_rows[...] = sum_s[...]
        for hop in range(1, tp_size):
            spreading(hop).start()

    @pl.when(step == count - 1)
    def _():
        for at in range(micro):
            raw_copy(at).wait()
            if at != late:
                ready(at).wait()
        for hop in range(1, tp_size):
            spreading(hop).wait()
        ssum[...] = jnp.zeros(ssum.shape, F32)
        taps, bias = staps_ref[...], sbias_ref[...]

        def state_group(turn, carry):
            group = micro * groups - 1 - turn
            at = pl.multiple_of(group * GROUP, GROUP)
            cols = cols_ref[pl.ds(at, GROUP), :]
            vbuf[HALO : HALO + GROUP, :] = raw_s[pl.ds(at, GROUP), :]
            ahead = pl.multiple_of(jnp.maximum(group * (GROUP // HALO) - 1, 0) * HALO, HALO)
            vbuf[0:HALO, :] = raw_s[pl.ds(ahead, HALO), :]
            moved = shifted_values(vbuf, cols)
            conv = conv_of(moved, taps, bias)
            sig = jax.nn.sigmoid(conv)
            grad = whole_s[pl.ds(at, GROUP), :].astype(F32) * (sig * (1.0 + conv * (1.0 - sig)))
            gcbuf[GROUP : GROUP + HALO, :] = gcbuf[0:HALO, :]
            gcbuf[0:GROUP, :] = grad
            back = taps[0:1, :] * grad
            for offset in range(1, CONV):
                up = jnp.where(
                    cols[:, 2 + offset : 3 + offset] > 0.0, gcbuf[offset : offset + GROUP, :], 0.0
                )
                back = back + taps[offset : offset + 1, :] * up
            low_s[pl.ds(at, GROUP), :] = back.astype(BF16)
            for offset in range(CONV):
                ssum[offset : offset + 1, :] += jnp.sum(grad * moved[offset], axis=0, keepdims=True)
            ssum[CONV : CONV + 1, :] += jnp.sum(grad, axis=0, keepdims=True)
            return carry

        lax.fori_loop(0, micro * groups, state_group, 0)
        ssum_pass.start()
        for at in range(micro):
            low_out[at] = low_s[pl.ds(pl.multiple_of((at * groups + line) * GROUP, GROUP), GROUP), :]

    def state_tile():
        length = groups * GROUP
        return mm_tn(cols_s[slot, 0], low_s[0:length, :]) + mm_tn(
            cols_s[slot, 1], low_s[length : 2 * length, :]
        )

    @pl.when((step >= count) & even)
    def _():
        sgive[hop] = state_tile().astype(BF16)
        sgiving(hop).start()

    @pl.when((step >= count) & jnp.logical_not(even))
    def _():
        stotal[...] = state_tile()
        sgiving(hop).wait_recv()
        stotal[...] += stook[hop].astype(F32)

        @pl.when(hop == 0)
        def _():
            skept_s[...] = stotal[...]

        @pl.when(hop > 0)
        def _():
            smine[hop - 1] = stotal[...].astype(BF16)
            ssending(hop).start()

    @pl.when(step == count + 1)
    def _():
        ssum_pass.wait()
        ssum_sum[...] = ssum[...] + ssum_took[...]
        ssum_slots[chip] = ssum_sum[...]
        for other in range(1, chips):
            ssum_send(other).start()

    @pl.when(step == steps - 1)
    def _():
        for sends, slots, out in ((pack_send, pack_slots, pack_out), (ssum_send, ssum_slots, ssum_out)):
            for other in range(1, chips):
                sends(other).wait()
            total = slots[0]
            for other in range(1, chips):
                total = total + slots[other]
            out[...] = total
        for other in (1, 2):
            sending(other).wait_recv()
            kept_s[...] += came[other - 1].astype(F32)
        for other in range(1, chips):
            ssending(other).wait_recv()
            skept_s[...] += scame[other - 1].astype(F32)
        state_out[...] = skept_s[...]
        at = 0
        for which, width in enumerate(widths):
            part = kept_s[:, at : at + width]
            outs[which][...] = part if which < 3 else jnp.transpose(part)
            at += width
        for other in (1, 2):
            passing(other).wait_send()
            sending(other).wait_send()
        for other in range(1, chips):
            ssending(other).wait_send()
        for other in range(chips):
            giving(other).wait_send()
            sgiving(other).wait_send()


def tail_call(count, tp_size, inputs, cotans, lows, parts, raws, cols, staps, sbias, pack):
    micro, length = len(inputs), inputs[0].shape[0]
    chips = count // 2
    order = [low[which] for which in range(4) for low in lows]
    widths = [low.shape[1] for low in order[::2]]
    total, narrow = sum(widths), 2 * STATE
    hbm = pl.BlockSpec(memory_space=pl.ANY)
    full = lambda array: pl.BlockSpec(array.shape, lambda i: (0,) * array.ndim, pipeline_mode=pl.Buffered(1))
    out_dims = [(BLOCK, width) for width in widths[:3]] + [(widths[3], BLOCK), (BLOCK, narrow)]
    out_shapes = [shape(dims) for dims in out_dims] + [
        shape(pack.shape), shape((8, narrow)), shape((micro, GROUP, narrow), BF16)
    ]
    dma = lambda *dims: pltpu.SemaphoreType.DMA(dims)
    return pl.pallas_call(
        partial(tail_kernel, chips, tp_size, micro, widths),
        grid=(2 * count,),
        in_specs=[hbm] * 4 + [full(low) for low in order] + [hbm] * 4
        + [full(cols), full(staps), full(sbias), full(pack)],
        out_specs=[full(each) for each in out_shapes],
        out_shape=out_shapes,
        scratch_shapes=[
            pltpu.VMEM((2, 4, length, BLOCK), BF16),
            pltpu.VMEM((chips, BLOCK, total), BF16),
            pltpu.VMEM((chips, BLOCK, total), BF16),
            pltpu.VMEM((3, BLOCK, total), BF16),
            pltpu.VMEM((2, BLOCK, total), BF16),
            pltpu.VMEM((BLOCK, total), BF16),
            pltpu.VMEM((BLOCK, total), F32),
            pltpu.VMEM((BLOCK, total), F32),
            pltpu.VMEM((chips, BLOCK, narrow), BF16),
            pltpu.VMEM((chips, BLOCK, narrow), BF16),
            pltpu.VMEM((chips - 1, BLOCK, narrow), BF16),
            pltpu.VMEM((chips - 1, BLOCK, narrow), BF16),
            pltpu.VMEM((BLOCK, narrow), F32),
            pltpu.VMEM((BLOCK, narrow), F32),
            pltpu.VMEM(pack.shape, F32),
            pltpu.VMEM(pack.shape, F32),
            pltpu.VMEM((chips,) + pack.shape, F32),
            pltpu.VMEM((8, narrow), F32),
            pltpu.VMEM((8, narrow), F32),
            pltpu.VMEM((8, narrow), F32),
            pltpu.VMEM((chips, 8, narrow), F32),
            pltpu.VMEM((micro * length, narrow), F32),
            pltpu.VMEM((GROUP, narrow), BF16),
            pltpu.VMEM((tp_size, GROUP, narrow), BF16),
            pltpu.VMEM((micro * length, narrow), BF16),
            pltpu.VMEM((GROUP, narrow), BF16),
            pltpu.VMEM((micro * length, narrow), BF16),
            pltpu.VMEM((GROUP + HALO, narrow), F32),
            pltpu.VMEM((GROUP + HALO, narrow), F32),
            dma(2, 4), dma(chips), dma(chips), dma(2), dma(2),
            dma(chips), dma(chips), dma(chips - 1), dma(chips - 1),
            dma(2, 2), dma(2, chips), dma(2, chips), dma(micro), dma(micro),
            dma(tp_size - 1), dma(tp_size - 1), dma(tp_size - 1), dma(tp_size - 1),
        ],
        compiler_params=pltpu.CompilerParams(
            collective_id=6, has_side_effects=True, vmem_limit_bytes=62 << 20
        ),
        cost_estimate=pl.CostEstimate(
            flops=4 * length * BLOCK * count * total, bytes_accessed=250 << 20, transcendentals=0
        ),
        name="weight_gradients",
    )(*inputs, *cotans, *order, *parts, *raws, cols, staps, sbias, pack)


def rows_kernel(
    sum0, sum1, low_ref, state_w, rows_ref, cot_ref, gain_ref, made0, made1, scale_ref,
    hidden_out, block_out, gain_out,
):
    step = pl.program_id(0)
    half = pl.num_programs(0) // 2
    gain = gain_ref[...]

    def work(summed, made):
        grad = summed[...].astype(F32) + mm_nt(low_ref[0], state_w[...])
        rows = rows_ref[0].astype(F32)
        inv_root = lax.rsqrt(jnp.mean(rows * rows, axis=1, keepdims=True) + EPSILON)
        part = jnp.sum(grad * (rows * inv_root), axis=0, keepdims=True)
        normed = grad * gain
        inner = jnp.mean(normed * rows, axis=1, keepdims=True)
        back = inv_root * normed - rows * (inv_root * inv_root * inv_root * inner)
        hidden_out[0] = (cot_ref[0].astype(F32) + back).astype(BF16)
        block_out[0] = (rows + made[...] * scale_ref[0][:, 0:1]).astype(BF16)
        width = gain_out.shape[1]
        for at in range(gain_out.shape[0]):
            piece = part[:, at * width : (at + 1) * width]

            @pl.when(step == 0)
            def _():
                gain_out[at : at + 1, :] = piece

            @pl.when(step > 0)
            def _():
                gain_out[at : at + 1, :] += piece

    @pl.when(step < half)
    def _():
        work(sum0, made0)

    @pl.when(step >= half)
    def _():
        work(sum1, made1)


def rows_call(sums, lows, state_w, rows, cotan, gain, made, scales):
    micro, length, model = rows.shape
    tiles = 2
    tile = length // tiles
    both = lambda width: pl.BlockSpec((1, tile, width), lambda i: (i // tiles, i % tiles, 0))
    former = pl.BlockSpec((tile, model), lambda i: (jnp.minimum(i, tiles - 1), 0))
    latter = pl.BlockSpec((tile, model), lambda i: (jnp.maximum(i - tiles, 0), 0))
    full = lambda dims: pl.BlockSpec(dims, lambda i: (0, 0))
    return pl.pallas_call(
        rows_kernel,
        grid=(micro * tiles,),
        in_specs=[
            former, latter, both(2 * STATE), full(state_w.shape), both(model), both(model),
            full(gain.shape), former, latter, both(128),
        ],
        out_specs=[both(model), both(model), full((8, model // 8))],
        out_shape=[shape(rows.shape, BF16), shape(rows.shape, BF16), shape((8, model // 8))],
        compiler_params=pltpu.CompilerParams(vmem_limit_bytes=50 << 20),
        cost_estimate=pl.CostEstimate(flops=1 << 30, bytes_accessed=18 << 20, transcendentals=0),
        name="finish_rows",
    )(*sums, lows, state_w, rows, cotan, gain, *made, scales)


def gain_kernel(
    tp_size, count, part, gain_out, line_slots, line_sum, slots, send_sem, recv_sem, far_send, far_recv,
):
    me, column = lax.axis_index("tp"), lax.axis_index("fsdp")
    greet(
        [(column, lax.rem(me + hop, tp_size)) for hop in range(1, tp_size)]
        + [(lax.rem(column + hop, count), me) for hop in range(1, count)]
    )
    line_slots[me] = part[...]
    copies = [
        remote_copy(
            part, line_slots.at[me], send_sem.at[hop - 1], recv_sem.at[hop - 1],
            (column, lax.rem(me + hop, tp_size)),
        )
        for hop in range(1, tp_size)
    ]
    for copy in copies:
        copy.start()
    for copy in copies:
        copy.wait()
    total = line_slots[0]
    for at in range(1, tp_size):
        total = total + line_slots[at]
    line_sum[...] = total
    slots[column] = total
    copies = [
        remote_copy(
            line_sum, slots.at[column], far_send.at[hop - 1], far_recv.at[hop - 1],
            (lax.rem(column + hop, count), me),
        )
        for hop in range(1, count)
    ]
    for copy in copies:
        copy.start()
    for copy in copies:
        copy.wait()
    total = slots[0]
    for at in range(1, count):
        total = total + slots[at]
    gain_out[...] = total


def gain_call(tp_size, count, part):
    vmem = pl.BlockSpec(memory_space=pltpu.VMEM)
    return pl.pallas_call(
        partial(gain_kernel, tp_size, count),
        in_specs=[vmem],
        out_specs=vmem,
        out_shape=shape(part.shape),
        scratch_shapes=[
            pltpu.VMEM((tp_size,) + part.shape, F32), pltpu.VMEM(part.shape, F32),
            pltpu.VMEM((count,) + part.shape, F32),
            pltpu.SemaphoreType.DMA((tp_size - 1,)), pltpu.SemaphoreType.DMA((tp_size - 1,)),
            pltpu.SemaphoreType.DMA((count - 1,)), pltpu.SemaphoreType.DMA((count - 1,)),
        ],
        compiler_params=pltpu.CompilerParams(
            collective_id=7, has_side_effects=True, vmem_limit_bytes=32 << 20
        ),
        cost_estimate=pl.CostEstimate(flops=0, bytes_accessed=1 << 20, transcendentals=0),
        name="gain_sum",
    )(part)


def unpack_kernel(heads, pack_ref, ssum_ref, rate_ref, gain, skip, conv, bias, sconv, sbias, step, decay):
    gain[...] = pack_ref[0:1, :]
    lanes = pack_ref.shape[1]
    place = (iota((lanes, 128), 0) // HEAD_DIM == iota((lanes, 128), 1)).astype(F32)
    sums = mm(pack_ref[0:8, :], place, PRECISE)
    skip[...] = sums[1:2, :heads]
    conv[...] = pack_ref[2 : 2 + CONV, :]
    bias[...] = pack_ref[2 + CONV : 3 + CONV, :]
    sconv[...] = ssum_ref[0:CONV, :]
    sbias[...] = ssum_ref[CONV : CONV + 1, :]
    step[...] = pack_ref[8:9, :heads]
    decay[...] = pack_ref[9:10, :heads] * rate_ref[:, :heads]


def unpack_call(pack, ssum, rate, heads):
    inner = pack.shape[1]
    vmem = pl.BlockSpec(memory_space=pltpu.VMEM)
    dims = [(1, inner), (1, heads), (CONV, inner), (1, inner), (CONV, 2 * STATE), (1, 2 * STATE),
            (1, heads), (1, heads)]
    return pl.pallas_call(
        partial(unpack_kernel, heads), in_specs=[vmem] * 3, out_specs=[vmem] * 8,
        out_shape=[shape(each) for each in dims], name="small_gradients",
        cost_estimate=pl.CostEstimate(flops=0, bytes_accessed=1 << 18, transcendentals=0),
    )(pack, ssum, rate)


def shift_down(values, offset):
    return jnp.pad(values, ((offset, 0), (0, 0)))[: values.shape[0]]


def shift_up(values, offset):
    return jnp.pad(values, ((0, offset), (0, 0)))[offset:]


def document_columns(seg_row):
    length = seg_row.shape[0]
    previous = jnp.concatenate([jnp.full((1,), -1, seg_row.dtype), seg_row[GROUP - 1 : -1 : GROUP]])
    last = seg_row[GROUP - 1 :: GROUP]
    columns = []
    for offset in range(1, CONV):
        columns.append(jnp.pad(seg_row, (offset, 0), constant_values=-1)[:length] == seg_row)
    for offset in range(1, CONV):
        columns.append(jnp.pad(seg_row, (0, offset), constant_values=-1)[offset:] == seg_row)
    columns.append(seg_row == jnp.repeat(previous, GROUP))
    columns.append(seg_row == jnp.repeat(last, GROUP))
    columns.append(jnp.repeat(last == previous, GROUP))
    columns.append(seg_row)
    columns = [column.astype(F32) for column in columns]
    return jnp.stack(columns + [columns[0]] * (16 - len(columns)), axis=1)


def state_gradient(grad_bc, state_raw, taps, bias, cols):
    moved = [state_raw]
    for offset in range(1, CONV):
        moved.append(shift_down(state_raw, offset) * cols[:, offset - 1 : offset])
    conv = bias
    for offset in range(CONV):
        conv = conv + taps[offset][None, :] * moved[offset]
    sig = jax.nn.sigmoid(conv)
    grad_conv = grad_bc * (sig * (1.0 + conv * (1.0 - sig)))
    grad_raw = taps[0][None, :] * grad_conv
    for offset in range(1, CONV):
        grad_raw = grad_raw + taps[offset][None, :] * (
            shift_up(grad_conv, offset) * cols[:, 2 + offset : 3 + offset]
        )
    grad_taps = jnp.stack([jnp.sum(grad_conv * each, axis=0) for each in moved])
    return grad_raw.astype(BF16), grad_taps, jnp.sum(grad_conv, axis=0)


def local(
    hidden_in, segment_ids, cotangent, norm_gain, proj_gate, proj_value, proj_state, proj_step,
    conv_value, conv_value_bias, conv_state, conv_state_bias, step_bias, decay_log, skip_gain,
    gate_gain, proj_out,
):
    micro = hidden_in.shape[0]
    heads = step_bias.shape[0]
    rows_here = hidden_in.shape[2]
    tp_size = lax.axis_size("tp")
    me = lax.axis_index("tp")
    decay_rate = -jnp.exp(decay_log)
    pad_heads = lambda values: jnp.pad(values, (0, 128 - heads))[None, :]
    rate = pad_heads(decay_rate)
    step_bias_line = pad_heads(step_bias)
    skip = jnp.repeat(skip_gain, HEAD_DIM)[None, :]
    gain = gate_gain[None, :]
    taps, bias = conv_value, conv_value_bias[None, :]
    staps, sbias = conv_state, conv_state_bias[None, :]

    input_rows = []
    for at in range(micro):
        rows_float = hidden_in[at, 0].astype(F32)
        inv_root = lax.rsqrt(jnp.mean(rows_float * rows_float, axis=-1, keepdims=True) + EPSILON)
        input_rows.append((rows_float * inv_root * norm_gain).astype(BF16))

    def gather_tp(values, *after):
        values = lax.optimization_barrier((values,) + after)[0]
        return lax.all_gather(values, "tp", axis=0, tiled=True)

    def scatter_tp(values, *after):
        values = lax.optimization_barrier((values,) + after)[0]
        return lax.psum_scatter(values, "tp", scatter_dimension=0, tiled=True)

    inputs = [gather_tp(input_rows[0])]
    fsdp_size = lax.axis_size("fsdp")
    model = hidden_in.shape[3]
    aligned = proj_out.shape[1] % 128 == 0
    axes = (0, 0, 0, 0, 1 if aligned else 2)
    step_block = jnp.pad(proj_step, ((0, 0), (0, 128 - heads)))
    gate_w, value_w, state_w, step_w, out_w = gather_call(
        fsdp_size, (proj_gate, proj_value, proj_state, step_block, proj_out), axes
    )
    if not aligned:
        out_w = jnp.transpose(out_w, (1, 0, 2)).reshape(-1, model)
    inputs.append(gather_tp(input_rows[1], inputs[0], step_w))
    forward_weights = (gate_w, value_w, state_w, step_w, out_w)
    vectors = (taps, bias, staps, sbias, step_bias_line, rate, skip)
    columns = [document_columns(segment_ids[at, 0]) for at in range(micro)]
    seg_lines = [segment_ids[at, 0].astype(F32)[None, :] for at in range(micro)]
    quick = [0, 3, 7, 11, 14, 15, 15, 15, 15, 15]
    paces = {4: [0, 3, 4, 6, 9, 12, 15, 17, 19, 19], 5: [0, 4, 4, 7, 10, 13, 18, 19]}

    def forward(at, hosted):
        return forward_call(
            inputs[at], forward_weights, vectors, gain, columns[at], seg_lines[at], hosted, quick
        )

    def backward(at, hosted, collective):
        done = backward_call(
            saved[at], cotans[at], (gate_w, value_w, step_w, out_w), (taps, bias, rate, skip),
            gain, columns[at], seg_lines[at], hosted, paces[collective], collective,
        )
        scales.append(done[8])
        return done

    scales, produced, summed = [], [], []
    saved = [forward(0, Hosted(tp_size))]
    *kept, made_sum, cotan = forward(1, Hosted(tp_size, saved[0][8], cotangent[0, 0]))
    saved.append(kept)
    produced.append(made_sum)
    cotans = [cotan]
    *former, made_sum, cotan = backward(0, Hosted(tp_size, saved[1][8], cotangent[1, 0]), 4)
    produced.append(made_sum)
    cotans.append(cotan)
    early = lax.psum(former[4], "tp")
    *latter, gin_sum = backward(1, Hosted(tp_size, former[5]), 5)
    summed = [gin_sum, scatter_tp(latter[5])]
    lows = [[each[1], each[2], each[3], each[0]] for each in (former, latter)]
    parts, raws = (early, latter[4]), [each[4] for each in saved]
    inner_here = proj_gate.shape[1]
    pack = jnp.concatenate(
        [former[6] + latter[6], jnp.pad(former[7] + latter[7], ((0, 0), (0, inner_here - 128)))], axis=0
    )
    if aligned and fsdp_size == 8 and model // fsdp_size == BLOCK:
        grad_gate, grad_value, grad_step, grad_out, grad_state, pack, state_sum, mine = tail_call(
            fsdp_size, tp_size, inputs, cotans, lows, parts, raws, jnp.concatenate(columns, axis=0),
            staps, sbias, pack,
        )
    else:
        mine, state_sum = [], 0.0
        for at in range(micro):
            grad_bc = (parts[at] if at == 0 else lax.psum(parts[at], "tp")).astype(F32)
            low_state, grad_staps, grad_sbias = state_gradient(
                grad_bc, raws[at], staps, sbias, columns[at]
            )
            mine.append(lax.dynamic_slice_in_dim(low_state, me * rows_here, rows_here, axis=0))
            lows[at].insert(2, low_state)
            state_sum = state_sum + jnp.concatenate(
                [grad_staps, grad_sbias[None, :], jnp.zeros((3, 2 * STATE), F32)], axis=0
            )
        mine = jnp.stack(mine)
        grad_out = outer_call([low[4] for low in lows], cotans)
        grad_gate, grad_value, grad_state, grad_step = weight_call(inputs, [low[:4] for low in lows])
        if not aligned:
            grad_out = jnp.transpose(grad_out.reshape(-1, fsdp_size, proj_out.shape[1]), (1, 0, 2))
        grad_gate, grad_value, grad_state, grad_step, grad_out = scatter_call(
            fsdp_size, (grad_gate, grad_value, grad_state, grad_step, grad_out), axes
        )
        pack, state_sum = lax.psum((pack, state_sum), "fsdp")
    grad_step = grad_step[:, :heads]
    my_scales = jnp.stack(
        [lax.dynamic_slice_in_dim(each, me * rows_here, rows_here, axis=0) for each in scales]
    )
    grad_hidden, block_rows, gain_part = rows_call(
        summed, mine, state_w, hidden_in[:, 0], cotangent[:, 0], norm_gain[None, :],
        produced, my_scales,
    )
    gain_total = gain_call(tp_size, fsdp_size, gain_part)
    grad_gain, grad_skip, grad_conv, grad_bias, grad_sconv, grad_sbias, grad_in, grad_decay = (
        unpack_call(pack, state_sum, rate, heads)
    )
    return (
        block_rows[:, None],
        grad_hidden[:, None],
        gain_total.reshape(-1),
        grad_gate,
        grad_value,
        grad_state,
        grad_step,
        grad_conv,
        grad_bias.reshape(-1),
        grad_sconv,
        grad_sbias.reshape(-1),
        grad_in.reshape(-1),
        grad_decay.reshape(-1),
        grad_skip.reshape(-1),
        grad_gain.reshape(-1),
        grad_out,
    )


def solution(mesh):
    in_specs = (
        P(None, "fsdp", "tp", None), P(None, "fsdp", None), P(None, "fsdp", "tp", None), P(),
        P("fsdp", "tp"), P("fsdp", "tp"), P("fsdp", None), P("fsdp", "tp"), P(None, "tp"), P("tp"),
        P(), P(), P("tp"), P("tp"), P("tp"), P("tp"), P("tp", "fsdp"),
    )
    out_specs = (
        P(None, "fsdp", "tp", None), P(None, "fsdp", "tp", None), P(), P("fsdp", "tp"),
        P("fsdp", "tp"), P("fsdp", None), P("fsdp", "tp"), P(None, "tp"), P("tp"), P(), P(),
        P("tp"), P("tp"), P("tp"), P("tp"), P("tp", "fsdp"),
    )
    return jax.shard_map(local, mesh=mesh, in_specs=in_specs, out_specs=out_specs, check_vma=False)
```

```python
from functools import partial

import jax
import jax.numpy as jnp
from jax import lax
from jax.experimental import pallas as pl
from jax.experimental.pallas import tpu as pltpu
from jax.sharding import PartitionSpec as P

HEAD_DIM = 64
STATE = 128
CONV = 4
GROUP = 256
HALF = GROUP // 2
BLOCK = 256
PER_BLOCK = BLOCK // HEAD_DIM
HALO = 8
INNER = 4096
EPSILON = 1e-05
PRECISE = lax.Precision.HIGHEST
PARTS = 2
FORWARD_INS, FORWARD_OUTS = 16, 9
BACKWARD_INS, BACKWARD_OUTS = 23, 9
F32 = jnp.float32
BF16 = jnp.bfloat16


def mm(former, latter, precision=None):
    return jnp.dot(former, latter, preferred_element_type=F32, precision=precision)


def head_sums(values, place):
    high = values.astype(BF16)
    rest = values - high.astype(F32)
    middle = rest.astype(BF16)
    low = (rest - middle.astype(F32)).astype(BF16)
    return mm(high, place) + (mm(middle, place) + mm(low, place))


def mm_nt(former, latter):
    return lax.dot_general(
        former, latter, (((1,), (1,)), ((), ())), preferred_element_type=F32
    )


def mm_tn(former, latter):
    return lax.dot_general(
        former, latter, (((0,), (0,)), ((), ())), preferred_element_type=F32
    )


def iota(shape, axis):
    return lax.broadcasted_iota(jnp.int32, shape, axis)


def expand(columns):
    rows = columns.shape[0]
    lane = iota((rows, 128), 1)
    parts = []
    for pair in range(PER_BLOCK // 2):
        former = jnp.broadcast_to(columns[:, 2 * pair : 2 * pair + 1], (rows, 128))
        latter = jnp.broadcast_to(columns[:, 2 * pair + 1 : 2 * pair + 2], (rows, 128))
        parts.append(jnp.where(lane < HEAD_DIM, former, latter))
    return jnp.concatenate(parts, axis=1)


def lane_mask(head):
    lane = iota((1, BLOCK), 1)
    return ((lane // HEAD_DIM) == head).astype(F32).astype(BF16)


def spread(ref, values, blocks):
    for block in range(blocks):
        shift = (128 - PER_BLOCK * block) % 128
        ref[block] = pltpu.roll(values, shift, 1) if shift else values


def token_quantities(step_in, cums, cols, decay_rate):
    step = jnp.maximum(step_in, 0.0) + jnp.log1p(jnp.exp(-jnp.abs(step_in)))
    final = cums[GROUP - 1 : GROUP, :]
    entering = jnp.exp(cums) * cols[:, 6:7]
    fading = jnp.exp(final - cums) * cols[:, 7:8]
    retain = jnp.exp(final) * cols[0:1, 8:9]
    return step, entering, fading, retain


def shifted_values(buf, cols):
    moved = [buf[HALO : HALO + GROUP, :]]
    for offset in range(1, CONV):
        before = buf[HALO - offset : HALO - offset + GROUP, :]
        moved.append(jnp.where(cols[:, offset - 1 : offset] > 0.0, before, 0.0))
    return moved


def conv_of(moved, taps, bias):
    total = bias + taps[0:1, :] * moved[0]
    for offset in range(1, CONV):
        total = total + taps[offset : offset + 1, :] * moved[offset]
    return total


MESH = pl.DeviceIdType.MESH


def part_of(ref, at, size, axis):
    if axis == 0:
        return ref.at[pl.ds(pl.multiple_of(at * size, size), size), :]
    if axis == 1:
        return ref.at[:, pl.ds(pl.multiple_of(at * size, size), size)]
    return ref.at[at]


def greet(devices):
    barrier = pltpu.get_barrier_semaphore()
    for device in devices:
        pl.semaphore_signal(barrier, inc=1, device_id=device, device_id_type=MESH)
    pl.semaphore_wait(barrier, len(devices))


def remote_copy(source, target, sends, receives, device):
    return pltpu.make_async_remote_copy(
        src_ref=source, dst_ref=target, send_sem=sends, recv_sem=receives,
        device_id=device, device_id_type=MESH,
    )


class LineScatter:
    def __init__(self, size, source, own, slots, last, own_sem, send_sem, recv_sem, last_sem):
        self.size, self.source, self.own, self.slots, self.last = size, source, own, slots, last
        self.own_sem, self.send_sem, self.recv_sem, self.last_sem = own_sem, send_sem, recv_sem, last_sem
        self.me, self.column = lax.axis_index("tp"), lax.axis_index("fsdp")
        self.rows = last.shape[0]

    @staticmethod
    def scratch(size, rows, width):
        hops = size - 1
        return [
            pltpu.VMEM((2, hops, rows, width), BF16), pltpu.VMEM((2, hops, rows, width), BF16),
            pltpu.VMEM((rows, width), BF16), pltpu.SemaphoreType.DMA((2, hops)),
            pltpu.SemaphoreType.DMA((2, hops, PARTS)), pltpu.SemaphoreType.DMA((2, hops, PARTS)),
            pltpu.SemaphoreType.DMA((1,)),
        ]

    def place(self, flow):
        return self.me if flow == 0 else self.size - 1 - self.me

    def part(self, part):
        rows = self.rows // PARTS
        return pl.ds(part * rows, rows)

    def local(self, flow, hop):
        block = self.size - 1 - hop + self.place(flow)
        if flow:
            block = self.size - 1 - block
        at = pl.multiple_of(block * self.rows, self.rows)
        return pltpu.make_async_copy(
            self.source.at[pl.ds(at, self.rows), :], self.own.at[flow, hop], self.own_sem.at[flow, hop]
        )

    def final(self):
        at = pl.multiple_of(self.me * self.rows, self.rows)
        return pltpu.make_async_copy(
            self.source.at[pl.ds(at, self.rows), :], self.last, self.last_sem.at[0]
        )

    def sending(self, flow, hop, part):
        neighbour = self.me + 1 if flow == 0 else self.me - 1
        neighbour = jnp.clip(neighbour, 0, self.size - 1)
        return remote_copy(
            self.own.at[flow, hop, self.part(part), :], self.slots.at[flow, hop, self.part(part), :],
            self.send_sem.at[flow, hop, part], self.recv_sem.at[flow, hop, part],
            (self.column, neighbour),
        )

    def begin(self):
        self.final().start()
        for hop in range(self.size - 1):
            for flow in range(2):

                @pl.when(self.place(flow) <= hop)
                def _():
                    self.local(flow, hop).start()

    def hop(self, hop, part):
        rows = self.part(part)
        for flow in range(2):
            place = self.place(flow)

            @pl.when(place <= hop)
            def _():
                if part == 0:
                    self.local(flow, hop).wait()
                if hop > 0:

                    @pl.when(place >= 1)
                    def _():
                        self.sending(flow, hop - 1, part).wait_recv()
                        total = self.own[flow, hop, rows, :].astype(F32)
                        total = total + self.slots[flow, hop - 1, rows, :].astype(F32)
                        self.own[flow, hop, rows, :] = total.astype(BF16)

                self.sending(flow, hop, part).start()

    def end(self, out, part):
        hops = self.size - 1
        rows = self.part(part)
        if part == 0:
            self.final().wait()
        out[rows, :] = self.last[rows, :].astype(F32)
        for flow in range(2):

            @pl.when(self.place(flow) >= 1)
            def _():
                self.sending(flow, hops - 1, part).wait_recv()
                out[rows, :] += self.slots[flow, hops - 1, rows, :].astype(F32)

        for hop in range(hops):
            for flow in range(2):

                @pl.when(self.place(flow) <= hop)
                def _():
                    self.sending(flow, hop, part).wait_send()


class LineGather:
    def __init__(self, size, source, target, own_sem, send_sem, recv_sem):
        self.size, self.source, self.target = size, source, target
        self.own_sem, self.send_sem, self.recv_sem = own_sem, send_sem, recv_sem
        self.me, self.column = lax.axis_index("tp"), lax.axis_index("fsdp")
        self.rows = source.shape[0]

    @staticmethod
    def scratch(size):
        return [
            pltpu.SemaphoreType.DMA((1,)), pltpu.SemaphoreType.DMA((2, size - 1, PARTS)),
            pltpu.SemaphoreType.DMA((2, size - 1, PARTS)),
        ]

    def place(self, flow):
        return self.me if flow == 0 else self.size - 1 - self.me

    def block(self, at):
        at = pl.multiple_of(jnp.clip(at, 0, self.size - 1) * self.rows, self.rows)
        return self.target.at[pl.ds(at, self.rows), :]

    def sending(self, flow, hop, part):
        neighbour = self.me + 1 if flow == 0 else self.me - 1
        neighbour = jnp.clip(neighbour, 0, self.size - 1)
        rows = pl.ds(part * (self.rows // PARTS), self.rows // PARTS)
        block = self.block(self.me - hop if flow == 0 else self.me + hop).at[rows, :]
        return remote_copy(
            self.source.at[rows, :] if hop == 0 else block, block, self.send_sem.at[flow, hop, part],
            self.recv_sem.at[flow, hop, part], (self.column, neighbour),
        )

    def local(self):
        return pltpu.make_async_copy(self.source, self.block(self.me), self.own_sem.at[0])

    def hop(self, hop, part):
        if hop == 0 and part == 0:
            self.local().start()
        for flow in range(2):
            place = self.place(flow)
            if hop > 0:

                @pl.when(place >= hop)
                def _():
                    self.sending(flow, hop - 1, part).wait_recv()

            if hop < self.size - 1:

                @pl.when((place >= hop) & (place < self.size - 1))
                def _():
                    self.sending(flow, hop, part).start()

    def end(self, part):
        self.hop(self.size - 1, part)
        if part == 0:
            self.local().wait()
        for hop in range(self.size - 1):
            for flow in range(2):
                place = self.place(flow)

                @pl.when((place >= hop) & (place < self.size - 1))
                def _():
                    self.sending(flow, hop, part).wait_send()


def run_line(step, steps, scatter, gather, out, early):
    size = (scatter or gather).size
    first = 1 if scatter and gather else 0
    actions = [[] for _ in range(PARTS * (size + first))]
    for part in range(PARTS):
        if gather:
            for hop in range(size - 1):
                actions[PARTS * hop + part].append(partial(gather.hop, hop, part))
            actions[PARTS * (size - 1) + part].append(partial(gather.end, part))
        if scatter:
            for hop in range(size - 1):
                actions[PARTS * (first + hop) + part].append(partial(scatter.hop, hop, part))
            actions[PARTS * (first + size - 1) + part].append(partial(scatter.end, out, part))
    if scatter:
        actions[0].insert(0, scatter.begin)
    for at in sorted(set(steps)):
        if (at == 0) != early:
            continue
        todo = [action for when, each in zip(steps, actions) if when == at for action in each]

        @pl.when(step == at)
        def _():
            for action in todo:
                action()


class Hosted:
    def __init__(self, size, scatter=None, gather=None):
        self.size, self.scatter, self.gather = size, scatter, gather

    def operands(self):
        return [each for each in (self.scatter, self.gather) if each is not None]

    def in_specs(self):
        return [pl.BlockSpec(memory_space=pl.ANY)] * len(self.operands())

    def outs(self):
        shapes, specs = [], []
        if self.scatter is not None:
            rows, width = self.scatter.shape[0] // self.size, self.scatter.shape[1]
            shapes.append(shape((rows, width)))
            specs.append(pl.BlockSpec((rows, width), lambda g, j: (0, 0)))
        if self.gather is not None:
            rows, width = self.gather.shape
            shapes.append(shape((rows * self.size, width), BF16))
            specs.append(pl.BlockSpec(memory_space=pl.ANY))
        return specs, shapes

    def scratch(self):
        needed = []
        if self.scatter is not None:
            rows, width = self.scatter.shape[0] // self.size, self.scatter.shape[1]
            needed += LineScatter.scratch(self.size, rows, width)
        if self.gather is not None:
            needed += LineGather.scratch(self.size)
        return needed

    def wrap(self, body, ins, outs, pace, resident):
        has_scatter, has_gather = self.scatter is not None, self.gather is not None
        hosts = has_scatter + has_gather
        size, spare, kept = self.size, len(self.scratch()), len(resident) + 1

        def kernel(*refs):
            refs, stored = refs[: len(refs) - kept], refs[len(refs) - kept :]
            tail = refs[len(refs) - spare :]
            sources, targets = refs[ins : ins + hosts], refs[ins + hosts + outs : ins + outs + 2 * hosts]
            step = pl.program_id(0) * pl.num_programs(1) + pl.program_id(1)
            me, column = lax.axis_index("tp"), lax.axis_index("fsdp")
            operands = list(refs[:ins])
            loads = []
            for at, (which, _, need) in enumerate(resident):
                copy = pltpu.make_async_copy(operands[which], stored[at], stored[-1].at[at])
                operands[which] = stored[at]
                loads.append((copy, need))

            @pl.when(step == 0)
            def _():
                for copy, _ in loads:
                    copy.start()
                if hosts:
                    greet([(column, lax.rem(me + hop, size)) for hop in range(1, size)])

            if hosts:
                scatter = LineScatter(size, sources[0], *tail[:7]) if has_scatter else None
                gather = LineGather(size, sources[-1], targets[-1], *tail[-3:]) if has_gather else None
                run_line(step, pace, scatter, gather, targets[0], True)
            for when in sorted(set(need for _, need in loads)):

                @pl.when(step == when)
                def _():
                    for copy, need in loads:
                        if need == when:
                            copy.wait()

            body(
                *operands, *refs[ins + hosts : ins + hosts + outs],
                *refs[ins + outs + 2 * hosts : len(refs) - spare],
            )
            if hosts:
                run_line(step, pace, scatter, gather, targets[0], False)

        return kernel


def resident_scratch(resident):
    return [pltpu.VMEM(array.shape, array.dtype) for _, array, _ in resident] + [
        pltpu.SemaphoreType.DMA((len(resident),))
    ]


def forward_kernel(
    in_ref, gate_w, value_w, state_w, step_w, taps_ref, bias_ref, staps_ref, sbias_ref,
    step_bias_ref, rate_ref, skip_ref, cols_ref, seg_ref, out_w, gain_ref,
    gate_out, value_out, mixed_out, bc_out, sraw_out, stepin_out, cums_out, held_out, made_out,
    vbuf, sbuf, gram_s, b_t, c_s, step_s, ent_s, fade_s, cums_s, cums_t, keep_s, hidden, made,
):
    g, j = pl.program_id(0), pl.program_id(1)
    blocks = pl.num_programs(1)
    nblocks = hidden.shape[0]
    rows = in_ref[...]
    cols = cols_ref[...]

    @pl.when(j == 0)
    def _():
        sbuf[0:HALO, :] = sbuf[GROUP : GROUP + HALO, :]
        raw = mm(rows, state_w[...])
        sbuf[HALO : HALO + GROUP, :] = raw
        sraw_out[...] = raw
        conv = conv_of(shifted_values(sbuf, cols), staps_ref[...], sbias_ref[...])
        bc = (conv * jax.nn.sigmoid(conv)).astype(BF16)
        bc_out[...] = bc
        b_low, c_low = bc[:, :STATE], bc[:, STATE:]
        b_t[...] = jnp.transpose(b_low.astype(F32)).astype(BF16)
        c_s[...] = c_low
        step_in = mm(rows, step_w[...]) + step_bias_ref[...]
        stepin_out[...] = step_in
        step = jnp.maximum(step_in, 0.0) + jnp.log1p(jnp.exp(-jnp.abs(step_in)))
        at_row, at_col = iota((GROUP, GROUP), 0), iota((GROUP, GROUP), 1)
        lower = (at_row >= at_col).astype(F32)
        cums = mm(lower, step * rate_ref[...], PRECISE)
        cums_out[...] = cums
        step, entering, fading, retain = token_quantities(step_in, cums, cols, rate_ref[...])
        spread(step_s, step, nblocks)
        spread(ent_s, entering, nblocks)
        spread(fade_s, fading, nblocks)
        spread(cums_s, cums, nblocks)
        spread(keep_s, jnp.broadcast_to(retain, (8, 128)), nblocks)
        cums_t[...] = jnp.transpose(cums)
        within = (at_row >= at_col) & (cols[:, 9:10] == seg_ref[...])
        gram_s[...] = jnp.where(within, mm_nt(c_low, b_low), 0.0)

    at = pl.multiple_of(j * BLOCK, BLOCK)
    gate = mm(rows, gate_w[:, pl.ds(at, BLOCK)])
    gate_out[...] = gate.astype(BF16)
    value = mm(rows, value_w[:, pl.ds(at, BLOCK)])
    value_out[...] = value
    mine = vbuf.at[j]
    mine[0:HALO, :] = mine[GROUP : GROUP + HALO, :]
    mine[HALO : HALO + GROUP, :] = value
    conv = conv_of(shifted_values(mine, cols), taps_ref[...], bias_ref[...])
    x_low = (conv * jax.nn.sigmoid(conv)).astype(BF16)
    x_float = x_low.astype(F32)
    scaled_float = expand(step_s[j]) * x_float
    scaled = scaled_float.astype(BF16)

    @pl.when(g == 0)
    def _():
        hidden[j] = jnp.zeros((STATE, BLOCK), F32)

    state = hidden[j]
    state_low = state.astype(BF16)
    held_out[0] = state_low
    total = expand(ent_s[j]) * mm(c_s[...], state_low)
    weighted = (expand(fade_s[j]) * scaled.astype(F32)).astype(BF16)
    hidden[j] = expand(keep_s[j])[0:1, :] * state + mm(b_t[...], weighted)
    cums_here = cums_s[j]
    top = jnp.zeros((HALF, BLOCK), F32)
    bottom = jnp.zeros((HALF, BLOCK), F32)
    for i in range(PER_BLOCK):
        to = cums_here[:, i : i + 1]
        frm = cums_t[pl.ds(j * PER_BLOCK + i, 1), :]
        only = scaled * lane_mask(i)
        decay = jnp.exp(jnp.minimum(to[:HALF] - frm[:, :HALF], 0.0))
        top = top + mm((gram_s[:HALF, :HALF] * decay).astype(BF16), only[:HALF])
        decay = jnp.exp(jnp.minimum(to[HALF:] - frm, 0.0))
        bottom = bottom + mm((gram_s[HALF:, :] * decay).astype(BF16), only)
    mixed = total + jnp.concatenate([top, bottom], axis=0) + skip_ref[...] * x_float
    mixed_out[...] = mixed
    scaled_gate = (mixed * (gate * jax.nn.sigmoid(gate)) * gain_ref[...]).astype(BF16)

    @pl.when(j == 0)
    def _():
        made[...] = mm(scaled_gate, out_w[pl.ds(at, BLOCK), :])

    @pl.when(j > 0)
    def _():
        made[...] += mm(scaled_gate, out_w[pl.ds(at, BLOCK), :])

    @pl.when(j == blocks - 1)
    def _():
        made_out[...] = made[...].astype(BF16)


def backward_kernel(
    tp_size, cot_ref, out_w, gate_rows, mixed_rows, gain_row,
    gate_ref, value_ref, before_ref, mixed_ref, bc_ref, stepin_ref, cums_ref, held_ref,
    gate_w, value_w, step_w, taps_ref, bias_ref, rate_ref, skip_ref, gain_ref, cols_ref, seg_ref,
    branch_out, lowgate_out, lowvalue_out, lowstep_out, gbc_out, gin_out, small_out, sums_out, stats_out,
    vbuf, gcbuf, gram_s, dgram, b_s, c_t, step_s, ent_s, fade_s, cums_s, cums_t, keep_s, grad_state,
    gin, gb_s, gc_s, u_s, v_s, fin_s, small_s, sums_s,
    branch_s, rowsum_s, slots_s, turn_s, stats_s, swap_send, swap_recv,
):
    g, j = pl.program_id(0) - 1, pl.program_id(1)
    groups, blocks = pl.num_programs(0) - 1, pl.num_programs(1)

    @pl.when(g < 0)
    def _():
        row_sums(
            tp_size, cot_ref, out_w, gate_rows, mixed_rows, gain_row,
            branch_s, rowsum_s, slots_s, swap_send, swap_recv,
        )

    scales = partial(
        row_scales, tp_size, gain_row.shape[1] * tp_size, rowsum_s, slots_s, turn_s, swap_send,
        swap_recv, stats_s, stats_out,
    )

    @pl.when(g >= 0)
    def _():
        backward_step(
            g, j, groups, blocks, gate_ref, value_ref, before_ref, mixed_ref,
            bc_ref, stepin_ref, cums_ref, held_ref,
            gate_w, value_w, step_w, taps_ref, bias_ref, rate_ref, skip_ref, gain_ref, cols_ref, seg_ref,
            branch_out, lowgate_out, lowvalue_out, lowstep_out, gbc_out, gin_out, small_out, sums_out,
            vbuf, gcbuf, gram_s, dgram, b_s, c_t, step_s, ent_s, fade_s, cums_s, cums_t, keep_s,
            grad_state, gin, gb_s, gc_s, u_s, v_s, fin_s, small_s, sums_s, branch_s, stats_s, scales,
        )


def row_sums(
    tp_size, cot_ref, out_w, gate_rows, mixed_rows, gain_row,
    branch_s, rowsum_s, slots_s, swap_send, swap_recv,
):
    step, groups = pl.program_id(1), pl.num_programs(1)
    me, column = lax.axis_index("tp"), lax.axis_index("fsdp")
    grad = mm_nt(cot_ref[...], out_w[...])
    branch_s[step] = grad.astype(BF16)
    gate = gate_rows[...].astype(F32)
    gated = mixed_rows[...] * (gate * jax.nn.sigmoid(gate))
    squares = jnp.sum(gated * gated, axis=1, keepdims=True)
    inner = jnp.sum(grad * gain_row[...] * gated, axis=1, keepdims=True)
    lane = iota((GROUP, 128), 1)
    both = jnp.where(lane == 0, squares, jnp.where(lane == 1, inner, 0.0))
    rowsum_s[step] = jnp.transpose(both)[:8]

    @pl.when(step == groups - 1)
    def _():
        slots_s[me] = rowsum_s[...]
        for copy in row_swaps(tp_size, rowsum_s, slots_s, swap_send, swap_recv):
            copy.start()


def row_swaps(tp_size, rowsum_s, slots_s, swap_send, swap_recv):
    me, column = lax.axis_index("tp"), lax.axis_index("fsdp")
    return [
        remote_copy(
            rowsum_s, slots_s.at[me], swap_send.at[hop - 1], swap_recv.at[hop - 1],
            (column, lax.rem(me + hop, tp_size)),
        )
        for hop in range(1, tp_size)
    ]


def row_scales(tp_size, total_inner, rowsum_s, slots_s, turn_s, swap_send, swap_recv, stats_s, stats_out):
    for copy in row_swaps(tp_size, rowsum_s, slots_s, swap_send, swap_recv):
        copy.wait()
    total = slots_s[0]
    for at in range(1, tp_size):
        total = total + slots_s[at]
    turn_s[...] = jnp.zeros(turn_s.shape, F32)
    scale = lax.rsqrt(total[:, 0:1, :] / total_inner + EPSILON)
    turn_s[:, 0:1, :] = scale
    turn_s[:, 1:2, :] = scale * scale * scale * (total[:, 1:2, :] / total_inner)
    for group in range(turn_s.shape[0]):
        stats_s[group * GROUP : (group + 1) * GROUP, :] = jnp.transpose(turn_s[group])
    rows = stats_out.shape[0]
    stats_out[...] = stats_s[pl.ds(pl.multiple_of(lax.axis_index("tp") * rows, rows), rows), :]


def backward_step(
    g, j, groups, blocks, gate_ref, value_ref, before_ref, mixed_ref,
    bc_ref, stepin_ref, cums_ref, held_ref,
    gate_w, value_w, step_w, taps_ref, bias_ref, rate_ref, skip_ref, gain_ref, cols_ref, seg_ref,
    branch_out, lowgate_out, lowvalue_out, lowstep_out, gbc_out, gin_out, small_out, sums_out,
    vbuf, gcbuf, gram_s, dgram, b_s, c_t, step_s, ent_s, fade_s, cums_s, cums_t, keep_s,
    grad_state, gin, gb_s, gc_s, u_s, v_s, fin_s, small_s, sums_s, branch_s, stats_ref, scales,
):
    group = groups - 1 - g
    nblocks = grad_state.shape[0]
    cols = cols_ref[...]
    at_row, at_col = iota((GROUP, GROUP), 0), iota((GROUP, GROUP), 1)

    @pl.when((g == 0) & (j == 0))
    def _():
        grad_state[...] = jnp.zeros(grad_state.shape, F32)
        small_s[...] = jnp.zeros(small_s.shape, F32)
        sums_s[...] = jnp.zeros(sums_s.shape, F32)
        gcbuf[...] = jnp.zeros(gcbuf.shape, F32)

    @pl.when(j == 0)
    def _():
        bc = bc_ref[...]
        b_low, c_low = bc[:, :STATE], bc[:, STATE:]
        b_s[...] = b_low
        c_t[...] = jnp.transpose(c_low.astype(F32)).astype(BF16)
        cums = cums_ref[...]
        step, entering, fading, retain = token_quantities(stepin_ref[...], cums, cols, rate_ref[...])
        spread(step_s, step, nblocks)
        spread(ent_s, entering, nblocks)
        spread(fade_s, fading, nblocks)
        spread(cums_s, cums, nblocks)
        spread(keep_s, jnp.broadcast_to(retain, (8, 128)), nblocks)
        cums_t[...] = jnp.transpose(cums)
        within = (at_row <= at_col) & (cols[:, 9:10] == seg_ref[...])
        gram_s[...] = jnp.where(within, mm_nt(b_low, c_low), 0.0)
        dgram[...] = jnp.zeros(dgram.shape, F32)
        gin[...] = jnp.zeros(gin.shape, F32)
        gb_s[...] = jnp.zeros(gb_s.shape, F32)
        gc_s[...] = jnp.zeros(gc_s.shape, F32)
        u_s[...] = jnp.zeros(u_s.shape, F32)
        v_s[...] = jnp.zeros(v_s.shape, F32)
        fin_s[...] = jnp.zeros(fin_s.shape, F32)

    @pl.when((g == 0) & (j == 0))
    def _():
        scales()

    at = pl.multiple_of(j * BLOCK, BLOCK)
    gate, mixed = gate_ref[...].astype(F32), mixed_ref[...]
    grad = branch_s[group, :, pl.ds(at, BLOCK)].astype(F32)
    gain, skip, taps = gain_ref[...], skip_ref[...], taps_ref[...]
    stats = stats_ref[pl.ds(pl.multiple_of(group * GROUP, GROUP), GROUP), :]
    scale, inner = stats[:, 0:1], stats[:, 1:2]
    sig = jax.nn.sigmoid(gate)
    act = gate * sig
    gated = mixed * act
    scaled_gated = gated * scale
    branch_out[...] = (scaled_gated * gain).astype(BF16)
    grad_gain = jnp.sum(grad * scaled_gated, axis=0, keepdims=True)
    grad_gated = scale * (grad * gain) - gated * inner
    grad_mixed = grad_gated * act
    low_gate = (grad_gated * mixed * (sig * (1.0 + gate * (1.0 - sig)))).astype(BF16)
    lowgate_out[...] = low_gate

    vbuf[0:HALO, :] = before_ref[...]
    vbuf[HALO : HALO + GROUP, :] = value_ref[...]
    moved = shifted_values(vbuf, cols)
    conv = conv_of(moved, taps, bias_ref[...])
    sig = jax.nn.sigmoid(conv)
    x_float = (conv * sig).astype(BF16).astype(F32)
    slope = sig * (1.0 + conv * (1.0 - sig))
    step_wide = expand(step_s[j])
    fade_wide = expand(fade_s[j])
    scaled = (step_wide * x_float).astype(BF16)
    scaled_float = scaled.astype(F32)
    grad_skip = jnp.sum(grad_mixed * x_float, axis=0, keepdims=True)
    grad_scan = grad_mixed.astype(BF16)
    grad_scan_float = grad_scan.astype(F32)
    scanned = mixed - skip * x_float

    own = grad_state[j]
    state_low = held_ref[0]
    own_low = own.astype(BF16)
    grad_weighted = mm(b_s[...], own_low)
    weighted = (fade_wide * scaled_float).astype(BF16)
    entered = (expand(ent_s[j]) * grad_scan_float).astype(BF16)
    gb_s[...] += mm_nt(weighted, own_low)
    gc_s[...] += mm_nt(entered, state_low)
    keep_wide = expand(keep_s[j])[0:1, :]
    kept = keep_wide * jnp.sum(state_low.astype(F32) * own, axis=0, keepdims=True)
    grad_state[j] = keep_wide * own + mm(c_t[...], entered)

    cums_here = cums_s[j]
    top = jnp.zeros((HALF, BLOCK), F32)
    bottom = jnp.zeros((HALF, BLOCK), F32)
    dtop = dgram[:HALF, :]
    dbottom = dgram[HALF:, HALF:]
    for i in range(PER_BLOCK):
        frm = cums_here[:, i : i + 1]
        to = cums_t[pl.ds(j * PER_BLOCK + i, 1), :]
        mask = lane_mask(i)
        only_grad = grad_scan * mask
        only = scaled * mask
        decay = jnp.exp(jnp.minimum(to - frm[:HALF], 0.0))
        top = top + mm((gram_s[:HALF, :] * decay).astype(BF16), only_grad)
        dtop = dtop + mm_nt(only[:HALF], grad_scan) * decay
        decay = jnp.exp(jnp.minimum(to[:, HALF:] - frm[HALF:], 0.0))
        bottom = bottom + mm((gram_s[HALF:, HALF:] * decay).astype(BF16), only_grad[HALF:])
        dbottom = dbottom + mm_nt(only[HALF:], grad_scan[HALF:]) * decay
    dgram[:HALF, :] = dtop
    dgram[HALF:, HALF:] = dbottom
    faded = fade_wide * grad_weighted
    through = jnp.concatenate([top, bottom], axis=0) + faded
    column = scaled_float * through
    final = kept + jnp.sum(scaled_float * faded, axis=0, keepdims=True)
    place = iota((BLOCK, 128), 1) == j * PER_BLOCK + iota((BLOCK, 128), 0) // HEAD_DIM
    place = place.astype(F32).astype(BF16)
    u_s[...] += head_sums(grad_scan_float * scanned - column, place)
    v_s[...] += head_sums(column, place)
    fin_s[...] += head_sums(jnp.broadcast_to(final, (8, BLOCK)), place)

    grad_conv = (step_wide * through + skip * grad_mixed) * slope
    after = gcbuf.at[j]
    after[GROUP : GROUP + HALO, :] = after[0:HALO, :]
    after[0:GROUP, :] = grad_conv
    grad_value = taps[0:1, :] * grad_conv
    for offset in range(1, CONV):
        up = jnp.where(cols[:, 2 + offset : 3 + offset] > 0.0, after[offset : offset + GROUP, :], 0.0)
        grad_value = grad_value + taps[offset : offset + 1, :] * up
    low_value = grad_value.astype(BF16)
    lowvalue_out[...] = low_value
    gin[...] += mm_nt(low_gate, gate_w[:, pl.ds(at, BLOCK)]) + mm_nt(low_value, value_w[:, pl.ds(at, BLOCK)])
    lines = [grad_gain, grad_skip]
    lines += [jnp.sum(grad_conv * moved[offset], axis=0, keepdims=True) for offset in range(CONV)]
    lines += [jnp.sum(grad_conv, axis=0, keepdims=True)]
    for at_line, line in enumerate(lines):
        small_s[j, at_line : at_line + 1, :] += line

    @pl.when(g == groups - 1)
    def _():
        small_out[:, pl.ds(at, BLOCK)] = small_s[j]

    @pl.when(j == blocks - 1)
    def _():
        bc = bc_ref[...]
        within = (at_row <= at_col) & (cols[:, 9:10] == seg_ref[...])
        dg = jnp.where(within, dgram[...], 0.0)
        grad_b = gb_s[...] + mm(dg.astype(BF16), bc[:, STATE:])
        grad_c = gc_s[...] + mm(jnp.transpose(dg).astype(BF16), bc[:, :STATE])
        gbc_out[:, :STATE] = grad_b.astype(BF16)
        gbc_out[:, STATE:] = grad_c.astype(BF16)
        last = iota((GROUP, 128), 0) == GROUP - 1
        grad_cums = u_s[...] + jnp.where(last, fin_s[0:1, :], 0.0)
        upper = (at_row <= at_col).astype(F32)
        grad_a = mm(upper, grad_cums, PRECISE)
        step_in = stepin_ref[...]
        step = jnp.maximum(step_in, 0.0) + jnp.log1p(jnp.exp(-jnp.abs(step_in)))
        sig_in = jax.nn.sigmoid(step_in)
        ratio = jnp.where(step_in < -15.0, 1.0, sig_in / step)
        grad_step = v_s[...] * ratio + grad_a * rate_ref[...] * sig_in
        low_step = grad_step.astype(BF16)
        lowstep_out[...] = low_step
        sums_s[0:1, :] += jnp.sum(grad_step, axis=0, keepdims=True)
        sums_s[1:2, :] += jnp.sum(grad_a * step, axis=0, keepdims=True)
        sums_out[...] = sums_s[...]
        gin_out[...] = (gin[...] + mm_nt(low_step, step_w[...])).astype(BF16)


def shape(dims, kind=F32):
    return jax.ShapeDtypeStruct(dims, kind)


def params(collective=None):
    extra = {} if collective is None else dict(collective_id=collective, has_side_effects=True)
    return pltpu.CompilerParams(
        dimension_semantics=("arbitrary", "arbitrary"), vmem_limit_bytes=60 << 20, **extra
    )


def whole(array):
    return pl.BlockSpec(
        array.shape, lambda g, j: (0,) * array.ndim, pipeline_mode=pl.Buffered(1)
    )


def forward_call(inputs, weights, vectors, gain, cols, seg_line, hosted, pace):
    gate_w, value_w, state_w, step_w, out_w = weights
    taps, bias, staps, sbias, step_bias, rate, skip = vectors
    length, model = inputs.shape
    inner = gate_w.shape[1]
    groups, blocks = length // GROUP, inner // BLOCK
    wide = pl.BlockSpec((GROUP, BLOCK), lambda g, j: (g, j))
    line = lambda rows: pl.BlockSpec((rows, BLOCK), lambda g, j: (0, j))
    rows_of = lambda width: pl.BlockSpec((GROUP, width), lambda g, j: (g, 0))
    specs, shapes = hosted.outs()
    hbm = pl.BlockSpec(memory_space=pl.ANY)
    resident = [(1, gate_w, 0), (2, value_w, 0), (3, state_w, 0), (4, step_w, 0), (14, out_w, 0)]
    return pl.pallas_call(
        hosted.wrap(forward_kernel, FORWARD_INS, FORWARD_OUTS, pace, resident),
        grid=(groups, blocks),
        in_specs=[
            rows_of(model), hbm, hbm, hbm, hbm,
            line(CONV), line(1), whole(staps), whole(sbias), whole(step_bias), whole(rate), line(1),
            rows_of(cols.shape[1]), pl.BlockSpec((1, GROUP), lambda g, j: (0, g)),
            hbm, line(1),
        ] + hosted.in_specs(),
        out_specs=[
            wide, wide, wide, rows_of(2 * STATE), rows_of(2 * STATE), rows_of(128), rows_of(128),
            pl.BlockSpec((1, STATE, BLOCK), lambda g, j: (g, 0, j)), rows_of(model),
        ] + specs,
        out_shape=[
            shape((length, inner), BF16), shape((length, inner)), shape((length, inner)),
            shape((length, 2 * STATE), BF16), shape((length, 2 * STATE)), shape((length, 128)),
            shape((length, 128)), shape((groups, STATE, inner), BF16), shape((length, model), BF16),
        ] + shapes,
        scratch_shapes=[
            pltpu.VMEM((blocks, GROUP + HALO, BLOCK), F32),
            pltpu.VMEM((GROUP + HALO, 2 * STATE), F32),
            pltpu.VMEM((GROUP, GROUP), F32),
            pltpu.VMEM((STATE, GROUP), BF16),
            pltpu.VMEM((GROUP, STATE), BF16),
            pltpu.VMEM((blocks, GROUP, 128), F32),
            pltpu.VMEM((blocks, GROUP, 128), F32),
            pltpu.VMEM((blocks, GROUP, 128), F32),
            pltpu.VMEM((blocks, GROUP, 128), F32),
            pltpu.VMEM((128, GROUP), F32),
            pltpu.VMEM((blocks, 8, 128), F32),
            pltpu.VMEM((blocks, STATE, BLOCK), F32),
            pltpu.VMEM((GROUP, model), F32),
        ] + hosted.scratch() + resident_scratch(resident),
        compiler_params=params(2 if hosted.operands() else None),
        cost_estimate=pl.CostEstimate(
            flops=2 * length * model * (3 * inner + 512), bytes_accessed=40 << 20, transcendentals=0
        ),
        name="ssd_forward",
    )(
        inputs, gate_w, value_w, state_w, step_w, taps, bias, staps, sbias, step_bias, rate, skip,
        cols, seg_line, out_w, gain, *hosted.operands(),
    )


def backward_call(saved, cotan, weights, vectors, gain, cols, seg_line, hosted, pace, collective):
    gate_raw, value_raw, mixed, bc, _, step_in, cums, held, _ = saved
    gate_w, value_w, step_w, out_w = weights
    taps, bias, rate, skip = vectors
    length, inner = gate_raw.shape
    model, tp_size = gate_w.shape[0], hosted.size
    specs, shapes = hosted.outs()
    groups, blocks = length // GROUP, inner // BLOCK
    assert groups == blocks
    last = groups - 1
    hbm = pl.BlockSpec(memory_space=pl.ANY)
    resident = [(1, out_w, 0), (13, gate_w, blocks), (14, value_w, blocks), (15, step_w, blocks)]
    row = lambda g: last - jnp.maximum(g - 1, 0)
    column = lambda g, j: jnp.where(g == 0, 0, j)
    wide = pl.BlockSpec((GROUP, BLOCK), lambda g, j: (row(g), column(g, j)))
    line = lambda rows: pl.BlockSpec((rows, BLOCK), lambda g, j: (0, column(g, j)))
    rows_of = lambda width: pl.BlockSpec((GROUP, width), lambda g, j: (row(g), 0))
    first = lambda width: pl.BlockSpec((GROUP, width), lambda g, j: (jnp.where(g == 0, j, last), 0))
    steps = GROUP // HALO
    before = pl.BlockSpec(
        (HALO, BLOCK), lambda g, j: (jnp.maximum(row(g) * steps - 1, 0), column(g, j))
    )
    return pl.pallas_call(
        hosted.wrap(partial(backward_kernel, tp_size), BACKWARD_INS, BACKWARD_OUTS, pace, resident),
        grid=(groups + 1, blocks),
        in_specs=[
            first(model), hbm, first(inner), first(inner), whole(gain),
            wide, wide, before, wide, rows_of(2 * STATE), rows_of(128), rows_of(128),
            pl.BlockSpec((1, STATE, BLOCK), lambda g, j: (row(g), 0, column(g, j))),
            hbm, hbm, hbm,
            line(CONV), line(1), whole(rate), line(1), line(1),
            rows_of(cols.shape[1]), pl.BlockSpec((1, GROUP), lambda g, j: (0, row(g))),
        ] + hosted.in_specs(),
        out_specs=[
            wide, wide, wide, rows_of(128), rows_of(2 * STATE),
            rows_of(model), pl.BlockSpec((8, inner), lambda g, j: (0, 0)), pl.BlockSpec((8, 128), lambda g, j: (0, 0)),
            pl.BlockSpec((length // tp_size, 128), lambda g, j: (0, 0)),
        ] + specs,
        out_shape=[
            shape((length, inner), BF16), shape((length, inner), BF16), shape((length, inner), BF16),
            shape((length, 128), BF16), shape((length, 2 * STATE), BF16),
            shape((length, model), BF16), shape((8, inner)), shape((8, 128)),
            shape((length // tp_size, 128)),
        ] + shapes,
        scratch_shapes=[
            pltpu.VMEM((GROUP + HALO, BLOCK), F32),
            pltpu.VMEM((blocks, GROUP + HALO, BLOCK), F32),
            pltpu.VMEM((GROUP, GROUP), F32),
            pltpu.VMEM((GROUP, GROUP), F32),
            pltpu.VMEM((GROUP, STATE), BF16),
            pltpu.VMEM((STATE, GROUP), BF16),
            pltpu.VMEM((blocks, GROUP, 128), F32),
            pltpu.VMEM((blocks, GROUP, 128), F32),
            pltpu.VMEM((blocks, GROUP, 128), F32),
            pltpu.VMEM((blocks, GROUP, 128), F32),
            pltpu.VMEM((128, GROUP), F32),
            pltpu.VMEM((blocks, 8, 128), F32),
            pltpu.VMEM((blocks, STATE, BLOCK), F32),
            pltpu.VMEM((GROUP, model), F32),
            pltpu.VMEM((GROUP, STATE), F32),
            pltpu.VMEM((GROUP, STATE), F32),
            pltpu.VMEM((GROUP, 128), F32),
            pltpu.VMEM((GROUP, 128), F32),
            pltpu.VMEM((8, 128), F32),
            pltpu.VMEM((blocks, 8, BLOCK), F32),
            pltpu.VMEM((8, 128), F32),
            pltpu.VMEM((groups, GROUP, inner), BF16),
            pltpu.VMEM((groups, 8, GROUP), F32),
            pltpu.VMEM((tp_size, groups, 8, GROUP), F32),
            pltpu.VMEM((groups, 128, GROUP), F32),
            pltpu.VMEM((length, 128), F32),
            pltpu.SemaphoreType.DMA((tp_size - 1,)),
            pltpu.SemaphoreType.DMA((tp_size - 1,)),
        ] + hosted.scratch() + resident_scratch(resident),
        compiler_params=params(collective),
        cost_estimate=pl.CostEstimate(
            flops=6 * length * model * inner, bytes_accessed=60 << 20, transcendentals=0
        ),
        name="ssd_backward",
    )(
        cotan, out_w, gate_raw, mixed, gain,
        gate_raw, value_raw, value_raw, mixed, bc, step_in, cums, held,
        gate_w, value_w, step_w, taps, bias, rate, skip, gain, cols, seg_line, *hosted.operands(),
    )

def gather_kernel(count, pieces, *refs):
    amount = len(pieces)
    sources, targets = refs[:amount], refs[amount : 2 * amount]
    own_sem, send_sem, recv_sem, pass_sem, took_sem = refs[2 * amount :]
    me, line = lax.axis_index("fsdp"), lax.axis_index("tp")
    chips = count // 2
    partner = me + 1 - 2 * lax.rem(me, 2)
    others = [lax.rem(me + 2 * hop, count) for hop in range(1, chips)]
    greet([(device, line) for device in others + [partner]])

    def remote(source, target, sends, receives, device):
        return pltpu.make_async_remote_copy(
            src_ref=source, dst_ref=target, send_sem=sends, recv_sem=receives,
            device_id=(device, line), device_id_type=MESH,
        )

    def place(which, at):
        size, axis = pieces[which]
        return part_of(targets[which], at, size, axis)

    started = []
    for which in range(amount):
        for hop in range(1, chips):
            copy = remote(
                sources[which], place(which, me), send_sem.at[hop, which],
                recv_sem.at[hop, which], lax.rem(me + 2 * hop, count),
            )
            copy.start()
            started.append(copy)
    for which in range(amount):
        copy = remote(
            sources[which], place(which, me), pass_sem.at[0, which], took_sem.at[0, which], partner
        )
        copy.start()
        started.append(copy)
    own = []
    for which in range(amount):
        copy = pltpu.make_async_copy(sources[which], place(which, me), own_sem.at[which])
        copy.start()
        own.append(copy)
    for which in range(amount):
        for hop in range(1, chips):
            origin = lax.rem(me - 2 * hop + count, count)
            block = place(which, origin)
            remote(
                block, block, send_sem.at[hop, which], recv_sem.at[hop, which], partner
            ).wait_recv()
            copy = remote(
                block, block, pass_sem.at[hop, which], took_sem.at[hop, which], partner
            )
            copy.start()
            started.append(copy)
    for which in range(amount):
        for hop in range(chips):
            block = place(which, lax.rem(partner - 2 * hop + count, count))
            remote(
                block, block, pass_sem.at[hop, which], took_sem.at[hop, which], partner
            ).wait_recv()
    for copy in started:
        copy.wait_send()
    for copy in own:
        copy.wait()


def gather_call(count, blocks, axes):
    pieces, shapes = [], []
    for block, axis in zip(blocks, axes):
        if axis == 2:
            pieces.append((0, 2))
            shapes.append(shape((count,) + block.shape, BF16))
        else:
            pieces.append((block.shape[axis], axis))
            dims = list(block.shape)
            dims[axis] *= count
            shapes.append(shape(tuple(dims), BF16))
    amount = len(blocks)
    sems = lambda: pltpu.SemaphoreType.DMA((count // 2, amount))
    return pl.pallas_call(
        partial(gather_kernel, count, pieces),
        in_specs=[pl.BlockSpec(memory_space=pl.ANY)] * amount,
        out_specs=[pl.BlockSpec(memory_space=pl.ANY)] * amount,
        out_shape=shapes,
        scratch_shapes=[pltpu.SemaphoreType.DMA((amount,)), sems(), sems(), sems(), sems()],
        compiler_params=pltpu.CompilerParams(collective_id=0, has_side_effects=True),
        cost_estimate=pl.CostEstimate(flops=0, bytes_accessed=250 << 20, transcendentals=0),
        name="gather_weights",
    )(*blocks)


def scatter_kernel(count, pieces, *refs):
    amount = len(pieces)
    sources, targets = refs[:amount], refs[amount : 2 * amount]
    scratch = refs[2 * amount :]
    mine, took, came = (scratch[at * amount : (at + 1) * amount] for at in range(3))
    own_sem, pass_sem, took_sem, send_sem, recv_sem = scratch[3 * amount :]
    me, line = lax.axis_index("fsdp"), lax.axis_index("tp")
    chips = count // 2
    partner = me + 1 - 2 * lax.rem(me, 2)
    others = [lax.rem(me + 2 * hop, count) for hop in range(1, chips)]
    greet([(device, line) for device in others + [partner]])

    def remote(source, target, sends, receives, device):
        return pltpu.make_async_remote_copy(
            src_ref=source, dst_ref=target, send_sem=sends, recv_sem=receives,
            device_id=(device, line), device_id_type=MESH,
        )

    def piece(which, at):
        size, axis = pieces[which]
        return part_of(sources[which], at, size, axis)

    order = list(range(1, chips)) + [0]
    handed, own = {}, {}
    for hop in order:
        for which in range(amount):
            copy = remote(
                piece(which, lax.rem(partner + 2 * hop, count)), took[which].at[hop],
                pass_sem.at[hop, which], took_sem.at[hop, which], partner,
            )
            copy.start()
            handed[hop, which] = copy
            copy = pltpu.make_async_copy(
                piece(which, lax.rem(me + 2 * hop, count)), mine[which].at[hop],
                own_sem.at[hop, which],
            )
            copy.start()
            own[hop, which] = copy
    sent = []
    for hop in order:
        for which in range(amount):
            own[hop, which].wait()
            handed[hop, which].wait_recv()
            total = mine[which][hop].astype(F32) + took[which][hop].astype(F32)
            if hop == 0:
                targets[which][...] = total
                continue
            mine[which][hop] = total.astype(BF16)
            copy = remote(
                mine[which].at[hop], came[which].at[hop - 1], send_sem.at[hop, which],
                recv_sem.at[hop, which], lax.rem(me + 2 * hop, count),
            )
            copy.start()
            sent.append(copy)
    for which in range(amount):
        for hop in range(1, chips):
            block = came[which].at[hop - 1]
            remote(
                block, block, send_sem.at[hop, which], recv_sem.at[hop, which], partner
            ).wait_recv()
            targets[which][...] += block[...].astype(F32)
    for copy in list(handed.values()) + sent:
        copy.wait_send()


def scatter_call(count, arrays, axes):
    pieces, shapes = [], []
    for array, axis in zip(arrays, axes):
        if axis == 2:
            pieces.append((0, 2))
            shapes.append(array.shape[1:])
        else:
            dims = list(array.shape)
            dims[axis] //= count
            pieces.append((dims[axis], axis))
            shapes.append(tuple(dims))
    amount, chips = len(arrays), count // 2
    sems = lambda: pltpu.SemaphoreType.DMA((chips, amount))
    return pl.pallas_call(
        partial(scatter_kernel, count, pieces),
        in_specs=[pl.BlockSpec(memory_space=pl.ANY)] * amount,
        out_specs=[pl.BlockSpec(memory_space=pltpu.VMEM)] * amount,
        out_shape=[shape(dims) for dims in shapes],
        scratch_shapes=[pltpu.VMEM((chips,) + dims, BF16) for dims in shapes]
        + [pltpu.VMEM((chips,) + dims, BF16) for dims in shapes]
        + [pltpu.VMEM((chips - 1,) + dims, BF16) for dims in shapes]
        + [sems(), sems(), sems(), sems(), sems()],
        compiler_params=pltpu.CompilerParams(
            collective_id=1, has_side_effects=True, vmem_limit_bytes=48 << 20
        ),
        cost_estimate=pl.CostEstimate(flops=0, bytes_accessed=250 << 20, transcendentals=0),
        name="scatter_gradients",
    )(*arrays)


def weight_kernel(micro, *refs):
    outs = refs[-4:]
    rows, lows = refs[:micro], refs[micro : 5 * micro]
    for which in range(4):
        total = mm_tn(rows[0][...], lows[which][...])
        for at in range(1, micro):
            total = total + mm_tn(rows[at][...], lows[4 * at + which][...])
        outs[which][...] = total.astype(BF16)


def weight_call(inputs, lows):
    micro, (length, model) = len(inputs), inputs[0].shape
    full = lambda array: pl.BlockSpec(array.shape, lambda g: (0, 0), pipeline_mode=pl.Buffered(1))
    flat = [array for low in lows for array in low]
    widths = [array.shape[1] for array in lows[0]]
    return pl.pallas_call(
        partial(weight_kernel, micro),
        grid=(model // BLOCK,),
        in_specs=[pl.BlockSpec((length, BLOCK), lambda g: (0, g))] * micro
        + [full(array) for array in flat],
        out_specs=[pl.BlockSpec((BLOCK, width), lambda g: (g, 0)) for width in widths],
        out_shape=[shape((model, width), BF16) for width in widths],
        compiler_params=pltpu.CompilerParams(vmem_limit_bytes=50 << 20),
        cost_estimate=pl.CostEstimate(
            flops=2 * micro * length * model * sum(widths), bytes_accessed=40 << 20, transcendentals=0
        ),
        name="weight_gradients",
    )(*inputs, *flat)


def outer_kernel(micro, *refs):
    total = mm_tn(refs[0][...], refs[micro][...])
    for at in range(1, micro):
        total = total + mm_tn(refs[at][...], refs[micro + at][...])
    refs[-1][...] = total.astype(BF16)


def outer_call(branches, cotans):
    micro, (length, inner) = len(branches), branches[0].shape
    model = cotans[0].shape[1]
    full = lambda array: pl.BlockSpec(array.shape, lambda g: (0, 0), pipeline_mode=pl.Buffered(1))
    return pl.pallas_call(
        partial(outer_kernel, micro),
        grid=(inner // BLOCK,),
        in_specs=[pl.BlockSpec((length, BLOCK), lambda g: (0, g))] * micro
        + [full(array) for array in cotans],
        out_specs=pl.BlockSpec((BLOCK, model), lambda g: (g, 0)),
        out_shape=shape((inner, model), BF16),
        compiler_params=pltpu.CompilerParams(vmem_limit_bytes=50 << 20),
        cost_estimate=pl.CostEstimate(
            flops=2 * micro * length * model * inner, bytes_accessed=30 << 20, transcendentals=0
        ),
        name="out_gradients",
    )(*branches, *cotans)


def tail_kernel(chips, tp_size, micro, widths, *refs):
    columns, lows, parts, raws = refs[:4], refs[4:12], refs[12:14], refs[14:16]
    cols_ref, staps_ref, sbias_ref = refs[16:19]
    pieces = refs[19:23]
    outs, state_out, pack_out, ssum_out, low_out = refs[23:27], refs[27], refs[28], refs[29], refs[30]
    (
        cols_s, give, took, mine, came, passed, total_s, kept_s,
        sgive, stook, smine, scame, stotal, skept_s,
        pack, pack_took, pack_sum, pack_slots, ssum, ssum_took, ssum_sum, ssum_slots,
        raw_s, own_s, slots_s, whole_s, sum_s, low_s, vbuf, gcbuf,
        cols_sem, give_sem, took_sem, send_sem, recv_sem, sgive_sem, stook_sem, ssend_sem, srecv_sem,
        pass_sem, pack_sem, ssum_sem, raw_sem, own_sem, part_send, part_recv, whole_send, whole_recv,
        *stored, low_sem,
    ) = refs[31:]
    loads = [
        pltpu.make_async_copy(low, kept, low_sem.at[at])
        for at, (low, kept) in enumerate(zip(lows, stored))
    ]
    lows = stored
    step, steps = pl.program_id(0), pl.num_programs(0)
    me, line = lax.axis_index("fsdp"), lax.axis_index("tp")
    count = 2 * chips
    core, chip = lax.rem(me, 2), me // 2
    partner = me + 1 - 2 * core
    split = total_s.shape[1] // 256 * 128

    def flipped(hop, which_core):
        x, y = lax.rem(chip, 2), chip // 2
        hop_x, hop_y = hop % 2, hop // 2
        x, y = x + hop_x - 2 * x * hop_x, y + hop_y - 2 * y * hop_y
        return (2 * y + x) * 2 + which_core

    def tile_of(at):
        pair = lax.rem(at, count) // 2
        hop = jnp.where(pair == 0, 3, pair - 1)
        return hop, flipped(hop, jnp.where(lax.rem(at, 2) == 0, 1 - core, core))

    def fetch(at, which):
        _, shard = tile_of(at)
        slot = lax.rem(at, 2)
        return pltpu.make_async_copy(
            columns[which].at[:, pl.ds(pl.multiple_of(shard * BLOCK, BLOCK), BLOCK)],
            cols_s.at[slot, which], cols_sem.at[slot, which],
        )

    def far(hop):
        return (flipped(hop, core), line)

    def giving(hop):
        return remote_copy(
            give.at[hop], took.at[hop], give_sem.at[hop], took_sem.at[hop], (partner, line)
        )

    def sending(hop):
        return remote_copy(
            mine.at[hop - 1], came.at[hop - 1], send_sem.at[hop - 1], recv_sem.at[hop - 1], far(hop)
        )

    def passing(hop):
        columns = pl.ds(0, split) if hop == 1 else pl.ds(split, total_s.shape[1] - split)
        return remote_copy(
            mine.at[2, :, columns], passed.at[:, columns], pass_sem.at[0, hop - 1],
            pass_sem.at[1, hop - 1], far(hop),
        )

    def sgiving(hop):
        return remote_copy(
            sgive.at[hop], stook.at[hop], sgive_sem.at[hop], stook_sem.at[hop], (partner, line)
        )

    def ssending(hop):
        return remote_copy(
            smine.at[hop - 1], scame.at[hop - 1], ssend_sem.at[hop - 1], srecv_sem.at[hop - 1], far(hop)
        )

    pack_pass = remote_copy(pack, pack_took, pack_sem.at[0, 0], pack_sem.at[1, 0], (partner, line))
    ssum_pass = remote_copy(ssum, ssum_took, ssum_sem.at[0, 0], ssum_sem.at[1, 0], (partner, line))

    def pack_send(hop):
        return remote_copy(
            pack_sum, pack_slots.at[chip], pack_sem.at[0, hop], pack_sem.at[1, hop], far(hop)
        )

    def ssum_send(hop):
        return remote_copy(
            ssum_sum, ssum_slots.at[chip], ssum_sem.at[0, hop], ssum_sem.at[1, hop], far(hop)
        )

    def rows_at(ref, at):
        return ref.at[pl.ds(pl.multiple_of(at * GROUP, GROUP), GROUP), :]

    def handing(hop):
        owner = lax.rem(line + hop, tp_size)
        return remote_copy(
            rows_at(parts[late], owner), slots_s.at[line], part_send.at[hop - 1],
            part_recv.at[hop - 1], (me, owner),
        )

    late = micro - 1

    def own_part():
        return pltpu.make_async_copy(rows_at(parts[late], line), own_s, own_sem.at[late])

    def ready(at):
        length = raws[at].shape[0]
        return pltpu.make_async_copy(
            parts[at], whole_s.at[pl.ds(at * length, length), :], own_sem.at[at]
        )

    def raw_copy(at):
        length = raws[at].shape[0]
        return pltpu.make_async_copy(
            raws[at], raw_s.at[pl.ds(at * length, length), :], raw_sem.at[at]
        )

    groups = raws[0].shape[0] // GROUP

    def spreading(hop):
        block = rows_at(whole_s, late * groups + line)
        return remote_copy(
            sum_s, block, whole_send.at[hop - 1], whole_recv.at[hop - 1],
            (me, lax.rem(line + hop, tp_size)),
        )

    @pl.when(step == 0)
    def _():
        for which in range(4):
            fetch(step, which).start()
        own_part().start()
        for at in range(micro):
            raw_copy(at).start()
            if at != late:
                ready(at).start()
        greet(
            [far(hop) for hop in range(1, chips)] + [(partner, line)]
            + [(me, lax.rem(line + hop, tp_size)) for hop in range(1, tp_size)]
        )
        for hop in range(1, tp_size):
            handing(hop).start()
        for load in loads:
            load.start()
        pack[0:8, :] = pieces[0][...] + pieces[1][...]
        pack[8:16, :] = jnp.zeros((8, pack.shape[1]), F32)
        pack[8:16, 0:128] = pieces[2][...] + pieces[3][...]
        pack_pass.start()

    @pl.when(step + 1 < count)
    def _():
        for which in range(4):
            fetch(step + 1, which).start()

    @pl.when((step + 1 >= count) & (step + 1 < steps))
    def _():
        for which in range(2):
            fetch(step + 1, which).start()

    for which in range(2):
        fetch(step, which).wait()

    @pl.when(step < count)
    def _():
        for which in range(2, 4):
            fetch(step, which).wait()

    slot = lax.rem(step, 2)
    hop, _ = tile_of(step)
    even = lax.rem(step, 2) == 0

    def tile(which):
        sides = (0, 1) if which < 3 else (2, 3)
        return mm_tn(cols_s[slot, sides[0]], lows[2 * which][...]) + mm_tn(
            cols_s[slot, sides[1]], lows[2 * which + 1][...]
        )

    @pl.when((step < count) & even)
    def _():
        at = 0
        for which, width in enumerate(widths):

            @pl.when(step == 0)
            def _():
                loads[2 * which].wait()
                loads[2 * which + 1].wait()

            give[hop, :, at : at + width] = tile(which).astype(BF16)
            at += width
        giving(hop).start()

    @pl.when((step < count) & jnp.logical_not(even))
    def _():
        at = 0
        for which, width in enumerate(widths):
            total_s[:, at : at + width] = tile(which)
            at += width
        giving(hop).wait_recv()
        total_s[...] += took[hop].astype(F32)

        @pl.when(hop == 3)
        def _():
            mine[2] = total_s[...].astype(BF16)
            passing(1).start()
            passing(2).start()

        @pl.when(hop == 0)
        def _():
            kept_s[...] = total_s[...]

        @pl.when(hop == 1)
        def _():
            passing(2).wait_recv()
            total_s[:, split:] += passed[:, split:].astype(F32)
            mine[0] = total_s[...].astype(BF16)
            sending(1).start()

        @pl.when(hop == 2)
        def _():
            passing(1).wait_recv()
            total_s[:, :split] += passed[:, :split].astype(F32)
            mine[1] = total_s[...].astype(BF16)
            sending(2).start()

    @pl.when(step == 1)
    def _():
        pack_pass.wait()
        pack_sum[...] = pack[...] + pack_took[...]
        pack_slots[chip] = pack_sum[...]
        for other in range(1, chips):
            pack_send(other).start()

    @pl.when(step == 5)
    def _():
        own_part().wait()
        slots_s[line] = own_s[...]
        for hop in range(1, tp_size):
            handing(hop).wait()
        total = slots_s[0].astype(F32)
        for other in range(1, tp_size):
            total = total + slots_s[other].astype(F32)
        sum_s[...] = total.astype(BF16)
        mine_rows = rows_at(whole_s, late * groups + line)
        mine_rows[...] = sum_s[...]
        for hop in range(1, tp_size):
            spreading(hop).start()

    @pl.when(step == count - 1)
    def _():
        for at in range(micro):
            raw_copy(at).wait()
            if at != late:
                ready(at).wait()
        for hop in range(1, tp_size):
            spreading(hop).wait()
        ssum[...] = jnp.zeros(ssum.shape, F32)
        taps, bias = staps_ref[...], sbias_ref[...]

        def state_group(turn, carry):
            group = micro * groups - 1 - turn
            at = pl.multiple_of(group * GROUP, GROUP)
            cols = cols_ref[pl.ds(at, GROUP), :]
            vbuf[HALO : HALO + GROUP, :] = raw_s[pl.ds(at, GROUP), :]
            ahead = pl.multiple_of(jnp.maximum(group * (GROUP // HALO) - 1, 0) * HALO, HALO)
            vbuf[0:HALO, :] = raw_s[pl.ds(ahead, HALO), :]
            moved = shifted_values(vbuf, cols)
            conv = conv_of(moved, taps, bias)
            sig = jax.nn.sigmoid(conv)
            grad = whole_s[pl.ds(at, GROUP), :].astype(F32) * (sig * (1.0 + conv * (1.0 - sig)))
            gcbuf[GROUP : GROUP + HALO, :] = gcbuf[0:HALO, :]
            gcbuf[0:GROUP, :] = grad
            back = taps[0:1, :] * grad
            for offset in range(1, CONV):
                up = jnp.where(
                    cols[:, 2 + offset : 3 + offset] > 0.0, gcbuf[offset : offset + GROUP, :], 0.0
                )
                back = back + taps[offset : offset + 1, :] * up
            low_s[pl.ds(at, GROUP), :] = back.astype(BF16)
            for offset in range(CONV):
                ssum[offset : offset + 1, :] += jnp.sum(grad * moved[offset], axis=0, keepdims=True)
            ssum[CONV : CONV + 1, :] += jnp.sum(grad, axis=0, keepdims=True)
            return carry

        lax.fori_loop(0, micro * groups, state_group, 0)
        ssum_pass.start()
        for at in range(micro):
            low_out[at] = low_s[pl.ds(pl.multiple_of((at * groups + line) * GROUP, GROUP), GROUP), :]

    def state_tile():
        length = groups * GROUP
        return mm_tn(cols_s[slot, 0], low_s[0:length, :]) + mm_tn(
            cols_s[slot, 1], low_s[length : 2 * length, :]
        )

    @pl.when((step >= count) & even)
    def _():
        sgive[hop] = state_tile().astype(BF16)
        sgiving(hop).start()

    @pl.when((step >= count) & jnp.logical_not(even))
    def _():
        stotal[...] = state_tile()
        sgiving(hop).wait_recv()
        stotal[...] += stook[hop].astype(F32)

        @pl.when(hop == 0)
        def _():
            skept_s[...] = stotal[...]

        @pl.when(hop > 0)
        def _():
            smine[hop - 1] = stotal[...].astype(BF16)
            ssending(hop).start()

    @pl.when(step == count + 1)
    def _():
        ssum_pass.wait()
        ssum_sum[...] = ssum[...] + ssum_took[...]
        ssum_slots[chip] = ssum_sum[...]
        for other in range(1, chips):
            ssum_send(other).start()

    @pl.when(step == steps - 1)
    def _():
        for sends, slots, out in ((pack_send, pack_slots, pack_out), (ssum_send, ssum_slots, ssum_out)):
            for other in range(1, chips):
                sends(other).wait()
            total = slots[0]
            for other in range(1, chips):
                total = total + slots[other]
            out[...] = total
        for other in (1, 2):
            sending(other).wait_recv()
            kept_s[...] += came[other - 1].astype(F32)
        for other in range(1, chips):
            ssending(other).wait_recv()
            skept_s[...] += scame[other - 1].astype(F32)
        state_out[...] = skept_s[...]
        at = 0
        for which, width in enumerate(widths):
            part = kept_s[:, at : at + width]
            outs[which][...] = part if which < 3 else jnp.transpose(part)
            at += width
        for other in (1, 2):
            passing(other).wait_send()
            sending(other).wait_send()
        for other in range(1, chips):
            ssending(other).wait_send()
        for other in range(chips):
            giving(other).wait_send()
            sgiving(other).wait_send()


def tail_call(count, tp_size, inputs, cotans, lows, parts, raws, cols, staps, sbias, pieces):
    micro, length = len(inputs), inputs[0].shape[0]
    chips = count // 2
    order = [low[which] for which in range(4) for low in lows]
    widths = [low.shape[1] for low in order[::2]]
    total, narrow = sum(widths), 2 * STATE
    packed = (16, pieces[0].shape[1])
    hbm = pl.BlockSpec(memory_space=pl.ANY)
    full = lambda array: pl.BlockSpec(array.shape, lambda i: (0,) * array.ndim, pipeline_mode=pl.Buffered(1))
    out_dims = [(BLOCK, width) for width in widths[:3]] + [(widths[3], BLOCK), (BLOCK, narrow)]
    out_shapes = [shape(dims) for dims in out_dims] + [
        shape(packed), shape((8, narrow)), shape((micro, GROUP, narrow), BF16)
    ]
    dma = lambda *dims: pltpu.SemaphoreType.DMA(dims)
    return pl.pallas_call(
        partial(tail_kernel, chips, tp_size, micro, widths),
        grid=(2 * count,),
        in_specs=[hbm] * 16 + [full(each) for each in (cols, staps, sbias) + pieces],
        out_specs=[full(each) for each in out_shapes],
        out_shape=out_shapes,
        scratch_shapes=[
            pltpu.VMEM((2, 4, length, BLOCK), BF16),
            pltpu.VMEM((chips, BLOCK, total), BF16),
            pltpu.VMEM((chips, BLOCK, total), BF16),
            pltpu.VMEM((3, BLOCK, total), BF16),
            pltpu.VMEM((2, BLOCK, total), BF16),
            pltpu.VMEM((BLOCK, total), BF16),
            pltpu.VMEM((BLOCK, total), F32),
            pltpu.VMEM((BLOCK, total), F32),
            pltpu.VMEM((chips, BLOCK, narrow), BF16),
            pltpu.VMEM((chips, BLOCK, narrow), BF16),
            pltpu.VMEM((chips - 1, BLOCK, narrow), BF16),
            pltpu.VMEM((chips - 1, BLOCK, narrow), BF16),
            pltpu.VMEM((BLOCK, narrow), F32),
            pltpu.VMEM((BLOCK, narrow), F32),
            pltpu.VMEM(packed, F32),
            pltpu.VMEM(packed, F32),
            pltpu.VMEM(packed, F32),
            pltpu.VMEM((chips,) + packed, F32),
            pltpu.VMEM((8, narrow), F32),
            pltpu.VMEM((8, narrow), F32),
            pltpu.VMEM((8, narrow), F32),
            pltpu.VMEM((chips, 8, narrow), F32),
            pltpu.VMEM((micro * length, narrow), F32),
            pltpu.VMEM((GROUP, narrow), BF16),
            pltpu.VMEM((tp_size, GROUP, narrow), BF16),
            pltpu.VMEM((micro * length, narrow), BF16),
            pltpu.VMEM((GROUP, narrow), BF16),
            pltpu.VMEM((micro * length, narrow), BF16),
            pltpu.VMEM((GROUP + HALO, narrow), F32),
            pltpu.VMEM((GROUP + HALO, narrow), F32),
            dma(2, 4), dma(chips), dma(chips), dma(2), dma(2),
            dma(chips), dma(chips), dma(chips - 1), dma(chips - 1),
            dma(2, 2), dma(2, chips), dma(2, chips), dma(micro), dma(micro),
            dma(tp_size - 1), dma(tp_size - 1), dma(tp_size - 1), dma(tp_size - 1),
        ] + [pltpu.VMEM(low.shape, BF16) for low in order] + [dma(len(order))],
        compiler_params=pltpu.CompilerParams(
            collective_id=6, has_side_effects=True, vmem_limit_bytes=62 << 20
        ),
        cost_estimate=pl.CostEstimate(
            flops=4 * length * BLOCK * count * total, bytes_accessed=250 << 20, transcendentals=0
        ),
        name="weight_gradients",
    )(*inputs, *cotans, *order, *parts, *raws, cols, staps, sbias, *pieces)


def rows_kernel(
    sum0, sum1, low_ref, state_w, rows_ref, cot_ref, gain_ref, made0, made1, scale0, scale1,
    hidden_out, block_out, gain_out,
):
    step = pl.program_id(0)
    half = pl.num_programs(0) // 2
    gain = gain_ref[...]

    def work(summed, made, scale_ref):
        grad = summed[...].astype(F32) + mm_nt(low_ref[0], state_w[...])
        rows = rows_ref[0].astype(F32)
        inv_root = lax.rsqrt(jnp.mean(rows * rows, axis=1, keepdims=True) + EPSILON)
        part = jnp.sum(grad * (rows * inv_root), axis=0, keepdims=True)
        normed = grad * gain
        inner = jnp.mean(normed * rows, axis=1, keepdims=True)
        back = inv_root * normed - rows * (inv_root * inv_root * inv_root * inner)
        hidden_out[0] = (cot_ref[0].astype(F32) + back).astype(BF16)
        block_out[0] = (rows + made[...] * scale_ref[:, 0:1]).astype(BF16)
        width = gain_out.shape[1]
        for at in range(gain_out.shape[0]):
            piece = part[:, at * width : (at + 1) * width]

            @pl.when(step == 0)
            def _():
                gain_out[at : at + 1, :] = piece

            @pl.when(step > 0)
            def _():
                gain_out[at : at + 1, :] += piece

    @pl.when(step < half)
    def _():
        work(sum0, made0, scale0)

    @pl.when(step >= half)
    def _():
        work(sum1, made1, scale1)


def rows_call(sums, lows, state_w, rows, cotan, gain, made, scales):
    micro, length, model = rows.shape
    tiles = 2
    tile = length // tiles
    both = lambda width: pl.BlockSpec((1, tile, width), lambda i: (i // tiles, i % tiles, 0))
    former_of = lambda width: pl.BlockSpec((tile, width), lambda i: (jnp.minimum(i, tiles - 1), 0))
    latter_of = lambda width: pl.BlockSpec((tile, width), lambda i: (jnp.maximum(i - tiles, 0), 0))
    former, latter = former_of(model), latter_of(model)
    full = lambda dims: pl.BlockSpec(dims, lambda i: (0, 0))
    return pl.pallas_call(
        rows_kernel,
        grid=(micro * tiles,),
        in_specs=[
            former, latter, both(2 * STATE), full(state_w.shape), both(model), both(model),
            full(gain.shape), former, latter, former_of(128), latter_of(128),
        ],
        out_specs=[both(model), both(model), full((8, model // 8))],
        out_shape=[shape(rows.shape, BF16), shape(rows.shape, BF16), shape((8, model // 8))],
        compiler_params=pltpu.CompilerParams(vmem_limit_bytes=50 << 20),
        cost_estimate=pl.CostEstimate(flops=1 << 30, bytes_accessed=18 << 20, transcendentals=0),
        name="finish_rows",
    )(*sums, lows, state_w, rows, cotan, gain, *made, *scales)


def gain_kernel(
    tp_size, count, part, gain_out, line_slots, line_sum, slots, send_sem, recv_sem, far_send, far_recv,
):
    me, column = lax.axis_index("tp"), lax.axis_index("fsdp")
    greet(
        [(column, lax.rem(me + hop, tp_size)) for hop in range(1, tp_size)]
        + [(lax.rem(column + hop, count), me) for hop in range(1, count)]
    )
    line_slots[me] = part[...]
    copies = [
        remote_copy(
            part, line_slots.at[me], send_sem.at[hop - 1], recv_sem.at[hop - 1],
            (column, lax.rem(me + hop, tp_size)),
        )
        for hop in range(1, tp_size)
    ]
    for copy in copies:
        copy.start()
    for copy in copies:
        copy.wait()
    total = line_slots[0]
    for at in range(1, tp_size):
        total = total + line_slots[at]
    line_sum[...] = total
    slots[column] = total
    copies = [
        remote_copy(
            line_sum, slots.at[column], far_send.at[hop - 1], far_recv.at[hop - 1],
            (lax.rem(column + hop, count), me),
        )
        for hop in range(1, count)
    ]
    for copy in copies:
        copy.start()
    for copy in copies:
        copy.wait()
    total = slots[0]
    for at in range(1, count):
        total = total + slots[at]
    gain_out[...] = total


def gain_call(tp_size, count, part):
    vmem = pl.BlockSpec(memory_space=pltpu.VMEM)
    return pl.pallas_call(
        partial(gain_kernel, tp_size, count),
        in_specs=[vmem],
        out_specs=vmem,
        out_shape=shape(part.shape),
        scratch_shapes=[
            pltpu.VMEM((tp_size,) + part.shape, F32), pltpu.VMEM(part.shape, F32),
            pltpu.VMEM((count,) + part.shape, F32),
            pltpu.SemaphoreType.DMA((tp_size - 1,)), pltpu.SemaphoreType.DMA((tp_size - 1,)),
            pltpu.SemaphoreType.DMA((count - 1,)), pltpu.SemaphoreType.DMA((count - 1,)),
        ],
        compiler_params=pltpu.CompilerParams(
            collective_id=7, has_side_effects=True, vmem_limit_bytes=32 << 20
        ),
        cost_estimate=pl.CostEstimate(flops=0, bytes_accessed=1 << 20, transcendentals=0),
        name="gain_sum",
    )(part)


def unpack_kernel(heads, pack_ref, ssum_ref, rate_ref, gain, skip, conv, bias, sconv, sbias, step, decay):
    gain[...] = pack_ref[0:1, :]
    lanes = pack_ref.shape[1]
    place = (iota((lanes, 128), 0) // HEAD_DIM == iota((lanes, 128), 1)).astype(F32)
    sums = mm(pack_ref[0:8, :], place, PRECISE)
    skip[...] = sums[1:2, :heads]
    conv[...] = pack_ref[2 : 2 + CONV, :]
    bias[...] = pack_ref[2 + CONV : 3 + CONV, :]
    sconv[...] = ssum_ref[0:CONV, :]
    sbias[...] = ssum_ref[CONV : CONV + 1, :]
    step[...] = pack_ref[8:9, :heads]
    decay[...] = pack_ref[9:10, :heads] * rate_ref[:, :heads]


def unpack_call(pack, ssum, rate, heads):
    inner = pack.shape[1]
    vmem = pl.BlockSpec(memory_space=pltpu.VMEM)
    dims = [(1, inner), (1, heads), (CONV, inner), (1, inner), (CONV, 2 * STATE), (1, 2 * STATE),
            (1, heads), (1, heads)]
    return pl.pallas_call(
        partial(unpack_kernel, heads), in_specs=[vmem] * 3, out_specs=[vmem] * 8,
        out_shape=[shape(each) for each in dims], name="small_gradients",
        cost_estimate=pl.CostEstimate(flops=0, bytes_accessed=1 << 18, transcendentals=0),
    )(pack, ssum, rate)


def shift_down(values, offset):
    return jnp.pad(values, ((offset, 0), (0, 0)))[: values.shape[0]]


def shift_up(values, offset):
    return jnp.pad(values, ((0, offset), (0, 0)))[offset:]


def document_columns(seg_row):
    length = seg_row.shape[0]
    previous = jnp.concatenate([jnp.full((1,), -1, seg_row.dtype), seg_row[GROUP - 1 : -1 : GROUP]])
    last = seg_row[GROUP - 1 :: GROUP]
    columns = []
    for offset in range(1, CONV):
        columns.append(jnp.pad(seg_row, (offset, 0), constant_values=-1)[:length] == seg_row)
    for offset in range(1, CONV):
        columns.append(jnp.pad(seg_row, (0, offset), constant_values=-1)[offset:] == seg_row)
    columns.append(seg_row == jnp.repeat(previous, GROUP))
    columns.append(seg_row == jnp.repeat(last, GROUP))
    columns.append(jnp.repeat(last == previous, GROUP))
    columns.append(seg_row)
    columns = [column.astype(F32) for column in columns]
    return jnp.stack(columns + [columns[0]] * (16 - len(columns)), axis=1)


def state_gradient(grad_bc, state_raw, taps, bias, cols):
    moved = [state_raw]
    for offset in range(1, CONV):
        moved.append(shift_down(state_raw, offset) * cols[:, offset - 1 : offset])
    conv = bias
    for offset in range(CONV):
        conv = conv + taps[offset][None, :] * moved[offset]
    sig = jax.nn.sigmoid(conv)
    grad_conv = grad_bc * (sig * (1.0 + conv * (1.0 - sig)))
    grad_raw = taps[0][None, :] * grad_conv
    for offset in range(1, CONV):
        grad_raw = grad_raw + taps[offset][None, :] * (
            shift_up(grad_conv, offset) * cols[:, 2 + offset : 3 + offset]
        )
    grad_taps = jnp.stack([jnp.sum(grad_conv * each, axis=0) for each in moved])
    return grad_raw.astype(BF16), grad_taps, jnp.sum(grad_conv, axis=0)


def local(
    hidden_in, segment_ids, cotangent, norm_gain, proj_gate, proj_value, proj_state, proj_step,
    conv_value, conv_value_bias, conv_state, conv_state_bias, step_bias, decay_log, skip_gain,
    gate_gain, proj_out,
):
    micro = hidden_in.shape[0]
    heads = step_bias.shape[0]
    rows_here = hidden_in.shape[2]
    tp_size = lax.axis_size("tp")
    me = lax.axis_index("tp")
    decay_rate = -jnp.exp(decay_log)
    pad_heads = lambda values: jnp.pad(values, (0, 128 - heads))[None, :]
    rate = pad_heads(decay_rate)
    step_bias_line = pad_heads(step_bias)
    skip = jnp.repeat(skip_gain, HEAD_DIM)[None, :]
    gain = gate_gain[None, :]
    taps, bias = conv_value, conv_value_bias[None, :]
    staps, sbias = conv_state, conv_state_bias[None, :]

    input_rows = []
    for at in range(micro):
        rows_float = hidden_in[at, 0].astype(F32)
        inv_root = lax.rsqrt(jnp.mean(rows_float * rows_float, axis=-1, keepdims=True) + EPSILON)
        input_rows.append((rows_float * inv_root * norm_gain).astype(BF16))

    def gather_tp(values, *after):
        values = lax.optimization_barrier((values,) + after)[0]
        return lax.all_gather(values, "tp", axis=0, tiled=True)

    def scatter_tp(values, *after):
        values = lax.optimization_barrier((values,) + after)[0]
        return lax.psum_scatter(values, "tp", scatter_dimension=0, tiled=True)

    inputs = [gather_tp(input_rows[0])]
    fsdp_size = lax.axis_size("fsdp")
    model = hidden_in.shape[3]
    aligned = proj_out.shape[1] % 128 == 0
    axes = (0, 0, 0, 0, 1 if aligned else 2)
    step_block = jnp.pad(proj_step, ((0, 0), (0, 128 - heads)))
    gate_w, value_w, state_w, step_w, out_w = gather_call(
        fsdp_size, (proj_gate, proj_value, proj_state, step_block, proj_out), axes
    )
    if not aligned:
        out_w = jnp.transpose(out_w, (1, 0, 2)).reshape(-1, model)
    inputs.append(gather_tp(input_rows[1], inputs[0], step_w))
    forward_weights = (gate_w, value_w, state_w, step_w, out_w)
    vectors = (taps, bias, staps, sbias, step_bias_line, rate, skip)
    columns = [document_columns(segment_ids[at, 0]) for at in range(micro)]
    seg_lines = [segment_ids[at, 0].astype(F32)[None, :] for at in range(micro)]
    quick = [0, 3, 7, 11, 14, 15, 15, 15, 15, 15]
    paces = {4: [0, 3, 4, 6, 9, 12, 15, 17, 19, 19], 5: [0, 4, 4, 7, 10, 13, 18, 19]}

    def forward(at, hosted):
        return forward_call(
            inputs[at], forward_weights, vectors, gain, columns[at], seg_lines[at], hosted, quick
        )

    def backward(at, hosted, collective):
        done = backward_call(
            saved[at], cotans[at], (gate_w, value_w, step_w, out_w), (taps, bias, rate, skip),
            gain, columns[at], seg_lines[at], hosted, paces[collective], collective,
        )
        scales.append(done[8])
        return done

    scales, produced, summed = [], [], []
    saved = [forward(0, Hosted(tp_size))]
    *kept, made_sum, cotan = forward(1, Hosted(tp_size, saved[0][8], cotangent[0, 0]))
    saved.append(kept)
    produced.append(made_sum)
    cotans = [cotan]
    *former, made_sum, cotan = backward(0, Hosted(tp_size, saved[1][8], cotangent[1, 0]), 4)
    produced.append(made_sum)
    cotans.append(cotan)
    early = lax.psum(former[4], "tp")
    *latter, gin_sum = backward(1, Hosted(tp_size, former[5]), 5)
    summed = [gin_sum, scatter_tp(latter[5])]
    lows = [[each[1], each[2], each[3], each[0]] for each in (former, latter)]
    parts, raws = (early, latter[4]), [each[4] for each in saved]
    pieces = (former[6], latter[6], former[7], latter[7])
    if aligned and fsdp_size == 8 and model // fsdp_size == BLOCK:
        grad_gate, grad_value, grad_step, grad_out, grad_state, pack, state_sum, mine = tail_call(
            fsdp_size, tp_size, inputs, cotans, lows, parts, raws, jnp.concatenate(columns, axis=0),
            staps, sbias, pieces,
        )
    else:
        mine, state_sum = [], 0.0
        for at in range(micro):
            grad_bc = (parts[at] if at == 0 else lax.psum(parts[at], "tp")).astype(F32)
            low_state, grad_staps, grad_sbias = state_gradient(
                grad_bc, raws[at], staps, sbias, columns[at]
            )
            mine.append(lax.dynamic_slice_in_dim(low_state, me * rows_here, rows_here, axis=0))
            lows[at].insert(2, low_state)
            state_sum = state_sum + jnp.concatenate(
                [grad_staps, grad_sbias[None, :], jnp.zeros((3, 2 * STATE), F32)], axis=0
            )
        mine = jnp.stack(mine)
        grad_out = outer_call([low[4] for low in lows], cotans)
        grad_gate, grad_value, grad_state, grad_step = weight_call(inputs, [low[:4] for low in lows])
        if not aligned:
            grad_out = jnp.transpose(grad_out.reshape(-1, fsdp_size, proj_out.shape[1]), (1, 0, 2))
        grad_gate, grad_value, grad_state, grad_step, grad_out = scatter_call(
            fsdp_size, (grad_gate, grad_value, grad_state, grad_step, grad_out), axes
        )
        narrow = jnp.pad(pieces[2] + pieces[3], ((0, 0), (0, proj_gate.shape[1] - 128)))
        pack = jnp.concatenate([pieces[0] + pieces[1], narrow], axis=0)
        pack, state_sum = lax.psum((pack, state_sum), "fsdp")
    grad_step = grad_step[:, :heads]
    grad_hidden, block_rows, gain_part = rows_call(
        summed, mine, state_w, hidden_in[:, 0], cotangent[:, 0], norm_gain[None, :],
        produced, scales,
    )
    gain_total = gain_call(tp_size, fsdp_size, gain_part)
    grad_gain, grad_skip, grad_conv, grad_bias, grad_sconv, grad_sbias, grad_in, grad_decay = (
        unpack_call(pack, state_sum, rate, heads)
    )
    return (
        block_rows[:, None],
        grad_hidden[:, None],
        gain_total.reshape(-1),
        grad_gate,
        grad_value,
        grad_state,
        grad_step,
        grad_conv,
        grad_bias.reshape(-1),
        grad_sconv,
        grad_sbias.reshape(-1),
        grad_in.reshape(-1),
        grad_decay.reshape(-1),
        grad_skip.reshape(-1),
        grad_gain.reshape(-1),
        grad_out,
    )


def solution(mesh):
    in_specs = (
        P(None, "fsdp", "tp", None), P(None, "fsdp", None), P(None, "fsdp", "tp", None), P(),
        P("fsdp", "tp"), P("fsdp", "tp"), P("fsdp", None), P("fsdp", "tp"), P(None, "tp"), P("tp"),
        P(), P(), P("tp"), P("tp"), P("tp"), P("tp"), P("tp", "fsdp"),
    )
    out_specs = (
        P(None, "fsdp", "tp", None), P(None, "fsdp", "tp", None), P(), P("fsdp", "tp"),
        P("fsdp", "tp"), P("fsdp", None), P("fsdp", "tp"), P(None, "tp"), P("tp"), P(), P(),
        P("tp"), P("tp"), P("tp"), P("tp"), P("tp", "fsdp"),
    )
    return jax.shard_map(local, mesh=mesh, in_specs=in_specs, out_specs=out_specs, check_vma=False)
```

```python
from functools import partial

import jax
import jax.numpy as jnp
from jax import lax
from jax.experimental import pallas as pl
from jax.experimental.pallas import tpu as pltpu
from jax.sharding import PartitionSpec as P

HEAD_DIM = 64
STATE = 128
CONV = 4
GROUP = 256
HALF = GROUP // 2
BLOCK = 256
PER_BLOCK = BLOCK // HEAD_DIM
HALO = 8
INNER = 4096
EPSILON = 1e-05
PRECISE = lax.Precision.HIGHEST
PARTS = 4
FORWARD_INS, FORWARD_OUTS = 16, 9
BACKWARD_INS, BACKWARD_OUTS = 23, 9
F32 = jnp.float32
BF16 = jnp.bfloat16


def mm(former, latter, precision=None):
    return jnp.dot(former, latter, preferred_element_type=F32, precision=precision)


def head_sums(values, place):
    high = values.astype(BF16)
    rest = values - high.astype(F32)
    middle = rest.astype(BF16)
    low = (rest - middle.astype(F32)).astype(BF16)
    return mm(high, place) + (mm(middle, place) + mm(low, place))


def mm_nt(former, latter):
    return lax.dot_general(
        former, latter, (((1,), (1,)), ((), ())), preferred_element_type=F32
    )


def mm_tn(former, latter):
    return lax.dot_general(
        former, latter, (((0,), (0,)), ((), ())), preferred_element_type=F32
    )


def iota(shape, axis):
    return lax.broadcasted_iota(jnp.int32, shape, axis)


def expand(columns):
    rows = columns.shape[0]
    lane = iota((rows, 128), 1)
    parts = []
    for pair in range(PER_BLOCK // 2):
        former = jnp.broadcast_to(columns[:, 2 * pair : 2 * pair + 1], (rows, 128))
        latter = jnp.broadcast_to(columns[:, 2 * pair + 1 : 2 * pair + 2], (rows, 128))
        parts.append(jnp.where(lane < HEAD_DIM, former, latter))
    return jnp.concatenate(parts, axis=1)


def lane_mask(head):
    lane = iota((1, BLOCK), 1)
    return ((lane // HEAD_DIM) == head).astype(F32).astype(BF16)


def spread(ref, values, blocks):
    for block in range(blocks):
        shift = (128 - PER_BLOCK * block) % 128
        ref[block] = pltpu.roll(values, shift, 1) if shift else values


def token_quantities(step_in, cums, cols, decay_rate):
    step = jnp.maximum(step_in, 0.0) + jnp.log1p(jnp.exp(-jnp.abs(step_in)))
    final = cums[GROUP - 1 : GROUP, :]
    entering = jnp.exp(cums) * cols[:, 6:7]
    fading = jnp.exp(final - cums) * cols[:, 7:8]
    retain = jnp.exp(final) * cols[0:1, 8:9]
    return step, entering, fading, retain


def shifted_values(buf, cols):
    moved = [buf[HALO : HALO + GROUP, :]]
    for offset in range(1, CONV):
        before = buf[HALO - offset : HALO - offset + GROUP, :]
        moved.append(jnp.where(cols[:, offset - 1 : offset] > 0.0, before, 0.0))
    return moved


def conv_of(moved, taps, bias):
    total = bias + taps[0:1, :] * moved[0]
    for offset in range(1, CONV):
        total = total + taps[offset : offset + 1, :] * moved[offset]
    return total


MESH = pl.DeviceIdType.MESH


def part_of(ref, at, size, axis):
    if axis == 0:
        return ref.at[pl.ds(pl.multiple_of(at * size, size), size), :]
    if axis == 1:
        return ref.at[:, pl.ds(pl.multiple_of(at * size, size), size)]
    return ref.at[at]


def greet(devices):
    barrier = pltpu.get_barrier_semaphore()
    for device in devices:
        pl.semaphore_signal(barrier, inc=1, device_id=device, device_id_type=MESH)
    pl.semaphore_wait(barrier, len(devices))


def remote_copy(source, target, sends, receives, device):
    return pltpu.make_async_remote_copy(
        src_ref=source, dst_ref=target, send_sem=sends, recv_sem=receives,
        device_id=device, device_id_type=MESH,
    )


class LineScatter:
    def __init__(self, size, source, own, slots, last, own_sem, send_sem, recv_sem, last_sem):
        self.size, self.source, self.own, self.slots, self.last = size, source, own, slots, last
        self.own_sem, self.send_sem, self.recv_sem, self.last_sem = own_sem, send_sem, recv_sem, last_sem
        self.me, self.column = lax.axis_index("tp"), lax.axis_index("fsdp")
        self.rows = last.shape[0]

    @staticmethod
    def scratch(size, rows, width):
        hops = size - 1
        return [
            pltpu.VMEM((2, hops, rows, width), BF16), pltpu.VMEM((2, hops, rows, width), BF16),
            pltpu.VMEM((rows, width), BF16), pltpu.SemaphoreType.DMA((2, hops)),
            pltpu.SemaphoreType.DMA((2, hops, PARTS)), pltpu.SemaphoreType.DMA((2, hops, PARTS)),
            pltpu.SemaphoreType.DMA((1,)),
        ]

    def place(self, flow):
        return self.me if flow == 0 else self.size - 1 - self.me

    def part(self, part):
        rows = self.rows // PARTS
        return pl.ds(part * rows, rows)

    def local(self, flow, hop):
        block = self.size - 1 - hop + self.place(flow)
        if flow:
            block = self.size - 1 - block
        at = pl.multiple_of(block * self.rows, self.rows)
        return pltpu.make_async_copy(
            self.source.at[pl.ds(at, self.rows), :], self.own.at[flow, hop], self.own_sem.at[flow, hop]
        )

    def final(self):
        at = pl.multiple_of(self.me * self.rows, self.rows)
        return pltpu.make_async_copy(
            self.source.at[pl.ds(at, self.rows), :], self.last, self.last_sem.at[0]
        )

    def sending(self, flow, hop, part):
        neighbour = self.me + 1 if flow == 0 else self.me - 1
        neighbour = jnp.clip(neighbour, 0, self.size - 1)
        return remote_copy(
            self.own.at[flow, hop, self.part(part), :], self.slots.at[flow, hop, self.part(part), :],
            self.send_sem.at[flow, hop, part], self.recv_sem.at[flow, hop, part],
            (self.column, neighbour),
        )

    def begin(self):
        self.final().start()
        for hop in range(self.size - 1):
            for flow in range(2):

                @pl.when(self.place(flow) <= hop)
                def _():
                    self.local(flow, hop).start()

    def hop(self, hop, part):
        rows = self.part(part)
        for flow in range(2):
            place = self.place(flow)

            @pl.when(place <= hop)
            def _():
                if part == 0:
                    self.local(flow, hop).wait()
                if hop > 0:

                    @pl.when(place >= 1)
                    def _():
                        self.sending(flow, hop - 1, part).wait_recv()
                        total = self.own[flow, hop, rows, :].astype(F32)
                        total = total + self.slots[flow, hop - 1, rows, :].astype(F32)
                        self.own[flow, hop, rows, :] = total.astype(BF16)

                self.sending(flow, hop, part).start()

    def end(self, out, part):
        hops = self.size - 1
        rows = self.part(part)
        if part == 0:
            self.final().wait()
        out[rows, :] = self.last[rows, :].astype(F32)
        for flow in range(2):

            @pl.when(self.place(flow) >= 1)
            def _():
                self.sending(flow, hops - 1, part).wait_recv()
                out[rows, :] += self.slots[flow, hops - 1, rows, :].astype(F32)

        for hop in range(hops):
            for flow in range(2):

                @pl.when(self.place(flow) <= hop)
                def _():
                    self.sending(flow, hop, part).wait_send()


class LineGather:
    def __init__(self, size, source, target, own_sem, send_sem, recv_sem):
        self.size, self.source, self.target = size, source, target
        self.own_sem, self.send_sem, self.recv_sem = own_sem, send_sem, recv_sem
        self.me, self.column = lax.axis_index("tp"), lax.axis_index("fsdp")
        self.rows = source.shape[0]

    @staticmethod
    def scratch(size):
        return [
            pltpu.SemaphoreType.DMA((1,)), pltpu.SemaphoreType.DMA((2, size - 1, PARTS)),
            pltpu.SemaphoreType.DMA((2, size - 1, PARTS)),
        ]

    def place(self, flow):
        return self.me if flow == 0 else self.size - 1 - self.me

    def block(self, at):
        at = pl.multiple_of(jnp.clip(at, 0, self.size - 1) * self.rows, self.rows)
        return self.target.at[pl.ds(at, self.rows), :]

    def sending(self, flow, hop, part):
        neighbour = self.me + 1 if flow == 0 else self.me - 1
        neighbour = jnp.clip(neighbour, 0, self.size - 1)
        rows = pl.ds(part * (self.rows // PARTS), self.rows // PARTS)
        block = self.block(self.me - hop if flow == 0 else self.me + hop).at[rows, :]
        return remote_copy(
            self.source.at[rows, :] if hop == 0 else block, block, self.send_sem.at[flow, hop, part],
            self.recv_sem.at[flow, hop, part], (self.column, neighbour),
        )

    def local(self):
        return pltpu.make_async_copy(self.source, self.block(self.me), self.own_sem.at[0])

    def hop(self, hop, part):
        if hop == 0 and part == 0:
            self.local().start()
        for flow in range(2):
            place = self.place(flow)
            if hop > 0:

                @pl.when(place >= hop)
                def _():
                    self.sending(flow, hop - 1, part).wait_recv()

            if hop < self.size - 1:

                @pl.when((place >= hop) & (place < self.size - 1))
                def _():
                    self.sending(flow, hop, part).start()

    def end(self, part):
        self.hop(self.size - 1, part)
        if part == 0:
            self.local().wait()
        for hop in range(self.size - 1):
            for flow in range(2):
                place = self.place(flow)

                @pl.when((place >= hop) & (place < self.size - 1))
                def _():
                    self.sending(flow, hop, part).wait_send()


def run_line(step, steps, scatter, gather, out, early):
    size = (scatter or gather).size
    first = 1 if scatter and gather else 0
    actions = [[] for _ in range(PARTS * (size + first))]
    for part in range(PARTS):
        if gather:
            for hop in range(size - 1):
                actions[PARTS * hop + part].append(partial(gather.hop, hop, part))
            actions[PARTS * (size - 1) + part].append(partial(gather.end, part))
        if scatter:
            for hop in range(size - 1):
                actions[PARTS * (first + hop) + part].append(partial(scatter.hop, hop, part))
            actions[PARTS * (first + size - 1) + part].append(partial(scatter.end, out, part))
    if scatter:
        actions[0].insert(0, scatter.begin)
    for at in sorted(set(steps)):
        if (at == 0) != early:
            continue
        todo = [action for when, each in zip(steps, actions) if when == at for action in each]

        @pl.when(step == at)
        def _():
            for action in todo:
                action()


class Hosted:
    def __init__(self, size, scatter=None, gather=None):
        self.size, self.scatter, self.gather = size, scatter, gather

    def operands(self):
        return [each for each in (self.scatter, self.gather) if each is not None]

    def in_specs(self):
        return [pl.BlockSpec(memory_space=pl.ANY)] * len(self.operands())

    def outs(self):
        shapes, specs = [], []
        if self.scatter is not None:
            rows, width = self.scatter.shape[0] // self.size, self.scatter.shape[1]
            shapes.append(shape((rows, width)))
            specs.append(pl.BlockSpec((rows, width), lambda g, j: (0, 0)))
        if self.gather is not None:
            rows, width = self.gather.shape
            shapes.append(shape((rows * self.size, width), BF16))
            specs.append(pl.BlockSpec(memory_space=pl.ANY))
        return specs, shapes

    def scratch(self):
        needed = []
        if self.scatter is not None:
            rows, width = self.scatter.shape[0] // self.size, self.scatter.shape[1]
            needed += LineScatter.scratch(self.size, rows, width)
        if self.gather is not None:
            needed += LineGather.scratch(self.size)
        return needed

    def wrap(self, body, ins, outs, pace, resident):
        has_scatter, has_gather = self.scatter is not None, self.gather is not None
        hosts = has_scatter + has_gather
        size, spare, kept = self.size, len(self.scratch()), len(resident) + 1

        def kernel(*refs):
            refs, stored = refs[: len(refs) - kept], refs[len(refs) - kept :]
            tail = refs[len(refs) - spare :]
            sources, targets = refs[ins : ins + hosts], refs[ins + hosts + outs : ins + outs + 2 * hosts]
            step = pl.program_id(0) * pl.num_programs(1) + pl.program_id(1)
            me, column = lax.axis_index("tp"), lax.axis_index("fsdp")
            operands = list(refs[:ins])
            loads = []
            for at, (which, _, need) in enumerate(resident):
                copy = pltpu.make_async_copy(operands[which], stored[at], stored[-1].at[at])
                operands[which] = stored[at]
                loads.append((copy, need))

            @pl.when(step == 0)
            def _():
                for copy, _ in loads:
                    copy.start()
                if hosts:
                    greet([(column, lax.rem(me + hop, size)) for hop in range(1, size)])

            if hosts:
                scatter = LineScatter(size, sources[0], *tail[:7]) if has_scatter else None
                gather = LineGather(size, sources[-1], targets[-1], *tail[-3:]) if has_gather else None
                run_line(step, pace, scatter, gather, targets[0], True)
            for when in sorted(set(need for _, need in loads)):

                @pl.when(step == when)
                def _():
                    for copy, need in loads:
                        if need == when:
                            copy.wait()

            body(
                *operands, *refs[ins + hosts : ins + hosts + outs],
                *refs[ins + outs + 2 * hosts : len(refs) - spare],
            )
            if hosts:
                run_line(step, pace, scatter, gather, targets[0], False)

        return kernel


def resident_scratch(resident):
    return [pltpu.VMEM(array.shape, array.dtype) for _, array, _ in resident] + [
        pltpu.SemaphoreType.DMA((len(resident),))
    ]


def forward_kernel(
    in_ref, gate_w, value_w, state_w, step_w, taps_ref, bias_ref, staps_ref, sbias_ref,
    step_bias_ref, rate_ref, skip_ref, cols_ref, seg_ref, out_w, gain_ref,
    gate_out, value_out, mixed_out, bc_out, sraw_out, stepin_out, cums_out, held_out, made_out,
    vbuf, sbuf, gram_s, b_t, c_s, step_s, ent_s, fade_s, cums_s, cums_t, keep_s, hidden, made,
):
    g, j = pl.program_id(0), pl.program_id(1)
    blocks = pl.num_programs(1)
    nblocks = hidden.shape[0]
    rows = in_ref[...]
    cols = cols_ref[...]

    @pl.when(j == 0)
    def _():
        sbuf[0:HALO, :] = sbuf[GROUP : GROUP + HALO, :]
        raw = mm(rows, state_w[...])
        sbuf[HALO : HALO + GROUP, :] = raw
        sraw_out[...] = raw
        conv = conv_of(shifted_values(sbuf, cols), staps_ref[...], sbias_ref[...])
        bc = (conv * jax.nn.sigmoid(conv)).astype(BF16)
        bc_out[...] = bc
        b_low, c_low = bc[:, :STATE], bc[:, STATE:]
        b_t[...] = jnp.transpose(b_low.astype(F32)).astype(BF16)
        c_s[...] = c_low
        step_in = mm(rows, step_w[...]) + step_bias_ref[...]
        stepin_out[...] = step_in
        step = jnp.maximum(step_in, 0.0) + jnp.log1p(jnp.exp(-jnp.abs(step_in)))
        at_row, at_col = iota((GROUP, GROUP), 0), iota((GROUP, GROUP), 1)
        lower = (at_row >= at_col).astype(F32)
        cums = mm(lower, step * rate_ref[...], PRECISE)
        cums_out[...] = cums
        step, entering, fading, retain = token_quantities(step_in, cums, cols, rate_ref[...])
        spread(step_s, step, nblocks)
        spread(ent_s, entering, nblocks)
        spread(fade_s, fading, nblocks)
        spread(cums_s, cums, nblocks)
        spread(keep_s, jnp.broadcast_to(retain, (8, 128)), nblocks)
        cums_t[...] = jnp.transpose(cums)
        within = (at_row >= at_col) & (cols[:, 9:10] == seg_ref[...])
        gram_s[...] = jnp.where(within, mm_nt(c_low, b_low), 0.0)

    at = pl.multiple_of(j * BLOCK, BLOCK)
    gate = mm(rows, gate_w[:, pl.ds(at, BLOCK)])
    gate_out[...] = gate.astype(BF16)
    value = mm(rows, value_w[:, pl.ds(at, BLOCK)])
    value_out[...] = value
    mine = vbuf.at[j]
    mine[0:HALO, :] = mine[GROUP : GROUP + HALO, :]
    mine[HALO : HALO + GROUP, :] = value
    conv = conv_of(shifted_values(mine, cols), taps_ref[...], bias_ref[...])
    x_low = (conv * jax.nn.sigmoid(conv)).astype(BF16)
    x_float = x_low.astype(F32)
    scaled_float = expand(step_s[j]) * x_float
    scaled = scaled_float.astype(BF16)

    @pl.when(g == 0)
    def _():
        hidden[j] = jnp.zeros((STATE, BLOCK), F32)

    state = hidden[j]
    state_low = state.astype(BF16)
    held_out[0] = state_low
    total = expand(ent_s[j]) * mm(c_s[...], state_low)
    weighted = (expand(fade_s[j]) * scaled.astype(F32)).astype(BF16)
    hidden[j] = expand(keep_s[j])[0:1, :] * state + mm(b_t[...], weighted)
    cums_here = cums_s[j]
    top = jnp.zeros((HALF, BLOCK), F32)
    bottom = jnp.zeros((HALF, BLOCK), F32)
    for i in range(PER_BLOCK):
        to = cums_here[:, i : i + 1]
        frm = cums_t[pl.ds(j * PER_BLOCK + i, 1), :]
        only = scaled * lane_mask(i)
        decay = jnp.exp(jnp.minimum(to[:HALF] - frm[:, :HALF], 0.0))
        top = top + mm((gram_s[:HALF, :HALF] * decay).astype(BF16), only[:HALF])
        decay = jnp.exp(jnp.minimum(to[HALF:] - frm, 0.0))
        bottom = bottom + mm((gram_s[HALF:, :] * decay).astype(BF16), only)
    mixed = total + jnp.concatenate([top, bottom], axis=0) + skip_ref[...] * x_float
    mixed_out[...] = mixed
    scaled_gate = (mixed * (gate * jax.nn.sigmoid(gate)) * gain_ref[...]).astype(BF16)

    @pl.when(j == 0)
    def _():
        made[...] = mm(scaled_gate, out_w[pl.ds(at, BLOCK), :])

    @pl.when(j > 0)
    def _():
        made[...] += mm(scaled_gate, out_w[pl.ds(at, BLOCK), :])

    @pl.when(j == blocks - 1)
    def _():
        made_out[...] = made[...].astype(BF16)


def backward_kernel(
    tp_size, cot_ref, out_w, gate_rows, mixed_rows, gain_row,
    gate_ref, value_ref, before_ref, mixed_ref, bc_ref, stepin_ref, cums_ref, held_ref,
    gate_w, value_w, step_w, taps_ref, bias_ref, rate_ref, skip_ref, gain_ref, cols_ref, seg_ref,
    branch_out, lowgate_out, lowvalue_out, lowstep_out, gbc_out, gin_out, small_out, sums_out, stats_out,
    vbuf, gcbuf, gram_s, dgram, b_s, c_t, step_s, ent_s, fade_s, cums_s, cums_t, keep_s, grad_state,
    gin, gb_s, gc_s, u_s, v_s, fin_s, small_s, sums_s,
    branch_s, rowsum_s, slots_s, turn_s, stats_s, swap_send, swap_recv,
):
    g, j = pl.program_id(0) - 1, pl.program_id(1)
    groups, blocks = pl.num_programs(0) - 1, pl.num_programs(1)

    @pl.when(g < 0)
    def _():
        row_sums(
            tp_size, cot_ref, out_w, gate_rows, mixed_rows, gain_row,
            branch_s, rowsum_s, slots_s, swap_send, swap_recv,
        )

    scales = partial(
        row_scales, tp_size, gain_row.shape[1] * tp_size, rowsum_s, slots_s, turn_s, swap_send,
        swap_recv, stats_s, stats_out,
    )

    @pl.when(g >= 0)
    def _():
        backward_step(
            g, j, groups, blocks, gate_ref, value_ref, before_ref, mixed_ref,
            bc_ref, stepin_ref, cums_ref, held_ref,
            gate_w, value_w, step_w, taps_ref, bias_ref, rate_ref, skip_ref, gain_ref, cols_ref, seg_ref,
            branch_out, lowgate_out, lowvalue_out, lowstep_out, gbc_out, gin_out, small_out, sums_out,
            vbuf, gcbuf, gram_s, dgram, b_s, c_t, step_s, ent_s, fade_s, cums_s, cums_t, keep_s,
            grad_state, gin, gb_s, gc_s, u_s, v_s, fin_s, small_s, sums_s, branch_s, stats_s, scales,
        )


def row_sums(
    tp_size, cot_ref, out_w, gate_rows, mixed_rows, gain_row,
    branch_s, rowsum_s, slots_s, swap_send, swap_recv,
):
    step, groups = pl.program_id(1), pl.num_programs(1)
    me, column = lax.axis_index("tp"), lax.axis_index("fsdp")
    grad = mm_nt(cot_ref[...], out_w[...])
    branch_s[step] = grad.astype(BF16)
    gate = gate_rows[...].astype(F32)
    gated = mixed_rows[...] * (gate * jax.nn.sigmoid(gate))
    squares = jnp.sum(gated * gated, axis=1, keepdims=True)
    inner = jnp.sum(grad * gain_row[...] * gated, axis=1, keepdims=True)
    lane = iota((GROUP, 128), 1)
    both = jnp.where(lane == 0, squares, jnp.where(lane == 1, inner, 0.0))
    rowsum_s[step] = jnp.transpose(both)[:8]

    @pl.when(step == groups - 1)
    def _():
        slots_s[me] = rowsum_s[...]
        for copy in row_swaps(tp_size, rowsum_s, slots_s, swap_send, swap_recv):
            copy.start()


def row_swaps(tp_size, rowsum_s, slots_s, swap_send, swap_recv):
    me, column = lax.axis_index("tp"), lax.axis_index("fsdp")
    return [
        remote_copy(
            rowsum_s, slots_s.at[me], swap_send.at[hop - 1], swap_recv.at[hop - 1],
            (column, lax.rem(me + hop, tp_size)),
        )
        for hop in range(1, tp_size)
    ]


def row_scales(tp_size, total_inner, rowsum_s, slots_s, turn_s, swap_send, swap_recv, stats_s, stats_out):
    for copy in row_swaps(tp_size, rowsum_s, slots_s, swap_send, swap_recv):
        copy.wait()
    total = slots_s[0]
    for at in range(1, tp_size):
        total = total + slots_s[at]
    turn_s[...] = jnp.zeros(turn_s.shape, F32)
    scale = lax.rsqrt(total[:, 0:1, :] / total_inner + EPSILON)
    turn_s[:, 0:1, :] = scale
    turn_s[:, 1:2, :] = scale * scale * scale * (total[:, 1:2, :] / total_inner)
    for group in range(turn_s.shape[0]):
        stats_s[group * GROUP : (group + 1) * GROUP, :] = jnp.transpose(turn_s[group])
    rows = stats_out.shape[0]
    stats_out[...] = stats_s[pl.ds(pl.multiple_of(lax.axis_index("tp") * rows, rows), rows), :]


def backward_step(
    g, j, groups, blocks, gate_ref, value_ref, before_ref, mixed_ref,
    bc_ref, stepin_ref, cums_ref, held_ref,
    gate_w, value_w, step_w, taps_ref, bias_ref, rate_ref, skip_ref, gain_ref, cols_ref, seg_ref,
    branch_out, lowgate_out, lowvalue_out, lowstep_out, gbc_out, gin_out, small_out, sums_out,
    vbuf, gcbuf, gram_s, dgram, b_s, c_t, step_s, ent_s, fade_s, cums_s, cums_t, keep_s,
    grad_state, gin, gb_s, gc_s, u_s, v_s, fin_s, small_s, sums_s, branch_s, stats_ref, scales,
):
    group = groups - 1 - g
    nblocks = grad_state.shape[0]
    cols = cols_ref[...]
    at_row, at_col = iota((GROUP, GROUP), 0), iota((GROUP, GROUP), 1)

    @pl.when((g == 0) & (j == 0))
    def _():
        grad_state[...] = jnp.zeros(grad_state.shape, F32)
        small_s[...] = jnp.zeros(small_s.shape, F32)
        sums_s[...] = jnp.zeros(sums_s.shape, F32)
        gcbuf[...] = jnp.zeros(gcbuf.shape, F32)

    @pl.when(j == 0)
    def _():
        bc = bc_ref[...]
        b_low, c_low = bc[:, :STATE], bc[:, STATE:]
        b_s[...] = b_low
        c_t[...] = jnp.transpose(c_low.astype(F32)).astype(BF16)
        cums = cums_ref[...]
        step, entering, fading, retain = token_quantities(stepin_ref[...], cums, cols, rate_ref[...])
        spread(step_s, step, nblocks)
        spread(ent_s, entering, nblocks)
        spread(fade_s, fading, nblocks)
        spread(cums_s, cums, nblocks)
        spread(keep_s, jnp.broadcast_to(retain, (8, 128)), nblocks)
        cums_t[...] = jnp.transpose(cums)
        within = (at_row <= at_col) & (cols[:, 9:10] == seg_ref[...])
        gram_s[...] = jnp.where(within, mm_nt(b_low, c_low), 0.0)
        dgram[...] = jnp.zeros(dgram.shape, F32)
        gin[...] = jnp.zeros(gin.shape, F32)
        gb_s[...] = jnp.zeros(gb_s.shape, F32)
        gc_s[...] = jnp.zeros(gc_s.shape, F32)
        u_s[...] = jnp.zeros(u_s.shape, F32)
        v_s[...] = jnp.zeros(v_s.shape, F32)
        fin_s[...] = jnp.zeros(fin_s.shape, F32)

    @pl.when((g == 0) & (j == 0))
    def _():
        scales()

    at = pl.multiple_of(j * BLOCK, BLOCK)
    gate, mixed = gate_ref[...].astype(F32), mixed_ref[...]
    grad = branch_s[group, :, pl.ds(at, BLOCK)].astype(F32)
    gain, skip, taps = gain_ref[...], skip_ref[...], taps_ref[...]
    stats = stats_ref[pl.ds(pl.multiple_of(group * GROUP, GROUP), GROUP), :]
    scale, inner = stats[:, 0:1], stats[:, 1:2]
    sig = jax.nn.sigmoid(gate)
    act = gate * sig
    gated = mixed * act
    scaled_gated = gated * scale
    branch_out[...] = (scaled_gated * gain).astype(BF16)
    grad_gain = jnp.sum(grad * scaled_gated, axis=0, keepdims=True)
    grad_gated = scale * (grad * gain) - gated * inner
    grad_mixed = grad_gated * act
    low_gate = (grad_gated * mixed * (sig * (1.0 + gate * (1.0 - sig)))).astype(BF16)
    lowgate_out[...] = low_gate

    vbuf[0:HALO, :] = before_ref[...]
    vbuf[HALO : HALO + GROUP, :] = value_ref[...]
    moved = shifted_values(vbuf, cols)
    conv = conv_of(moved, taps, bias_ref[...])
    sig = jax.nn.sigmoid(conv)
    x_float = (conv * sig).astype(BF16).astype(F32)
    slope = sig * (1.0 + conv * (1.0 - sig))
    step_wide = expand(step_s[j])
    fade_wide = expand(fade_s[j])
    scaled = (step_wide * x_float).astype(BF16)
    scaled_float = scaled.astype(F32)
    grad_skip = jnp.sum(grad_mixed * x_float, axis=0, keepdims=True)
    grad_scan = grad_mixed.astype(BF16)
    grad_scan_float = grad_scan.astype(F32)
    scanned = mixed - skip * x_float

    own = grad_state[j]
    state_low = held_ref[0]
    own_low = own.astype(BF16)
    grad_weighted = mm(b_s[...], own_low)
    weighted = (fade_wide * scaled_float).astype(BF16)
    entered = (expand(ent_s[j]) * grad_scan_float).astype(BF16)
    gb_s[...] += mm_nt(weighted, own_low)
    gc_s[...] += mm_nt(entered, state_low)
    keep_wide = expand(keep_s[j])[0:1, :]
    kept = keep_wide * jnp.sum(state_low.astype(F32) * own, axis=0, keepdims=True)
    grad_state[j] = keep_wide * own + mm(c_t[...], entered)

    cums_here = cums_s[j]
    top = jnp.zeros((HALF, BLOCK), F32)
    bottom = jnp.zeros((HALF, BLOCK), F32)
    dtop = dgram[:HALF, :]
    dbottom = dgram[HALF:, HALF:]
    for i in range(PER_BLOCK):
        frm = cums_here[:, i : i + 1]
        to = cums_t[pl.ds(j * PER_BLOCK + i, 1), :]
        mask = lane_mask(i)
        only_grad = grad_scan * mask
        only = scaled * mask
        decay = jnp.exp(jnp.minimum(to - frm[:HALF], 0.0))
        top = top + mm((gram_s[:HALF, :] * decay).astype(BF16), only_grad)
        dtop = dtop + mm_nt(only[:HALF], grad_scan) * decay
        decay = jnp.exp(jnp.minimum(to[:, HALF:] - frm[HALF:], 0.0))
        bottom = bottom + mm((gram_s[HALF:, HALF:] * decay).astype(BF16), only_grad[HALF:])
        dbottom = dbottom + mm_nt(only[HALF:], grad_scan[HALF:]) * decay
    dgram[:HALF, :] = dtop
    dgram[HALF:, HALF:] = dbottom
    faded = fade_wide * grad_weighted
    through = jnp.concatenate([top, bottom], axis=0) + faded
    column = scaled_float * through
    final = kept + jnp.sum(scaled_float * faded, axis=0, keepdims=True)
    place = iota((BLOCK, 128), 1) == j * PER_BLOCK + iota((BLOCK, 128), 0) // HEAD_DIM
    place = place.astype(F32).astype(BF16)
    u_s[...] += head_sums(grad_scan_float * scanned - column, place)
    v_s[...] += head_sums(column, place)
    fin_s[...] += head_sums(jnp.broadcast_to(final, (8, BLOCK)), place)

    grad_conv = (step_wide * through + skip * grad_mixed) * slope
    after = gcbuf.at[j]
    after[GROUP : GROUP + HALO, :] = after[0:HALO, :]
    after[0:GROUP, :] = grad_conv
    grad_value = taps[0:1, :] * grad_conv
    for offset in range(1, CONV):
        up = jnp.where(cols[:, 2 + offset : 3 + offset] > 0.0, after[offset : offset + GROUP, :], 0.0)
        grad_value = grad_value + taps[offset : offset + 1, :] * up
    low_value = grad_value.astype(BF16)
    lowvalue_out[...] = low_value
    gin[...] += mm_nt(low_gate, gate_w[:, pl.ds(at, BLOCK)]) + mm_nt(low_value, value_w[:, pl.ds(at, BLOCK)])
    lines = [grad_gain, grad_skip]
    lines += [jnp.sum(grad_conv * moved[offset], axis=0, keepdims=True) for offset in range(CONV)]
    lines += [jnp.sum(grad_conv, axis=0, keepdims=True)]
    for at_line, line in enumerate(lines):
        small_s[j, at_line : at_line + 1, :] += line

    @pl.when(g == groups - 1)
    def _():
        small_out[:, pl.ds(at, BLOCK)] = small_s[j]

    @pl.when(j == blocks - 1)
    def _():
        bc = bc_ref[...]
        within = (at_row <= at_col) & (cols[:, 9:10] == seg_ref[...])
        dg = jnp.where(within, dgram[...], 0.0)
        grad_b = gb_s[...] + mm(dg.astype(BF16), bc[:, STATE:])
        grad_c = gc_s[...] + mm(jnp.transpose(dg).astype(BF16), bc[:, :STATE])
        gbc_out[:, :STATE] = grad_b.astype(BF16)
        gbc_out[:, STATE:] = grad_c.astype(BF16)
        last = iota((GROUP, 128), 0) == GROUP - 1
        grad_cums = u_s[...] + jnp.where(last, fin_s[0:1, :], 0.0)
        upper = (at_row <= at_col).astype(F32)
        grad_a = mm(upper, grad_cums, PRECISE)
        step_in = stepin_ref[...]
        step = jnp.maximum(step_in, 0.0) + jnp.log1p(jnp.exp(-jnp.abs(step_in)))
        sig_in = jax.nn.sigmoid(step_in)
        ratio = jnp.where(step_in < -15.0, 1.0, sig_in / step)
        grad_step = v_s[...] * ratio + grad_a * rate_ref[...] * sig_in
        low_step = grad_step.astype(BF16)
        lowstep_out[...] = low_step
        sums_s[0:1, :] += jnp.sum(grad_step, axis=0, keepdims=True)
        sums_s[1:2, :] += jnp.sum(grad_a * step, axis=0, keepdims=True)
        sums_out[...] = sums_s[...]
        gin_out[...] = (gin[...] + mm_nt(low_step, step_w[...])).astype(BF16)


def shape(dims, kind=F32):
    return jax.ShapeDtypeStruct(dims, kind)


def params(collective=None):
    extra = {} if collective is None else dict(collective_id=collective, has_side_effects=True)
    return pltpu.CompilerParams(
        dimension_semantics=("arbitrary", "arbitrary"), vmem_limit_bytes=60 << 20, **extra
    )


def whole(array):
    return pl.BlockSpec(
        array.shape, lambda g, j: (0,) * array.ndim, pipeline_mode=pl.Buffered(1)
    )


def forward_call(inputs, weights, vectors, gain, cols, seg_line, hosted, pace):
    gate_w, value_w, state_w, step_w, out_w = weights
    taps, bias, staps, sbias, step_bias, rate, skip = vectors
    length, model = inputs.shape
    inner = gate_w.shape[1]
    groups, blocks = length // GROUP, inner // BLOCK
    wide = pl.BlockSpec((GROUP, BLOCK), lambda g, j: (g, j))
    line = lambda rows: pl.BlockSpec((rows, BLOCK), lambda g, j: (0, j))
    rows_of = lambda width: pl.BlockSpec((GROUP, width), lambda g, j: (g, 0))
    specs, shapes = hosted.outs()
    hbm = pl.BlockSpec(memory_space=pl.ANY)
    resident = [(1, gate_w, 0), (2, value_w, 0), (3, state_w, 0), (4, step_w, 0), (14, out_w, 0)]
    return pl.pallas_call(
        hosted.wrap(forward_kernel, FORWARD_INS, FORWARD_OUTS, pace, resident),
        grid=(groups, blocks),
        in_specs=[
            rows_of(model), hbm, hbm, hbm, hbm,
            line(CONV), line(1), whole(staps), whole(sbias), whole(step_bias), whole(rate), line(1),
            rows_of(cols.shape[1]), pl.BlockSpec((1, GROUP), lambda g, j: (0, g)),
            hbm, line(1),
        ] + hosted.in_specs(),
        out_specs=[
            wide, wide, wide, rows_of(2 * STATE), rows_of(2 * STATE), rows_of(128), rows_of(128),
            pl.BlockSpec((1, STATE, BLOCK), lambda g, j: (g, 0, j)), rows_of(model),
        ] + specs,
        out_shape=[
            shape((length, inner), BF16), shape((length, inner)), shape((length, inner)),
            shape((length, 2 * STATE), BF16), shape((length, 2 * STATE)), shape((length, 128)),
            shape((length, 128)), shape((groups, STATE, inner), BF16), shape((length, model), BF16),
        ] + shapes,
        scratch_shapes=[
            pltpu.VMEM((blocks, GROUP + HALO, BLOCK), F32),
            pltpu.VMEM((GROUP + HALO, 2 * STATE), F32),
            pltpu.VMEM((GROUP, GROUP), F32),
            pltpu.VMEM((STATE, GROUP), BF16),
            pltpu.VMEM((GROUP, STATE), BF16),
            pltpu.VMEM((blocks, GROUP, 128), F32),
            pltpu.VMEM((blocks, GROUP, 128), F32),
            pltpu.VMEM((blocks, GROUP, 128), F32),
            pltpu.VMEM((blocks, GROUP, 128), F32),
            pltpu.VMEM((128, GROUP), F32),
            pltpu.VMEM((blocks, 8, 128), F32),
            pltpu.VMEM((blocks, STATE, BLOCK), F32),
            pltpu.VMEM((GROUP, model), F32),
        ] + hosted.scratch() + resident_scratch(resident),
        compiler_params=params(2 if hosted.operands() else None),
        cost_estimate=pl.CostEstimate(
            flops=2 * length * model * (3 * inner + 512), bytes_accessed=40 << 20, transcendentals=0
        ),
        name="ssd_forward",
    )(
        inputs, gate_w, value_w, state_w, step_w, taps, bias, staps, sbias, step_bias, rate, skip,
        cols, seg_line, out_w, gain, *hosted.operands(),
    )


def backward_call(saved, cotan, weights, vectors, gain, cols, seg_line, hosted, pace, collective):
    gate_raw, value_raw, mixed, bc, _, step_in, cums, held, _ = saved
    gate_w, value_w, step_w, out_w = weights
    taps, bias, rate, skip = vectors
    length, inner = gate_raw.shape
    model, tp_size = gate_w.shape[0], hosted.size
    specs, shapes = hosted.outs()
    groups, blocks = length // GROUP, inner // BLOCK
    assert groups == blocks
    last = groups - 1
    hbm = pl.BlockSpec(memory_space=pl.ANY)
    resident = [(1, out_w, 0), (13, gate_w, blocks), (14, value_w, blocks), (15, step_w, blocks)]
    row = lambda g: last - jnp.maximum(g - 1, 0)
    column = lambda g, j: jnp.where(g == 0, 0, j)
    wide = pl.BlockSpec((GROUP, BLOCK), lambda g, j: (row(g), column(g, j)))
    line = lambda rows: pl.BlockSpec((rows, BLOCK), lambda g, j: (0, column(g, j)))
    rows_of = lambda width: pl.BlockSpec((GROUP, width), lambda g, j: (row(g), 0))
    first = lambda width: pl.BlockSpec((GROUP, width), lambda g, j: (jnp.where(g == 0, j, last), 0))
    steps = GROUP // HALO
    before = pl.BlockSpec(
        (HALO, BLOCK), lambda g, j: (jnp.maximum(row(g) * steps - 1, 0), column(g, j))
    )
    return pl.pallas_call(
        hosted.wrap(partial(backward_kernel, tp_size), BACKWARD_INS, BACKWARD_OUTS, pace, resident),
        grid=(groups + 1, blocks),
        in_specs=[
            first(model), hbm, first(inner), first(inner), whole(gain),
            wide, wide, before, wide, rows_of(2 * STATE), rows_of(128), rows_of(128),
            pl.BlockSpec((1, STATE, BLOCK), lambda g, j: (row(g), 0, column(g, j))),
            hbm, hbm, hbm,
            line(CONV), line(1), whole(rate), line(1), line(1),
            rows_of(cols.shape[1]), pl.BlockSpec((1, GROUP), lambda g, j: (0, row(g))),
        ] + hosted.in_specs(),
        out_specs=[
            wide, wide, wide, rows_of(128), rows_of(2 * STATE),
            rows_of(model), pl.BlockSpec((8, inner), lambda g, j: (0, 0)), pl.BlockSpec((8, 128), lambda g, j: (0, 0)),
            pl.BlockSpec((length // tp_size, 128), lambda g, j: (0, 0)),
        ] + specs,
        out_shape=[
            shape((length, inner), BF16), shape((length, inner), BF16), shape((length, inner), BF16),
            shape((length, 128), BF16), shape((length, 2 * STATE), BF16),
            shape((length, model), BF16), shape((8, inner)), shape((8, 128)),
            shape((length // tp_size, 128)),
        ] + shapes,
        scratch_shapes=[
            pltpu.VMEM((GROUP + HALO, BLOCK), F32),
            pltpu.VMEM((blocks, GROUP + HALO, BLOCK), F32),
            pltpu.VMEM((GROUP, GROUP), F32),
            pltpu.VMEM((GROUP, GROUP), F32),
            pltpu.VMEM((GROUP, STATE), BF16),
            pltpu.VMEM((STATE, GROUP), BF16),
            pltpu.VMEM((blocks, GROUP, 128), F32),
            pltpu.VMEM((blocks, GROUP, 128), F32),
            pltpu.VMEM((blocks, GROUP, 128), F32),
            pltpu.VMEM((blocks, GROUP, 128), F32),
            pltpu.VMEM((128, GROUP), F32),
            pltpu.VMEM((blocks, 8, 128), F32),
            pltpu.VMEM((blocks, STATE, BLOCK), F32),
            pltpu.VMEM((GROUP, model), F32),
            pltpu.VMEM((GROUP, STATE), F32),
            pltpu.VMEM((GROUP, STATE), F32),
            pltpu.VMEM((GROUP, 128), F32),
            pltpu.VMEM((GROUP, 128), F32),
            pltpu.VMEM((8, 128), F32),
            pltpu.VMEM((blocks, 8, BLOCK), F32),
            pltpu.VMEM((8, 128), F32),
            pltpu.VMEM((groups, GROUP, inner), BF16),
            pltpu.VMEM((groups, 8, GROUP), F32),
            pltpu.VMEM((tp_size, groups, 8, GROUP), F32),
            pltpu.VMEM((groups, 128, GROUP), F32),
            pltpu.VMEM((length, 128), F32),
            pltpu.SemaphoreType.DMA((tp_size - 1,)),
            pltpu.SemaphoreType.DMA((tp_size - 1,)),
        ] + hosted.scratch() + resident_scratch(resident),
        compiler_params=params(collective),
        cost_estimate=pl.CostEstimate(
            flops=6 * length * model * inner, bytes_accessed=60 << 20, transcendentals=0
        ),
        name="ssd_backward",
    )(
        cotan, out_w, gate_raw, mixed, gain,
        gate_raw, value_raw, value_raw, mixed, bc, step_in, cums, held,
        gate_w, value_w, step_w, taps, bias, rate, skip, gain, cols, seg_line, *hosted.operands(),
    )

def gather_kernel(count, pieces, *refs):
    amount = len(pieces)
    sources, targets = refs[:amount], refs[amount : 2 * amount]
    own_sem, send_sem, recv_sem, pass_sem, took_sem = refs[2 * amount :]
    me, line = lax.axis_index("fsdp"), lax.axis_index("tp")
    chips = count // 2
    partner = me + 1 - 2 * lax.rem(me, 2)
    others = [lax.rem(me + 2 * hop, count) for hop in range(1, chips)]
    greet([(device, line) for device in others + [partner]])

    def remote(source, target, sends, receives, device):
        return pltpu.make_async_remote_copy(
            src_ref=source, dst_ref=target, send_sem=sends, recv_sem=receives,
            device_id=(device, line), device_id_type=MESH,
        )

    def place(which, at):
        size, axis = pieces[which]
        return part_of(targets[which], at, size, axis)

    started = []
    for which in range(amount):
        for hop in range(1, chips):
            copy = remote(
                sources[which], place(which, me), send_sem.at[hop, which],
                recv_sem.at[hop, which], lax.rem(me + 2 * hop, count),
            )
            copy.start()
            started.append(copy)
    for which in range(amount):
        copy = remote(
            sources[which], place(which, me), pass_sem.at[0, which], took_sem.at[0, which], partner
        )
        copy.start()
        started.append(copy)
    own = []
    for which in range(amount):
        copy = pltpu.make_async_copy(sources[which], place(which, me), own_sem.at[which])
        copy.start()
        own.append(copy)
    for which in range(amount):
        for hop in range(1, chips):
            origin = lax.rem(me - 2 * hop + count, count)
            block = place(which, origin)
            remote(
                block, block, send_sem.at[hop, which], recv_sem.at[hop, which], partner
            ).wait_recv()
            copy = remote(
                block, block, pass_sem.at[hop, which], took_sem.at[hop, which], partner
            )
            copy.start()
            started.append(copy)
    for which in range(amount):
        for hop in range(chips):
            block = place(which, lax.rem(partner - 2 * hop + count, count))
            remote(
                block, block, pass_sem.at[hop, which], took_sem.at[hop, which], partner
            ).wait_recv()
    for copy in started:
        copy.wait_send()
    for copy in own:
        copy.wait()


def gather_call(count, blocks, axes):
    pieces, shapes = [], []
    for block, axis in zip(blocks, axes):
        if axis == 2:
            pieces.append((0, 2))
            shapes.append(shape((count,) + block.shape, BF16))
        else:
            pieces.append((block.shape[axis], axis))
            dims = list(block.shape)
            dims[axis] *= count
            shapes.append(shape(tuple(dims), BF16))
    amount = len(blocks)
    sems = lambda: pltpu.SemaphoreType.DMA((count // 2, amount))
    return pl.pallas_call(
        partial(gather_kernel, count, pieces),
        in_specs=[pl.BlockSpec(memory_space=pl.ANY)] * amount,
        out_specs=[pl.BlockSpec(memory_space=pl.ANY)] * amount,
        out_shape=shapes,
        scratch_shapes=[pltpu.SemaphoreType.DMA((amount,)), sems(), sems(), sems(), sems()],
        compiler_params=pltpu.CompilerParams(collective_id=0, has_side_effects=True),
        cost_estimate=pl.CostEstimate(flops=0, bytes_accessed=250 << 20, transcendentals=0),
        name="gather_weights",
    )(*blocks)


def scatter_kernel(count, pieces, *refs):
    amount = len(pieces)
    sources, targets = refs[:amount], refs[amount : 2 * amount]
    scratch = refs[2 * amount :]
    mine, took, came = (scratch[at * amount : (at + 1) * amount] for at in range(3))
    own_sem, pass_sem, took_sem, send_sem, recv_sem = scratch[3 * amount :]
    me, line = lax.axis_index("fsdp"), lax.axis_index("tp")
    chips = count // 2
    partner = me + 1 - 2 * lax.rem(me, 2)
    others = [lax.rem(me + 2 * hop, count) for hop in range(1, chips)]
    greet([(device, line) for device in others + [partner]])

    def remote(source, target, sends, receives, device):
        return pltpu.make_async_remote_copy(
            src_ref=source, dst_ref=target, send_sem=sends, recv_sem=receives,
            device_id=(device, line), device_id_type=MESH,
        )

    def piece(which, at):
        size, axis = pieces[which]
        return part_of(sources[which], at, size, axis)

    order = list(range(1, chips)) + [0]
    handed, own = {}, {}
    for hop in order:
        for which in range(amount):
            copy = remote(
                piece(which, lax.rem(partner + 2 * hop, count)), took[which].at[hop],
                pass_sem.at[hop, which], took_sem.at[hop, which], partner,
            )
            copy.start()
            handed[hop, which] = copy
            copy = pltpu.make_async_copy(
                piece(which, lax.rem(me + 2 * hop, count)), mine[which].at[hop],
                own_sem.at[hop, which],
            )
            copy.start()
            own[hop, which] = copy
    sent = []
    for hop in order:
        for which in range(amount):
            own[hop, which].wait()
            handed[hop, which].wait_recv()
            total = mine[which][hop].astype(F32) + took[which][hop].astype(F32)
            if hop == 0:
                targets[which][...] = total
                continue
            mine[which][hop] = total.astype(BF16)
            copy = remote(
                mine[which].at[hop], came[which].at[hop - 1], send_sem.at[hop, which],
                recv_sem.at[hop, which], lax.rem(me + 2 * hop, count),
            )
            copy.start()
            sent.append(copy)
    for which in range(amount):
        for hop in range(1, chips):
            block = came[which].at[hop - 1]
            remote(
                block, block, send_sem.at[hop, which], recv_sem.at[hop, which], partner
            ).wait_recv()
            targets[which][...] += block[...].astype(F32)
    for copy in list(handed.values()) + sent:
        copy.wait_send()


def scatter_call(count, arrays, axes):
    pieces, shapes = [], []
    for array, axis in zip(arrays, axes):
        if axis == 2:
            pieces.append((0, 2))
            shapes.append(array.shape[1:])
        else:
            dims = list(array.shape)
            dims[axis] //= count
            pieces.append((dims[axis], axis))
            shapes.append(tuple(dims))
    amount, chips = len(arrays), count // 2
    sems = lambda: pltpu.SemaphoreType.DMA((chips, amount))
    return pl.pallas_call(
        partial(scatter_kernel, count, pieces),
        in_specs=[pl.BlockSpec(memory_space=pl.ANY)] * amount,
        out_specs=[pl.BlockSpec(memory_space=pltpu.VMEM)] * amount,
        out_shape=[shape(dims) for dims in shapes],
        scratch_shapes=[pltpu.VMEM((chips,) + dims, BF16) for dims in shapes]
        + [pltpu.VMEM((chips,) + dims, BF16) for dims in shapes]
        + [pltpu.VMEM((chips - 1,) + dims, BF16) for dims in shapes]
        + [sems(), sems(), sems(), sems(), sems()],
        compiler_params=pltpu.CompilerParams(
            collective_id=1, has_side_effects=True, vmem_limit_bytes=48 << 20
        ),
        cost_estimate=pl.CostEstimate(flops=0, bytes_accessed=250 << 20, transcendentals=0),
        name="scatter_gradients",
    )(*arrays)


def weight_kernel(micro, *refs):
    outs = refs[-4:]
    rows, lows = refs[:micro], refs[micro : 5 * micro]
    for which in range(4):
        total = mm_tn(rows[0][...], lows[which][...])
        for at in range(1, micro):
            total = total + mm_tn(rows[at][...], lows[4 * at + which][...])
        outs[which][...] = total.astype(BF16)


def weight_call(inputs, lows):
    micro, (length, model) = len(inputs), inputs[0].shape
    full = lambda array: pl.BlockSpec(array.shape, lambda g: (0, 0), pipeline_mode=pl.Buffered(1))
    flat = [array for low in lows for array in low]
    widths = [array.shape[1] for array in lows[0]]
    return pl.pallas_call(
        partial(weight_kernel, micro),
        grid=(model // BLOCK,),
        in_specs=[pl.BlockSpec((length, BLOCK), lambda g: (0, g))] * micro
        + [full(array) for array in flat],
        out_specs=[pl.BlockSpec((BLOCK, width), lambda g: (g, 0)) for width in widths],
        out_shape=[shape((model, width), BF16) for width in widths],
        compiler_params=pltpu.CompilerParams(vmem_limit_bytes=50 << 20),
        cost_estimate=pl.CostEstimate(
            flops=2 * micro * length * model * sum(widths), bytes_accessed=40 << 20, transcendentals=0
        ),
        name="weight_gradients",
    )(*inputs, *flat)


def outer_kernel(micro, *refs):
    total = mm_tn(refs[0][...], refs[micro][...])
    for at in range(1, micro):
        total = total + mm_tn(refs[at][...], refs[micro + at][...])
    refs[-1][...] = total.astype(BF16)


def outer_call(branches, cotans):
    micro, (length, inner) = len(branches), branches[0].shape
    model = cotans[0].shape[1]
    full = lambda array: pl.BlockSpec(array.shape, lambda g: (0, 0), pipeline_mode=pl.Buffered(1))
    return pl.pallas_call(
        partial(outer_kernel, micro),
        grid=(inner // BLOCK,),
        in_specs=[pl.BlockSpec((length, BLOCK), lambda g: (0, g))] * micro
        + [full(array) for array in cotans],
        out_specs=pl.BlockSpec((BLOCK, model), lambda g: (g, 0)),
        out_shape=shape((inner, model), BF16),
        compiler_params=pltpu.CompilerParams(vmem_limit_bytes=50 << 20),
        cost_estimate=pl.CostEstimate(
            flops=2 * micro * length * model * inner, bytes_accessed=30 << 20, transcendentals=0
        ),
        name="out_gradients",
    )(*branches, *cotans)


def tail_kernel(chips, tp_size, micro, widths, *refs):
    columns, lows, parts, raws = refs[:4], refs[4:12], refs[12:14], refs[14:16]
    cols_ref, staps_ref, sbias_ref = refs[16:19]
    pieces = refs[19:23]
    outs, state_out, pack_out, ssum_out, low_out = refs[23:27], refs[27], refs[28], refs[29], refs[30]
    (
        cols_s, give, took, mine, came, passed, total_s, kept_s,
        sgive, stook, smine, scame, stotal, skept_s,
        pack, pack_took, pack_sum, pack_slots, ssum, ssum_took, ssum_sum, ssum_slots,
        raw_s, own_s, slots_s, whole_s, sum_s, low_s, vbuf, gcbuf,
        cols_sem, give_sem, took_sem, send_sem, recv_sem, sgive_sem, stook_sem, ssend_sem, srecv_sem,
        pass_sem, pack_sem, ssum_sem, raw_sem, own_sem, part_send, part_recv, whole_send, whole_recv,
        *stored, low_sem,
    ) = refs[31:]
    loads = [
        pltpu.make_async_copy(low, kept, low_sem.at[at])
        for at, (low, kept) in enumerate(zip(lows, stored))
    ]
    lows = stored
    step, steps = pl.program_id(0), pl.num_programs(0)
    me, line = lax.axis_index("fsdp"), lax.axis_index("tp")
    count = 2 * chips
    core, chip = lax.rem(me, 2), me // 2
    partner = me + 1 - 2 * core
    split = total_s.shape[1] // 256 * 128

    def flipped(hop, which_core):
        x, y = lax.rem(chip, 2), chip // 2
        hop_x, hop_y = hop % 2, hop // 2
        x, y = x + hop_x - 2 * x * hop_x, y + hop_y - 2 * y * hop_y
        return (2 * y + x) * 2 + which_core

    def tile_of(at):
        pair = lax.rem(at, count) // 2
        hop = jnp.where(pair == 0, 3, pair - 1)
        return hop, flipped(hop, jnp.where(lax.rem(at, 2) == 0, 1 - core, core))

    def fetch(at, which):
        _, shard = tile_of(at)
        slot = lax.rem(at, 2)
        return pltpu.make_async_copy(
            columns[which].at[:, pl.ds(pl.multiple_of(shard * BLOCK, BLOCK), BLOCK)],
            cols_s.at[slot, which], cols_sem.at[slot, which],
        )

    def far(hop):
        return (flipped(hop, core), line)

    def giving(hop):
        return remote_copy(
            give.at[hop], took.at[hop], give_sem.at[hop], took_sem.at[hop], (partner, line)
        )

    def sending(hop):
        return remote_copy(
            mine.at[hop - 1], came.at[hop - 1], send_sem.at[hop - 1], recv_sem.at[hop - 1], far(hop)
        )

    def passing(hop):
        columns = pl.ds(0, split) if hop == 1 else pl.ds(split, total_s.shape[1] - split)
        return remote_copy(
            mine.at[2, :, columns], passed.at[:, columns], pass_sem.at[0, hop - 1],
            pass_sem.at[1, hop - 1], far(hop),
        )

    def sgiving(hop):
        return remote_copy(
            sgive.at[hop], stook.at[hop], sgive_sem.at[hop], stook_sem.at[hop], (partner, line)
        )

    def ssending(hop):
        return remote_copy(
            smine.at[hop - 1], scame.at[hop - 1], ssend_sem.at[hop - 1], srecv_sem.at[hop - 1], far(hop)
        )

    pack_pass = remote_copy(pack, pack_took, pack_sem.at[0, 0], pack_sem.at[1, 0], (partner, line))
    ssum_pass = remote_copy(ssum, ssum_took, ssum_sem.at[0, 0], ssum_sem.at[1, 0], (partner, line))

    def pack_send(hop):
        return remote_copy(
            pack_sum, pack_slots.at[chip], pack_sem.at[0, hop], pack_sem.at[1, hop], far(hop)
        )

    def ssum_send(hop):
        return remote_copy(
            ssum_sum, ssum_slots.at[chip], ssum_sem.at[0, hop], ssum_sem.at[1, hop], far(hop)
        )

    def rows_at(ref, at):
        return ref.at[pl.ds(pl.multiple_of(at * GROUP, GROUP), GROUP), :]

    def handing(hop):
        owner = lax.rem(line + hop, tp_size)
        return remote_copy(
            rows_at(parts[late], owner), slots_s.at[line], part_send.at[hop - 1],
            part_recv.at[hop - 1], (me, owner),
        )

    late = micro - 1

    def own_part():
        return pltpu.make_async_copy(rows_at(parts[late], line), own_s, own_sem.at[late])

    def ready(at):
        length = raws[at].shape[0]
        return pltpu.make_async_copy(
            parts[at], whole_s.at[pl.ds(at * length, length), :], own_sem.at[at]
        )

    def raw_copy(at):
        length = raws[at].shape[0]
        return pltpu.make_async_copy(
            raws[at], raw_s.at[pl.ds(at * length, length), :], raw_sem.at[at]
        )

    groups = raws[0].shape[0] // GROUP

    def spreading(hop):
        block = rows_at(whole_s, late * groups + line)
        return remote_copy(
            sum_s, block, whole_send.at[hop - 1], whole_recv.at[hop - 1],
            (me, lax.rem(line + hop, tp_size)),
        )

    @pl.when(step == 0)
    def _():
        for which in range(4):
            fetch(step, which).start()
        own_part().start()
        for at in range(micro):
            raw_copy(at).start()
            if at != late:
                ready(at).start()
        greet(
            [far(hop) for hop in range(1, chips)] + [(partner, line)]
            + [(me, lax.rem(line + hop, tp_size)) for hop in range(1, tp_size)]
        )
        for hop in range(1, tp_size):
            handing(hop).start()
        for load in loads:
            load.start()
        pack[0:8, :] = pieces[0][...] + pieces[1][...]
        pack[8:16, :] = jnp.zeros((8, pack.shape[1]), F32)
        pack[8:16, 0:128] = pieces[2][...] + pieces[3][...]
        pack_pass.start()

    @pl.when(step + 1 < count)
    def _():
        for which in range(4):
            fetch(step + 1, which).start()

    @pl.when((step + 1 >= count) & (step + 1 < steps))
    def _():
        for which in range(2):
            fetch(step + 1, which).start()

    for which in range(2):
        fetch(step, which).wait()

    @pl.when(step < count)
    def _():
        for which in range(2, 4):
            fetch(step, which).wait()

    slot = lax.rem(step, 2)
    hop, _ = tile_of(step)
    even = lax.rem(step, 2) == 0

    def tile(which):
        sides = (0, 1) if which < 3 else (2, 3)
        return mm_tn(cols_s[slot, sides[0]], lows[2 * which][...]) + mm_tn(
            cols_s[slot, sides[1]], lows[2 * which + 1][...]
        )

    @pl.when((step < count) & even)
    def _():
        at = 0
        for which, width in enumerate(widths):

            @pl.when(step == 0)
            def _():
                loads[2 * which].wait()
                loads[2 * which + 1].wait()

            give[hop, :, at : at + width] = tile(which).astype(BF16)
            at += width
        giving(hop).start()

    @pl.when((step < count) & jnp.logical_not(even))
    def _():
        at = 0
        for which, width in enumerate(widths):
            total_s[:, at : at + width] = tile(which)
            at += width
        giving(hop).wait_recv()
        total_s[...] += took[hop].astype(F32)

        @pl.when(hop == 3)
        def _():
            mine[2] = total_s[...].astype(BF16)
            passing(1).start()
            passing(2).start()

        @pl.when(hop == 0)
        def _():
            kept_s[...] = total_s[...]

        @pl.when(hop == 1)
        def _():
            passing(2).wait_recv()
            total_s[:, split:] += passed[:, split:].astype(F32)
            mine[0] = total_s[...].astype(BF16)
            sending(1).start()

        @pl.when(hop == 2)
        def _():
            passing(1).wait_recv()
            total_s[:, :split] += passed[:, :split].astype(F32)
            mine[1] = total_s[...].astype(BF16)
            sending(2).start()

    @pl.when(step == 1)
    def _():
        pack_pass.wait()
        pack_sum[...] = pack[...] + pack_took[...]
        pack_slots[chip] = pack_sum[...]
        for other in range(1, chips):
            pack_send(other).start()

    @pl.when(step == 5)
    def _():
        own_part().wait()
        slots_s[line] = own_s[...]
        for hop in range(1, tp_size):
            handing(hop).wait()
        total = slots_s[0].astype(F32)
        for other in range(1, tp_size):
            total = total + slots_s[other].astype(F32)
        sum_s[...] = total.astype(BF16)
        mine_rows = rows_at(whole_s, late * groups + line)
        mine_rows[...] = sum_s[...]
        for hop in range(1, tp_size):
            spreading(hop).start()

    @pl.when(step == count - 1)
    def _():
        for at in range(micro):
            raw_copy(at).wait()
            if at != late:
                ready(at).wait()
        for hop in range(1, tp_size):
            spreading(hop).wait()
        ssum[...] = jnp.zeros(ssum.shape, F32)
        taps, bias = staps_ref[...], sbias_ref[...]

        def state_group(turn, carry):
            group = micro * groups - 1 - turn
            at = pl.multiple_of(group * GROUP, GROUP)
            cols = cols_ref[pl.ds(at, GROUP), :]
            vbuf[HALO : HALO + GROUP, :] = raw_s[pl.ds(at, GROUP), :]
            ahead = pl.multiple_of(jnp.maximum(group * (GROUP // HALO) - 1, 0) * HALO, HALO)
            vbuf[0:HALO, :] = raw_s[pl.ds(ahead, HALO), :]
            moved = shifted_values(vbuf, cols)
            conv = conv_of(moved, taps, bias)
            sig = jax.nn.sigmoid(conv)
            grad = whole_s[pl.ds(at, GROUP), :].astype(F32) * (sig * (1.0 + conv * (1.0 - sig)))
            gcbuf[GROUP : GROUP + HALO, :] = gcbuf[0:HALO, :]
            gcbuf[0:GROUP, :] = grad
            back = taps[0:1, :] * grad
            for offset in range(1, CONV):
                up = jnp.where(
                    cols[:, 2 + offset : 3 + offset] > 0.0, gcbuf[offset : offset + GROUP, :], 0.0
                )
                back = back + taps[offset : offset + 1, :] * up
            low_s[pl.ds(at, GROUP), :] = back.astype(BF16)
            for offset in range(CONV):
                ssum[offset : offset + 1, :] += jnp.sum(grad * moved[offset], axis=0, keepdims=True)
            ssum[CONV : CONV + 1, :] += jnp.sum(grad, axis=0, keepdims=True)
            return carry

        lax.fori_loop(0, micro * groups, state_group, 0)
        ssum_pass.start()
        for at in range(micro):
            low_out[at] = low_s[pl.ds(pl.multiple_of((at * groups + line) * GROUP, GROUP), GROUP), :]

    def state_tile():
        length = groups * GROUP
        return mm_tn(cols_s[slot, 0], low_s[0:length, :]) + mm_tn(
            cols_s[slot, 1], low_s[length : 2 * length, :]
        )

    @pl.when((step >= count) & even)
    def _():
        sgive[hop] = state_tile().astype(BF16)
        sgiving(hop).start()

    @pl.when((step >= count) & jnp.logical_not(even))
    def _():
        stotal[...] = state_tile()
        sgiving(hop).wait_recv()
        stotal[...] += stook[hop].astype(F32)

        @pl.when(hop == 0)
        def _():
            skept_s[...] = stotal[...]

        @pl.when(hop > 0)
        def _():
            smine[hop - 1] = stotal[...].astype(BF16)
            ssending(hop).start()

    @pl.when(step == count + 1)
    def _():
        ssum_pass.wait()
        ssum_sum[...] = ssum[...] + ssum_took[...]
        ssum_slots[chip] = ssum_sum[...]
        for other in range(1, chips):
            ssum_send(other).start()

    @pl.when(step == steps - 1)
    def _():
        for sends, slots, out in ((pack_send, pack_slots, pack_out), (ssum_send, ssum_slots, ssum_out)):
            for other in range(1, chips):
                sends(other).wait()
            total = slots[0]
            for other in range(1, chips):
                total = total + slots[other]
            out[...] = total
        for other in (1, 2):
            sending(other).wait_recv()
            kept_s[...] += came[other - 1].astype(F32)
        for other in range(1, chips):
            ssending(other).wait_recv()
            skept_s[...] += scame[other - 1].astype(F32)
        state_out[...] = skept_s[...]
        at = 0
        for which, width in enumerate(widths):
            part = kept_s[:, at : at + width]
            outs[which][...] = part if which < 3 else jnp.transpose(part)
            at += width
        for other in (1, 2):
            passing(other).wait_send()
            sending(other).wait_send()
        for other in range(1, chips):
            ssending(other).wait_send()
        for other in range(chips):
            giving(other).wait_send()
            sgiving(other).wait_send()


def tail_call(count, tp_size, inputs, cotans, lows, parts, raws, cols, staps, sbias, pieces):
    micro, length = len(inputs), inputs[0].shape[0]
    chips = count // 2
    order = [low[which] for which in range(4) for low in lows]
    widths = [low.shape[1] for low in order[::2]]
    total, narrow = sum(widths), 2 * STATE
    packed = (16, pieces[0].shape[1])
    hbm = pl.BlockSpec(memory_space=pl.ANY)
    full = lambda array: pl.BlockSpec(array.shape, lambda i: (0,) * array.ndim, pipeline_mode=pl.Buffered(1))
    out_dims = [(BLOCK, width) for width in widths[:3]] + [(widths[3], BLOCK), (BLOCK, narrow)]
    out_shapes = [shape(dims) for dims in out_dims] + [
        shape(packed), shape((8, narrow)), shape((micro, GROUP, narrow), BF16)
    ]
    dma = lambda *dims: pltpu.SemaphoreType.DMA(dims)
    return pl.pallas_call(
        partial(tail_kernel, chips, tp_size, micro, widths),
        grid=(2 * count,),
        in_specs=[hbm] * 16 + [full(each) for each in (cols, staps, sbias) + pieces],
        out_specs=[full(each) for each in out_shapes],
        out_shape=out_shapes,
        scratch_shapes=[
            pltpu.VMEM((2, 4, length, BLOCK), BF16),
            pltpu.VMEM((chips, BLOCK, total), BF16),
            pltpu.VMEM((chips, BLOCK, total), BF16),
            pltpu.VMEM((3, BLOCK, total), BF16),
            pltpu.VMEM((2, BLOCK, total), BF16),
            pltpu.VMEM((BLOCK, total), BF16),
            pltpu.VMEM((BLOCK, total), F32),
            pltpu.VMEM((BLOCK, total), F32),
            pltpu.VMEM((chips, BLOCK, narrow), BF16),
            pltpu.VMEM((chips, BLOCK, narrow), BF16),
            pltpu.VMEM((chips - 1, BLOCK, narrow), BF16),
            pltpu.VMEM((chips - 1, BLOCK, narrow), BF16),
            pltpu.VMEM((BLOCK, narrow), F32),
            pltpu.VMEM((BLOCK, narrow), F32),
            pltpu.VMEM(packed, F32),
            pltpu.VMEM(packed, F32),
            pltpu.VMEM(packed, F32),
            pltpu.VMEM((chips,) + packed, F32),
            pltpu.VMEM((8, narrow), F32),
            pltpu.VMEM((8, narrow), F32),
            pltpu.VMEM((8, narrow), F32),
            pltpu.VMEM((chips, 8, narrow), F32),
            pltpu.VMEM((micro * length, narrow), F32),
            pltpu.VMEM((GROUP, narrow), BF16),
            pltpu.VMEM((tp_size, GROUP, narrow), BF16),
            pltpu.VMEM((micro * length, narrow), BF16),
            pltpu.VMEM((GROUP, narrow), BF16),
            pltpu.VMEM((micro * length, narrow), BF16),
            pltpu.VMEM((GROUP + HALO, narrow), F32),
            pltpu.VMEM((GROUP + HALO, narrow), F32),
            dma(2, 4), dma(chips), dma(chips), dma(2), dma(2),
            dma(chips), dma(chips), dma(chips - 1), dma(chips - 1),
            dma(2, 2), dma(2, chips), dma(2, chips), dma(micro), dma(micro),
            dma(tp_size - 1), dma(tp_size - 1), dma(tp_size - 1), dma(tp_size - 1),
        ] + [pltpu.VMEM(low.shape, BF16) for low in order] + [dma(len(order))],
        compiler_params=pltpu.CompilerParams(
            collective_id=6, has_side_effects=True, vmem_limit_bytes=62 << 20
        ),
        cost_estimate=pl.CostEstimate(
            flops=4 * length * BLOCK * count * total, bytes_accessed=250 << 20, transcendentals=0
        ),
        name="weight_gradients",
    )(*inputs, *cotans, *order, *parts, *raws, cols, staps, sbias, *pieces)


def rows_kernel(
    sum0, sum1, low_ref, state_w, rows_ref, cot_ref, gain_ref, made0, made1, scale0, scale1,
    hidden_out, block_out, gain_out,
):
    step = pl.program_id(0)
    half = pl.num_programs(0) // 2
    gain = gain_ref[...]

    def work(summed, made, scale_ref):
        grad = summed[...].astype(F32) + mm_nt(low_ref[0], state_w[...])
        rows = rows_ref[0].astype(F32)
        inv_root = lax.rsqrt(jnp.mean(rows * rows, axis=1, keepdims=True) + EPSILON)
        part = jnp.sum(grad * (rows * inv_root), axis=0, keepdims=True)
        normed = grad * gain
        inner = jnp.mean(normed * rows, axis=1, keepdims=True)
        back = inv_root * normed - rows * (inv_root * inv_root * inv_root * inner)
        hidden_out[0] = (cot_ref[0].astype(F32) + back).astype(BF16)
        block_out[0] = (rows + made[...] * scale_ref[:, 0:1]).astype(BF16)
        width = gain_out.shape[1]
        for at in range(gain_out.shape[0]):
            piece = part[:, at * width : (at + 1) * width]

            @pl.when(step == 0)
            def _():
                gain_out[at : at + 1, :] = piece

            @pl.when(step > 0)
            def _():
                gain_out[at : at + 1, :] += piece

    @pl.when(step < half)
    def _():
        work(sum0, made0, scale0)

    @pl.when(step >= half)
    def _():
        work(sum1, made1, scale1)


def rows_call(sums, lows, state_w, rows, cotan, gain, made, scales):
    micro, length, model = rows.shape
    tiles = 2
    tile = length // tiles
    both = lambda width: pl.BlockSpec((1, tile, width), lambda i: (i // tiles, i % tiles, 0))
    former_of = lambda width: pl.BlockSpec((tile, width), lambda i: (jnp.minimum(i, tiles - 1), 0))
    latter_of = lambda width: pl.BlockSpec((tile, width), lambda i: (jnp.maximum(i - tiles, 0), 0))
    former, latter = former_of(model), latter_of(model)
    full = lambda dims: pl.BlockSpec(dims, lambda i: (0, 0))
    return pl.pallas_call(
        rows_kernel,
        grid=(micro * tiles,),
        in_specs=[
            former, latter, both(2 * STATE), full(state_w.shape), both(model), both(model),
            full(gain.shape), former, latter, former_of(128), latter_of(128),
        ],
        out_specs=[both(model), both(model), full((8, model // 8))],
        out_shape=[shape(rows.shape, BF16), shape(rows.shape, BF16), shape((8, model // 8))],
        compiler_params=pltpu.CompilerParams(vmem_limit_bytes=50 << 20),
        cost_estimate=pl.CostEstimate(flops=1 << 30, bytes_accessed=18 << 20, transcendentals=0),
        name="finish_rows",
    )(*sums, lows, state_w, rows, cotan, gain, *made, *scales)


def gain_kernel(
    tp_size, count, part, gain_out, line_slots, line_sum, slots, send_sem, recv_sem, far_send, far_recv,
):
    me, column = lax.axis_index("tp"), lax.axis_index("fsdp")
    greet(
        [(column, lax.rem(me + hop, tp_size)) for hop in range(1, tp_size)]
        + [(lax.rem(column + hop, count), me) for hop in range(1, count)]
    )
    line_slots[me] = part[...]
    copies = [
        remote_copy(
            part, line_slots.at[me], send_sem.at[hop - 1], recv_sem.at[hop - 1],
            (column, lax.rem(me + hop, tp_size)),
        )
        for hop in range(1, tp_size)
    ]
    for copy in copies:
        copy.start()
    for copy in copies:
        copy.wait()
    total = line_slots[0]
    for at in range(1, tp_size):
        total = total + line_slots[at]
    line_sum[...] = total
    slots[column] = total
    copies = [
        remote_copy(
            line_sum, slots.at[column], far_send.at[hop - 1], far_recv.at[hop - 1],
            (lax.rem(column + hop, count), me),
        )
        for hop in range(1, count)
    ]
    for copy in copies:
        copy.start()
    for copy in copies:
        copy.wait()
    total = slots[0]
    for at in range(1, count):
        total = total + slots[at]
    gain_out[...] = total


def gain_call(tp_size, count, part):
    vmem = pl.BlockSpec(memory_space=pltpu.VMEM)
    return pl.pallas_call(
        partial(gain_kernel, tp_size, count),
        in_specs=[vmem],
        out_specs=vmem,
        out_shape=shape(part.shape),
        scratch_shapes=[
            pltpu.VMEM((tp_size,) + part.shape, F32), pltpu.VMEM(part.shape, F32),
            pltpu.VMEM((count,) + part.shape, F32),
            pltpu.SemaphoreType.DMA((tp_size - 1,)), pltpu.SemaphoreType.DMA((tp_size - 1,)),
            pltpu.SemaphoreType.DMA((count - 1,)), pltpu.SemaphoreType.DMA((count - 1,)),
        ],
        compiler_params=pltpu.CompilerParams(
            collective_id=7, has_side_effects=True, vmem_limit_bytes=32 << 20
        ),
        cost_estimate=pl.CostEstimate(flops=0, bytes_accessed=1 << 20, transcendentals=0),
        name="gain_sum",
    )(part)


def unpack_kernel(heads, pack_ref, ssum_ref, rate_ref, gain, skip, conv, bias, sconv, sbias, step, decay):
    gain[...] = pack_ref[0:1, :]
    lanes = pack_ref.shape[1]
    place = (iota((lanes, 128), 0) // HEAD_DIM == iota((lanes, 128), 1)).astype(F32)
    sums = mm(pack_ref[0:8, :], place, PRECISE)
    skip[...] = sums[1:2, :heads]
    conv[...] = pack_ref[2 : 2 + CONV, :]
    bias[...] = pack_ref[2 + CONV : 3 + CONV, :]
    sconv[...] = ssum_ref[0:CONV, :]
    sbias[...] = ssum_ref[CONV : CONV + 1, :]
    step[...] = pack_ref[8:9, :heads]
    decay[...] = pack_ref[9:10, :heads] * rate_ref[:, :heads]


def unpack_call(pack, ssum, rate, heads):
    inner = pack.shape[1]
    vmem = pl.BlockSpec(memory_space=pltpu.VMEM)
    dims = [(1, inner), (1, heads), (CONV, inner), (1, inner), (CONV, 2 * STATE), (1, 2 * STATE),
            (1, heads), (1, heads)]
    return pl.pallas_call(
        partial(unpack_kernel, heads), in_specs=[vmem] * 3, out_specs=[vmem] * 8,
        out_shape=[shape(each) for each in dims], name="small_gradients",
        cost_estimate=pl.CostEstimate(flops=0, bytes_accessed=1 << 18, transcendentals=0),
    )(pack, ssum, rate)


def shift_down(values, offset):
    return jnp.pad(values, ((offset, 0), (0, 0)))[: values.shape[0]]


def shift_up(values, offset):
    return jnp.pad(values, ((0, offset), (0, 0)))[offset:]


def document_columns(seg_row):
    length = seg_row.shape[0]
    previous = jnp.concatenate([jnp.full((1,), -1, seg_row.dtype), seg_row[GROUP - 1 : -1 : GROUP]])
    last = seg_row[GROUP - 1 :: GROUP]
    columns = []
    for offset in range(1, CONV):
        columns.append(jnp.pad(seg_row, (offset, 0), constant_values=-1)[:length] == seg_row)
    for offset in range(1, CONV):
        columns.append(jnp.pad(seg_row, (0, offset), constant_values=-1)[offset:] == seg_row)
    columns.append(seg_row == jnp.repeat(previous, GROUP))
    columns.append(seg_row == jnp.repeat(last, GROUP))
    columns.append(jnp.repeat(last == previous, GROUP))
    columns.append(seg_row)
    columns = [column.astype(F32) for column in columns]
    return jnp.stack(columns + [columns[0]] * (16 - len(columns)), axis=1)


def state_gradient(grad_bc, state_raw, taps, bias, cols):
    moved = [state_raw]
    for offset in range(1, CONV):
        moved.append(shift_down(state_raw, offset) * cols[:, offset - 1 : offset])
    conv = bias
    for offset in range(CONV):
        conv = conv + taps[offset][None, :] * moved[offset]
    sig = jax.nn.sigmoid(conv)
    grad_conv = grad_bc * (sig * (1.0 + conv * (1.0 - sig)))
    grad_raw = taps[0][None, :] * grad_conv
    for offset in range(1, CONV):
        grad_raw = grad_raw + taps[offset][None, :] * (
            shift_up(grad_conv, offset) * cols[:, 2 + offset : 3 + offset]
        )
    grad_taps = jnp.stack([jnp.sum(grad_conv * each, axis=0) for each in moved])
    return grad_raw.astype(BF16), grad_taps, jnp.sum(grad_conv, axis=0)


def local(
    hidden_in, segment_ids, cotangent, norm_gain, proj_gate, proj_value, proj_state, proj_step,
    conv_value, conv_value_bias, conv_state, conv_state_bias, step_bias, decay_log, skip_gain,
    gate_gain, proj_out,
):
    micro = hidden_in.shape[0]
    heads = step_bias.shape[0]
    rows_here = hidden_in.shape[2]
    tp_size = lax.axis_size("tp")
    me = lax.axis_index("tp")
    decay_rate = -jnp.exp(decay_log)
    pad_heads = lambda values: jnp.pad(values, (0, 128 - heads))[None, :]
    rate = pad_heads(decay_rate)
    step_bias_line = pad_heads(step_bias)
    skip = jnp.repeat(skip_gain, HEAD_DIM)[None, :]
    gain = gate_gain[None, :]
    taps, bias = conv_value, conv_value_bias[None, :]
    staps, sbias = conv_state, conv_state_bias[None, :]

    input_rows = []
    for at in range(micro):
        rows_float = hidden_in[at, 0].astype(F32)
        inv_root = lax.rsqrt(jnp.mean(rows_float * rows_float, axis=-1, keepdims=True) + EPSILON)
        input_rows.append((rows_float * inv_root * norm_gain).astype(BF16))

    def gather_tp(values, *after):
        values = lax.optimization_barrier((values,) + after)[0]
        return lax.all_gather(values, "tp", axis=0, tiled=True)

    def scatter_tp(values, *after):
        values = lax.optimization_barrier((values,) + after)[0]
        return lax.psum_scatter(values, "tp", scatter_dimension=0, tiled=True)

    inputs = [gather_tp(input_rows[0])]
    fsdp_size = lax.axis_size("fsdp")
    model = hidden_in.shape[3]
    aligned = proj_out.shape[1] % 128 == 0
    axes = (0, 0, 0, 0, 1 if aligned else 2)
    step_block = jnp.pad(proj_step, ((0, 0), (0, 128 - heads)))
    gate_w, value_w, state_w, step_w, out_w = gather_call(
        fsdp_size, (proj_gate, proj_value, proj_state, step_block, proj_out), axes
    )
    if not aligned:
        out_w = jnp.transpose(out_w, (1, 0, 2)).reshape(-1, model)
    inputs.append(gather_tp(input_rows[1], inputs[0], step_w))
    forward_weights = (gate_w, value_w, state_w, step_w, out_w)
    vectors = (taps, bias, staps, sbias, step_bias_line, rate, skip)
    columns = [document_columns(segment_ids[at, 0]) for at in range(micro)]
    seg_lines = [segment_ids[at, 0].astype(F32)[None, :] for at in range(micro)]
    quick = [0, 2, 4, 6, 7, 9, 11, 13, 14] + [15] * 11
    paces = {
        4: [0, 1, 3, 4, 4, 5, 6, 8, 9, 11, 12, 13, 15, 16, 17, 18, 19, 19, 19, 19],
        5: [0, 0, 4, 4, 4, 5, 7, 8, 10, 11, 13, 14, 17, 18, 19, 19],
    }

    def forward(at, hosted):
        return forward_call(
            inputs[at], forward_weights, vectors, gain, columns[at], seg_lines[at], hosted, quick
        )

    def backward(at, hosted, collective):
        done = backward_call(
            saved[at], cotans[at], (gate_w, value_w, step_w, out_w), (taps, bias, rate, skip),
            gain, columns[at], seg_lines[at], hosted, paces[collective], collective,
        )
        scales.append(done[8])
        return done

    scales, produced, summed = [], [], []
    saved = [forward(0, Hosted(tp_size))]
    *kept, made_sum, cotan = forward(1, Hosted(tp_size, saved[0][8], cotangent[0, 0]))
    saved.append(kept)
    produced.append(made_sum)
    cotans = [cotan]
    *former, made_sum, cotan = backward(0, Hosted(tp_size, saved[1][8], cotangent[1, 0]), 4)
    produced.append(made_sum)
    cotans.append(cotan)
    early = lax.psum(former[4], "tp")
    *latter, gin_sum = backward(1, Hosted(tp_size, former[5]), 5)
    summed = [gin_sum, scatter_tp(latter[5])]
    lows = [[each[1], each[2], each[3], each[0]] for each in (former, latter)]
    parts, raws = (early, latter[4]), [each[4] for each in saved]
    pieces = (former[6], latter[6], former[7], latter[7])
    if aligned and fsdp_size == 8 and model // fsdp_size == BLOCK:
        grad_gate, grad_value, grad_step, grad_out, grad_state, pack, state_sum, mine = tail_call(
            fsdp_size, tp_size, inputs, cotans, lows, parts, raws, jnp.concatenate(columns, axis=0),
            staps, sbias, pieces,
        )
    else:
        mine, state_sum = [], 0.0
        for at in range(micro):
            grad_bc = (parts[at] if at == 0 else lax.psum(parts[at], "tp")).astype(F32)
            low_state, grad_staps, grad_sbias = state_gradient(
                grad_bc, raws[at], staps, sbias, columns[at]
            )
            mine.append(lax.dynamic_slice_in_dim(low_state, me * rows_here, rows_here, axis=0))
            lows[at].insert(2, low_state)
            state_sum = state_sum + jnp.concatenate(
                [grad_staps, grad_sbias[None, :], jnp.zeros((3, 2 * STATE), F32)], axis=0
            )
        mine = jnp.stack(mine)
        grad_out = outer_call([low[4] for low in lows], cotans)
        grad_gate, grad_value, grad_state, grad_step = weight_call(inputs, [low[:4] for low in lows])
        if not aligned:
            grad_out = jnp.transpose(grad_out.reshape(-1, fsdp_size, proj_out.shape[1]), (1, 0, 2))
        grad_gate, grad_value, grad_state, grad_step, grad_out = scatter_call(
            fsdp_size, (grad_gate, grad_value, grad_state, grad_step, grad_out), axes
        )
        narrow = jnp.pad(pieces[2] + pieces[3], ((0, 0), (0, proj_gate.shape[1] - 128)))
        pack = jnp.concatenate([pieces[0] + pieces[1], narrow], axis=0)
        pack, state_sum = lax.psum((pack, state_sum), "fsdp")
    grad_step = grad_step[:, :heads]
    grad_hidden, block_rows, gain_part = rows_call(
        summed, mine, state_w, hidden_in[:, 0], cotangent[:, 0], norm_gain[None, :],
        produced, scales,
    )
    gain_total = gain_call(tp_size, fsdp_size, gain_part)
    grad_gain, grad_skip, grad_conv, grad_bias, grad_sconv, grad_sbias, grad_in, grad_decay = (
        unpack_call(pack, state_sum, rate, heads)
    )
    return (
        block_rows[:, None],
        grad_hidden[:, None],
        gain_total.reshape(-1),
        grad_gate,
        grad_value,
        grad_state,
        grad_step,
        grad_conv,
        grad_bias.reshape(-1),
        grad_sconv,
        grad_sbias.reshape(-1),
        grad_in.reshape(-1),
        grad_decay.reshape(-1),
        grad_skip.reshape(-1),
        grad_gain.reshape(-1),
        grad_out,
    )


def solution(mesh):
    in_specs = (
        P(None, "fsdp", "tp", None), P(None, "fsdp", None), P(None, "fsdp", "tp", None), P(),
        P("fsdp", "tp"), P("fsdp", "tp"), P("fsdp", None), P("fsdp", "tp"), P(None, "tp"), P("tp"),
        P(), P(), P("tp"), P("tp"), P("tp"), P("tp"), P("tp", "fsdp"),
    )
    out_specs = (
        P(None, "fsdp", "tp", None), P(None, "fsdp", "tp", None), P(), P("fsdp", "tp"),
        P("fsdp", "tp"), P("fsdp", None), P("fsdp", "tp"), P(None, "tp"), P("tp"), P(), P(),
        P("tp"), P("tp"), P("tp"), P("tp"), P("tp", "fsdp"),
    )
    return jax.shard_map(local, mesh=mesh, in_specs=in_specs, out_specs=out_specs, check_vma=False)
```
